32 devices in a mesh: dp: 32 (over z, y, x, core).
Axes of the slice: x: 2, y: 2, z: 4, core: 2. Of those that a mesh axis runs over, the one named last changes fastest.
Arguments:
- tokens: bfloat16 [8192, 1536], P('dp'), may hold values from -6 to 6
- teacher: bfloat16 [8192, 1536], P('dp'), may hold values from -6 to 6
- valid_mask: int32 [8192], P('dp'), may hold values from 0 to 1, as said below
- w_query: bfloat16 [1536, 1536], P('dp'), may hold values from -0.15625 to 0.15625
- key_weight_matrix: bfloat16 [1536, 768], P('dp'), may hold values from -0.15625 to 0.15625
- value_weight_matrix: bfloat16 [1536, 768], P('dp'), may hold values from -0.15625 to 0.15625
- w_output: bfloat16 [1536, 1536], P('dp'), may hold values from -1.25 to 1.25
- w_gate: bfloat16 [1536, 4096], P('dp'), may hold values from -0.15625 to 0.15625
- w_up: bfloat16 [1536, 4096], P('dp'), may hold values from -0.15625 to 0.15625
- w_down: bfloat16 [4096, 1536], P('dp'), may hold values from -0.09375 to 0.09375
- attn_gain: bfloat16 [1536], P('dp'), may hold values from 0.5 to 1.5
- ffn_gain: bfloat16 [1536], P('dp'), may hold values from 0.5 to 1.5
Outputs:
- out_act: bfloat16 [8192, 1536], P('dp')
- loss: float32 [], replicated
- input_grad: bfloat16 [8192, 1536], P('dp')
- grad_w_query: float32 [1536, 1536], P('dp')
- grad_w_key: float32 [1536, 768], P('dp')
- grad_w_value: float32 [1536, 768], P('dp')
- grad_w_output: float32 [1536, 1536], P('dp')
- grad_w_gate: float32 [1536, 4096], P('dp')
- grad_w_up: float32 [1536, 4096], P('dp')
- grad_w_down: float32 [4096, 1536], P('dp')
- grad_attn_gain: float32 [1536], P('dp')
- grad_ffn_gain: float32 [1536], P('dp')
The draws below stay inside these ranges and needn't reach their ends.
Inputs may be any that keep to these rules, and one draw needn't show every extreme that they name: The first token of every sequence (rows that are multiples of 128) has valid_mask 1.
All inputs are finite; a program needn't handle non-finite values.
Results may differ from the reference program's by a relative error of at most 0.012.
Values may be sent and summed in bfloat16 or wider, within the bound.
No kernel may reach another device: no remote copies, remote signals or barrier semaphores. Data moves between devices by JAX's collectives and lax.ppermute only.
A program may use at most 320 MiB of HBM per device.

```python
import math
import jax
import jax.numpy as jnp
from jax import lax

MODEL_WIDTH = 1536
QUERY_HEAD_COUNT = 16
KEY_VALUE_HEADS = 8
HEAD_SIZE = 96
FF = 4096
SEQ = 128
TOKENS = 8192


def draw_valid_mask(key, part):
    row_index = jnp.arange(TOKENS, dtype=jnp.int32)
    seq_number = row_index // SEQ
    keep_limit = 250 + 650 * seq_number // (TOKENS // SEQ)
    dice_roll = jax.random.randint(key, (TOKENS,), 0, 1000, dtype=jnp.int32)
    seq_start = row_index % SEQ == 0
    return jnp.where(seq_start | (dice_roll < keep_limit), 1, 0).astype(jnp.int32)


def strengthened(values, own_key, source, target, parts, factor):
    def block_of(dim):
        return (jnp.arange(values.shape[dim]) // (values.shape[dim] // parts)).reshape((-1,) + (1,) * (values.ndim - 1 - dim))

    near = jax.random.permutation(own_key, parts)[block_of(target)]
    second = (block_of(target) + parts // 2) % parts
    return jnp.where((block_of(source) == near) | (block_of(source) == second), factor * values, values)


def level_of(key, dims, split, least, top_value):
    loudness = 1.0
    for dim, parts in split:
        steps = jax.random.uniform(jax.random.fold_in(jax.random.fold_in(key, 6), dim), (parts,), jnp.float32, least / len(split), top_value / len(split))
        loudness = loudness * jnp.repeat(jnp.exp(steps), dims[dim] // parts).reshape((-1,) + (1,) * (len(dims) - 1 - dim))
    return loudness


def noise(rng, extent, scale, bound, cuts=(), kind=jnp.bfloat16):
    array = jax.random.normal(rng, extent, jnp.float32) * scale
    if len(cuts) > 0:
        array = level_of(rng, extent, cuts, -0.22, 0.18) * array
    return jnp.clip(array, min=-bound, max=bound).astype(kind)


def gaussian_with(rng, dims, spread, bound, cuts, heavy, kind=jnp.bfloat16):
    values = spread * jax.random.normal(rng, dims, jnp.float32)
    if cuts:
        values = values * level_of(rng, dims, cuts, -0.22, 0.18)
    return jnp.clip(strengthened(values, jax.random.fold_in(rng, 3), *heavy), -bound, bound).astype(kind)


def setup_inputs(seed: int = 0) -> dict:
    keys = jax.random.split(jax.random.key(seed), 13)
    tokens = gaussian_with(keys[0], (TOKENS, MODEL_WIDTH), 1.0, 6.0, ((0, 32),), (0, 1, 32, 2.75))
    teacher = noise(keys[1], (TOKENS, MODEL_WIDTH), 1.0, 6.0, ((0, 32),))
    valid_mask = draw_valid_mask(jax.random.fold_in(keys[12], 71), 0)
    w_query = noise(keys[3], (MODEL_WIDTH, MODEL_WIDTH), MODEL_WIDTH ** -0.5, 0.15625, ((0, 32),))
    key_weight_matrix = noise(keys[4], (MODEL_WIDTH, KEY_VALUE_HEADS * HEAD_SIZE), MODEL_WIDTH ** -0.5, 0.15625, ((0, 32),))
    value_weight_matrix = noise(keys[5], (MODEL_WIDTH, KEY_VALUE_HEADS * HEAD_SIZE), MODEL_WIDTH ** -0.5, 0.15625, ((0, 32),))
    w_output = noise(keys[6], (MODEL_WIDTH, MODEL_WIDTH), (max(2 * MODEL_WIDTH // SEQ, 1)) ** -0.5, 1.25, ((0, 32),))
    w_gate = noise(keys[7], (MODEL_WIDTH, FF), MODEL_WIDTH ** -0.5, 0.15625, ((0, 32),))
    w_up = noise(keys[8], (MODEL_WIDTH, FF), MODEL_WIDTH ** -0.5, 0.15625, ((0, 32),))
    w_down = noise(keys[9], (FF, MODEL_WIDTH), FF ** -0.5, 0.09375, ((0, 32),))
    attn_gain = jnp.clip(1.0 + 0.1 * jax.random.normal(keys[10], (MODEL_WIDTH,), jnp.float32), 0.5, 1.5).astype(jnp.bfloat16)
    ffn_gain = jnp.clip(1.0 + 0.1 * jax.random.normal(keys[11], (MODEL_WIDTH,), jnp.float32), 0.5, 1.5).astype(jnp.bfloat16)
    return {"tokens": tokens, "teacher": teacher, "valid_mask": valid_mask, "w_query": w_query, "key_weight_matrix": key_weight_matrix, "value_weight_matrix": value_weight_matrix, "w_output": w_output, "w_gate": w_gate, "w_up": w_up, "w_down": w_down, "attn_gain": attn_gain, "ffn_gain": ffn_gain}


EPSILON = 1e-05
ROPE_BASE = 100000.0
MASK_FILL = -1e+30

@jax.custom_vjp
def low(v):
    return lax.optimization_barrier(v.astype(jnp.bfloat16)).astype(jnp.float32)

@jax.custom_vjp
def low_back(v):
    return v

def low_keep(v):
    return (low(v), None)

def low_pass(kept, grad):
    return (grad,)

def back_keep(v):
    return (v, None)

def back_low(kept, grad):
    return (low(grad),)
low.defvjp(low_keep, low_pass)
low_back.defvjp(back_keep, back_low)

def rotation_tables(length, width):
    half_width = width // 2
    position = jnp.arange(length, dtype=jnp.float32)[:, None]
    freq_rate = ROPE_BASE ** (-2.0 * jnp.arange(half_width, dtype=jnp.float32) / width)
    angle_table = position * freq_rate[None, :]
    return (jnp.cos(angle_table)[:, None, :], jnp.sin(angle_table)[:, None, :])

def apply_rotary(heads_in, cosine_lookup, sine_lookup):
    half_width = heads_in.shape[-1] // 2
    left_part = heads_in[..., :half_width]
    right_part = heads_in[..., half_width:]
    return jnp.concatenate([left_part * cosine_lookup - right_part * sine_lookup, right_part * cosine_lookup + left_part * sine_lookup], axis=-1)

def rms_norm(field_in, gain_vec):
    return field_in * lax.rsqrt(lax.optimization_barrier(jnp.mean(field_in * field_in, axis=-1, keepdims=True)) + EPSILON) * gain_vec

def forward(inputs_f, w_query, key_weight_matrix, value_weight_matrix, w_output, w_gate, w_up, w_down, attn_gain, ffn_gain):
    high_prec = lax.Precision.HIGHEST
    sequence_count = inputs_f.shape[0]
    total_row_count = inputs_f.shape[1]
    head_groups = QUERY_HEAD_COUNT // KEY_VALUE_HEADS
    cosine_lookup, sine_lookup = rotation_tables(total_row_count, HEAD_SIZE)
    normed_in = low(rms_norm(inputs_f, attn_gain))
    query_raw = low_back(jnp.einsum('bsd,de->bse', normed_in, w_query, precision=high_prec))
    unrotated_keys = low_back(jnp.einsum('bsd,de->bse', normed_in, key_weight_matrix, precision=high_prec))
    value_rows = low(low_back(jnp.einsum('bsd,de->bse', normed_in, value_weight_matrix, precision=high_prec)))
    value_rows = value_rows.reshape(sequence_count, total_row_count, KEY_VALUE_HEADS, HEAD_SIZE)
    query_head_rows = low(apply_rotary(query_raw.reshape(sequence_count, total_row_count, QUERY_HEAD_COUNT, HEAD_SIZE), cosine_lookup, sine_lookup))
    query_head_rows = query_head_rows.reshape(sequence_count, total_row_count, KEY_VALUE_HEADS, head_groups, HEAD_SIZE)
    key_head_rows = low(apply_rotary(unrotated_keys.reshape(sequence_count, total_row_count, KEY_VALUE_HEADS, HEAD_SIZE), cosine_lookup, sine_lookup))
    score_scale = 1.0 / math.sqrt(HEAD_SIZE)
    raw_scores = low_back(jnp.einsum('bqhrd,bkhd->bhrqk', query_head_rows, key_head_rows, precision=high_prec) * score_scale)
    causal = jnp.arange(total_row_count)[:, None] >= jnp.arange(total_row_count)[None, :]
    scores = jnp.where(causal, raw_scores, MASK_FILL)
    attn_probs = jax.nn.softmax(scores, axis=-1)
    mixed_heads = jnp.einsum('bhrqk,bkhd->bqhrd', low(attn_probs), value_rows, precision=high_prec)
    mixed_heads = low(low_back(mixed_heads.reshape(sequence_count, total_row_count, MODEL_WIDTH)))
    hidden_res = inputs_f + low_back(jnp.einsum('bsd,de->bse', mixed_heads, w_output, precision=high_prec))
    normed_mid = low(rms_norm(hidden_res, ffn_gain))
    gate_pre = low_back(jnp.einsum('bsd,df->bsf', normed_mid, w_gate, precision=high_prec))
    up_pre = low_back(jnp.einsum('bsd,df->bsf', normed_mid, w_up, precision=high_prec))
    hidden_act = low(jax.nn.silu(gate_pre) * up_pre)
    return hidden_res + low_back(jnp.einsum('bsf,fd->bsd', hidden_act, w_down, precision=high_prec))

def reference(tokens, teacher, valid_mask, w_query, key_weight_matrix, value_weight_matrix, w_output, w_gate, w_up, w_down, attn_gain, ffn_gain):
    weight_list = tuple((weight.astype(jnp.float32) for weight in (w_query, key_weight_matrix, value_weight_matrix, w_output, w_gate, w_up, w_down, attn_gain, ffn_gain)))
    sequence_count = TOKENS // SEQ
    group_size = math.gcd(max(4096 // SEQ, 1), sequence_count)
    group_count = sequence_count // group_size
    token_groups = tokens.astype(jnp.float32).reshape(group_count, group_size, SEQ, MODEL_WIDTH)
    teacher_groups = teacher.astype(jnp.float32).reshape(group_count, group_size, SEQ, MODEL_WIDTH)
    mask_groups = valid_mask.astype(jnp.float32).reshape(group_count, group_size, SEQ)

    def scan_step(carry, scan_item):
        grad_acc, loss_total = carry
        inputs_f, target_f, mask_f = scan_item
        result, pull_back = jax.vjp(forward, inputs_f, *weight_list)
        residual_err = (result - target_f) * mask_f[..., None]
        pulled = pull_back(residual_err)
        grad_acc = tuple((acc_part + new_part for acc_part, new_part in zip(grad_acc, pulled[1:])))
        loss_total = loss_total + jnp.sum(residual_err * residual_err)
        return ((grad_acc, loss_total), (result.astype(jnp.bfloat16), pulled[0].astype(jnp.bfloat16)))
    start_acc = tuple((jnp.zeros(weight.shape, jnp.float32) for weight in weight_list))
    (grad_acc, loss_total), (results, input_grads) = lax.scan(scan_step, (start_acc, jnp.zeros((), jnp.float32)), (token_groups, teacher_groups, mask_groups))
    valid_count = jnp.sum(valid_mask).astype(jnp.float32)
    loss = loss_total / (valid_count * MODEL_WIDTH)
    return (results.reshape(TOKENS, MODEL_WIDTH), loss, input_grads.reshape(TOKENS, MODEL_WIDTH), grad_acc[0], grad_acc[1], grad_acc[2], grad_acc[3], grad_acc[4], grad_acc[5], grad_acc[6], grad_acc[7], grad_acc[8])
```

```python
import math

import jax
import jax.numpy as jnp
from jax import lax
from jax.sharding import PartitionSpec as P

QUERY_HEAD_COUNT = 16
KEY_VALUE_HEADS = 8
HEAD_SIZE = 96
SEQ = 128
EPSILON = 1e-05
ROPE_BASE = 100000.0
MASK_FILL = -1e30
LANES = 128
LONGEST_LINE = 8

BF = jnp.bfloat16
F32 = jnp.float32


def dot(a, b, dims):
    return lax.dot_general(a, b, (dims, ((), ())), preferred_element_type=F32)


def mm(a, b):
    return dot(a, b, ((1,), (0,)))


def mm_t(a, b):
    return dot(a, b, ((1,), (1,)))


def t_mm(a, b):
    return dot(a, b, ((0,), (0,)))


def swap(value, mask):
    n = lax.axis_size("dp")
    return lax.ppermute(value, "dp", [(i, i ^ mask) for i in range(n)])


def shift(value, step, direction):
    n = lax.axis_size("dp")
    planes = n // 8
    if direction > 0:
        pairs = [(i, i + 8) for i in range(n) if i // 8 >= step - 1 and i + 8 < n]
    else:
        pairs = [(i, i - 8) for i in range(n) if i // 8 <= planes - step and i >= 8]
    return lax.ppermute(value, "dp", pairs)


def collect_shift(value, step, direction):
    n = lax.axis_size("dp")
    planes = n // 8
    far = planes - step
    if direction > 0:
        pairs = [(i, i + 8) for i in range(n) if i + 8 * far < n and i + 8 < n]
    else:
        pairs = [(i, i - 8) for i in range(n) if i - 8 * far >= 0 and i >= 8]
    return lax.ppermute(value, "dp", pairs)


def column_groups(with_core):
    n = lax.axis_size("dp")
    planes = n // 8
    if with_core:
        return [[8 * z + 2 * p + c for z in range(planes) for c in range(2)] for p in range(4)]
    return [[8 * z + 2 * p + c for z in range(planes)] for p in range(4) for c in range(2)]


def z_gather(value, z):
    planes = lax.axis_size("dp") // 8
    if planes > LONGEST_LINE:
        return lax.all_gather(value, "dp", axis_index_groups=column_groups(False), axis=0)
    below, above = [], []
    up = down = value
    for step in range(1, planes):
        up = shift(up, step, 1)
        down = shift(down, step, -1)
        below.append(up)
        above.append(down)
    line = jnp.stack(below[::-1] + [value] + above)
    return lax.dynamic_slice_in_dim(line, planes - 1 - z, planes)


def z_reduce(parts, z):
    planes = lax.axis_size("dp") // 8
    if planes > LONGEST_LINE:
        return lax.psum_scatter(
            parts.astype(BF), "dp", axis_index_groups=column_groups(False), scatter_dimension=0
        ).astype(F32)

    def entry(k):
        return lax.dynamic_index_in_dim(parts, k, 0, keepdims=False)

    up = down = None
    for step in range(1, planes):
        far = planes - step
        send_up, send_down = entry(z + far), entry(z - far)
        if step > 1:
            send_up = send_up + up.astype(F32)
            send_down = send_down + down.astype(F32)
        up = collect_shift(send_up.astype(BF), step, 1)
        down = collect_shift(send_down.astype(BF), step, -1)
    own = entry(z)
    if planes > 1:
        own = own + up.astype(F32) + down.astype(F32)
    return own


def place(out, piece, where):
    return lax.dynamic_update_slice(out, piece, where)


def gather_rows(value, place_bits):
    z, y, x, c = place_bits
    planes = lax.axis_size("dp") // 8
    rows, columns = value.shape
    half = planes // 2
    own = z_gather(value, z)
    a, b = own[:half], own[half:]
    a_x = swap(a, 2)
    b_y = swap(b, 4)
    a_far = swap(jnp.stack([a, a_x]), 4)
    b_far = swap(jnp.stack([b, b_y]), 2)
    out = jnp.zeros((planes, 2, 2, 2, rows, columns), value.dtype)
    for core, move in ((c, lambda v: v), (1 - c, lambda v: swap(v, 1))):
        for piece, start, at_y, at_x in (
            (own, 0, y, x),
            (a_x, 0, y, 1 - x),
            (b_y, half, 1 - y, x),
        ):
            piece = move(piece)
            out = place(out, piece[:, None, None, None], (start, at_y, at_x, core, 0, 0))
        a_core, b_core = move(a_far), move(b_far)
        out = place(out, a_core[0][:, None, None, None], (0, 1 - y, x, core, 0, 0))
        out = place(out, a_core[1][:, None, None, None], (0, 1 - y, 1 - x, core, 0, 0))
        out = place(out, b_core[0][:, None, None, None], (half, y, 1 - x, core, 0, 0))
        out = place(out, b_core[1][:, None, None, None], (half, 1 - y, 1 - x, core, 0, 0))
    return out.reshape(planes * 8 * rows, columns)


def pick(parts, index, axis):
    return lax.dynamic_index_in_dim(parts, index, axis, keepdims=False)


def scatter_rows(partial, place_bits):
    z, y, x, c = place_bits
    planes = lax.axis_size("dp") // 8
    columns = partial.shape[1]
    parts = partial.reshape(planes, 2, 2, 2, -1, columns)
    half = planes // 2
    came = swap(pick(parts, 1 - c, 3).astype(BF), 1)
    parts = pick(parts, c, 3) + came.astype(F32)
    a, b = parts[:half], parts[half:]
    came_a = swap(pick(a, 1 - y, 1).astype(BF), 4)
    came_b = swap(pick(b, 1 - x, 2).astype(BF), 2)
    a = pick(a, y, 1) + came_a.astype(F32)
    b = pick(b, x, 2) + came_b.astype(F32)
    came_a = swap(pick(a, 1 - x, 1).astype(BF), 2)
    came_b = swap(pick(b, 1 - y, 1).astype(BF), 4)
    a = pick(a, x, 1) + came_a.astype(F32)
    b = pick(b, y, 1) + came_b.astype(F32)
    return z_reduce(jnp.concatenate([a, b]), z)


def split_gather(rows):
    half = rows.shape[0] // 2
    a, b = rows[:half], rows[half:]
    a_x = swap(a, 2)
    b_y = swap(b, 4)
    a_far = swap(jnp.concatenate([a, a_x]), 4)
    b_far = swap(jnp.concatenate([b, b_y]), 2)
    return (jnp.concatenate([a, a_x, b, b_y]), jnp.concatenate([a_far, b_far]))


def split_reduce(near, far):
    two = far.shape[0] // 2
    one = two // 2
    low = far.astype(BF)
    came_a = swap(low[:two], 4)
    came_b = swap(low[two:], 2)
    a = near[:two] + came_a.astype(F32)
    b = near[two:] + came_b.astype(F32)
    came_a = swap(a[one:].astype(BF), 2)
    came_b = swap(b[one:].astype(BF), 4)
    return jnp.concatenate([a[:one] + came_a.astype(F32), b[:one] + came_b.astype(F32)])


def total_of(value):
    n = lax.axis_size("dp")
    mask = 1
    while mask < n:
        value = value + swap(value, mask)
        mask *= 2
    return value


def rotation_tables(length, width):
    half_width = width // 2
    position = jnp.arange(length, dtype=F32)[:, None]
    freq_rate = ROPE_BASE ** (-2.0 * jnp.arange(half_width, dtype=F32) / width)
    angle_table = position * freq_rate[None, :]
    return (jnp.cos(angle_table)[:, None, :], jnp.sin(angle_table)[:, None, :])


def turn(heads_in, cosine_lookup, sine_lookup):
    half_width = heads_in.shape[-1] // 2
    left_part = heads_in[..., :half_width]
    right_part = heads_in[..., half_width:]
    return jnp.concatenate(
        [
            left_part * cosine_lookup - right_part * sine_lookup,
            right_part * cosine_lookup + left_part * sine_lookup,
        ],
        axis=-1,
    )


def norm_rows(field_in, gain_vec):
    inv_scale = lax.rsqrt(jnp.mean(field_in * field_in, axis=-1, keepdims=True) + EPSILON)
    return (field_in * inv_scale * gain_vec, inv_scale)


def norm_back(upstream, field_in, inv_scale, gain_vec):
    gain_grad = jnp.sum(upstream * field_in * inv_scale, axis=0)
    scaled_up = upstream * gain_vec
    field_grad = inv_scale * scaled_up - field_in * inv_scale**3 * jnp.mean(
        scaled_up * field_in, axis=-1, keepdims=True
    )
    return (gain_grad, field_grad)


def probabilities(query_heads, key_heads):
    score_scale = 1.0 / math.sqrt(HEAD_SIZE)
    raw_scores = (
        jnp.einsum("bqhrd,bkhd->bhrqk", query_heads, key_heads, preferred_element_type=F32)
        * score_scale
    )
    causal = jnp.arange(SEQ)[:, None] >= jnp.arange(SEQ)[None, :]
    scores = jnp.where(causal, raw_scores, MASK_FILL)
    row_max = jnp.max(scores, axis=-1, keepdims=True)
    weights = jnp.exp(scores - row_max)
    return weights / jnp.sum(weights, axis=-1, keepdims=True)


def ffn_forward(rows, w_gate, w_up, w_down):
    gate_pre = mm(rows, w_gate)
    up_pre = mm(rows, w_up)
    hidden = (jax.nn.silu(gate_pre) * up_pre).astype(BF)
    return (mm(hidden, w_down), gate_pre, up_pre, hidden)


def ffn_backward(grad_low, gate_pre, up_pre, w_gate, w_up, w_down):
    grad_hidden = mm_t(grad_low, w_down)
    gate_sigmoid = jax.nn.sigmoid(gate_pre)
    grad_gate = (
        grad_hidden * up_pre * gate_sigmoid * (1.0 + gate_pre * (1.0 - gate_sigmoid))
    ).astype(BF)
    grad_up = (grad_hidden * gate_pre * gate_sigmoid).astype(BF)
    return (mm_t(grad_gate, w_gate) + mm_t(grad_up, w_up), grad_gate, grad_up)


def body(
    tokens,
    teacher,
    valid_mask,
    w_query,
    key_weight_matrix,
    value_weight_matrix,
    w_output,
    w_gate,
    w_up,
    w_down,
    attn_gain,
    ffn_gain,
):
    n = lax.axis_size("dp")
    planes = n // 8
    position = lax.axis_index("dp")
    c, x, y, z = position % 2, position // 2 % 2, position // 4 % 2, position // 8
    bits = (z, y, x, c)
    p = position // 2 % 4
    rows = w_query.shape[0]
    width = w_query.shape[1]
    kv_width = key_weight_matrix.shape[1]
    ff_rows = w_down.shape[0]
    ff = w_gate.shape[1]
    count = tokens.shape[0]
    sequences = count // SEQ
    groups = QUERY_HEAD_COUNT // KEY_VALUE_HEADS
    score_scale = 1.0 / math.sqrt(HEAD_SIZE)
    cosine_lookup, sine_lookup = rotation_tables(SEQ, HEAD_SIZE)

    with jax.named_scope("ffn_weights_to_columns"):
        both = jnp.stack([w_gate, w_up]).reshape(2, rows, planes, 4, 2 * ff_rows)

        def columns_for(r):
            return pick(both, p ^ r, 3).reshape(2, rows, ff // 4)

        by_source = jnp.zeros((2, 4, rows, ff // 4), BF)
        for r in range(4):
            piece = columns_for(r)
            if r:
                piece = swap(piece, r << 1)
            by_source = place(by_source, piece[:, None], (0, p ^ r, 0, 0))

    with jax.named_scope("attention_weights"):
        gains = jnp.stack([attn_gain, ffn_gain], axis=1)
        gains = jnp.pad(gains, ((0, 0), (0, LANES - 2)))
        qkv_local = jnp.concatenate(
            [w_query, key_weight_matrix, value_weight_matrix, gains], axis=1
        )
        qkv = gather_rows(qkv_local, bits)
        wo = gather_rows(w_output, bits)

    with jax.named_scope("ffn_weights_along_z"):
        column = z_gather(by_source, z)
        other = swap(column, 1)
        gate_up = jnp.zeros((2, planes, 4, 2, rows, ff // 4), BF)
        gate_up = place(gate_up, jnp.swapaxes(column, 0, 1)[:, :, :, None], (0, 0, 0, c, 0, 0))
        gate_up = place(gate_up, jnp.swapaxes(other, 0, 1)[:, :, :, None], (0, 0, 0, 1 - c, 0, 0))
        gate_up = gate_up.reshape(2, n * rows, ff // 4)
        wg, wu = gate_up[0], gate_up[1]
        wd = lax.all_gather(
            w_down, "dp", axis_index_groups=column_groups(True), axis=0, tiled=True
        )

    with jax.named_scope("attention_forward"):
        wq = qkv[:, :width]
        wk = qkv[:, width : width + kv_width]
        wv = qkv[:, width + kv_width : width + 2 * kv_width]
        gain_in = qkv[:, width + 2 * kv_width].astype(F32)
        gain_mid = qkv[:, width + 2 * kv_width + 1].astype(F32)
        inputs_f = tokens.astype(F32)
        normed, inv_attn = norm_rows(inputs_f, gain_in)
        normed_in = normed.astype(BF)
        heads = (sequences, SEQ, QUERY_HEAD_COUNT, HEAD_SIZE)
        kv_heads = (sequences, SEQ, KEY_VALUE_HEADS, HEAD_SIZE)
        grouped = (sequences, SEQ, KEY_VALUE_HEADS, groups, HEAD_SIZE)
        query = turn(mm(normed_in, wq).reshape(heads), cosine_lookup, sine_lookup)
        query = query.astype(BF).reshape(grouped)
        key = turn(mm(normed_in, wk).reshape(kv_heads), cosine_lookup, sine_lookup).astype(BF)
        value = mm(normed_in, wv).astype(BF).reshape(kv_heads)
        probs = probabilities(query, key)
        probs_low = probs.astype(BF)
        mixed = jnp.einsum("bhrqk,bkhd->bqhrd", probs_low, value, preferred_element_type=F32)
        mixed = mixed.reshape(count, width).astype(BF)
        hidden_res = inputs_f + mm(mixed, wo)
        normed_two, inv_ffn = norm_rows(hidden_res, gain_mid)
        normed_mid = normed_two.astype(BF)

    with jax.named_scope("ffn_forward"):
        near, far = split_gather(normed_mid)
        y_near, gate_near, up_near, hid_near = ffn_forward(near, wg, wu, wd)
        y_far, gate_far, up_far, hid_far = ffn_forward(far, wg, wu, wd)
        result = hidden_res + split_reduce(y_near, y_far)
        out_act = result.astype(BF)

    with jax.named_scope("loss"):
        mask_f = valid_mask.astype(F32)
        grad_out = (result - teacher.astype(F32)) * mask_f[:, None]
        sums = jnp.stack([jnp.sum(grad_out * grad_out), jnp.sum(mask_f)])
        sums = total_of(jnp.broadcast_to(sums[:, None], (2, LANES)))
        loss = sums[0, 0] / (sums[1, 0] * width)

    with jax.named_scope("ffn_backward"):
        grad_low = grad_out.astype(BF)
        d_near, d_far = split_gather(grad_low)
        m_near, dg_near, du_near = ffn_backward(d_near, gate_near, up_near, wg, wu, wd)
        m_far, dg_far, du_far = ffn_backward(d_far, gate_far, up_far, wg, wu, wd)
        grad_mid = split_reduce(m_near, m_far)

    with jax.named_scope("ffn_weight_gradients"):
        hid = jnp.concatenate([hid_near, hid_far])
        d_all = jnp.concatenate([d_near, d_far])
        mid_all = jnp.concatenate([near, far])
        dg_all = jnp.concatenate([dg_near, dg_far])
        du_all = jnp.concatenate([du_near, du_far])
        grad_down = t_mm(hid, d_all).astype(BF)
        grad_down = lax.psum_scatter(
            grad_down,
            "dp",
            axis_index_groups=column_groups(True),
            scatter_dimension=0,
            tiled=True,
        ).astype(F32)
        shape = (planes, 4, 2, rows, ff // 4)
        order = (0, 2, 1, 3, 4)
        g_gate = t_mm(mid_all, dg_all).astype(BF).reshape(shape).transpose(order)
        g_up = t_mm(mid_all, du_all).astype(BF).reshape(shape).transpose(order)
        both = jnp.stack([g_gate, g_up], axis=2).reshape(n * 2 * rows, ff // 4)
        both = lax.psum_scatter(
            both, "dp", axis_index_groups=column_groups(True), scatter_dimension=0, tiled=True
        ).reshape(2, 4, rows, ff // 4)
        spread = jnp.zeros((2, rows, planes, 4, 2 * ff_rows), BF)
        for r in range(4):
            piece = pick(both, p ^ r, 1)
            if r:
                piece = swap(piece, r << 1)
            piece = piece.reshape(2, rows, planes, 1, 2 * ff_rows)
            spread = place(spread, piece, (0, 0, 0, p ^ r, 0))
        spread = spread.reshape(2, rows, ff).astype(F32)
        grad_gate, grad_up = spread[0], spread[1]

    with jax.named_scope("attention_backward"):
        grad_gain_mid, grad_res = norm_back(grad_mid, hidden_res, inv_ffn, gain_mid)
        grad_res = grad_out + grad_res
        res_low = grad_res.astype(BF)
        g_wo = t_mm(mixed, res_low)
        grad_mixed = mm_t(res_low, wo).astype(BF).reshape(grouped)
        grad_probs = jnp.einsum(
            "bqhrd,bkhd->bhrqk", grad_mixed, value, preferred_element_type=F32
        )
        grad_scores = probs * (grad_probs - jnp.sum(probs * grad_probs, axis=-1, keepdims=True))
        grad_scores = grad_scores.astype(BF)
        grad_query = score_scale * jnp.einsum(
            "bhrqk,bkhd->bqhrd", grad_scores, key, preferred_element_type=F32
        )
        grad_key = score_scale * jnp.einsum(
            "bhrqk,bqhrd->bkhd", grad_scores, query, preferred_element_type=F32
        )
        grad_value = jnp.einsum(
            "bhrqk,bqhrd->bkhd", probs_low, grad_mixed, preferred_element_type=F32
        )
        query_back = turn(grad_query.reshape(heads), cosine_lookup, -sine_lookup)
        query_back = query_back.reshape(count, width).astype(BF)
        key_back = turn(grad_key, cosine_lookup, -sine_lookup).reshape(count, kv_width).astype(BF)
        value_back = grad_value.reshape(count, kv_width).astype(BF)
        grad_in = mm_t(query_back, wq) + mm_t(key_back, wk) + mm_t(value_back, wv)
        grad_gain_in, grad_tokens = norm_back(grad_in, inputs_f, inv_attn, gain_in)
        input_grad = (grad_res + grad_tokens).astype(BF)

    with jax.named_scope("attention_weight_gradients"):
        g_wo = scatter_rows(g_wo, bits)
        g_gains = jnp.stack([grad_gain_in, grad_gain_mid], axis=1)
        g_gains = jnp.pad(g_gains, ((0, 0), (0, LANES - 2)))
        g_qkv = jnp.concatenate(
            [
                t_mm(normed_in, query_back),
                t_mm(normed_in, key_back),
                t_mm(normed_in, value_back),
                g_gains,
            ],
            axis=1,
        )
        g_qkv = scatter_rows(g_qkv, bits)
        g_wq = g_qkv[:, :width]
        g_wk = g_qkv[:, width : width + kv_width]
        g_wv = g_qkv[:, width + kv_width : width + 2 * kv_width]
        g_gain_in = g_qkv[:, width + 2 * kv_width]
        g_gain_mid = g_qkv[:, width + 2 * kv_width + 1]

    return (
        out_act,
        loss,
        input_grad,
        g_wq,
        g_wk,
        g_wv,
        g_wo,
        grad_gate,
        grad_up,
        grad_down,
        g_gain_in,
        g_gain_mid,
    )


def solution(mesh):
    wide, flat = P("dp", None), P("dp")
    in_specs = (wide, wide, flat) + (wide,) * 7 + (flat, flat)
    out_specs = (wide, P(), wide) + (wide,) * 7 + (flat, flat)
    return jax.shard_map(body, mesh=mesh, in_specs=in_specs, out_specs=out_specs, check_vma=False)
```

```python
import math

import jax
import jax.numpy as jnp
from jax import lax
from jax.sharding import PartitionSpec as P

QUERY_HEAD_COUNT = 16
KEY_VALUE_HEADS = 8
HEAD_SIZE = 96
SEQ = 128
EPSILON = 1e-05
ROPE_BASE = 100000.0
MASK_FILL = -1e30
LANES = 128

BF = jnp.bfloat16
F32 = jnp.float32


def dot(a, b, dims):
    return lax.dot_general(a, b, (dims, ((), ())), preferred_element_type=F32)


def mm(a, b):
    return dot(a, b, ((1,), (0,)))


def mm_t(a, b):
    return dot(a, b, ((1,), (1,)))


def t_mm(a, b):
    return dot(a, b, ((0,), (0,)))


def swap(value, mask):
    n = lax.axis_size("dp")
    return lax.ppermute(value, "dp", [(i, i ^ mask) for i in range(n)])


def column_groups():
    n = lax.axis_size("dp")
    return [[8 * z + 2 * p + c for z in range(n // 8)] for p in range(4) for c in range(2)]


def z_pieces(value, z):
    planes = lax.axis_size("dp") // 8
    if planes != 4:
        whole = lax.all_gather(value, "dp", axis_index_groups=column_groups(), axis=0)
        return [(whole, 0)]
    return [(value[None], z)] + [(swap(value, 8 * k)[None], z ^ k) for k in (1, 2, 3)]


def z_reduce(parts, z):
    planes = lax.axis_size("dp") // 8
    if planes != 4:
        return lax.psum_scatter(
            parts.astype(BF), "dp", axis_index_groups=column_groups(), scatter_dimension=0
        ).astype(F32)
    came = [swap(pick(parts, z ^ k, 0).astype(BF), 8 * k) for k in (3, 2, 1)]
    own = pick(parts, z, 0)
    for piece in came:
        own = own + piece.astype(F32)
    return own


def place(out, piece, where):
    return lax.dynamic_update_slice(out, piece, where)


def pick(parts, index, axis):
    return lax.dynamic_index_in_dim(parts, index, axis, keepdims=False)


def both(first, second):
    return lax.optimization_barrier((first, second))


def plane_reduce(parts, place_bits):
    z, y, x, c = place_bits
    half = parts.shape[0] // 2
    a, b = parts[:half], parts[half:]
    came_a, came_b = both(
        swap(pick(a, 1 - y, 1).astype(BF), 4), swap(pick(b, 1 - x, 2).astype(BF), 2)
    )
    a = pick(a, y, 1) + came_a.astype(F32)
    b = pick(b, x, 2) + came_b.astype(F32)
    came_a, came_b = both(
        swap(pick(a, 1 - x, 1).astype(BF), 2), swap(pick(b, 1 - y, 1).astype(BF), 4)
    )
    a = pick(a, x, 1) + came_a.astype(F32)
    b = pick(b, y, 1) + came_b.astype(F32)
    return z_reduce(jnp.concatenate([a, b]), z)


def core_first(count, rows):
    order = jnp.arange(count)
    per_core = count // 2
    core, rest = order // per_core, order % per_core
    source = (rest // rows * 2 + core) * rows + rest % rows
    return (jnp.arange(count)[:, None] == source[None, :]).astype(BF)


def core_halves(values, c):
    width = values.shape[1] // 2
    return (
        lax.dynamic_slice_in_dim(values, c * width, width, 1),
        lax.dynamic_slice_in_dim(values, (1 - c) * width, width, 1),
    )


def core_gradient(features, grads, c):
    mine, theirs = core_halves(features, c)
    came = swap(t_mm(theirs, grads).astype(BF), 1)
    return t_mm(mine, grads) + came.astype(F32)


def split_gather(rows):
    half = rows.shape[0] // 2
    a, b = rows[:half], rows[half:]
    a_x, b_y = both(swap(a, 2), swap(b, 4))
    a_far, b_far = both(
        swap(jnp.concatenate([a, a_x]), 4), swap(jnp.concatenate([b, b_y]), 2)
    )
    return (jnp.concatenate([a, a_x, b, b_y]), jnp.concatenate([a_far, b_far]))


def split_reduce(near, far):
    two = far.shape[0] // 2
    one = two // 2
    low = far.astype(BF)
    came_a, came_b = both(swap(low[:two], 4), swap(low[two:], 2))
    a = near[:two] + came_a.astype(F32)
    b = near[two:] + came_b.astype(F32)
    came_a, came_b = both(swap(a[one:].astype(BF), 2), swap(b[one:].astype(BF), 4))
    return jnp.concatenate([a[:one] + came_a.astype(F32), b[:one] + came_b.astype(F32)])


def total_of(value):
    n = lax.axis_size("dp")
    mask = 1
    while mask < n:
        value = value + swap(value, mask)
        mask *= 2
    return value


def scatter_gains(partial, position):
    n = lax.axis_size("dp")
    rows = partial.shape[1] // n
    return lax.dynamic_slice_in_dim(total_of(partial), position * rows, rows, 1)


def rotation_tables(length, width):
    half_width = width // 2
    position = jnp.arange(length, dtype=F32)[:, None]
    freq_rate = ROPE_BASE ** (-2.0 * jnp.arange(half_width, dtype=F32) / width)
    angle_table = position * freq_rate[None, :]
    return (jnp.cos(angle_table)[:, None, :], jnp.sin(angle_table)[:, None, :])


def turn(heads_in, cosine_lookup, sine_lookup):
    half_width = heads_in.shape[-1] // 2
    left_part = heads_in[..., :half_width]
    right_part = heads_in[..., half_width:]
    return jnp.concatenate(
        [
            left_part * cosine_lookup - right_part * sine_lookup,
            right_part * cosine_lookup + left_part * sine_lookup,
        ],
        axis=-1,
    )


def norm_rows(field_in, gain_vec):
    inv_scale = lax.rsqrt(jnp.mean(field_in * field_in, axis=-1, keepdims=True) + EPSILON)
    return (field_in * inv_scale * gain_vec, inv_scale)


def norm_back(upstream, field_in, inv_scale, gain_vec):
    gain_grad = jnp.sum(upstream * field_in * inv_scale, axis=0)
    scaled_up = upstream * gain_vec
    field_grad = inv_scale * scaled_up - field_in * inv_scale**3 * jnp.mean(
        scaled_up * field_in, axis=-1, keepdims=True
    )
    return (gain_grad, field_grad)


def probabilities(query_heads, key_heads):
    score_scale = 1.0 / math.sqrt(HEAD_SIZE)
    raw_scores = (
        jnp.einsum("bqhrd,bkhd->bhrqk", query_heads, key_heads, preferred_element_type=F32)
        * score_scale
    )
    causal = jnp.arange(SEQ)[:, None] >= jnp.arange(SEQ)[None, :]
    scores = jnp.where(causal, raw_scores, MASK_FILL)
    row_max = jnp.max(scores, axis=-1, keepdims=True)
    weights = jnp.exp(scores - row_max)
    return weights / jnp.sum(weights, axis=-1, keepdims=True)


def ffn_forward(rows, w_both, w_down):
    pre = mm(rows, w_both)
    units = pre.shape[1] // 2
    hidden = (jax.nn.silu(pre[:, :units]) * pre[:, units:]).astype(BF)
    return (mm(hidden, w_down), pre, hidden)


def ffn_backward(grad_low, pre, w_both, w_down):
    grad_hidden = mm_t(grad_low, w_down)
    units = pre.shape[1] // 2
    gate_pre, up_pre = pre[:, :units], pre[:, units:]
    gate_sigmoid = jax.nn.sigmoid(gate_pre)
    grad_gate = grad_hidden * up_pre * gate_sigmoid * (1.0 + gate_pre * (1.0 - gate_sigmoid))
    grad_up = grad_hidden * gate_pre * gate_sigmoid
    grads = jnp.concatenate([grad_gate.astype(BF), grad_up.astype(BF)], axis=1)
    return (mm_t(grads, w_both), grads)


def body(
    tokens,
    teacher,
    valid_mask,
    w_query,
    key_weight_matrix,
    value_weight_matrix,
    w_output,
    w_gate,
    w_up,
    w_down,
    attn_gain,
    ffn_gain,
):
    n = lax.axis_size("dp")
    planes = n // 8
    position = lax.axis_index("dp")
    c, x, y, z = position % 2, position // 2 % 2, position // 4 % 2, position // 8
    bits = (z, y, x, c)
    p = position // 2 % 4
    rows = w_query.shape[0]
    width = w_query.shape[1]
    kv_width = key_weight_matrix.shape[1]
    ff_rows = w_down.shape[0]
    ff = w_gate.shape[1]
    count = tokens.shape[0]
    sequences = count // SEQ
    groups = QUERY_HEAD_COUNT // KEY_VALUE_HEADS
    score_scale = 1.0 / math.sqrt(HEAD_SIZE)
    cosine_lookup, sine_lookup = rotation_tables(SEQ, HEAD_SIZE)

    with jax.named_scope("attention_weights"):
        gains = jnp.stack([attn_gain, ffn_gain], axis=1)
        gains = jnp.pad(gains, ((0, 0), (0, LANES - 2)))
        local = jnp.concatenate(
            [w_query, key_weight_matrix, value_weight_matrix, w_output, gains], axis=1
        )
        gathered = lax.all_gather(local, "dp", axis=0, tiled=True)

    part = 2 * ff_rows
    units = planes * part

    with jax.named_scope("ffn_weights_to_columns"):
        gate_cut = w_gate.reshape(rows, planes, 4, part)
        up_cut = w_up.reshape(rows, planes, 4, part)

        def columns_for(r):
            gate = pick(gate_cut, p ^ r, 2).reshape(rows, units)
            up = pick(up_cut, p ^ r, 2).reshape(rows, units)
            return jnp.concatenate([gate, up], axis=1)

        by_source = jnp.zeros((4, rows, 2 * units), BF)
        for r in (3, 1, 2, 0):
            piece = columns_for(r)
            if r:
                piece = swap(piece, r << 1)
            by_source = place(by_source, piece[None], (p ^ r, 0, 0))

    with jax.named_scope("ffn_weights_along_z"):
        wb = jnp.zeros((planes, 4, 2, rows, 2 * units), BF)
        for piece, at in z_pieces(by_source, z):
            other = swap(piece, 1)
            wb = place(wb, piece[:, :, None], (at, 0, c, 0, 0))
            wb = place(wb, other[:, :, None], (at, 0, 1 - c, 0, 0))
        wb = wb.reshape(n * rows, 2 * units)
        wd = jnp.zeros((planes, 2, ff_rows, width), BF)
        for piece, at in z_pieces(w_down, z):
            other = swap(piece, 1)
            wd = place(wd, piece[:, None], (at, c, 0, 0))
            wd = place(wd, other[:, None], (at, 1 - c, 0, 0))
        wd = wd.reshape(units, width)

    with jax.named_scope("attention_forward"):
        wide = width + 2 * kv_width
        wqkv = gathered[:, :wide]
        wo = gathered[:, wide : wide + width]
        gain_in = gathered[:, wide + width].astype(F32)
        gain_mid = gathered[:, wide + width + 1].astype(F32)
        inputs_f = tokens.astype(F32)
        normed, inv_attn = norm_rows(inputs_f, gain_in)
        normed_in = normed.astype(BF)
        heads = (sequences, SEQ, QUERY_HEAD_COUNT, HEAD_SIZE)
        kv_heads = (sequences, SEQ, KEY_VALUE_HEADS, HEAD_SIZE)
        grouped = (sequences, SEQ, KEY_VALUE_HEADS, groups, HEAD_SIZE)
        raw = mm(normed_in, wqkv)
        query = turn(raw[:, :width].reshape(heads), cosine_lookup, sine_lookup)
        query = query.astype(BF).reshape(grouped)
        key = raw[:, width : width + kv_width].reshape(kv_heads)
        key = turn(key, cosine_lookup, sine_lookup).astype(BF)
        value = raw[:, width + kv_width :].astype(BF).reshape(kv_heads)
        probs = probabilities(query, key)
        probs_low = probs.astype(BF)
        mixed = jnp.einsum("bhrqk,bkhd->bqhrd", probs_low, value, preferred_element_type=F32)
        mixed = mixed.reshape(count, width).astype(BF)
        hidden_res = inputs_f + mm(mixed, wo)
        normed_two, inv_ffn = norm_rows(hidden_res, gain_mid)
        normed_mid = normed_two.astype(BF)

    with jax.named_scope("ffn_forward"):
        near, far = split_gather(normed_mid)
        y_near, pre_near, hid_near = ffn_forward(near, wb, wd)
        y_far, pre_far, hid_far = ffn_forward(far, wb, wd)
        result = hidden_res + split_reduce(y_near, y_far)
        out_act = result.astype(BF)

    with jax.named_scope("loss"):
        mask_f = valid_mask.astype(F32)
        grad_out = (result - teacher.astype(F32)) * mask_f[:, None]
        sums = jnp.stack([jnp.sum(grad_out * grad_out), jnp.sum(mask_f)])
        sums = total_of(jnp.broadcast_to(sums[:, None], (2, LANES)))
        loss = sums[0, 0] / (sums[1, 0] * width)

    with jax.named_scope("ffn_backward"):
        grad_low = grad_out.astype(BF)
        d_near, d_far = split_gather(grad_low)
        m_near, g_near = ffn_backward(d_near, pre_near, wb, wd)
        m_far, g_far = ffn_backward(d_far, pre_far, wb, wd)
        grad_mid = split_reduce(m_near, m_far)

    with jax.named_scope("ffn_weight_gradients"):
        by_core = core_first(width, rows)
        hid = jnp.concatenate([hid_near, hid_far])
        d_all = jnp.concatenate([d_near, d_far])
        grad_down = t_mm(hid, d_all).reshape(planes, 2, ff_rows, width)
        came = swap(pick(grad_down, 1 - c, 1).astype(BF), 1)
        grad_down = z_reduce(pick(grad_down, c, 1) + came.astype(F32), z)
        mid_all = mm(jnp.concatenate([near, far]), by_core).astype(BF)
        g_all = jnp.concatenate([g_near, g_far])
        g_both = core_gradient(mid_all, g_all, c)
        g_both = z_reduce(g_both.reshape(planes, 4, rows, 2 * units), z).astype(BF)
        came = [pick(g_both, p, 0)]
        for r in (1, 2, 3):
            came.append(swap(pick(g_both, p ^ r, 0), r << 1))
        natural = []
        for q in range(4):
            piece = came[3]
            for r in (0, 1, 2):
                piece = jnp.where(p == (q ^ r), came[r], piece)
            natural.append(piece.astype(F32))
        grad_gate = jnp.concatenate(
            [natural[q][:, k * part : (k + 1) * part] for k in range(planes) for q in range(4)],
            axis=1,
        )
        grad_up = jnp.concatenate(
            [
                natural[q][:, units + k * part : units + (k + 1) * part]
                for k in range(planes)
                for q in range(4)
            ],
            axis=1,
        )

    with jax.named_scope("attention_backward"):
        grad_gain_mid, grad_res = norm_back(grad_mid, hidden_res, inv_ffn, gain_mid)
        grad_res = grad_out + grad_res
        res_low = grad_res.astype(BF)
        grad_mixed = mm_t(res_low, wo).astype(BF).reshape(grouped)
        grad_probs = jnp.einsum(
            "bqhrd,bkhd->bhrqk", grad_mixed, value, preferred_element_type=F32
        )
        grad_scores = probs * (grad_probs - jnp.sum(probs * grad_probs, axis=-1, keepdims=True))
        grad_scores = grad_scores.astype(BF)
        grad_query = score_scale * jnp.einsum(
            "bhrqk,bkhd->bqhrd", grad_scores, key, preferred_element_type=F32
        )
        grad_key = score_scale * jnp.einsum(
            "bhrqk,bqhrd->bkhd", grad_scores, query, preferred_element_type=F32
        )
        grad_value = jnp.einsum(
            "bhrqk,bqhrd->bkhd", probs_low, grad_mixed, preferred_element_type=F32
        )
        query_back = turn(grad_query.reshape(heads), cosine_lookup, -sine_lookup)
        query_back = query_back.reshape(count, width).astype(BF)
        key_back = turn(grad_key, cosine_lookup, -sine_lookup).reshape(count, kv_width).astype(BF)
        value_back = grad_value.reshape(count, kv_width).astype(BF)
        grad_raw = jnp.concatenate([query_back, key_back, value_back], axis=1)
        grad_in = mm_t(grad_raw, wqkv)
        grad_gain_in, grad_tokens = norm_back(grad_in, inputs_f, inv_attn, gain_in)
        input_grad = (grad_res + grad_tokens).astype(BF)

    with jax.named_scope("attention_weight_gradients"):
        shape = (planes, 2, 2, rows, -1)
        mixed_by_core = mm(mixed, by_core).astype(BF)
        g_wo = core_gradient(mixed_by_core, res_low, c)
        g_wo = plane_reduce(g_wo.reshape(shape), bits)
        normed_by_core = mm(normed_in, by_core).astype(BF)
        g_raw = core_gradient(normed_by_core, grad_raw, c)
        g_raw = plane_reduce(g_raw.reshape(shape), bits)
        g_wq = g_raw[:, :width]
        g_wk = g_raw[:, width : width + kv_width]
        g_wv = g_raw[:, width + kv_width :]

    with jax.named_scope("gain_gradients"):
        g_gains = jnp.stack([grad_gain_in, grad_gain_mid])
        g_gains = scatter_gains(g_gains, position)

    return (
        out_act,
        loss,
        input_grad,
        g_wq,
        g_wk,
        g_wv,
        g_wo,
        grad_gate,
        grad_up,
        grad_down,
        g_gains[0],
        g_gains[1],
    )


def solution(mesh):
    wide, flat = P("dp", None), P("dp")
    in_specs = (wide, wide, flat) + (wide,) * 7 + (flat, flat)
    out_specs = (wide, P(), wide) + (wide,) * 7 + (flat, flat)
    return jax.shard_map(body, mesh=mesh, in_specs=in_specs, out_specs=out_specs, check_vma=False)
```

```python
import math

import jax
import jax.numpy as jnp
from jax import lax
from jax.experimental import pallas as pl
from jax.experimental.pallas import tpu as pltpu
from jax.sharding import PartitionSpec as P

QUERY_HEAD_COUNT = 16
KEY_VALUE_HEADS = 8
HEAD_SIZE = 96
SEQ = 128
EPSILON = 1e-05
ROPE_BASE = 100000.0
MASK_FILL = -1e30
LANES = 128

BF = jnp.bfloat16
F32 = jnp.float32


def dot(a, b, dims):
    return lax.dot_general(a, b, (dims, ((), ())), preferred_element_type=F32)


def mm(a, b):
    return dot(a, b, ((1,), (0,)))


def mm_t(a, b):
    return dot(a, b, ((1,), (1,)))


def t_mm(a, b):
    return dot(a, b, ((0,), (0,)))


def swap(value, mask):
    n = lax.axis_size("dp")
    return lax.ppermute(value, "dp", [(i, i ^ mask) for i in range(n)])


def column_groups(with_core):
    n = lax.axis_size("dp")
    planes = range(n // 8)
    if with_core:
        return [[8 * z + 2 * p + c for z in planes for c in range(2)] for p in range(4)]
    return [[8 * z + 2 * p + c for z in planes] for p in range(4) for c in range(2)]


def z_reduce(parts, z):
    if parts.shape[0] != 4:
        return lax.psum_scatter(
            parts.astype(BF), "dp", axis_index_groups=column_groups(False), scatter_dimension=0
        ).astype(F32)
    came = [swap(pick(parts, z ^ k, 0).astype(BF), 8 * k) for k in (3, 2, 1)]
    own = pick(parts, z, 0)
    for piece in came:
        own = own + piece.astype(F32)
    return own


def walk_start(parts, z):
    payload = jnp.stack(
        [pick(parts, jnp.where(z == 0, 2, 1), 0), pick(parts, jnp.where(z == 0, 3, 0), 0)]
    )
    return along_z(payload.astype(BF), [(0, 1), (3, 2)])


def walk_end(parts, came, z):
    came = came.astype(F32)
    across = pick(parts, 3 - z, 0) + came[0]
    far = pick(parts, jnp.where(z == 1, 3, 0), 0) + came[1]
    up = jnp.where(z == 1, across, pick(parts, jnp.minimum(z + 1, 3), 0))
    down = jnp.where(z == 2, across, pick(parts, jnp.maximum(z - 1, 0), 0))
    return (
        along_z(up.astype(BF), [(0, 1), (1, 2), (2, 3)]),
        along_z(down.astype(BF), [(1, 0), (2, 1), (3, 2)]),
        along_z(far.astype(BF), [(2, 0), (1, 3)]),
    )


def owned(parts, came, z):
    own = pick(parts, z, 0)
    for piece in came:
        own = own + piece.astype(F32)
    return own


def along_z(value, pairs):
    return lax.ppermute(
        value, "dp", [(8 * a + i, 8 * b + i) for a, b in pairs for i in range(8)]
    )


def tied(*values):
    return lax.optimization_barrier(values)


def place(out, piece, where):
    return lax.dynamic_update_slice(out, piece, where)


def pick(parts, index, axis):
    return lax.dynamic_index_in_dim(parts, index, axis, keepdims=False)


def column_cuts(w_gate, w_up, p, part):
    rows = w_gate.shape[0]
    gate_cut = w_gate.reshape(rows, -1, 4, part)
    up_cut = w_up.reshape(rows, -1, 4, part)
    cuts = []
    for r in range(4):
        gate = pick(gate_cut, p ^ r, 2).reshape(rows, -1)
        up = pick(up_cut, p ^ r, 2).reshape(rows, -1)
        cuts.append(jnp.concatenate([gate, up], axis=1))
    return cuts


def by_source(came, p):
    out = jnp.zeros((4,) + came[0].shape, BF)
    for r in range(4):
        out = place(out, came[r][None], (p ^ r, 0, 0))
    return out


def gather_columns(mine, rows):
    n = lax.axis_size("dp")
    columns = mine.shape[2]
    whole = lax.all_gather(
        mine.reshape(4 * rows, columns),
        "dp",
        axis_index_groups=column_groups(True),
        axis=0,
        tiled=True,
    )
    whole = whole.reshape(n // 8, 2, 4, rows, columns).transpose(0, 2, 1, 3, 4)
    return whole.reshape(n * rows, columns)


def gather_weights_plainly(local, w_gate, w_up, w_down, p):
    rows = local.shape[0]
    gathered = lax.all_gather(local, "dp", axis=0, tiled=True)
    cuts = column_cuts(w_gate, w_up, p, 2 * w_down.shape[0])
    came = [cuts[0]] + [swap(cuts[r], r << 1) for r in (1, 2, 3)]
    wb = gather_columns(by_source(came, p), rows)
    wd = lax.all_gather(
        w_down, "dp", axis_index_groups=column_groups(True), axis=0, tiled=True
    )
    return gathered, wb, wd


def unset(shape, dtype):
    return pl.pallas_call(
        lambda out: None,
        out_shape=jax.ShapeDtypeStruct(shape, dtype),
        out_specs=pl.BlockSpec(memory_space=pl.ANY),
        name="unset",
    )()


def packed(pieces):
    widths = [piece.shape[1] for piece in pieces]
    rows = pieces[0].shape[0]

    def kernel(*refs):
        out = refs[-1]
        at = 0
        for ref, size in zip(refs[:-1], widths):
            out[:, at : at + size] = ref[...]
            at += size

    return pl.pallas_call(
        kernel,
        out_shape=jax.ShapeDtypeStruct((rows, sum(widths)), pieces[0].dtype),
        name="packed",
    )(*pieces)


def column_cuts_kernel(w_gate, w_up, p, part):
    rows, ff = w_gate.shape
    planes = ff // (4 * part)
    units = planes * part

    def kernel(p_ref, gate, up, *outs):
        for r, out in enumerate(outs):
            q = p_ref[0] ^ r
            for k in range(planes):
                start = pl.multiple_of((4 * k + q) * part, LANES)
                out[:, k * part : (k + 1) * part] = gate[:, pl.ds(start, part)]
                out[:, units + k * part : units + (k + 1) * part] = up[:, pl.ds(start, part)]

    shape = jax.ShapeDtypeStruct((rows, 2 * units), w_gate.dtype)
    return pl.pallas_call(
        kernel,
        out_shape=[shape] * 4,
        in_specs=[pl.BlockSpec(memory_space=pltpu.SMEM)]
        + [pl.BlockSpec(memory_space=pltpu.VMEM)] * 2,
        name="column_cuts",
    )(p[None], w_gate, w_up)


def gather_weights(local, w_gate, w_up, w_down, place_bits):
    z, y, x, c = place_bits
    p = 2 * y + x
    rows, columns = local.shape
    ff_rows, width = w_down.shape
    end = (z == 0) | (z == 3)
    up_pairs = [(0, 1), (1, 2), (2, 3)]
    down_pairs = [(1, 0), (2, 1), (3, 2)]
    far_pairs = [(0, 2), (3, 1)]
    out_pairs = [(1, 0), (2, 3)]
    z_b = jnp.where(z == 0, 1, z - 1)
    z_c = jnp.where(z < 2, 2, jnp.where(z == 2, 3, 1))
    z_d = jnp.where(z < 2, 3, 0)
    out = unset((4, 2, 2, 2, rows, columns), BF)

    def near_side(up, down):
        return jnp.where(z == 0, down, up)

    def to_pass_on(up, down):
        return jnp.where(z == 1, down, up)

    def put_x(out, piece, z_k, at_y, core):
        return place(out, piece[None, None, :, None], (z_k, at_y, 0, core, 0, 0))

    def put_y(out, piece, z_k, at_x, core):
        return place(out, piece[None, :, None, None], (z_k, 0, at_x, core, 0, 0))

    def in_order(bit, mine, theirs):
        return jnp.stack([jnp.where(bit == 0, mine, theirs), jnp.where(bit == 0, theirs, mine)])

    with jax.named_scope("phase_0"):
        cuts = column_cuts_kernel(w_gate, w_up, p, 2 * ff_rows)
        up, down, came_x, came_y, came_xy = tied(
            along_z(local, up_pairs),
            along_z(local, down_pairs),
            swap(cuts[1], 2),
            swap(cuts[2], 4),
            swap(cuts[3], 6),
        )
    with jax.named_scope("phase_1"):
        a, b = local, near_side(up, down)
        a_x, b_y, far, first = tied(
            swap(a, 2),
            swap(b, 4),
            along_z(tied(local, up, down)[0], far_pairs),
            along_z(to_pass_on(up, down), out_pairs),
        )
        gu = unset((4, rows, cuts[0].shape[1]), BF)
        for r, piece in enumerate((cuts[0], came_x, came_y, came_xy)):
            gu = place(gu, piece[None], (p ^ r, 0, 0))
        a2, b2 = in_order(x, a, a_x), in_order(y, b, b_y)
    with jax.named_scope("phase_2"):
        a_far, b_far = tied(swap(a2, 4), swap(b2, 2))
        second, a2_core, b2_core = tied(along_z(far, out_pairs), swap(a2, 1), swap(b2, 1))
        gu_in = tied(gu, second)[0]
        g_up, g_down = along_z(gu_in, up_pairs), along_z(gu_in, down_pairs)
        out = put_x(out, a2, z, y, c)
        out = put_y(out, b2, z_b, x, c)
        out = put_x(out, a2_core, z, y, 1 - c)
        out = put_y(out, b2_core, z_b, x, 1 - c)
    with jax.named_scope("phase_3"):
        a, b = jnp.where(end, first, down), jnp.where(end, second, far)
        a, b, a_far, b_far = tied(a, b, a_far, b_far)
        a_x, b_y, g_up, g_down = tied(swap(a, 2), swap(b, 4), g_up, g_down)
        a_core, b_core = swap(a_far, 1), swap(b_far, 1)
        out = put_x(out, a_far, z, 1 - y, c)
        out = put_y(out, b_far, z_b, 1 - x, c)
        out = put_x(out, a_core, z, 1 - y, 1 - c)
        out = put_y(out, b_core, z_b, 1 - x, 1 - c)
        a2, b2 = in_order(x, a, a_x), in_order(y, b, b_y)
    with jax.named_scope("phase_4"):
        g_far = along_z(tied(gu, g_up)[0], far_pairs)
        g_first = along_z(to_pass_on(g_up, g_down), out_pairs)
        a_far, b_far = tied(swap(a2, 4), swap(b2, 2))
        a2_core, b2_core = swap(a2, 1), swap(b2, 1)
        out = put_x(out, a2, z_c, y, c)
        out = put_y(out, b2, z_d, x, c)
        out = put_x(out, a2_core, z_c, y, 1 - c)
        out = put_y(out, b2_core, z_d, x, 1 - c)
    with jax.named_scope("phase_5"):
        a_core, b_core, g_far, g_first = tied(swap(a_far, 1), swap(b_far, 1), g_far, g_first)
        out = put_x(out, a_far, z_c, 1 - y, c)
        out = put_y(out, b_far, z_d, 1 - x, c)
        out = put_x(out, a_core, z_c, 1 - y, 1 - c)
        out = put_y(out, b_core, z_d, 1 - x, 1 - c)
        gathered = out.reshape(32 * rows, columns)
        g_second = along_z(g_far, out_pairs)


    def step_1(beside):
        d_in, *pieces = tied(w_down, gu, near_side(g_up, g_down), jnp.where(end, g_first, g_down), beside)[:4]
        return (
            tied(along_z(d_in, up_pairs), along_z(d_in, down_pairs)),
            pieces,
            [swap(piece, 1) for piece in pieces],
        )

    def step_2(state, beside):
        (d_up, d_down), pieces, others = state
        d_up, d_down, last, beside = tied(d_up, d_down, jnp.where(end, g_second, g_far), beside)
        d_far = along_z(tied(w_down, d_up)[0], far_pairs)
        d_first = along_z(to_pass_on(d_up, d_down), out_pairs)
        wb = unset((4, 4, 2) + gu.shape[1:], BF)
        for piece, other, z_k in zip(pieces + [last], others + [swap(last, 1)], (z, z_b, z_c, z_d)):
            wb = place(wb, piece[None, :, None], (z_k, 0, c, 0, 0))
            wb = place(wb, other[None, :, None], (z_k, 0, 1 - c, 0, 0))
        return beside, (d_up, d_down, d_far, d_first), wb.reshape(32 * rows, -1)

    def step_3(state):
        d_up, d_down, d_far, d_first = state
        d_second = along_z(d_far, out_pairs)
        wd = unset((4, 2, ff_rows, width), BF)
        for piece, z_k in (
            (w_down, z),
            (near_side(d_up, d_down), z_b),
            (jnp.where(end, d_first, d_down), z_c),
            (jnp.where(end, d_second, d_far), z_d),
        ):
            wd = place(wd, piece[None, None], (z_k, c, 0, 0))
            wd = place(wd, swap(piece, 1)[None, None], (z_k, 1 - c, 0, 0))
        return wd.reshape(8 * ff_rows, width)

    return gathered, step_1, step_2, step_3


def plane_reduce(parts, place_bits):
    z, y, x, c = place_bits
    half = parts.shape[0] // 2
    a, b = parts[:half], parts[half:]
    came_a, came_b = tied(
        swap(pick(a, 1 - y, 1).astype(BF), 4), swap(pick(b, 1 - x, 2).astype(BF), 2)
    )
    a = pick(a, y, 1) + came_a.astype(F32)
    b = pick(b, x, 2) + came_b.astype(F32)
    came_a, came_b = tied(
        swap(pick(a, 1 - x, 1).astype(BF), 2), swap(pick(b, 1 - y, 1).astype(BF), 4)
    )
    a = pick(a, x, 1) + came_a.astype(F32)
    b = pick(b, y, 1) + came_b.astype(F32)
    return jnp.concatenate([a, b])


def core_first(count, rows):
    order = jnp.arange(count)
    per_core = count // 2
    core, rest = order // per_core, order % per_core
    source = (rest // rows * 2 + core) * rows + rest % rows
    return (jnp.arange(count)[:, None] == source[None, :]).astype(BF)


def core_halves(values, c):
    width = values.shape[1] // 2
    return (
        lax.dynamic_slice_in_dim(values, c * width, width, 1),
        lax.dynamic_slice_in_dim(values, (1 - c) * width, width, 1),
    )


def split_gather(rows, beside=()):
    half = rows.shape[0] // 2
    a, b = rows[:half], rows[half:]
    a_x, b_y, *beside = tied(swap(a, 2), swap(b, 4), *beside)
    a_far, b_far = tied(swap(jnp.concatenate([a, a_x]), 4), swap(jnp.concatenate([b, b_y]), 2))
    return (jnp.concatenate([a, a_x, b, b_y]), jnp.concatenate([a_far, b_far]), beside)


def split_reduce(near, far, beside=lambda: (), later=lambda *values: ()):
    two = far.shape[0] // 2
    one = two // 2
    low = far.astype(BF)
    came_a, came_b, *done = tied(swap(low[:two], 4), swap(low[two:], 2), *beside())
    a = near[:two] + came_a.astype(F32)
    b = near[two:] + came_b.astype(F32)
    came_a, came_b, *done = tied(
        swap(a[one:].astype(BF), 2), swap(b[one:].astype(BF), 4), *later(*done)
    )
    own = jnp.concatenate([a[:one] + came_a.astype(F32), b[:one] + came_b.astype(F32)])
    return (own, *done)


def spread_columns(came, p, part):
    units = came[0].shape[1] // 2
    natural = []
    for q in range(4):
        piece = came[3]
        for r in (0, 1, 2):
            piece = jnp.where(p == (q ^ r), came[r], piece)
        natural.append(piece.astype(F32))
    return tuple(
        jnp.concatenate(
            [
                natural[q][:, start + k * part : start + (k + 1) * part]
                for k in range(units // part)
                for q in range(4)
            ],
            axis=1,
        )
        for start in (0, units)
    )


def total_of(value):
    n = lax.axis_size("dp")
    mask = 1
    while mask < n:
        value = value + swap(value, mask)
        mask *= 2
    return value


def scatter_gains(partial, position):
    n = lax.axis_size("dp")
    rows = partial.shape[1] // n
    return lax.dynamic_slice_in_dim(total_of(partial), position * rows, rows, 1)


def rotation_tables(length, width):
    half_width = width // 2
    position = jnp.arange(length, dtype=F32)[:, None]
    freq_rate = ROPE_BASE ** (-2.0 * jnp.arange(half_width, dtype=F32) / width)
    angle_table = position * freq_rate[None, :]
    return (jnp.cos(angle_table)[:, None, :], jnp.sin(angle_table)[:, None, :])


def turn(heads_in, cosine_lookup, sine_lookup):
    half_width = heads_in.shape[-1] // 2
    left_part = heads_in[..., :half_width]
    right_part = heads_in[..., half_width:]
    return jnp.concatenate(
        [
            left_part * cosine_lookup - right_part * sine_lookup,
            right_part * cosine_lookup + left_part * sine_lookup,
        ],
        axis=-1,
    )


def norm_rows(field_in, gain_vec):
    inv_scale = lax.rsqrt(jnp.mean(field_in * field_in, axis=-1, keepdims=True) + EPSILON)
    return (field_in * inv_scale * gain_vec, inv_scale)


def norm_back(upstream, field_in, inv_scale, gain_vec):
    gain_grad = jnp.sum(upstream * field_in * inv_scale, axis=0)
    scaled_up = upstream * gain_vec
    field_grad = inv_scale * scaled_up - field_in * inv_scale**3 * jnp.mean(
        scaled_up * field_in, axis=-1, keepdims=True
    )
    return (gain_grad, field_grad)


def probabilities(query_heads, key_heads):
    score_scale = 1.0 / math.sqrt(HEAD_SIZE)
    raw_scores = (
        jnp.einsum("bqhrd,bkhd->bhrqk", query_heads, key_heads, preferred_element_type=F32)
        * score_scale
    )
    causal = jnp.arange(SEQ)[:, None] >= jnp.arange(SEQ)[None, :]
    scores = jnp.where(causal, raw_scores, MASK_FILL)
    row_max = jnp.max(scores, axis=-1, keepdims=True)
    weights = jnp.exp(scores - row_max)
    return weights / jnp.sum(weights, axis=-1, keepdims=True)


def ffn_forward(rows, w_both, w_down):
    pre = mm(rows, w_both)
    units = pre.shape[1] // 2
    hidden = (jax.nn.silu(pre[:, :units]) * pre[:, units:]).astype(BF)
    return (mm(hidden, w_down), pre, hidden)


def ffn_backward(grad_low, pre, w_both, w_down):
    grad_hidden = mm_t(grad_low, w_down)
    units = pre.shape[1] // 2
    gate_pre, up_pre = pre[:, :units], pre[:, units:]
    gate_sigmoid = jax.nn.sigmoid(gate_pre)
    grad_gate = grad_hidden * up_pre * gate_sigmoid * (1.0 + gate_pre * (1.0 - gate_sigmoid))
    grad_up = grad_hidden * gate_pre * gate_sigmoid
    grads = jnp.concatenate([grad_gate.astype(BF), grad_up.astype(BF)], axis=1)
    return (mm_t(grads, w_both), grads)


def body(
    tokens,
    teacher,
    valid_mask,
    w_query,
    key_weight_matrix,
    value_weight_matrix,
    w_output,
    w_gate,
    w_up,
    w_down,
    attn_gain,
    ffn_gain,
):
    n = lax.axis_size("dp")
    planes = n // 8
    position = lax.axis_index("dp")
    c, x, y, z = position % 2, position // 2 % 2, position // 4 % 2, position // 8
    bits = (z, y, x, c)
    p = position // 2 % 4
    rows = w_query.shape[0]
    width = w_query.shape[1]
    kv_width = key_weight_matrix.shape[1]
    ff_rows = w_down.shape[0]
    ff = w_gate.shape[1]
    count = tokens.shape[0]
    sequences = count // SEQ
    groups = QUERY_HEAD_COUNT // KEY_VALUE_HEADS
    score_scale = 1.0 / math.sqrt(HEAD_SIZE)
    cosine_lookup, sine_lookup = rotation_tables(SEQ, HEAD_SIZE)

    part = 2 * ff_rows
    units = planes * part
    gains = jnp.stack([attn_gain, ffn_gain], axis=1)
    gains = jnp.pad(gains, ((0, 0), (0, LANES - 2)))
    local = packed([w_query, key_weight_matrix, value_weight_matrix, w_output, gains])
    if planes == 4:
        gathered, step_1, step_2, step_3 = gather_weights(local, w_gate, w_up, w_down, bits)
    else:
        gathered, wb, wd = gather_weights_plainly(local, w_gate, w_up, w_down, p)

    with jax.named_scope("attention_forward"):
        wide = width + 2 * kv_width
        wqkv = gathered[:, :wide]
        wo = gathered[:, wide : wide + width]
        gain_in = gathered[:, wide + width].astype(F32)
        gain_mid = gathered[:, wide + width + 1].astype(F32)
        inputs_f = tokens.astype(F32)
        normed, inv_attn = norm_rows(inputs_f, gain_in)
        normed_in = normed.astype(BF)
        heads = (sequences, SEQ, QUERY_HEAD_COUNT, HEAD_SIZE)
        kv_heads = (sequences, SEQ, KEY_VALUE_HEADS, HEAD_SIZE)
        grouped = (sequences, SEQ, KEY_VALUE_HEADS, groups, HEAD_SIZE)
        raw = mm(normed_in, wqkv)
        if planes == 4:
            moving = step_1(raw)
        query = turn(raw[:, :width].reshape(heads), cosine_lookup, sine_lookup)
        query = query.astype(BF).reshape(grouped)
        key = raw[:, width : width + kv_width].reshape(kv_heads)
        key = turn(key, cosine_lookup, sine_lookup).astype(BF)
        value = raw[:, width + kv_width :].astype(BF).reshape(kv_heads)
        probs = probabilities(query, key)
        probs_low = probs.astype(BF)
        mixed = jnp.einsum("bhrqk,bkhd->bqhrd", probs_low, value, preferred_element_type=F32)
        mixed = mixed.reshape(count, width).astype(BF)
        if planes == 4:
            mixed, moving, wb = step_2(moving, mixed)
        hidden_res = inputs_f + mm(mixed, wo)
        normed_two, inv_ffn = norm_rows(hidden_res, gain_mid)
        normed_mid = normed_two.astype(BF)

    with jax.named_scope("ffn_forward"):
        if planes == 4:
            near, far, moving = split_gather(normed_mid, moving)
            wd = step_3(moving)
        else:
            near, far, moving = split_gather(normed_mid)
        y_near, pre_near, hid_near = ffn_forward(near, wb, wd)
        y_far, pre_far, hid_far = ffn_forward(far, wb, wd)
        result = hidden_res + split_reduce(y_near, y_far)[0]
        out_act = result.astype(BF)

    with jax.named_scope("loss"):
        mask_f = valid_mask.astype(F32)
        grad_out = (result - teacher.astype(F32)) * mask_f[:, None]
        sums = jnp.stack([jnp.sum(grad_out * grad_out), jnp.sum(mask_f)])
        sums = total_of(jnp.broadcast_to(sums[:, None], (2, LANES)))
        loss = sums[0, 0] / (sums[1, 0] * width)

    with jax.named_scope("ffn_backward"):
        grad_low = grad_out.astype(BF)
        d_near, d_far, _ = split_gather(grad_low)
        m_near, g_near = ffn_backward(d_near, pre_near, wb, wd)
        m_far, g_far = ffn_backward(d_far, pre_far, wb, wd)
        by_core = core_first(width, rows)
        hid = jnp.concatenate([hid_near, hid_far])
        d_all = jnp.concatenate([d_near, d_far])
        mid_all = mm(jnp.concatenate([near, far]), by_core).astype(BF)
        g_all = jnp.concatenate([g_near, g_far])
        mid_mine, mid_theirs = core_halves(mid_all, c)

        def beside():
            g_down = t_mm(hid, d_all).reshape(planes, 2, ff_rows, width)
            came = swap(pick(g_down, 1 - c, 1).astype(BF), 1)
            return (pick(g_down, c, 1), came, t_mm(mid_theirs, g_all).astype(BF))

        def later(own, came, theirs):
            g_down = own + came.astype(F32)
            started = (walk_start(g_down, z),) if planes == 4 else ()
            return (t_mm(mid_mine, g_all), swap(theirs, 1), g_down, *started)

        grad_mid, g_both, came, g_down, *moving_down = split_reduce(m_near, m_far, beside, later)
        g_both = (g_both + came.astype(F32)).reshape(planes, 4, rows, 2 * units)
        if planes == 4:
            moving_both = walk_start(g_both, z)
            moving_down = walk_end(g_down, moving_down[0], z)

    with jax.named_scope("attention_backward"):
        grad_gain_mid, grad_res = norm_back(grad_mid, hidden_res, inv_ffn, gain_mid)
        grad_res = grad_out + grad_res
        res_low = grad_res.astype(BF)
        mixed_mine, mixed_theirs = core_halves(mm(mixed, by_core).astype(BF), c)
        wo_came = swap(t_mm(mixed_theirs, res_low).astype(BF), 1)
        g_wo = t_mm(mixed_mine, res_low) + wo_came.astype(F32)
        shape = (planes, 2, 2, rows, -1)
        g_wo = plane_reduce(g_wo.reshape(shape), bits)
        grad_mixed = mm_t(res_low, wo).astype(BF).reshape(grouped)
        grad_probs = jnp.einsum(
            "bqhrd,bkhd->bhrqk", grad_mixed, value, preferred_element_type=F32
        )
        grad_scores = probs * (grad_probs - jnp.sum(probs * grad_probs, axis=-1, keepdims=True))
        grad_scores = grad_scores.astype(BF)
        grad_query = score_scale * jnp.einsum(
            "bhrqk,bkhd->bqhrd", grad_scores, key, preferred_element_type=F32
        )
        grad_key = score_scale * jnp.einsum(
            "bhrqk,bqhrd->bkhd", grad_scores, query, preferred_element_type=F32
        )
        grad_value = jnp.einsum(
            "bhrqk,bqhrd->bkhd", probs_low, grad_mixed, preferred_element_type=F32
        )
        query_back = turn(grad_query.reshape(heads), cosine_lookup, -sine_lookup)
        query_back = query_back.reshape(count, width).astype(BF)
        key_back = turn(grad_key, cosine_lookup, -sine_lookup).reshape(count, kv_width).astype(BF)
        value_back = grad_value.reshape(count, kv_width).astype(BF)
        grad_raw = jnp.concatenate([query_back, key_back, value_back], axis=1)
        normed_mine, normed_theirs = core_halves(mm(normed_in, by_core).astype(BF), c)
        if planes == 4:
            grad_raw, moving_both, g_wo, *moving_down = tied(
                grad_raw, moving_both, g_wo, *moving_down
            )
            moving_both = walk_end(g_both, moving_both, z)
            g_down = owned(g_down, moving_down, z)
        else:
            g_down = z_reduce(g_down, z)
        q_came = swap(t_mm(normed_theirs, grad_raw[:, :width]).astype(BF), 1)
        kv_came = swap(t_mm(normed_theirs, grad_raw[:, width:]).astype(BF), 1)
        g_q = t_mm(normed_mine, grad_raw[:, :width]) + q_came.astype(F32)
        g_kv = t_mm(normed_mine, grad_raw[:, width:]) + kv_came.astype(F32)
        grad_in = mm_t(grad_raw, wqkv)
        grad_gain_in, grad_tokens = norm_back(grad_in, inputs_f, inv_attn, gain_in)
        input_grad = (grad_res + grad_tokens).astype(BF)

    with jax.named_scope("weight_gradients_to_owners"):
        if planes == 4:
            g_both = owned(g_both, moving_both, z).astype(BF)
        else:
            g_both = z_reduce(g_both, z).astype(BF)
        g_q = plane_reduce(g_q.reshape(shape), bits)
        came = [pick(g_both, p, 0)]
        for r in (1, 2, 3):
            came.append(swap(pick(g_both, p ^ r, 0), r << 1))
        grad_gate, grad_up = spread_columns(came, p, part)
        g_kv = plane_reduce(g_kv.reshape(shape), bits)
        g_wo = z_reduce(g_wo, z)
        g_wq = z_reduce(g_q, z)
        g_kv = z_reduce(g_kv, z)
        g_wk, g_wv = g_kv[:, :kv_width], g_kv[:, kv_width:]

    with jax.named_scope("gain_gradients"):
        g_gains = jnp.stack([grad_gain_in, grad_gain_mid])
        g_gains = scatter_gains(g_gains, position)

    return (
        out_act,
        loss,
        input_grad,
        g_wq,
        g_wk,
        g_wv,
        g_wo,
        grad_gate,
        grad_up,
        g_down,
        g_gains[0],
        g_gains[1],
    )


def solution(mesh):
    wide, flat = P("dp", None), P("dp")
    in_specs = (wide, wide, flat) + (wide,) * 7 + (flat, flat)
    out_specs = (wide, P(), wide) + (wide,) * 7 + (flat, flat)
    return jax.shard_map(body, mesh=mesh, in_specs=in_specs, out_specs=out_specs, check_vma=False)
```

```python
import math

import jax
import jax.numpy as jnp
from jax import lax
from jax.experimental import pallas as pl
from jax.experimental.pallas import tpu as pltpu
from jax.sharding import PartitionSpec as P

QUERY_HEAD_COUNT = 16
KEY_VALUE_HEADS = 8
HEAD_SIZE = 96
SEQ = 128
EPSILON = 1e-05
ROPE_BASE = 100000.0
MASK_FILL = -1e30
LANES = 128

BF = jnp.bfloat16
F32 = jnp.float32


def dot(a, b, dims):
    return lax.dot_general(a, b, (dims, ((), ())), preferred_element_type=F32)


def mm(a, b):
    return dot(a, b, ((1,), (0,)))


def mm_t(a, b):
    return dot(a, b, ((1,), (1,)))


def t_mm(a, b):
    return dot(a, b, ((0,), (0,)))


def swap(value, mask):
    n = lax.axis_size("dp")
    return lax.ppermute(value, "dp", [(i, i ^ mask) for i in range(n)])


def column_groups(with_core):
    n = lax.axis_size("dp")
    planes = range(n // 8)
    if with_core:
        return [[8 * z + 2 * p + c for z in planes for c in range(2)] for p in range(4)]
    return [[8 * z + 2 * p + c for z in planes] for p in range(4) for c in range(2)]


def z_reduce(parts, z):
    if parts.shape[0] != 4:
        return lax.psum_scatter(
            parts.astype(BF), "dp", axis_index_groups=column_groups(False), scatter_dimension=0
        ).astype(F32)
    came = [swap(pick(parts, z ^ k, 0).astype(BF), 8 * k) for k in (3, 2, 1)]
    own = pick(parts, z, 0)
    for piece in came:
        own = own + piece.astype(F32)
    return own


def walk_start(parts, z):
    payload = jnp.stack(
        [pick(parts, jnp.where(z == 0, 2, 1), 0), pick(parts, jnp.where(z == 0, 3, 0), 0)]
    )
    return along_z(payload.astype(BF), [(0, 1), (3, 2)])


def walk_end(parts, came, z):
    came = came.astype(F32)
    across = pick(parts, 3 - z, 0) + came[0]
    far = pick(parts, jnp.where(z == 1, 3, 0), 0) + came[1]
    up = jnp.where(z == 1, across, pick(parts, jnp.minimum(z + 1, 3), 0))
    down = jnp.where(z == 2, across, pick(parts, jnp.maximum(z - 1, 0), 0))
    return (
        along_z(up.astype(BF), [(0, 1), (1, 2), (2, 3)]),
        along_z(down.astype(BF), [(1, 0), (2, 1), (3, 2)]),
        along_z(far.astype(BF), [(2, 0), (1, 3)]),
    )


def owned(parts, came, z):
    own = pick(parts, z, 0)
    for piece in came:
        own = own + piece.astype(F32)
    return own


def along_z(value, pairs):
    return lax.ppermute(
        value, "dp", [(8 * a + i, 8 * b + i) for a, b in pairs for i in range(8)]
    )


def tied(*values):
    return lax.optimization_barrier(values)


def place(out, piece, where):
    return lax.dynamic_update_slice(out, piece, where)


def pick(parts, index, axis):
    return lax.dynamic_index_in_dim(parts, index, axis, keepdims=False)


def column_cuts(w_gate, w_up, p, part):
    rows = w_gate.shape[0]
    gate_cut = w_gate.reshape(rows, -1, 4, part)
    up_cut = w_up.reshape(rows, -1, 4, part)
    cuts = []
    for r in range(4):
        gate = pick(gate_cut, p ^ r, 2).reshape(rows, -1)
        up = pick(up_cut, p ^ r, 2).reshape(rows, -1)
        cuts.append(jnp.concatenate([gate, up], axis=1))
    return cuts


def by_source(came, p):
    out = jnp.zeros((4,) + came[0].shape, BF)
    for r in range(4):
        out = place(out, came[r][None], (p ^ r, 0, 0))
    return out


def gather_columns(mine, rows):
    n = lax.axis_size("dp")
    columns = mine.shape[2]
    whole = lax.all_gather(
        mine.reshape(4 * rows, columns),
        "dp",
        axis_index_groups=column_groups(True),
        axis=0,
        tiled=True,
    )
    whole = whole.reshape(n // 8, 2, 4, rows, columns).transpose(0, 2, 1, 3, 4)
    return whole.reshape(n * rows, columns)


def gather_weights_plainly(local, w_gate, w_up, w_down, p):
    rows = local.shape[0]
    gathered = lax.all_gather(local, "dp", axis=0, tiled=True)
    cuts = column_cuts(w_gate, w_up, p, 2 * w_down.shape[0])
    came = [cuts[0]] + [swap(cuts[r], r << 1) for r in (1, 2, 3)]
    wb = gather_columns(by_source(came, p), rows)
    wd = lax.all_gather(
        w_down, "dp", axis_index_groups=column_groups(True), axis=0, tiled=True
    )
    return gathered, wb, wd


def unset(shape, dtype):
    return pl.pallas_call(
        lambda out: None,
        out_shape=jax.ShapeDtypeStruct(shape, dtype),
        out_specs=pl.BlockSpec(memory_space=pl.ANY),
        name="unset",
    )()


def packed(pieces):
    widths = [piece.shape[1] for piece in pieces]
    rows = pieces[0].shape[0]

    def kernel(*refs):
        out = refs[-1]
        at = 0
        for ref, size in zip(refs[:-1], widths):
            out[:, at : at + size] = ref[...]
            at += size

    return pl.pallas_call(
        kernel,
        out_shape=jax.ShapeDtypeStruct((rows, sum(widths)), pieces[0].dtype),
        name="packed",
    )(*pieces)


def column_cuts_kernel(w_gate, w_up, p, part):
    rows, ff = w_gate.shape
    planes = ff // (4 * part)
    units = planes * part

    def kernel(p_ref, gate, up, *outs):
        for r, out in enumerate(outs):
            q = p_ref[0] ^ r
            for k in range(planes):
                start = pl.multiple_of((4 * k + q) * part, LANES)
                out[:, k * part : (k + 1) * part] = gate[:, pl.ds(start, part)]
                out[:, units + k * part : units + (k + 1) * part] = up[:, pl.ds(start, part)]

    shape = jax.ShapeDtypeStruct((rows, 2 * units), w_gate.dtype)
    return pl.pallas_call(
        kernel,
        out_shape=[shape] * 4,
        in_specs=[pl.BlockSpec(memory_space=pltpu.SMEM)]
        + [pl.BlockSpec(memory_space=pltpu.VMEM)] * 2,
        name="column_cuts",
    )(p[None], w_gate, w_up)


def gather_weights(local, w_gate, w_up, w_down, place_bits):
    z, y, x, c = place_bits
    p = 2 * y + x
    rows, columns = local.shape
    ff_rows, width = w_down.shape
    end = (z == 0) | (z == 3)
    up_pairs = [(0, 1), (1, 2), (2, 3)]
    down_pairs = [(1, 0), (2, 1), (3, 2)]
    far_pairs = [(0, 2), (3, 1)]
    out_pairs = [(1, 0), (2, 3)]
    z_b = jnp.where(z == 0, 1, z - 1)
    z_c = jnp.where(z < 2, 2, jnp.where(z == 2, 3, 1))
    z_d = jnp.where(z < 2, 3, 0)
    out = unset((4, 2, 2, 2, rows, columns), BF)

    def near_side(up, down):
        return jnp.where(z == 0, down, up)

    def to_pass_on(up, down):
        return jnp.where(z == 1, down, up)

    def put_x(out, piece, z_k, at_y, core):
        return place(out, piece[None, None, :, None], (z_k, at_y, 0, core, 0, 0))

    def put_y(out, piece, z_k, at_x, core):
        return place(out, piece[None, :, None, None], (z_k, 0, at_x, core, 0, 0))

    def in_order(bit, mine, theirs):
        return jnp.stack([jnp.where(bit == 0, mine, theirs), jnp.where(bit == 0, theirs, mine)])

    def put(out, pair, z_a, z_b, at_y, at_x, core):
        out = put_x(out, pair[0], z_a, at_y, core)
        return put_y(out, pair[1], z_b, at_x, core)

    with jax.named_scope("phase_0"):
        cuts = column_cuts_kernel(w_gate, w_up, p, 2 * ff_rows)
        up, down, came_x, came_y, came_xy = tied(
            along_z(local, up_pairs),
            along_z(local, down_pairs),
            swap(cuts[1], 2),
            swap(cuts[2], 4),
            swap(cuts[3], 6),
        )
    with jax.named_scope("phase_1"):
        b = near_side(up, down)
        a, b, passing = tied(local, b, to_pass_on(up, down))
        a_x, b_y, far, first = tied(
            swap(a, 2), swap(b, 4), along_z(a, far_pairs), along_z(passing, out_pairs)
        )
        gu = unset((4, rows, cuts[0].shape[1]), BF)
        for r, piece in enumerate((cuts[0], came_x, came_y, came_xy)):
            gu = place(gu, piece[None], (p ^ r, 0, 0))
    with jax.named_scope("phase_2"):
        a2, b2, far, gu = tied(in_order(x, a, a_x), in_order(y, b, b_y), far, gu)
        g_up, g_down = along_z(gu, up_pairs), along_z(gu, down_pairs)
        a_far, b_far, second = tied(swap(a2, 4), swap(b2, 2), along_z(far, out_pairs))
        near_1 = jnp.stack([a2, b2])
        out = put(out, near_1, z, z_b, y, x, c)
    with jax.named_scope("phase_3"):
        a, b = jnp.where(end, first, down), jnp.where(end, second, far)
        a, b, near_1 = tied(a, b, near_1)
        a_x, b_y, g_up, g_down, core_1 = tied(
            swap(a, 2), swap(b, 4), g_up, g_down, swap(near_1, 1)
        )
        out = put(out, jnp.stack([a_far, b_far]), z, z_b, 1 - y, 1 - x, c)
    with jax.named_scope("phase_4"):
        a2, b2, gu, passing, far_1 = tied(
            in_order(x, a, a_x),
            in_order(y, b, b_y),
            gu,
            to_pass_on(g_up, g_down),
            jnp.stack([a_far, b_far]),
        )
        g_far, g_first = along_z(gu, far_pairs), along_z(passing, out_pairs)
        a_far, b_far, core_2 = tied(swap(a2, 4), swap(b2, 2), swap(far_1, 1))
        out = put(out, core_1, z, z_b, y, x, 1 - c)
        near_2 = jnp.stack([a2, b2])
        out = put(out, near_2, z_c, z_d, y, x, c)
    with jax.named_scope("phase_5"):
        near_2, far_2 = tied(near_2, jnp.stack([a_far, b_far]))
        core_3, core_4 = tied(swap(near_2, 1), swap(far_2, 1))
        out = put(out, core_2, z, z_b, 1 - y, 1 - x, 1 - c)
        out = put(out, far_2, z_c, z_d, 1 - y, 1 - x, c)
        out = put(out, core_3, z_c, z_d, y, x, 1 - c)
        out = put(out, core_4, z_c, z_d, 1 - y, 1 - x, 1 - c)
        gathered = out.reshape(32 * rows, columns)


    def step_1(beside):
        g_in, f_in, d_in, beside = tied(g_far, g_first, w_down, beside)
        g_second = along_z(g_in, out_pairs)
        return beside, (g_in, f_in, g_second, along_z(d_in, up_pairs), along_z(d_in, down_pairs))

    def step_2(state, beside):
        g_in, f_in, g_second, d_up, d_down = state
        pieces = jnp.stack(
            [gu, near_side(g_up, g_down), jnp.where(end, f_in, g_down), jnp.where(end, g_second, g_in)]
        )
        pieces, d_in, d_pass, d_up, d_down, beside = tied(
            pieces, w_down, to_pass_on(d_up, d_down), d_up, d_down, beside
        )
        moving = (swap(pieces, 1), along_z(d_in, far_pairs), along_z(d_pass, out_pairs))

        def step_3(others, d_far, d_first):
            d_second = along_z(d_far, out_pairs)
            wb = unset((4, 4, 2) + gu.shape[1:], BF)
            places = (z, z_b, z_c, z_d)
            for k in range(4):
                wb = place(wb, pieces[k][None, :, None], (places[k], 0, c, 0, 0))
                wb = place(wb, others[k][None, :, None], (places[k], 0, 1 - c, 0, 0))
            d_all = jnp.stack(
                [
                    w_down,
                    near_side(d_up, d_down),
                    jnp.where(end, d_first, d_down),
                    jnp.where(end, d_second, d_far),
                ]
            )
            d_others = swap(d_all, 1)
            wd = unset((4, 2, ff_rows, width), BF)
            for k in range(4):
                wd = place(wd, d_all[k][None, None], (places[k], c, 0, 0))
                wd = place(wd, d_others[k][None, None], (places[k], 1 - c, 0, 0))
            return wb.reshape(32 * rows, -1), wd.reshape(8 * ff_rows, width)

        return beside, moving, step_3

    return gathered, step_1, step_2


def plane_step_1(parts, place_bits):
    z, y, x, c = place_bits
    half = parts.shape[0] // 2
    a, b = parts[:half], parts[half:]
    return (swap(pick(a, 1 - y, 1).astype(BF), 4), swap(pick(b, 1 - x, 2).astype(BF), 2))


def plane_step_2(parts, came, place_bits):
    z, y, x, c = place_bits
    half = parts.shape[0] // 2
    a = pick(parts[:half], y, 1) + came[0].astype(F32)
    b = pick(parts[half:], x, 2) + came[1].astype(F32)
    moving = (swap(pick(a, 1 - x, 1).astype(BF), 2), swap(pick(b, 1 - y, 1).astype(BF), 4))
    return (a, b), moving


def plane_step_3(sums, came, place_bits):
    z, y, x, c = place_bits
    a = pick(sums[0], x, 1) + came[0].astype(F32)
    b = pick(sums[1], y, 1) + came[1].astype(F32)
    return jnp.concatenate([a, b])


def core_first(count, rows):
    order = jnp.arange(count)
    per_core = count // 2
    core, rest = order // per_core, order % per_core
    source = (rest // rows * 2 + core) * rows + rest % rows
    return (jnp.arange(count)[:, None] == source[None, :]).astype(BF)


def core_halves(values, c):
    width = values.shape[1] // 2
    return (
        lax.dynamic_slice_in_dim(values, c * width, width, 1),
        lax.dynamic_slice_in_dim(values, (1 - c) * width, width, 1),
    )


def split_gather(rows, beside=(), then=lambda *values: values):
    half = rows.shape[0] // 2
    a, b = rows[:half], rows[half:]
    a_x, b_y, *beside = tied(swap(a, 2), swap(b, 4), *beside)
    a2, b2 = tied(jnp.concatenate([a, a_x]), jnp.concatenate([b, b_y]))
    a_far, b_far = swap(a2, 4), swap(b2, 2)
    beside = then(*beside)
    a_far, b_far = tied(a_far, b_far)
    return (jnp.concatenate([a2, b2]), jnp.concatenate([a_far, b_far]), beside)


def split_reduce(near, far, beside=(), later=lambda *values: values):
    two = far.shape[0] // 2
    one = two // 2
    low = far.astype(BF)
    came_a, came_b, *beside = tied(swap(low[:two], 4), swap(low[two:], 2), *beside)
    a = near[:two] + came_a.astype(F32)
    b = near[two:] + came_b.astype(F32)
    came_a, came_b, *beside = tied(
        swap(a[one:].astype(BF), 2), swap(b[one:].astype(BF), 4), *later(*beside)
    )
    own = jnp.concatenate([a[:one] + came_a.astype(F32), b[:one] + came_b.astype(F32)])
    return (own, *beside)


def spread_columns(came, p, part):
    units = came[0].shape[1] // 2
    natural = []
    for q in range(4):
        piece = came[3]
        for r in (0, 1, 2):
            piece = jnp.where(p == (q ^ r), came[r], piece)
        natural.append(piece.astype(F32))
    return tuple(
        jnp.concatenate(
            [
                natural[q][:, start + k * part : start + (k + 1) * part]
                for k in range(units // part)
                for q in range(4)
            ],
            axis=1,
        )
        for start in (0, units)
    )


def rotation_tables(length, width):
    half_width = width // 2
    position = jnp.arange(length, dtype=F32)[:, None]
    freq_rate = ROPE_BASE ** (-2.0 * jnp.arange(half_width, dtype=F32) / width)
    angle_table = position * freq_rate[None, :]
    return (jnp.cos(angle_table)[:, None, :], jnp.sin(angle_table)[:, None, :])


def turn(heads_in, cosine_lookup, sine_lookup):
    half_width = heads_in.shape[-1] // 2
    left_part = heads_in[..., :half_width]
    right_part = heads_in[..., half_width:]
    return jnp.concatenate(
        [
            left_part * cosine_lookup - right_part * sine_lookup,
            right_part * cosine_lookup + left_part * sine_lookup,
        ],
        axis=-1,
    )


def norm_rows(field_in, gain_vec):
    inv_scale = lax.rsqrt(jnp.mean(field_in * field_in, axis=-1, keepdims=True) + EPSILON)
    return (field_in * inv_scale * gain_vec, inv_scale)


def norm_back(upstream, field_in, inv_scale, gain_vec):
    gain_grad = jnp.sum(upstream * field_in * inv_scale, axis=0)
    scaled_up = upstream * gain_vec
    field_grad = inv_scale * scaled_up - field_in * inv_scale**3 * jnp.mean(
        scaled_up * field_in, axis=-1, keepdims=True
    )
    return (gain_grad, field_grad)


def probabilities(query_heads, key_heads):
    score_scale = 1.0 / math.sqrt(HEAD_SIZE)
    raw_scores = (
        jnp.einsum("bqhrd,bkhd->bhrqk", query_heads, key_heads, preferred_element_type=F32)
        * score_scale
    )
    causal = jnp.arange(SEQ)[:, None] >= jnp.arange(SEQ)[None, :]
    scores = jnp.where(causal, raw_scores, MASK_FILL)
    row_max = jnp.max(scores, axis=-1, keepdims=True)
    weights = jnp.exp(scores - row_max)
    return weights / jnp.sum(weights, axis=-1, keepdims=True)


def ffn_forward(rows, w_both, w_down):
    pre = mm(rows, w_both)
    units = pre.shape[1] // 2
    hidden = (jax.nn.silu(pre[:, :units]) * pre[:, units:]).astype(BF)
    return (mm(hidden, w_down), pre, hidden)


def ffn_backward(grad_low, pre, w_both, w_down):
    grad_hidden = mm_t(grad_low, w_down)
    units = pre.shape[1] // 2
    gate_pre, up_pre = pre[:, :units], pre[:, units:]
    gate_sigmoid = jax.nn.sigmoid(gate_pre)
    grad_gate = grad_hidden * up_pre * gate_sigmoid * (1.0 + gate_pre * (1.0 - gate_sigmoid))
    grad_up = grad_hidden * gate_pre * gate_sigmoid
    grads = jnp.concatenate([grad_gate.astype(BF), grad_up.astype(BF)], axis=1)
    return (mm_t(grads, w_both), grads)


def body(
    tokens,
    teacher,
    valid_mask,
    w_query,
    key_weight_matrix,
    value_weight_matrix,
    w_output,
    w_gate,
    w_up,
    w_down,
    attn_gain,
    ffn_gain,
):
    n = lax.axis_size("dp")
    planes = n // 8
    position = lax.axis_index("dp")
    c, x, y, z = position % 2, position // 2 % 2, position // 4 % 2, position // 8
    bits = (z, y, x, c)
    p = position // 2 % 4
    rows = w_query.shape[0]
    width = w_query.shape[1]
    kv_width = key_weight_matrix.shape[1]
    ff_rows = w_down.shape[0]
    ff = w_gate.shape[1]
    count = tokens.shape[0]
    sequences = count // SEQ
    groups = QUERY_HEAD_COUNT // KEY_VALUE_HEADS
    score_scale = 1.0 / math.sqrt(HEAD_SIZE)
    cosine_lookup, sine_lookup = rotation_tables(SEQ, HEAD_SIZE)

    part = 2 * ff_rows
    units = planes * part
    gains = jnp.stack([attn_gain, ffn_gain], axis=1)
    gains = jnp.pad(gains, ((0, 0), (0, LANES - 2)))
    local = packed([w_query, key_weight_matrix, value_weight_matrix, w_output, gains])
    if planes == 4:
        gathered, step_1, step_2 = gather_weights(local, w_gate, w_up, w_down, bits)
    else:
        gathered, wb, wd = gather_weights_plainly(local, w_gate, w_up, w_down, p)

    with jax.named_scope("attention_forward"):
        wide = width + 2 * kv_width
        wqkv = gathered[:, :wide]
        wo = gathered[:, wide : wide + width]
        gain_in = gathered[:, wide + width].astype(F32)
        gain_mid = gathered[:, wide + width + 1].astype(F32)
        inputs_f = tokens.astype(F32)
        normed, inv_attn = norm_rows(inputs_f, gain_in)
        normed_in = normed.astype(BF)
        heads = (sequences, SEQ, QUERY_HEAD_COUNT, HEAD_SIZE)
        kv_heads = (sequences, SEQ, KEY_VALUE_HEADS, HEAD_SIZE)
        grouped = (sequences, SEQ, KEY_VALUE_HEADS, groups, HEAD_SIZE)
        raw = mm(normed_in, wqkv)
        if planes == 4:
            raw, moving = step_1(raw)
        query = turn(raw[:, :width].reshape(heads), cosine_lookup, sine_lookup)
        query = query.astype(BF).reshape(grouped)
        key = raw[:, width : width + kv_width].reshape(kv_heads)
        key = turn(key, cosine_lookup, sine_lookup).astype(BF)
        value = raw[:, width + kv_width :].astype(BF).reshape(kv_heads)
        probs = probabilities(query, key)
        probs_low = probs.astype(BF)
        mixed = jnp.einsum("bhrqk,bkhd->bqhrd", probs_low, value, preferred_element_type=F32)
        mixed = mixed.reshape(count, width).astype(BF)
        hidden_res = inputs_f + mm(mixed, wo)
        normed_two, inv_ffn = norm_rows(hidden_res, gain_mid)
        normed_mid = normed_two.astype(BF)

    with jax.named_scope("ffn_forward"):
        if planes == 4:
            normed_mid, moving, step_3 = step_2(moving, normed_mid)
            near, far, moving = split_gather(normed_mid, moving)
            wb, wd = step_3(*moving)
        else:
            near, far, moving = split_gather(normed_mid)
        y_near, pre_near, hid_near = ffn_forward(near, wb, wd)
        y_far, pre_far, hid_far = ffn_forward(far, wb, wd)
        result = hidden_res + split_reduce(y_near, y_far)[0]
        out_act = result.astype(BF)

    with jax.named_scope("loss"):
        mask_f = valid_mask.astype(F32)
        grad_out = (result - teacher.astype(F32)) * mask_f[:, None]
        sums = jnp.stack([jnp.sum(grad_out * grad_out), jnp.sum(mask_f)])
        sums = jnp.broadcast_to(sums[:, None], (2, LANES))

    high = n // 2
    rest = [1 << k for k in range(4, n.bit_length() - 2)]

    with jax.named_scope("ffn_backward"):
        grad_low, sums = tied(grad_out.astype(BF), sums)

        def sums_further(*came):
            value = sums + came[0]
            for mask in rest:
                value = value + swap(value, mask)
            return (value, swap(value, 8))

        d_near, d_far, (sums, sums_came) = split_gather(grad_low, (swap(sums, 1),), sums_further)
        m_near, g_near = ffn_backward(d_near, pre_near, wb, wd)
        m_far, g_far = ffn_backward(d_far, pre_far, wb, wd)
        m_near, m_far, sums, sums_came = tied(m_near, m_far, sums, sums_came)
        sums = sums + sums_came
        by_core = core_first(width, rows)
        hid = jnp.concatenate([hid_near, hid_far])
        d_all = jnp.concatenate([d_near, d_far])
        mid_all = mm(jnp.concatenate([near, far]), by_core).astype(BF)
        g_all = jnp.concatenate([g_near, g_far])
        mid_mine, mid_theirs = core_halves(mid_all, c)
        g_down = t_mm(hid, d_all).reshape(planes, 2, ff_rows, width)
        beside = (
            swap(pick(g_down, 1 - c, 1).astype(BF), 1),
            pick(g_down, c, 1),
            t_mm(mid_theirs, g_all).astype(BF),
            sums,
            swap(sums, high),
        )

        def later(came, own, theirs, sums, sums_came):
            g_down = own + came.astype(F32)
            sums = sums + sums_came
            started = (walk_start(g_down, z),) if planes == 4 else ()
            return (swap(theirs, 1), sums, swap(sums, 2), g_down, started)

        def later_flat(*values):
            theirs_came, sums, sums_came, g_down, started = later(*values)
            moving.extend(started)
            return (theirs_came, sums, sums_came, g_down)

        moving = []
        grad_mid, both_came, sums, sums_came, g_down = split_reduce(
            m_near, m_far, beside, later_flat
        )
        sums = sums + sums_came
        g_both = t_mm(mid_mine, g_all) + both_came.astype(F32)
        g_both = g_both.reshape(planes, 4, rows, 2 * units)

    with jax.named_scope("attention_backward"):
        grad_gain_mid, grad_res = norm_back(grad_mid, hidden_res, inv_ffn, gain_mid)
        grad_res = grad_out + grad_res
        res_low = grad_res.astype(BF)
        mixed_mine, mixed_theirs = core_halves(mm(mixed, by_core).astype(BF), c)
        wo_came, sums_came = tied(swap(t_mm(mixed_theirs, res_low).astype(BF), 1), swap(sums, 4))
        sums = sums + sums_came
        loss = sums[0, 0] / (sums[1, 0] * width)
        shape = (planes, 2, 2, rows, -1)
        g_wo = (t_mm(mixed_mine, res_low) + wo_came.astype(F32)).reshape(shape)
        if planes == 4:
            g_wo, down_came, g_down = tied(g_wo, moving[0], g_down)
            down_moving = walk_end(g_down, down_came, z)
        wo_moving = plane_step_1(g_wo, bits)
        grad_mixed = mm_t(res_low, wo).astype(BF).reshape(grouped)
        grad_probs = jnp.einsum(
            "bqhrd,bkhd->bhrqk", grad_mixed, value, preferred_element_type=F32
        )
        grad_scores = probs * (grad_probs - jnp.sum(probs * grad_probs, axis=-1, keepdims=True))
        grad_scores = grad_scores.astype(BF)
        if planes == 4:
            grad_scores, g_both, *came = tied(grad_scores, g_both, *wo_moving, *down_moving)
            wo_came, down_came = came[:2], came[2:]
            g_down = owned(g_down, down_came, z)
            both_moving = walk_start(g_both, z)
        else:
            wo_came = wo_moving
            g_down = z_reduce(g_down, z)
        g_wo, wo_moving = plane_step_2(g_wo, wo_came, bits)
        grad_query = score_scale * jnp.einsum(
            "bhrqk,bkhd->bqhrd", grad_scores, key, preferred_element_type=F32
        )
        grad_key = score_scale * jnp.einsum(
            "bhrqk,bqhrd->bkhd", grad_scores, query, preferred_element_type=F32
        )
        grad_value = jnp.einsum(
            "bhrqk,bqhrd->bkhd", probs_low, grad_mixed, preferred_element_type=F32
        )
        query_back = turn(grad_query.reshape(heads), cosine_lookup, -sine_lookup)
        query_back = query_back.reshape(count, width).astype(BF)
        key_back = turn(grad_key, cosine_lookup, -sine_lookup).reshape(count, kv_width).astype(BF)
        value_back = grad_value.reshape(count, kv_width).astype(BF)
        grad_raw = jnp.concatenate([query_back, key_back, value_back], axis=1)
        normed_mine, normed_theirs = core_halves(mm(normed_in, by_core).astype(BF), c)
        grad_raw, *wo_came = tied(grad_raw, *wo_moving)
        g_wo = plane_step_3(g_wo, wo_came, bits)

    with jax.named_scope("input_gradient"):
        qkv_came = swap(t_mm(normed_theirs, grad_raw).astype(BF), 1)
        g_qkv = t_mm(normed_mine, grad_raw) + qkv_came.astype(F32)
        grad_in = mm_t(grad_raw, wqkv)
        grad_gain_in, grad_tokens = norm_back(grad_in, inputs_f, inv_attn, gain_in)
        input_grad = (grad_res + grad_tokens).astype(BF)
        gains = jnp.stack([grad_gain_in, grad_gain_mid])

    with jax.named_scope("weight_gradients_to_owners"):
        g_qkv = g_qkv.reshape(shape)
        g_qkv, gains = tied(g_qkv, gains)
        qkv_came = tied(*plane_step_1(g_qkv, bits), swap(gains, 1))
        gains = gains + qkv_came[2]
        if planes == 4:
            g_both, both_came, *qkv_came = tied(g_both, both_moving, *qkv_came[:2])
            both_moving = walk_end(g_both, both_came, z)
        else:
            g_both = z_reduce(g_both, z)
        g_qkv, qkv_moving = plane_step_2(g_qkv, qkv_came[:2], bits)
        if planes == 4:
            *qkv_came, both_0, both_1, both_2 = tied(*qkv_moving, *both_moving)
            g_both = owned(g_both, (both_0, both_1, both_2), z)
        else:
            qkv_came = qkv_moving
        g_qkv = plane_step_3(g_qkv, qkv_came, bits)
        g_both = g_both.astype(BF)
        g_all = jnp.concatenate([g_qkv, g_wo], axis=2)
        gains, g_all, g_both = tied(gains, g_all, g_both)
        if planes == 4:
            all_moving = walk_start(g_all, z)
        came = [pick(g_both, p ^ r, 0) for r in range(4)]
        gains_came, *moved = tied(
            swap(gains, 2), *[swap(came[r], r << 1) for r in (1, 2, 3)]
        )
        gains = gains + gains_came
        for mask in rest:
            gains = gains + swap(gains, mask)
        grad_gate, grad_up = spread_columns([came[0]] + moved, p, part)
        gains_came = swap(gains, 4)
        if planes == 4:
            g_all, all_came, gains_came = tied(g_all, all_moving, gains_came)
            gains = gains + gains_came
            all_0, all_1, all_2, gains_came = tied(*walk_end(g_all, all_came, z), swap(gains, 8))
            g_all = owned(g_all, (all_0, all_1, all_2), z)
        else:
            gains = gains + gains_came
            gains_came = swap(gains, 8)
            g_all = z_reduce(g_all, z)
        gains = gains + gains_came
        gains = gains + swap(gains, high)
        g_gains = lax.dynamic_slice_in_dim(gains, position * rows, rows, 1)
        g_wq = g_all[:, :width]
        g_wk = g_all[:, width : width + kv_width]
        g_wv = g_all[:, width + kv_width : wide]
        g_wo = g_all[:, wide:]

    return (
        out_act,
        loss,
        input_grad,
        g_wq,
        g_wk,
        g_wv,
        g_wo,
        grad_gate,
        grad_up,
        g_down,
        g_gains[0],
        g_gains[1],
    )


def solution(mesh):
    wide, flat = P("dp", None), P("dp")
    in_specs = (wide, wide, flat) + (wide,) * 7 + (flat, flat)
    out_specs = (wide, P(), wide) + (wide,) * 7 + (flat, flat)
    return jax.shard_map(body, mesh=mesh, in_specs=in_specs, out_specs=out_specs, check_vma=False)
```

```python
import math

import jax
import jax.numpy as jnp
from jax import lax
from jax.experimental import pallas as pl
from jax.experimental.pallas import tpu as pltpu
from jax.sharding import PartitionSpec as P

QUERY_HEAD_COUNT = 16
KEY_VALUE_HEADS = 8
HEAD_SIZE = 96
SEQ = 128
EPSILON = 1e-05
ROPE_BASE = 100000.0
MASK_FILL = -1e30
LANES = 128

BF = jnp.bfloat16
F32 = jnp.float32


def dot(a, b, dims):
    return lax.dot_general(a, b, (dims, ((), ())), preferred_element_type=F32)


def mm(a, b):
    return dot(a, b, ((1,), (0,)))


def mm_t(a, b):
    return dot(a, b, ((1,), (1,)))


def t_mm(a, b):
    return dot(a, b, ((0,), (0,)))


def swap(value, mask):
    n = lax.axis_size("dp")
    return lax.ppermute(value, "dp", [(i, i ^ mask) for i in range(n)])


def column_groups(with_core):
    n = lax.axis_size("dp")
    planes = range(n // 8)
    if with_core:
        return [[8 * z + 2 * p + c for z in planes for c in range(2)] for p in range(4)]
    return [[8 * z + 2 * p + c for z in planes] for p in range(4) for c in range(2)]


def z_reduce(parts):
    total = sum(part.astype(F32) for part in parts)
    return lax.psum_scatter(
        total.astype(BF), "dp", axis_index_groups=column_groups(False), scatter_dimension=0
    ).astype(F32)


def summed(parts, index, axis):
    total = pick(parts[0], index, axis).astype(F32)
    for part in parts[1:]:
        total = total + pick(part, index, axis).astype(F32)
    return total


def walk_1(parts, z):
    return along_z(summed(parts, 3 - z, 0).astype(BF), [(0, 1), (3, 2)])


def walk_2(parts, came, z):
    across = summed(parts, jnp.where(z == 0, 2, 1), 0)
    far = summed(parts, jnp.where(z == 1, 3, 0), 0) + came.astype(F32)
    return (
        along_z(across.astype(BF), [(0, 1), (3, 2)]),
        along_z(far.astype(BF), [(1, 3), (2, 0)]),
    )


def walk_3(parts, came, z):
    up = summed(parts, jnp.minimum(z + 1, 3), 0)
    down = summed(parts, jnp.maximum(z - 1, 0), 0)
    came = came.astype(F32)
    up = jnp.where(z == 1, up + came, up)
    down = jnp.where(z == 2, down + came, down)
    return (
        along_z(up.astype(BF), [(0, 1), (1, 2), (2, 3)]),
        along_z(down.astype(BF), [(1, 0), (2, 1), (3, 2)]),
    )


def owned(parts, came, z):
    own = summed(parts, z, 0)
    for piece in came:
        own = own + piece.astype(F32)
    return own


def direct(parts, z):
    return [swap(summed(parts, z ^ k, 0).astype(BF), 8 * k) for k in (3, 2, 1)]


def along_z(value, pairs):
    return lax.ppermute(
        value, "dp", [(8 * a + i, 8 * b + i) for a, b in pairs for i in range(8)]
    )


def tied(*values):
    return lax.optimization_barrier(values)


def place(out, piece, where):
    return lax.dynamic_update_slice(out, piece, where)


def pick(parts, index, axis):
    return lax.dynamic_index_in_dim(parts, index, axis, keepdims=False)


def column_cuts(w_gate, w_up, p, part):
    rows = w_gate.shape[0]
    gate_cut = w_gate.reshape(rows, -1, 4, part)
    up_cut = w_up.reshape(rows, -1, 4, part)
    cuts = []
    for r in range(4):
        gate = pick(gate_cut, p ^ r, 2).reshape(rows, -1)
        up = pick(up_cut, p ^ r, 2).reshape(rows, -1)
        cuts.append(jnp.concatenate([gate, up], axis=1))
    return cuts


def by_source(came, p):
    out = jnp.zeros((4,) + came[0].shape, BF)
    for r in range(4):
        out = place(out, came[r][None], (p ^ r, 0, 0))
    return out


def gather_columns(mine, rows):
    n = lax.axis_size("dp")
    columns = mine.shape[2]
    whole = lax.all_gather(
        mine.reshape(4 * rows, columns),
        "dp",
        axis_index_groups=column_groups(True),
        axis=0,
        tiled=True,
    )
    whole = whole.reshape(n // 8, 2, 4, rows, columns).transpose(0, 2, 1, 3, 4)
    return whole.reshape(n * rows, columns)


def gather_weights_plainly(local, w_gate, w_up, w_down, p):
    rows = local.shape[0]
    gathered = lax.all_gather(local, "dp", axis=0, tiled=True)
    cuts = column_cuts(w_gate, w_up, p, 2 * w_down.shape[0])
    came = [cuts[0]] + [swap(cuts[r], r << 1) for r in (1, 2, 3)]
    wb = gather_columns(by_source(came, p), rows)
    wd = lax.all_gather(
        w_down, "dp", axis_index_groups=column_groups(True), axis=0, tiled=True
    )
    return gathered, wb, wd


def unset(shape, dtype):
    return pl.pallas_call(
        lambda out: None,
        out_shape=jax.ShapeDtypeStruct(shape, dtype),
        out_specs=pl.BlockSpec(memory_space=pl.ANY),
        name="unset",
    )()


def packed(pieces):
    widths = [piece.shape[1] for piece in pieces]
    rows = pieces[0].shape[0]

    def kernel(*refs):
        out = refs[-1]
        at = 0
        for ref, size in zip(refs[:-1], widths):
            out[:, at : at + size] = ref[...]
            at += size

    return pl.pallas_call(
        kernel,
        out_shape=jax.ShapeDtypeStruct((rows, sum(widths)), pieces[0].dtype),
        name="packed",
    )(*pieces)


def column_cuts_kernel(w_gate, w_up, p, part):
    rows, ff = w_gate.shape
    planes = ff // (4 * part)
    units = planes * part

    def kernel(p_ref, gate, up, *outs):
        for r, out in enumerate(outs):
            q = p_ref[0] ^ r
            for k in range(planes):
                start = pl.multiple_of((4 * k + q) * part, LANES)
                out[:, k * part : (k + 1) * part] = gate[:, pl.ds(start, part)]
                out[:, units + k * part : units + (k + 1) * part] = up[:, pl.ds(start, part)]

    shape = jax.ShapeDtypeStruct((rows, 2 * units), w_gate.dtype)
    return pl.pallas_call(
        kernel,
        out_shape=[shape] * 4,
        in_specs=[pl.BlockSpec(memory_space=pltpu.SMEM)]
        + [pl.BlockSpec(memory_space=pltpu.VMEM)] * 2,
        name="column_cuts",
    )(p[None], w_gate, w_up)


def assembled(pieces, places):
    blocks, rows, columns = pieces[0].shape
    count = len(pieces)

    def kernel(at, *refs):
        out, sems = refs[count], refs[count + 1]
        copies = []
        for i in range(count):
            for j in range(blocks):
                start = pl.multiple_of(at[i, j], 16)
                copy = pltpu.make_async_copy(
                    refs[i].at[j], out.at[pl.ds(start, rows)], sems.at[i, j]
                )
                copy.start()
                copies.append(copy)
        for copy in copies:
            copy.wait()

    size = count * blocks * rows * columns * 2
    return pl.pallas_call(
        kernel,
        out_shape=jax.ShapeDtypeStruct((count * blocks * rows, columns), pieces[0].dtype),
        in_specs=[pl.BlockSpec(memory_space=pltpu.SMEM)]
        + [pl.BlockSpec(memory_space=pl.ANY)] * count,
        out_specs=pl.BlockSpec(memory_space=pltpu.VMEM),
        scratch_shapes=[pltpu.SemaphoreType.DMA((count, blocks))],
        compiler_params=pltpu.CompilerParams(vmem_limit_bytes=16 * 2**20),
        cost_estimate=pl.CostEstimate(flops=0, bytes_accessed=2 * size, transcendentals=0),
        name="assembled",
    )(places, *pieces)


def gather_weights(local, w_gate, w_up, w_down, place_bits):
    z, y, x, c = place_bits
    p = 2 * y + x
    rows, columns = local.shape
    ff_rows, width = w_down.shape
    end = (z == 0) | (z == 3)
    up_pairs = [(0, 1), (1, 2), (2, 3)]
    down_pairs = [(1, 0), (2, 1), (3, 2)]
    far_pairs = [(0, 2), (3, 1)]
    out_pairs = [(1, 0), (2, 3)]
    z_b = jnp.where(z == 0, 1, z - 1)
    z_c = jnp.where(z < 2, 2, jnp.where(z == 2, 3, 1))
    z_d = jnp.where(z < 2, 3, 0)
    out = unset((4, 2, 2, 2, rows, columns), BF)

    def near_side(up, down):
        return jnp.where(z == 0, down, up)

    def to_pass_on(up, down):
        return jnp.where(z == 1, down, up)

    def put_x(out, piece, z_k, at_y, core):
        return place(out, piece[None, None, :, None], (z_k, at_y, 0, core, 0, 0))

    def put_y(out, piece, z_k, at_x, core):
        return place(out, piece[None, :, None, None], (z_k, 0, at_x, core, 0, 0))

    def in_order(bit, mine, theirs):
        return jnp.stack([jnp.where(bit == 0, mine, theirs), jnp.where(bit == 0, theirs, mine)])

    def put(out, pair, z_a, z_b, at_y, at_x, core):
        out = put_x(out, pair[0], z_a, at_y, core)
        return put_y(out, pair[1], z_b, at_x, core)

    with jax.named_scope("phase_0"):
        cuts = column_cuts_kernel(w_gate, w_up, p, 2 * ff_rows)
        up, down, came_x, came_y, came_xy = tied(
            along_z(local, up_pairs),
            along_z(local, down_pairs),
            swap(cuts[1], 2),
            swap(cuts[2], 4),
            swap(cuts[3], 6),
        )
    with jax.named_scope("phase_1"):
        b = near_side(up, down)
        a, b, passing = tied(local, b, to_pass_on(up, down))
        a_x, b_y, far, first = tied(
            swap(a, 2), swap(b, 4), along_z(a, far_pairs), along_z(passing, out_pairs)
        )
        gu = unset((4, rows, cuts[0].shape[1]), BF)
        for r, piece in enumerate((cuts[0], came_x, came_y, came_xy)):
            gu = place(gu, piece[None], (p ^ r, 0, 0))
    with jax.named_scope("phase_2"):
        a2, b2, far, gu = tied(in_order(x, a, a_x), in_order(y, b, b_y), far, gu)
        g_up, g_down = along_z(gu, up_pairs), along_z(gu, down_pairs)
        a_far, b_far, second = tied(swap(a2, 4), swap(b2, 2), along_z(far, out_pairs))
        near_1 = jnp.stack([a2, b2])
        out = put(out, near_1, z, z_b, y, x, c)
    with jax.named_scope("phase_3"):
        a, b = jnp.where(end, first, down), jnp.where(end, second, far)
        a, b, near_1 = tied(a, b, near_1)
        a_x, b_y, g_up, g_down, core_1 = tied(
            swap(a, 2), swap(b, 4), g_up, g_down, swap(near_1, 1)
        )
        out = put(out, jnp.stack([a_far, b_far]), z, z_b, 1 - y, 1 - x, c)
    with jax.named_scope("phase_4"):
        a2, b2, gu, passing, far_1 = tied(
            in_order(x, a, a_x),
            in_order(y, b, b_y),
            gu,
            to_pass_on(g_up, g_down),
            jnp.stack([a_far, b_far]),
        )
        g_far, g_first = along_z(gu, far_pairs), along_z(passing, out_pairs)
        a_far, b_far, core_2 = tied(swap(a2, 4), swap(b2, 2), swap(far_1, 1))
        out = put(out, core_1, z, z_b, y, x, 1 - c)
        near_2 = jnp.stack([a2, b2])
        out = put(out, near_2, z_c, z_d, y, x, c)
    with jax.named_scope("phase_5"):
        near_2, far_2, g_far, g_first = tied(
            near_2, jnp.stack([a_far, b_far]), g_far, g_first
        )
        g_second = along_z(g_far, out_pairs)
        core_3, core_4 = tied(swap(near_2, 1), swap(far_2, 1))
        out = put(out, core_2, z, z_b, 1 - y, 1 - x, 1 - c)
        out = put(out, far_2, z_c, z_d, 1 - y, 1 - x, c)
        out = put(out, core_3, z_c, z_d, y, x, 1 - c)
        out = put(out, core_4, z_c, z_d, 1 - y, 1 - x, 1 - c)
        gathered = out.reshape(32 * rows, columns)


    def step_1(beside):
        last, d_in, beside = tied(g_second, w_down, beside)
        return beside, (last, along_z(d_in, up_pairs), along_z(d_in, down_pairs))

    def step_2(state, beside):
        last, d_up, d_down, beside = tied(*state, beside)
        pieces = tied(
            gu,
            near_side(g_up, g_down),
            jnp.where(end, g_first, g_down),
            jnp.where(end, last, g_far),
        )
        d_in, d_pass = tied(w_down, to_pass_on(d_up, d_down))
        moving = (along_z(d_in, far_pairs), along_z(d_pass, out_pairs))
        return beside, (pieces, d_up, d_down, swap(jnp.stack(pieces), 1), *moving)

    def step_3(state, beside):
        pieces, d_up, d_down, *state = state
        others, d_far, d_first, beside = tied(*state, beside)
        moving = (along_z(d_far, out_pairs),)
        along = jnp.stack([z, z_b, z_c, z_d])

        def step_4(d_second):
            mine = 8 * along[:, None] + 2 * jnp.arange(4)[None, :] + c
            theirs = 8 * along[:, None] + 2 * jnp.arange(4)[None, :] + 1 - c
            places = jnp.concatenate([mine, theirs]) * rows
            wb = assembled(list(pieces) + [others[k] for k in range(4)], places.astype(jnp.int32))
            d_all = jnp.stack(
                [
                    w_down,
                    near_side(d_up, d_down),
                    jnp.where(end, d_first, d_down),
                    jnp.where(end, d_second, d_far),
                ]
            )
            d_others = swap(d_all, 1)
            places = jnp.stack([2 * along + c, 2 * along + 1 - c]) * ff_rows
            wd = assembled([d_all, d_others], places.astype(jnp.int32))
            return wb, wd

        return beside, moving, step_4

    return gathered, step_1, step_2, step_3


def halves(parts):
    half = parts[0].shape[2] // 2
    return [part[:, :, :half] for part in parts], [part[:, :, half:] for part in parts]


def plane_step_1(parts, place_bits):
    z, y, x, c = place_bits
    a, b = halves(parts)
    return (swap(summed(a, 1 - y, 1).astype(BF), 4), swap(summed(b, 1 - x, 0).astype(BF), 2))


def plane_step_2(parts, came, place_bits):
    z, y, x, c = place_bits
    a, b = halves(parts)
    a = [summed(a, y, 1), came[0]]
    b = [summed(b, x, 0), came[1]]
    moving = (swap(summed(a, 1 - x, 0).astype(BF), 2), swap(summed(b, 1 - y, 0).astype(BF), 4))
    return (a, b), moving


def plane_step_3(sums, came, place_bits):
    z, y, x, c = place_bits
    a = summed(sums[0], x, 0) + came[0].astype(F32)
    b = summed(sums[1], y, 0) + came[1].astype(F32)
    return jnp.concatenate([a, b])


def core_first(count, rows, chip_order):
    order = jnp.arange(count)
    row, place_of = order % rows, order // rows
    chips = count // rows // 2
    core, chip = place_of // chips, place_of % chips
    if chip_order == "xyz":
        planes = chips // 4
        x, y, z = chip // (2 * planes), chip // planes % 2, chip % planes
        chip = 4 * z + 2 * y + x
    source = (2 * chip + core) * rows + row
    return (jnp.arange(count)[:, None] == source[None, :]).astype(BF)


def core_halves(values, c):
    width = values.shape[1] // 2
    return (
        lax.dynamic_slice_in_dim(values, c * width, width, 1),
        lax.dynamic_slice_in_dim(values, (1 - c) * width, width, 1),
    )


def split_gather(rows, beside=(), then=lambda *values: values):
    half = rows.shape[0] // 2
    a, b = rows[:half], rows[half:]
    a_x, b_y, *beside = tied(swap(a, 2), swap(b, 4), *beside)
    a2, b2 = tied(jnp.concatenate([a, a_x]), jnp.concatenate([b, b_y]))
    a_far, b_far = swap(a2, 4), swap(b2, 2)
    beside = then(*beside)
    a_far, b_far = tied(a_far, b_far)
    return (jnp.concatenate([a2, b2]), jnp.concatenate([a_far, b_far]), beside)


def split_reduce(near, far, beside=(), later=lambda *values: values):
    two = far.shape[0] // 2
    one = two // 2
    low = far.astype(BF)
    came_a, came_b, *beside = tied(swap(low[:two], 4), swap(low[two:], 2), *beside)
    a = near[:two] + came_a.astype(F32)
    b = near[two:] + came_b.astype(F32)
    came_a, came_b, *beside = tied(
        swap(a[one:].astype(BF), 2), swap(b[one:].astype(BF), 4), *later(*beside)
    )
    own = jnp.concatenate([a[:one] + came_a.astype(F32), b[:one] + came_b.astype(F32)])
    return (own, *beside)


def spread_columns(came, p, part):
    units = came[0].shape[1] // 2
    natural = []
    for q in range(4):
        piece = came[3]
        for r in (0, 1, 2):
            piece = jnp.where(p == (q ^ r), came[r], piece)
        natural.append(piece.astype(F32))
    return tuple(
        jnp.concatenate(
            [
                natural[q][:, start + k * part : start + (k + 1) * part]
                for k in range(units // part)
                for q in range(4)
            ],
            axis=1,
        )
        for start in (0, units)
    )


def rotation_tables(length, width):
    half_width = width // 2
    position = jnp.arange(length, dtype=F32)[:, None]
    freq_rate = ROPE_BASE ** (-2.0 * jnp.arange(half_width, dtype=F32) / width)
    angle_table = position * freq_rate[None, :]
    return (jnp.cos(angle_table)[:, None, :], jnp.sin(angle_table)[:, None, :])


def turn(heads_in, cosine_lookup, sine_lookup):
    half_width = heads_in.shape[-1] // 2
    left_part = heads_in[..., :half_width]
    right_part = heads_in[..., half_width:]
    return jnp.concatenate(
        [
            left_part * cosine_lookup - right_part * sine_lookup,
            right_part * cosine_lookup + left_part * sine_lookup,
        ],
        axis=-1,
    )


def norm_rows(field_in, gain_vec):
    inv_scale = lax.rsqrt(jnp.mean(field_in * field_in, axis=-1, keepdims=True) + EPSILON)
    return (field_in * inv_scale * gain_vec, inv_scale)


def norm_back(upstream, field_in, inv_scale, gain_vec):
    gain_grad = jnp.sum(upstream * field_in * inv_scale, axis=0)
    scaled_up = upstream * gain_vec
    field_grad = inv_scale * scaled_up - field_in * inv_scale**3 * jnp.mean(
        scaled_up * field_in, axis=-1, keepdims=True
    )
    return (gain_grad, field_grad)


def probabilities(query_heads, key_heads):
    score_scale = 1.0 / math.sqrt(HEAD_SIZE)
    raw_scores = (
        jnp.einsum("bqhrd,bkhd->bhrqk", query_heads, key_heads, preferred_element_type=F32)
        * score_scale
    )
    causal = jnp.arange(SEQ)[:, None] >= jnp.arange(SEQ)[None, :]
    scores = jnp.where(causal, raw_scores, MASK_FILL)
    row_max = jnp.max(scores, axis=-1, keepdims=True)
    weights = jnp.exp(scores - row_max)
    return weights / jnp.sum(weights, axis=-1, keepdims=True)


def ffn_forward(rows, w_both, w_down):
    pre = mm(rows, w_both)
    units = pre.shape[1] // 2
    hidden = (jax.nn.silu(pre[:, :units]) * pre[:, units:]).astype(BF)
    return (mm(hidden, w_down), pre, hidden)


def ffn_backward(grad_low, pre, w_both, w_down):
    grad_hidden = mm_t(grad_low, w_down)
    units = pre.shape[1] // 2
    gate_pre, up_pre = pre[:, :units], pre[:, units:]
    gate_sigmoid = jax.nn.sigmoid(gate_pre)
    grad_gate = grad_hidden * up_pre * gate_sigmoid * (1.0 + gate_pre * (1.0 - gate_sigmoid))
    grad_up = grad_hidden * gate_pre * gate_sigmoid
    grads = jnp.concatenate([grad_gate.astype(BF), grad_up.astype(BF)], axis=1)
    return (mm_t(grads, w_both), grads)


def body(
    tokens,
    teacher,
    valid_mask,
    w_query,
    key_weight_matrix,
    value_weight_matrix,
    w_output,
    w_gate,
    w_up,
    w_down,
    attn_gain,
    ffn_gain,
):
    n = lax.axis_size("dp")
    planes = n // 8
    position = lax.axis_index("dp")
    c, x, y, z = position % 2, position // 2 % 2, position // 4 % 2, position // 8
    bits = (z, y, x, c)
    p = position // 2 % 4
    rows = w_query.shape[0]
    width = w_query.shape[1]
    kv_width = key_weight_matrix.shape[1]
    ff_rows = w_down.shape[0]
    ff = w_gate.shape[1]
    count = tokens.shape[0]
    sequences = count // SEQ
    groups = QUERY_HEAD_COUNT // KEY_VALUE_HEADS
    score_scale = 1.0 / math.sqrt(HEAD_SIZE)
    cosine_lookup, sine_lookup = rotation_tables(SEQ, HEAD_SIZE)

    part = 2 * ff_rows
    units = planes * part
    gains = jnp.stack([attn_gain, ffn_gain], axis=1)
    gains = jnp.pad(gains, ((0, 0), (0, LANES - 2)))
    local = packed([w_query, key_weight_matrix, value_weight_matrix, w_output, gains])
    if planes == 4:
        gathered, step_1, step_2, step_3 = gather_weights(local, w_gate, w_up, w_down, bits)
    else:
        gathered, wb, wd = gather_weights_plainly(local, w_gate, w_up, w_down, p)

    with jax.named_scope("attention_forward"):
        wide = width + 2 * kv_width
        wqkv = gathered[:, :wide]
        wo = gathered[:, wide : wide + width]
        gain_in = gathered[:, wide + width].astype(F32)
        gain_mid = gathered[:, wide + width + 1].astype(F32)
        inputs_f = tokens.astype(F32)
        normed, inv_attn = norm_rows(inputs_f, gain_in)
        normed_in = normed.astype(BF)
        heads = (sequences, SEQ, QUERY_HEAD_COUNT, HEAD_SIZE)
        kv_heads = (sequences, SEQ, KEY_VALUE_HEADS, HEAD_SIZE)
        grouped = (sequences, SEQ, KEY_VALUE_HEADS, groups, HEAD_SIZE)
        raw = mm(normed_in, wqkv)
        if planes == 4:
            raw, moving = step_1(raw)
        query = turn(raw[:, :width].reshape(heads), cosine_lookup, sine_lookup)
        query = query.astype(BF).reshape(grouped)
        key = raw[:, width : width + kv_width].reshape(kv_heads)
        key = turn(key, cosine_lookup, sine_lookup).astype(BF)
        value = raw[:, width + kv_width :].astype(BF).reshape(kv_heads)
        probs = probabilities(query, key)
        if planes == 4:
            probs, moving = step_2(moving, probs)
        probs_low = probs.astype(BF)
        mixed = jnp.einsum("bhrqk,bkhd->bqhrd", probs_low, value, preferred_element_type=F32)
        mixed = mixed.reshape(count, width).astype(BF)
        hidden_res = inputs_f + mm(mixed, wo)
        normed_two, inv_ffn = norm_rows(hidden_res, gain_mid)
        normed_mid = normed_two.astype(BF)

    with jax.named_scope("ffn_forward"):
        if planes == 4:
            normed_mid, moving, step_4 = step_3(moving, normed_mid)
            near, far, moving = split_gather(normed_mid, moving)
            wb, wd = step_4(*moving)
        else:
            near, far, moving = split_gather(normed_mid)
        y_near, pre_near, hid_near = ffn_forward(near, wb, wd)
        y_far, pre_far, hid_far = ffn_forward(far, wb, wd)
        by_plane = core_first(width, rows, "zyx")
        by_side = core_first(width, rows, "xyz")
        beside = (
            *core_halves(mm(near, by_plane).astype(BF), c),
            *core_halves(mm(far, by_plane).astype(BF), c),
            *core_halves(mm(mixed, by_side).astype(BF), c),
            *core_halves(mm(normed_in, by_side).astype(BF), c),
        )
        result, *halves = split_reduce(y_near, y_far, beside)
        near_mine, near_theirs, far_mine, far_theirs = halves[:4]
        mixed_mine, mixed_theirs, normed_mine, normed_theirs = halves[4:]
        result = hidden_res + result
        out_act = result.astype(BF)

    with jax.named_scope("loss"):
        mask_f = valid_mask.astype(F32)
        grad_out = (result - teacher.astype(F32)) * mask_f[:, None]
        sums = jnp.stack([jnp.sum(grad_out * grad_out), jnp.sum(mask_f)])
        sums = jnp.broadcast_to(sums[:, None], (2, LANES))

    high = n // 2
    rest = [1 << k for k in range(4, n.bit_length() - 2)]

    with jax.named_scope("ffn_backward"):
        grad_low, sums = tied(grad_out.astype(BF), sums)

        def sums_further(*came):
            value = sums + came[0]
            for mask in rest:
                value = value + swap(value, mask)
            return (value, swap(value, 8))

        d_near, d_far, (sums, sums_came) = split_gather(grad_low, (swap(sums, 1),), sums_further)
        m_near, g_near = ffn_backward(d_near, pre_near, wb, wd)
        m_far, g_far = ffn_backward(d_far, pre_far, wb, wd)
        m_near, m_far, sums, sums_came = tied(m_near, m_far, sums, sums_came)
        sums = sums + sums_came
        g_down = (t_mm(hid_near, d_near) + t_mm(hid_far, d_far)).reshape(planes, 2, ff_rows, width)
        beside = (
            swap(pick(g_down, 1 - c, 1).astype(BF), 1),
            pick(g_down, c, 1),
            (t_mm(near_theirs, g_near) + t_mm(far_theirs, g_far)).astype(BF),
            sums,
            swap(sums, high),
        )

        def later(came, own, theirs, sums, sums_came):
            sums = sums + sums_came
            started = (walk_1((own, came), z),) if planes == 4 else ()
            return (swap(theirs, 1), sums, swap(sums, 2), own, came, *started)

        grad_mid, both_came, sums, sums_came, *down, = split_reduce(m_near, m_far, beside, later)
        sums = sums + sums_came
        down, moving = down[:2], down[2:]
        g_both = (t_mm(near_mine, g_near) + t_mm(far_mine, g_far), both_came)
        g_both = [part.reshape(planes, 4, rows, 2 * units) for part in g_both]

    with jax.named_scope("attention_backward"):
        grad_gain_mid, grad_res = norm_back(grad_mid, hidden_res, inv_ffn, gain_mid)
        grad_res = grad_out + grad_res
        res_low = grad_res.astype(BF)
        if planes == 4:
            res_low, moving = tied(res_low, *moving)
            moving, down_far = walk_2(down, moving, z)
        wo_came, sums_came = tied(swap(t_mm(mixed_theirs, res_low).astype(BF), 1), swap(sums, 4))
        sums = sums + sums_came
        loss = sums[0, 0] / (sums[1, 0] * width)
        shape = (2, 2, planes, rows, -1)
        g_wo = [t_mm(mixed_mine, res_low).reshape(shape), wo_came.reshape(shape)]
        wo_moving = plane_step_1(g_wo, bits)
        grad_mixed = mm_t(res_low, wo).astype(BF).reshape(grouped)
        grad_probs = jnp.einsum(
            "bqhrd,bkhd->bhrqk", grad_mixed, value, preferred_element_type=F32
        )
        grad_scores = probs * (grad_probs - jnp.sum(probs * grad_probs, axis=-1, keepdims=True))
        grad_scores = grad_scores.astype(BF)
        if planes == 4:
            wo_0, wo_1, moving, down_far, grad_scores = tied(
                *wo_moving, moving, down_far, grad_scores
            )
            moving = walk_3(down, moving, z)
            wo_came = (wo_0, wo_1)
        else:
            wo_came = wo_moving
            g_down = z_reduce(down)
        g_wo, wo_moving = plane_step_2(g_wo, wo_came, bits)
        grad_query = score_scale * jnp.einsum(
            "bhrqk,bkhd->bqhrd", grad_scores, key, preferred_element_type=F32
        )
        grad_key = score_scale * jnp.einsum(
            "bhrqk,bqhrd->bkhd", grad_scores, query, preferred_element_type=F32
        )
        grad_value = jnp.einsum(
            "bhrqk,bqhrd->bkhd", probs_low, grad_mixed, preferred_element_type=F32
        )
        query_back = turn(grad_query.reshape(heads), cosine_lookup, -sine_lookup)
        query_back = query_back.reshape(count, width).astype(BF)
        key_back = turn(grad_key, cosine_lookup, -sine_lookup).reshape(count, kv_width).astype(BF)
        value_back = grad_value.reshape(count, kv_width).astype(BF)
        grad_raw = jnp.concatenate([query_back, key_back, value_back], axis=1)
        if planes == 4:
            grad_raw, wo_0, wo_1, down_0, down_1 = tied(grad_raw, *wo_moving, *moving)
            wo_came = (wo_0, wo_1)
            g_down = owned(down, (down_far, down_0, down_1), z)
            moving = walk_1(g_both, z)
        else:
            wo_came = wo_moving
        g_wo = plane_step_3(g_wo, wo_came, bits)

    with jax.named_scope("q_k_v_weight_gradients"):
        qkv_came = swap(t_mm(normed_theirs, grad_raw).astype(BF), 1)
        g_qkv = t_mm(normed_mine, grad_raw)
        if planes == 4:
            qkv_came, g_qkv, moving = tied(qkv_came, g_qkv, moving)
            moving, both_far = walk_2(g_both, moving, z)
        g_qkv = [g_qkv.reshape(shape), qkv_came.reshape(shape)]
        qkv_moving = plane_step_1(g_qkv, bits)

    with jax.named_scope("input_gradient"):
        grad_in = mm_t(grad_raw, wqkv)
        grad_gain_in, grad_tokens = norm_back(grad_in, inputs_f, inv_attn, gain_in)
        input_grad = (grad_res + grad_tokens).astype(BF)
        gains = jnp.stack([grad_gain_in, grad_gain_mid])
        gains_came = swap(gains, 1)

    with jax.named_scope("weight_gradients_to_owners"):
        if planes == 4:
            *qkv_came, moving, both_far, gains_came, gains = tied(
                *qkv_moving, moving, both_far, gains_came, gains
            )
            moving = walk_3(g_both, moving, z)
        else:
            qkv_came = qkv_moving
            both = z_reduce(g_both)
        gains = gains + gains_came
        g_qkv, qkv_moving = plane_step_2(g_qkv, qkv_came, bits)
        gains_came = swap(gains, 8)
        if planes == 4:
            qkv_0, qkv_1, both_0, both_1, gains_came = tied(*qkv_moving, *moving, gains_came)
            qkv_came = (qkv_0, qkv_1)
            both = owned(g_both, (both_far, both_0, both_1), z)
        else:
            qkv_came = qkv_moving
        gains = gains + gains_came
        g_qkv = plane_step_3(g_qkv, qkv_came, bits)
        both = both.astype(BF)
        if planes == 4:
            moving = direct([g_qkv], z) + direct([g_wo], z)
        gains_came = swap(gains, high)
        gains, gains_came, both = tied(gains, gains_came, both)
        gains = gains + gains_came
        came = [pick(both, p ^ r, 0) for r in range(4)]
        gains_came, *moved = tied(swap(gains, 2), *[swap(came[r], r << 1) for r in (1, 2, 3)])
        gains = gains + gains_came
        for mask in rest:
            gains = gains + swap(gains, mask)
        grad_gate, grad_up = spread_columns([came[0]] + moved, p, part)
        gains = gains + swap(gains, 4)
        g_gains = lax.dynamic_slice_in_dim(gains, position * rows, rows, 1)
        if planes == 4:
            g_qkv = owned([g_qkv], moving[:3], z)
            g_wo = owned([g_wo], moving[3:], z)
        else:
            g_qkv, g_wo = z_reduce([g_qkv]), z_reduce([g_wo])
        g_wq = g_qkv[:, :width]
        g_wk = g_qkv[:, width : width + kv_width]
        g_wv = g_qkv[:, width + kv_width :]

    return (
        out_act,
        loss,
        input_grad,
        g_wq,
        g_wk,
        g_wv,
        g_wo,
        grad_gate,
        grad_up,
        g_down,
        g_gains[0],
        g_gains[1],
    )


def solution(mesh):
    wide, flat = P("dp", None), P("dp")
    in_specs = (wide, wide, flat) + (wide,) * 7 + (flat, flat)
    out_specs = (wide, P(), wide) + (wide,) * 7 + (flat, flat)
    return jax.shard_map(body, mesh=mesh, in_specs=in_specs, out_specs=out_specs, check_vma=False)
```

```python
import math

import jax
import jax.numpy as jnp
from jax import lax
from jax.experimental import pallas as pl
from jax.experimental.pallas import tpu as pltpu
from jax.sharding import PartitionSpec as P

HEAD_SIZE = 96
SEQ = 128
EPSILON = 1e-05
ROPE_BASE = 100000.0
MASK_FILL = -1e30
LANES = 128

BF = jnp.bfloat16
F32 = jnp.float32
NO_COST = pl.CostEstimate(flops=1, bytes_accessed=1, transcendentals=0)


def dot(a, b, dims):
    return lax.dot_general(a, b, (dims, ((), ())), preferred_element_type=F32)


def mm(a, b):
    return dot(a, b, ((1,), (0,)))


def mm_t(a, b):
    return dot(a, b, ((1,), (1,)))


def t_mm(a, b):
    return dot(a, b, ((0,), (0,)))


def swap(value, mask):
    n = lax.axis_size("dp")
    return lax.ppermute(value, "dp", [(i, i ^ mask) for i in range(n)])


def column_groups(with_core):
    n = lax.axis_size("dp")
    planes = range(n // 8)
    if with_core:
        return [[8 * z + 2 * p + c for z in planes for c in range(2)] for p in range(4)]
    return [[8 * z + 2 * p + c for z in planes] for p in range(4) for c in range(2)]


def z_reduce(parts):
    total = sum(part.astype(F32) for part in parts)
    return lax.psum_scatter(
        total.astype(BF), "dp", axis_index_groups=column_groups(False), scatter_dimension=0
    ).astype(F32)


def summed(parts, index, axis):
    total = pick(parts[0], index, axis).astype(F32)
    for part in parts[1:]:
        total = total + pick(part, index, axis).astype(F32)
    return total


def owned(parts, came, z):
    own = summed(parts, z, 0)
    for piece in came:
        own = own + piece.astype(F32)
    return own


def direct(parts, z):
    return [swap(summed(parts, z ^ k, 0).astype(BF), 8 * k) for k in (3, 2, 1)]


def along_z(value, pairs):
    return lax.ppermute(
        value, "dp", [(8 * a + i, 8 * b + i) for a, b in pairs for i in range(8)]
    )


def tied(*values):
    return lax.optimization_barrier(values)


def place(out, piece, where):
    return lax.dynamic_update_slice(out, piece, where)


def pick(parts, index, axis):
    return lax.dynamic_index_in_dim(parts, index, axis, keepdims=False)


def column_cuts(w_gate, w_up, p, part):
    rows = w_gate.shape[0]
    gate_cut = w_gate.reshape(rows, -1, 4, part)
    up_cut = w_up.reshape(rows, -1, 4, part)
    cuts = []
    for r in range(4):
        gate = pick(gate_cut, p ^ r, 2).reshape(rows, -1)
        up = pick(up_cut, p ^ r, 2).reshape(rows, -1)
        cuts.append(jnp.concatenate([gate, up], axis=1))
    return cuts


def by_source(came, p):
    out = jnp.zeros((4,) + came[0].shape, BF)
    for r in range(4):
        out = place(out, came[r][None], (p ^ r, 0, 0))
    return out


def along_column(value):
    return lax.all_gather(
        value, "dp", axis_index_groups=column_groups(True), axis=0, tiled=True
    )


def sum_to_owners(partial):
    return lax.psum_scatter(
        partial, "dp", axis_index_groups=column_groups(True), scatter_dimension=0, tiled=True
    )


def gather_weights_plainly(local, w_gate, w_up, w_down, p):
    gathered = lax.all_gather(local, "dp", axis=0, tiled=True)
    cuts = column_cuts(w_gate, w_up, p, 2 * w_down.shape[0])
    came = [cuts[0]] + [swap(cuts[r], r << 1) for r in (1, 2, 3)]
    mine = by_source(came, p)
    wb = along_column(mine.reshape(-1, mine.shape[2]))
    return gathered, wb, along_column(w_down)


def merged(came, w_down, p):
    rows, columns = came[0].shape
    ff_rows, width = w_down.shape
    tall = 4 * rows
    side = width * ff_rows // tall
    rest = width - side
    low = tall - ff_rows

    def kernel(p_ref, *refs):
        wd, out = refs[4:]
        for r in range(4):
            start = pl.multiple_of((p_ref[0] ^ r) * rows, 16)
            out[pl.ds(start, rows), :columns] = refs[r][...]
        out[:ff_rows, columns:] = wd[:, :side]
        for k in range(ff_rows // low):
            at = columns + k * rest
            out[ff_rows:, at : at + rest] = wd[k * low : (k + 1) * low, side:]

    return pl.pallas_call(
        kernel,
        out_shape=jax.ShapeDtypeStruct((tall, columns + side), w_down.dtype),
        in_specs=[pl.BlockSpec(memory_space=pltpu.SMEM)]
        + [pl.BlockSpec(memory_space=pltpu.VMEM)] * 5,
        cost_estimate=NO_COST,
        name="merged",
    )(p[None], *came, w_down)


def w_down_from(whole, ff_rows, columns, width):
    side = whole.shape[1] - columns
    rest = width - side
    tall = width * ff_rows // side
    low = tall - ff_rows
    devices = whole.shape[0] // tall

    def kernel(ref, out, sem):
        copies = []
        for i in range(devices):
            top, to = i * tall, i * ff_rows
            pairs = [
                (
                    ref.at[pl.ds(top, ff_rows), pl.ds(columns, side)],
                    out.at[pl.ds(to, ff_rows), pl.ds(0, side)],
                )
            ]
            for k in range(ff_rows // low):
                pairs.append(
                    (
                        ref.at[pl.ds(top + ff_rows, low), pl.ds(columns + k * rest, rest)],
                        out.at[pl.ds(to + k * low, low), pl.ds(side, rest)],
                    )
                )
            for k, (source, target) in enumerate(pairs):
                copies.append(pltpu.make_async_copy(source, target, sem.at[i, k]))
        for copy in copies:
            copy.start()
        for copy in copies:
            copy.wait()

    return pl.pallas_call(
        kernel,
        out_shape=jax.ShapeDtypeStruct((devices * ff_rows, width), whole.dtype),
        in_specs=[pl.BlockSpec(memory_space=pl.ANY)],
        out_specs=pl.BlockSpec(memory_space=pltpu.VMEM),
        scratch_shapes=[pltpu.SemaphoreType.DMA((devices, 1 + ff_rows // low))],
        cost_estimate=NO_COST,
        name="w_down_from",
    )(whole)


def unset(shape, dtype):
    return pl.pallas_call(
        lambda out: None,
        out_shape=jax.ShapeDtypeStruct(shape, dtype),
        out_specs=pl.BlockSpec(memory_space=pl.ANY),
        name="unset",
    )()


def packed(pieces):
    widths = [piece.shape[1] for piece in pieces]
    rows = pieces[0].shape[0]

    def kernel(*refs):
        out = refs[-1]
        at = 0
        for ref, size in zip(refs[:-1], widths):
            out[:, at : at + size] = ref[...]
            at += size

    return pl.pallas_call(
        kernel,
        out_shape=jax.ShapeDtypeStruct((rows, sum(widths)), pieces[0].dtype),
        name="packed",
    )(*pieces)


def column_cuts_kernel(w_gate, w_up, p, part):
    rows, ff = w_gate.shape
    planes = ff // (4 * part)
    units = planes * part

    def kernel(p_ref, gate, up, *outs):
        for r, out in enumerate(outs):
            q = p_ref[0] ^ r
            for k in range(planes):
                start = pl.multiple_of((4 * k + q) * part, LANES)
                out[:, k * part : (k + 1) * part] = gate[:, pl.ds(start, part)]
                out[:, units + k * part : units + (k + 1) * part] = up[:, pl.ds(start, part)]

    shape = jax.ShapeDtypeStruct((rows, 2 * units), w_gate.dtype)
    return pl.pallas_call(
        kernel,
        out_shape=[shape] * 4,
        in_specs=[pl.BlockSpec(memory_space=pltpu.SMEM)]
        + [pl.BlockSpec(memory_space=pltpu.VMEM)] * 2,
        name="column_cuts",
    )(p[None], w_gate, w_up)


def gather_weights(local, w_gate, w_up, w_down, place_bits):
    z, y, x, c = place_bits
    p = 2 * y + x
    rows, columns = local.shape
    ff_rows, width = w_down.shape
    end = (z == 0) | (z == 3)
    up_pairs = [(0, 1), (1, 2), (2, 3)]
    down_pairs = [(1, 0), (2, 1), (3, 2)]
    far_pairs = [(0, 2), (3, 1)]
    out_pairs = [(1, 0), (2, 3)]
    z_b = jnp.where(z == 0, 1, z - 1)
    z_c = jnp.where(z < 2, 2, jnp.where(z == 2, 3, 1))
    z_d = jnp.where(z < 2, 3, 0)
    out = unset((4, 2, 2, 2, rows, columns), BF)

    def near_side(up, down):
        return jnp.where(z == 0, down, up)

    def to_pass_on(up, down):
        return jnp.where(z == 1, down, up)

    def put_x(out, piece, z_k, at_y, core):
        return place(out, piece[None, None, :, None], (z_k, at_y, 0, core, 0, 0))

    def put_y(out, piece, z_k, at_x, core):
        return place(out, piece[None, :, None, None], (z_k, 0, at_x, core, 0, 0))

    def in_order(bit, mine, theirs):
        return jnp.stack([jnp.where(bit == 0, mine, theirs), jnp.where(bit == 0, theirs, mine)])

    def put(out, pair, z_a, z_b, at_y, at_x, core):
        out = put_x(out, pair[0], z_a, at_y, core)
        return put_y(out, pair[1], z_b, at_x, core)

    with jax.named_scope("phase_0"):
        cuts = column_cuts_kernel(w_gate, w_up, p, 2 * ff_rows)
        up, down, came_x, came_y, came_xy = tied(
            along_z(local, up_pairs),
            along_z(local, down_pairs),
            swap(cuts[1], 2),
            swap(cuts[2], 4),
            swap(cuts[3], 6),
        )
    with jax.named_scope("phase_1"):
        b = near_side(up, down)
        a, b, passing = tied(local, b, to_pass_on(up, down))
        a_x, b_y, far, first = tied(
            swap(a, 2), swap(b, 4), along_z(a, far_pairs), along_z(passing, out_pairs)
        )
        ffn = merged((cuts[0], came_x, came_y, came_xy), w_down, p)
    with jax.named_scope("phase_2"):
        a2, b2, far = tied(in_order(x, a, a_x), in_order(y, b, b_y), far)
        near_1 = jnp.stack([a2, b2])
        a_far, b_far, second = tied(swap(a2, 4), swap(b2, 2), along_z(far, out_pairs))
        out = put(out, near_1, z, z_b, y, x, c)
    with jax.named_scope("ffn_weights"):
        ffn = along_column(tied(ffn, second)[0])
    with jax.named_scope("phase_3"):
        a, b = jnp.where(end, first, down), jnp.where(end, second, far)
        a, b, near_1 = tied(a, b, near_1)
        a_x, b_y, core_1 = tied(swap(a, 2), swap(b, 4), swap(near_1, 1))
        far_1 = jnp.stack([a_far, b_far])
        out = put(out, far_1, z, z_b, 1 - y, 1 - x, c)
    with jax.named_scope("phase_4"):
        a2, b2, far_1 = tied(in_order(x, a, a_x), in_order(y, b, b_y), far_1)
        a_far, b_far, core_2 = tied(swap(a2, 4), swap(b2, 2), swap(far_1, 1))
        out = put(out, core_1, z, z_b, y, x, 1 - c)
        near_2 = jnp.stack([a2, b2])
        out = put(out, near_2, z_c, z_d, y, x, c)
    with jax.named_scope("phase_5"):
        near_2, far_2 = tied(near_2, jnp.stack([a_far, b_far]))
        core_3, core_4 = tied(swap(near_2, 1), swap(far_2, 1))
        out = put(out, core_2, z, z_b, 1 - y, 1 - x, 1 - c)
        out = put(out, far_2, z_c, z_d, 1 - y, 1 - x, c)
        out = put(out, core_3, z_c, z_d, y, x, 1 - c)
        out = put(out, core_4, z_c, z_d, 1 - y, 1 - x, 1 - c)
        gathered = out.reshape(32 * rows, columns)
    return gathered, ffn


def halves(parts):
    half = parts[0].shape[2] // 2
    return [part[:, :, :half] for part in parts], [part[:, :, half:] for part in parts]


def plane_step_1(parts, place_bits):
    z, y, x, c = place_bits
    a, b = halves(parts)
    return (swap(summed(a, 1 - y, 1).astype(BF), 4), swap(summed(b, 1 - x, 0).astype(BF), 2))


def plane_step_2(parts, came, place_bits):
    z, y, x, c = place_bits
    a, b = halves(parts)
    a = [summed(a, y, 1), came[0]]
    b = [summed(b, x, 0), came[1]]
    moving = (swap(summed(a, 1 - x, 0).astype(BF), 2), swap(summed(b, 1 - y, 0).astype(BF), 4))
    return (a, b), moving


def plane_step_3(sums, came, place_bits):
    z, y, x, c = place_bits
    a = summed(sums[0], x, 0) + came[0].astype(F32)
    b = summed(sums[1], y, 0) + came[1].astype(F32)
    return jnp.concatenate([a, b])


def reordered(count, rows, order):
    place_of, row = jnp.arange(count) // rows, jnp.arange(count) % rows
    planes = count // rows // 8
    if order == "cxyz":
        core, chip = place_of // (4 * planes), place_of % (4 * planes)
        x, y, z = chip // (2 * planes), chip // planes % 2, chip % planes
    else:
        z, core, y, x = place_of // 8, place_of // 4 % 2, place_of // 2 % 2, place_of % 2
    source = (8 * z + 4 * y + 2 * x + core) * rows + row
    return (jnp.arange(count)[:, None] == source[None, :]).astype(BF)


def core_halves(values, c):
    width = values.shape[1] // 2
    return (
        lax.dynamic_slice_in_dim(values, c * width, width, 1),
        lax.dynamic_slice_in_dim(values, (1 - c) * width, width, 1),
    )


def split_gather(rows, beside=(), then=lambda pieces, *values: values):
    half = rows.shape[0] // 2
    a, b = rows[:half], rows[half:]
    a_x, b_y, *beside = tied(swap(a, 2), swap(b, 4), *beside)
    a2, b2 = tied(jnp.concatenate([a, a_x]), jnp.concatenate([b, b_y]))
    a_far, b_far, *beside = tied(swap(a2, 4), swap(b2, 2), *then((a2, b2), *beside))
    return (jnp.concatenate([a_far, b_far]), *beside)


def split_reduce(near, low, beside=(), later=lambda *values: values):
    two = low.shape[0] // 2
    one = two // 2
    came_a, came_b, *beside = tied(swap(low[:two], 4), swap(low[two:], 2), *beside)
    a = near[:two] + came_a.astype(F32)
    b = near[two:] + came_b.astype(F32)
    came_a, came_b, *beside = tied(
        swap(a[one:].astype(BF), 2), swap(b[one:].astype(BF), 4), *later(*beside)
    )
    own = jnp.concatenate([a[:one] + came_a.astype(F32), b[:one] + came_b.astype(F32)])
    return (own, *beside)


def spread_columns(came, p, part):
    units = came[0].shape[1] // 2
    natural = []
    for q in range(4):
        piece = came[3]
        for r in (0, 1, 2):
            piece = jnp.where(p == (q ^ r), came[r], piece)
        natural.append(piece.astype(F32))
    return tuple(
        jnp.concatenate(
            [
                natural[q][:, start + k * part : start + (k + 1) * part]
                for k in range(units // part)
                for q in range(4)
            ],
            axis=1,
        )
        for start in (0, units)
    )


def rotation_tables(length, width):
    half_width = width // 2
    position = jnp.arange(length, dtype=F32)[:, None]
    freq_rate = ROPE_BASE ** (-2.0 * jnp.arange(half_width, dtype=F32) / width)
    angle_table = position * freq_rate[None, :]
    return (jnp.cos(angle_table)[:, None, :], jnp.sin(angle_table)[:, None, :])


HEADS_AT_ONCE = 8


def rotation_lanes():
    cosine, sine = rotation_tables(SEQ, HEAD_SIZE)
    lanes = HEADS_AT_ONCE * 2
    return (jnp.tile(cosine[:, 0], (1, lanes)), jnp.tile(sine[:, 0], (1, lanes)))


def turned(value, cosine, sine, back):
    size = value.shape[1]
    half = HEAD_SIZE // 2
    lane = lax.broadcasted_iota(jnp.int32, value.shape, 1)
    right = pltpu.roll(value, size - half, 1)
    left = pltpu.roll(value, half, 1)
    first = lane % HEAD_SIZE < half
    other = jnp.where(first, right, -left) if back else jnp.where(first, -right, left)
    return value * cosine + other * sine


def head_of(value, i):
    size = value.shape[1]
    period = 3 * LANES
    group = value[:, i // 4 * period : (i // 4 + 1) * period]
    if i % 4:
        group = pltpu.roll(group, period - i % 4 * HEAD_SIZE, 1)
    head = group[:, :LANES]
    lane = lax.broadcasted_iota(jnp.int32, head.shape, 1)
    return jnp.where(lane < HEAD_SIZE, head, 0.0)


def side_by_side(heads):
    rows = heads[0].shape[0]
    total = None
    for i, head in enumerate(heads):
        wide = jnp.concatenate([head, jnp.zeros((rows, 2 * LANES), head.dtype)], axis=1)
        if i:
            wide = pltpu.roll(wide, i * HEAD_SIZE, 1)
        total = wide if total is None else total + wide
    return total


def row_softmax(query, key):
    scores = lax.dot_general(
        query, key, (((1,), (1,)), ((), ())), preferred_element_type=F32
    ) * (1.0 / math.sqrt(HEAD_SIZE))
    row = lax.broadcasted_iota(jnp.int32, scores.shape, 0)
    column = lax.broadcasted_iota(jnp.int32, scores.shape, 1)
    scores = jnp.where(row >= column, scores, MASK_FILL)
    weights = jnp.exp(scores - jnp.max(scores, axis=1, keepdims=True))
    return weights * (1.0 / jnp.sum(weights, axis=1, keepdims=True))


def attention_blocks(width, kv_width):
    q_size = HEADS_AT_ONCE * HEAD_SIZE
    kv_size = q_size * kv_width // width
    return q_size, kv_size


def attention_forward(raw, cosine, sine, width, kv_width):
    count = raw.shape[0]
    q_size, kv_size = attention_blocks(width, kv_width)
    steps = width // q_size
    per_kv = width // kv_width

    def kernel(q_raw, k_raw, v_raw, cosine, sine, q_out, k_out, v_out, mixed):
        q = turned(q_raw[...], cosine[...], sine[...], False).astype(BF)
        k = turned(k_raw[...], cosine[:, :kv_size], sine[:, :kv_size], False).astype(BF)
        v = v_raw[...].astype(BF)
        q_out[...] = q
        k_out[...] = k
        v_out[...] = v
        q, k, v = q.astype(F32), k.astype(F32), v.astype(F32)
        for group in range(HEADS_AT_ONCE // 4):
            outs = []
            for i in range(4 * group, 4 * group + 4):
                if i % per_kv == 0:
                    key = head_of(k, i // per_kv).astype(BF)
                    value = head_of(v, i // per_kv).astype(BF)
                probs = row_softmax(head_of(q, i).astype(BF), key)
                outs.append(jnp.dot(probs.astype(BF), value, preferred_element_type=F32))
            mixed[:, 384 * group : 384 * group + 384] = side_by_side(outs).astype(BF)

    def block(size, at):
        return pl.BlockSpec((SEQ, size), lambda s, j: (s, at // size + j))

    table = pl.BlockSpec((SEQ, q_size), lambda s, j: (0, 0))
    return pl.pallas_call(
        kernel,
        grid=(count // SEQ, steps),
        out_shape=[
            jax.ShapeDtypeStruct((count, width), BF),
            jax.ShapeDtypeStruct((count, kv_width), BF),
            jax.ShapeDtypeStruct((count, kv_width), BF),
            jax.ShapeDtypeStruct((count, width), BF),
        ],
        in_specs=[
            block(q_size, 0),
            block(kv_size, width),
            block(kv_size, width + kv_width),
            table,
            table,
        ],
        out_specs=[block(q_size, 0), block(kv_size, 0), block(kv_size, 0), block(q_size, 0)],
        cost_estimate=NO_COST,
        name="attention_forward",
    )(raw, raw, raw, cosine, sine)


def attention_backward(grad_mixed, q, k, v, cosine, sine):
    count, width = q.shape
    kv_width = k.shape[1]
    q_size, kv_size = attention_blocks(width, kv_width)
    steps = width // q_size
    per_kv = width // kv_width
    scale = 1.0 / math.sqrt(HEAD_SIZE)
    rows_rows = (((0,), (0,)), ((), ()))
    lanes_lanes = (((1,), (1,)), ((), ()))

    def kernel(d_ref, q_ref, k_ref, v_ref, cosine, sine, out):
        d, q = d_ref[...].astype(F32), q_ref[...].astype(F32)
        k, v = k_ref[...].astype(F32), v_ref[...].astype(F32)
        d_q, d_k, d_v = [], [], []
        for i in range(HEADS_AT_ONCE):
            if i % per_kv == 0:
                key = head_of(k, i // per_kv).astype(BF)
                value = head_of(v, i // per_kv).astype(BF)
            query, upstream = head_of(q, i).astype(BF), head_of(d, i).astype(BF)
            probs = row_softmax(query, key)
            d_probs = lax.dot_general(upstream, value, lanes_lanes, preferred_element_type=F32)
            d_scores = probs * (d_probs - jnp.sum(probs * d_probs, axis=1, keepdims=True))
            d_scores = d_scores.astype(BF)
            d_q.append(jnp.dot(d_scores, key, preferred_element_type=F32) * scale)
            part_k = lax.dot_general(d_scores, query, rows_rows, preferred_element_type=F32)
            part_v = lax.dot_general(
                probs.astype(BF), upstream, rows_rows, preferred_element_type=F32
            )
            if i % per_kv == 0:
                d_k.append(part_k)
                d_v.append(part_v)
            else:
                d_k[-1] += part_k
                d_v[-1] += part_v
        d_q = jnp.concatenate([side_by_side(d_q[g : g + 4]) for g in range(0, len(d_q), 4)], axis=1)
        d_q = turned(d_q, cosine[...], sine[...], True).astype(BF)
        d_k = side_by_side([part * scale for part in d_k])
        d_k = turned(d_k, cosine[:, :kv_size], sine[:, :kv_size], True).astype(BF)
        j = pl.program_id(1)
        out[:, pl.ds(pl.multiple_of(j * q_size, LANES), q_size)] = d_q
        at = pl.multiple_of(width + j * kv_size, LANES)
        out[:, pl.ds(at, kv_size)] = d_k
        at = pl.multiple_of(width + kv_width + j * kv_size, LANES)
        out[:, pl.ds(at, kv_size)] = side_by_side(d_v).astype(BF)

    def block(size):
        return pl.BlockSpec((SEQ, size), lambda s, j: (s, j))

    table = pl.BlockSpec((SEQ, q_size), lambda s, j: (0, 0))
    return pl.pallas_call(
        kernel,
        grid=(count // SEQ, steps),
        out_shape=jax.ShapeDtypeStruct((count, width + 2 * kv_width), BF),
        in_specs=[block(q_size), block(q_size), block(kv_size), block(kv_size), table, table],
        out_specs=pl.BlockSpec((SEQ, width + 2 * kv_width), lambda s, j: (s, 0)),
        cost_estimate=NO_COST,
        name="attention_backward",
    )(grad_mixed, q, k, v, cosine, sine)


def norm_rows(field_in, gain_vec):
    inv_scale = lax.rsqrt(jnp.mean(field_in * field_in, axis=-1, keepdims=True) + EPSILON)
    return (field_in * inv_scale * gain_vec, inv_scale)


def norm_back(upstream, field_in, inv_scale, gain_vec):
    gain_grad = jnp.sum(upstream * field_in * inv_scale, axis=0)
    scaled_up = upstream * gain_vec
    field_grad = inv_scale * scaled_up - field_in * inv_scale**3 * jnp.mean(
        scaled_up * field_in, axis=-1, keepdims=True
    )
    return (gain_grad, field_grad)


def ffn_forward(rows, w_both, w_down):
    units = w_down.shape[0]
    pre = mm(rows, w_both[:, : 2 * units])
    hidden = (jax.nn.silu(pre[:, :units]) * pre[:, units:]).astype(BF)
    return (mm(hidden, w_down), pre, hidden)


def ffn_backward(grad_low, pre, w_both, w_down):
    grad_hidden = mm_t(grad_low, w_down)
    units = w_down.shape[0]
    gate_pre, up_pre = pre[:, :units], pre[:, units:]
    gate_sigmoid = jax.nn.sigmoid(gate_pre)
    grad_gate = grad_hidden * up_pre * gate_sigmoid * (1.0 + gate_pre * (1.0 - gate_sigmoid))
    grad_up = grad_hidden * gate_pre * gate_sigmoid
    grads = jnp.concatenate([grad_gate.astype(BF), grad_up.astype(BF)], axis=1)
    return (mm_t(grads, w_both[:, : 2 * units]), grads)


FFN_TILE = 256
FFN_VMEM = 48 * 2**20


def tiles_of(w_both, w_down, units):
    width = w_down.shape[1]
    steps = units // FFN_TILE
    return [
        pl.BlockSpec((width, FFN_TILE), lambda j: (0, j)),
        pl.BlockSpec((width, FFN_TILE), lambda j: (0, j + steps)),
        pl.BlockSpec((FFN_TILE, width), lambda j: (j, 0)),
    ]


def whole(array):
    return pl.BlockSpec(array.shape, lambda j: (0,) * array.ndim)


def sigmoid(value):
    return 1.0 / (1.0 + jnp.exp(-value))


def ffn_forward_beside(pieces, w_both, w_down):
    units, width = w_down.shape
    steps = units // FFN_TILE
    sizes = [piece.shape[0] for piece in pieces]
    count = sum(sizes)
    kinds = ((width, BF), (units, BF), (units, F32), (units, F32))
    kept_specs = [
        pl.BlockSpec((count, width), lambda j: (0, 0)),
        pl.BlockSpec((count, FFN_TILE), lambda j: (0, j)),
        pl.BlockSpec((count, FFN_TILE), lambda j: (0, j)),
        pl.BlockSpec((count, FFN_TILE), lambda j: (0, j)),
    ]
    first = len(pieces) + 3

    def kernel(*refs):
        w_gate, w_up, w_low = refs[len(pieces) : first]
        y, rows, hidden, gate, up, total = refs[-6:]
        j = pl.program_id(0)

        @pl.when(j == 0)
        def _():
            at = 0
            for ref, size in zip(refs, sizes):
                rows[at : at + size] = ref[...]
                at += size

        gate_pre = jnp.dot(rows[...], w_gate[...], preferred_element_type=F32)
        up_pre = jnp.dot(rows[...], w_up[...], preferred_element_type=F32)
        gate[...] = gate_pre
        up[...] = up_pre
        hid = (gate_pre * sigmoid(gate_pre) * up_pre).astype(BF)
        hidden[...] = hid
        part = jnp.dot(hid, w_low[...], preferred_element_type=F32)

        @pl.when(j == 0)
        def _():
            total[...] = part

        @pl.when(j > 0)
        def _():
            total[...] += part

        @pl.when(j == steps - 1)
        def _():
            y[...] = total[...].astype(y.dtype)

    y_shape = jax.ShapeDtypeStruct((count, width), F32)
    outs = pl.pallas_call(
        kernel,
        grid=(steps,),
        out_shape=[y_shape] + [jax.ShapeDtypeStruct((count, w), t) for w, t in kinds],
        in_specs=[whole(piece) for piece in pieces]
        + tiles_of(w_both, w_down, units),
        out_specs=[whole(y_shape)] + kept_specs,
        scratch_shapes=[pltpu.VMEM((count, width), F32)],
        compiler_params=pltpu.CompilerParams(vmem_limit_bytes=FFN_VMEM),
        cost_estimate=NO_COST,
        name="ffn_forward_beside",
    )(*pieces, w_both, w_both, w_down)
    return tuple(outs)


def ffn_backward_beside(pieces, gate_pre, up_pre, w_both, w_down):
    units, width = w_down.shape
    steps = units // FFN_TILE
    sizes = [piece.shape[0] for piece in pieces]
    count = sum(sizes)
    kinds = ((width, BF), (2 * units, BF))
    kept_specs = [
        pl.BlockSpec((count, width), lambda j: (0, 0)),
        pl.BlockSpec((count, 2 * units), lambda j: (0, 0)),
    ]
    pre_spec = pl.BlockSpec((count, FFN_TILE), lambda j: (0, j))
    first = len(pieces) + 5
    dims = (((1,), (1,)), ((), ()))

    def kernel(*refs):
        gate, up, w_gate, w_up, w_low = refs[len(pieces) : first]
        m, rows, grads, total = refs[-4:]
        j = pl.program_id(0)

        @pl.when(j == 0)
        def _():
            at = 0
            for ref, size in zip(refs, sizes):
                rows[at : at + size] = ref[...]
                at += size

        grad_hidden = lax.dot_general(rows[...], w_low[...], dims, preferred_element_type=F32)
        g = gate[...]
        s = sigmoid(g)
        grad_gate = (grad_hidden * up[...] * s * (1.0 + g * (1.0 - s))).astype(BF)
        grad_up = (grad_hidden * g * s).astype(BF)
        start = pl.multiple_of(j * FFN_TILE, LANES)
        grads[:, pl.ds(start, FFN_TILE)] = grad_gate
        grads[:, pl.ds(start + units, FFN_TILE)] = grad_up
        part = lax.dot_general(grad_gate, w_gate[...], dims, preferred_element_type=F32)
        part += lax.dot_general(grad_up, w_up[...], dims, preferred_element_type=F32)

        @pl.when(j == 0)
        def _():
            total[...] = part

        @pl.when(j > 0)
        def _():
            total[...] += part

        @pl.when(j == steps - 1)
        def _():
            m[...] = total[...].astype(m.dtype)

    m_shape = jax.ShapeDtypeStruct((count, width), F32)
    outs = pl.pallas_call(
        kernel,
        grid=(steps,),
        out_shape=[m_shape] + [jax.ShapeDtypeStruct((count, w), t) for w, t in kinds],
        in_specs=[whole(piece) for piece in pieces]
        + [pre_spec] * 2
        + tiles_of(w_both, w_down, units),
        out_specs=[whole(m_shape)] + kept_specs,
        scratch_shapes=[pltpu.VMEM((count, width), F32)],
        compiler_params=pltpu.CompilerParams(vmem_limit_bytes=FFN_VMEM),
        cost_estimate=NO_COST,
        name="ffn_backward_beside",
    )(*pieces, gate_pre, up_pre, w_both, w_both, w_down)
    return tuple(outs)


def products(pairs, dtype):
    tokens, rows = pairs[0][0].shape
    columns = pairs[0][1].shape[1]
    tile = columns // 4

    def kernel(*refs):
        total = None
        for i in range(len(pairs)):
            part = lax.dot_general(
                refs[2 * i][...],
                refs[2 * i + 1][...],
                (((0,), (0,)), ((), ())),
                preferred_element_type=F32,
            )
            total = part if total is None else total + part
        refs[-1][...] = total.astype(dtype)

    specs = [
        pl.BlockSpec((tokens, rows), lambda j: (0, 0)),
        pl.BlockSpec((tokens, tile), lambda j: (0, j)),
    ]
    return pl.pallas_call(
        kernel,
        grid=(columns // tile,),
        out_shape=jax.ShapeDtypeStruct((rows, columns), dtype),
        in_specs=specs * len(pairs),
        out_specs=pl.BlockSpec((rows, tile), lambda j: (0, j)),
        compiler_params=pltpu.CompilerParams(vmem_limit_bytes=FFN_VMEM),
        cost_estimate=NO_COST,
        name="products",
    )(*[array for pair in pairs for array in pair])


def body(
    tokens,
    teacher,
    valid_mask,
    w_query,
    key_weight_matrix,
    value_weight_matrix,
    w_output,
    w_gate,
    w_up,
    w_down,
    attn_gain,
    ffn_gain,
):
    n = lax.axis_size("dp")
    planes = n // 8
    position = lax.axis_index("dp")
    c, x, y, z = position % 2, position // 2 % 2, position // 4 % 2, position // 8
    bits = (z, y, x, c)
    p = position // 2 % 4
    rows = w_query.shape[0]
    width = w_query.shape[1]
    kv_width = key_weight_matrix.shape[1]
    ff_rows = w_down.shape[0]
    ff = w_gate.shape[1]
    count = tokens.shape[0]
    cosine, sine = rotation_lanes()

    part = 2 * ff_rows
    units = planes * part
    gains = jnp.stack([attn_gain, ffn_gain], axis=1)
    gains = jnp.pad(gains, ((0, 0), (0, LANES - 2)))
    local = packed([w_query, key_weight_matrix, value_weight_matrix, w_output, gains])
    if planes == 4:
        gathered, wb = gather_weights(local, w_gate, w_up, w_down, bits)
        wd = w_down_from(wb, ff_rows, 2 * units, width)
    else:
        gathered, wb, wd = gather_weights_plainly(local, w_gate, w_up, w_down, p)

    with jax.named_scope("attention_forward"):
        wide = width + 2 * kv_width
        wqkv = gathered[:, :wide]
        wo = gathered[:, wide : wide + width]
        gain_in = gathered[:, wide + width].astype(F32)
        gain_mid = gathered[:, wide + width + 1].astype(F32)
        inputs_f = tokens.astype(F32)
        normed, inv_attn = norm_rows(inputs_f, gain_in)
        normed_in = normed.astype(BF)
        raw = mm(normed_in, wqkv)
        query, key, value, mixed = attention_forward(raw, cosine, sine, width, kv_width)
        hidden_res = inputs_f + mm(mixed, wo)
        normed_two, inv_ffn = norm_rows(hidden_res, gain_mid)
        normed_mid = normed_two.astype(BF)

    with jax.named_scope("ffn_forward"):
        to_column = reordered(width, rows, "zcyx")
        far, y_near, *kept = split_gather(
            mm(normed_mid, to_column).astype(BF),
            (),
            lambda pieces: ffn_forward_beside(pieces, wb, wd),
        )
        near, hid_near, gate_near, up_near = kept
        y_far, pre_far, hid_far = ffn_forward(far, wb, wd)
        y_far, mixed, normed_in = tied(y_far, mixed, normed_in)
        by_side = reordered(width, rows, "cxyz")
        beside = (
            *core_halves(mm(mixed, by_side).astype(BF), c),
            *core_halves(mm(normed_in, by_side).astype(BF), c),
        )
        result, *halves = split_reduce(y_near, y_far.astype(BF), beside)
        mixed_mine, mixed_theirs, normed_mine, normed_theirs = halves
        result = hidden_res + result
        out_act = result.astype(BF)

    with jax.named_scope("loss"):
        mask_f = valid_mask.astype(F32)
        grad_out = (result - teacher.astype(F32)) * mask_f[:, None]
        sums = jnp.stack([jnp.sum(grad_out * grad_out), jnp.sum(mask_f)])
        sums = jnp.broadcast_to(sums[:, None], (2, LANES))

    high = n // 2
    rest = [1 << k for k in range(4, n.bit_length() - 2)]

    with jax.named_scope("ffn_backward"):
        grad_low, sums = tied(grad_out.astype(BF), sums)

        def near_backward(pieces, came):
            value = sums + came
            for mask in rest:
                value = value + swap(value, mask)
            near = ffn_backward_beside(pieces, gate_near, up_near, wb, wd)
            return (value, swap(value, 8), *near)

        d_far, sums, sums_came, m_near, d_near, g_near = split_gather(
            grad_low, (swap(sums, 1),), near_backward
        )
        m_far, g_far = ffn_backward(d_far, pre_far, wb, wd)
        m_far = m_far.astype(BF)
        m_near, m_far, sums, sums_came = tied(m_near, m_far, sums, sums_came)
        sums = sums + sums_came
        g_both = products([(near, g_near), (far, g_far)], BF)
        g_down = products([(hid_near, d_near), (hid_far, d_far)], BF)
        g_both, g_down = sum_to_owners(g_both), sum_to_owners(g_down)

        def later(sums, sums_came):
            sums = sums + sums_came
            return (sums, swap(sums, 2))

        grad_mid, sums, sums_came = split_reduce(m_near, m_far, (sums, swap(sums, high)), later)
        sums = sums + sums_came
        high_part = grad_mid.astype(BF)
        low_part = (grad_mid - high_part.astype(F32)).astype(BF)
        grad_mid = mm_t(high_part, to_column) + mm_t(low_part, to_column)

    with jax.named_scope("attention_backward"):
        grad_gain_mid, grad_res = norm_back(grad_mid, hidden_res, inv_ffn, gain_mid)
        grad_res = grad_out + grad_res
        res_low = grad_res.astype(BF)
        wo_came, sums_came = tied(swap(t_mm(mixed_theirs, res_low).astype(BF), 1), swap(sums, 4))
        sums = sums + sums_came
        loss = sums[0, 0] / (sums[1, 0] * width)
        shape = (2, 2, planes, rows, -1)
        g_wo = [t_mm(mixed_mine, res_low).reshape(shape), wo_came.reshape(shape)]
        wo_moving = plane_step_1(g_wo, bits)
        grad_mixed = mm_t(res_low, wo).astype(BF)
        grad_raw = attention_backward(grad_mixed, query, key, value, cosine, sine)
        *wo_came, grad_raw = tied(*wo_moving, grad_raw)
        g_wo, wo_moving = plane_step_2(g_wo, wo_came, bits)

    with jax.named_scope("q_k_v_weight_gradients"):
        qkv_came = swap(t_mm(normed_theirs, grad_raw).astype(BF), 1)
        g_qkv = t_mm(normed_mine, grad_raw)
        qkv_came, g_qkv, grad_raw, *wo_came = tied(qkv_came, g_qkv, grad_raw, *wo_moving)
        g_wo = plane_step_3(g_wo, wo_came, bits)
        g_qkv = [g_qkv.reshape(shape), qkv_came.reshape(shape)]
        qkv_moving = plane_step_1(g_qkv, bits)

    with jax.named_scope("input_gradient"):
        grad_in = mm_t(grad_raw, wqkv)
        grad_gain_in, grad_tokens = norm_back(grad_in, inputs_f, inv_attn, gain_in)
        input_grad = (grad_res + grad_tokens).astype(BF)
        gains = jnp.stack([grad_gain_in, grad_gain_mid])
        gains_came = swap(gains, 1)

    with jax.named_scope("weight_gradients_to_owners"):
        *qkv_came, gains_came, gains = tied(*qkv_moving, gains_came, gains)
        gains = gains + gains_came
        g_qkv, qkv_moving = plane_step_2(g_qkv, qkv_came, bits)
        *qkv_came, gains_came = tied(*qkv_moving, swap(gains, 8))
        gains = gains + gains_came
        g_qkv = plane_step_3(g_qkv, qkv_came, bits)
        if planes == 4:
            moving = direct([g_qkv], z) + direct([g_wo], z)
        gains_came = swap(gains, high)
        g_both = g_both.reshape(4, rows, 2 * units)
        gains, gains_came, g_both = tied(gains, gains_came, g_both)
        gains = gains + gains_came
        came = [pick(g_both, p ^ r, 0) for r in range(4)]
        gains_came, *moved = tied(swap(gains, 2), *[swap(came[r], r << 1) for r in (1, 2, 3)])
        gains = gains + gains_came
        for mask in rest:
            gains = gains + swap(gains, mask)
        grad_gate, grad_up = spread_columns([came[0]] + moved, p, part)
        gains = gains + swap(gains, 4)
        g_gains = lax.dynamic_slice_in_dim(gains, position * rows, rows, 1)
        if planes == 4:
            g_qkv = owned([g_qkv], moving[:3], z)
            g_wo = owned([g_wo], moving[3:], z)
        else:
            g_qkv, g_wo = z_reduce([g_qkv]), z_reduce([g_wo])
        g_wq = g_qkv[:, :width]
        g_wk = g_qkv[:, width : width + kv_width]
        g_wv = g_qkv[:, width + kv_width :]

    return (
        out_act,
        loss,
        input_grad,
        g_wq,
        g_wk,
        g_wv,
        g_wo,
        grad_gate,
        grad_up,
        g_down.astype(F32),
        g_gains[0],
        g_gains[1],
    )


def solution(mesh):
    wide, flat = P("dp", None), P("dp")
    in_specs = (wide, wide, flat) + (wide,) * 7 + (flat, flat)
    out_specs = (wide, P(), wide) + (wide,) * 7 + (flat, flat)
    return jax.shard_map(body, mesh=mesh, in_specs=in_specs, out_specs=out_specs, check_vma=False)
```

```python
import math

import jax
import jax.numpy as jnp
from jax import lax
from jax.experimental import pallas as pl
from jax.experimental.pallas import tpu as pltpu
from jax.sharding import PartitionSpec as P

HEAD_SIZE = 96
SEQ = 128
EPSILON = 1e-05
ROPE_BASE = 100000.0
MASK_FILL = -1e30
LANES = 128

BF = jnp.bfloat16
F32 = jnp.float32
NO_COST = pl.CostEstimate(flops=1, bytes_accessed=1, transcendentals=0)


def dot(a, b, dims):
    return lax.dot_general(a, b, (dims, ((), ())), preferred_element_type=F32)


def mm(a, b):
    return dot(a, b, ((1,), (0,)))


def mm_t(a, b):
    return dot(a, b, ((1,), (1,)))


def t_mm(a, b):
    return dot(a, b, ((0,), (0,)))


def swap(value, mask):
    n = lax.axis_size("dp")
    return lax.ppermute(value, "dp", [(i, i ^ mask) for i in range(n)])


def column_groups(with_core):
    n = lax.axis_size("dp")
    planes = range(n // 8)
    if with_core:
        return [[8 * z + 2 * p + c for z in planes for c in range(2)] for p in range(4)]
    return [[8 * z + 2 * p + c for z in planes] for p in range(4) for c in range(2)]


def z_reduce(parts):
    total = sum(part.astype(F32) for part in parts)
    return lax.psum_scatter(
        total.astype(BF), "dp", axis_index_groups=column_groups(False), scatter_dimension=0
    ).astype(F32)


def summed(parts, index, axis):
    total = pick(parts[0], index, axis).astype(F32)
    for part in parts[1:]:
        total = total + pick(part, index, axis).astype(F32)
    return total


def owned(parts, came, z):
    own = summed(parts, z, 0)
    for piece in came:
        own = own + piece.astype(F32)
    return own


def direct(parts, z):
    return [swap(summed(parts, z ^ k, 0).astype(BF), 8 * k) for k in (3, 2, 1)]


def along_z(value, pairs):
    return lax.ppermute(
        value, "dp", [(8 * a + i, 8 * b + i) for a, b in pairs for i in range(8)]
    )


def tied(*values):
    return lax.optimization_barrier(values)


def place(out, piece, where):
    return lax.dynamic_update_slice(out, piece, where)


def pick(parts, index, axis):
    return lax.dynamic_index_in_dim(parts, index, axis, keepdims=False)


def column_cuts(w_gate, w_up, p, part):
    rows = w_gate.shape[0]
    gate_cut = w_gate.reshape(rows, -1, 4, part)
    up_cut = w_up.reshape(rows, -1, 4, part)
    cuts = []
    for r in range(4):
        gate = pick(gate_cut, p ^ r, 2).reshape(rows, -1)
        up = pick(up_cut, p ^ r, 2).reshape(rows, -1)
        cuts.append(jnp.concatenate([gate, up], axis=1))
    return cuts


def by_source(came, p):
    out = jnp.zeros((4,) + came[0].shape, BF)
    for r in range(4):
        out = place(out, came[r][None], (p ^ r, 0, 0))
    return out


def along_column(value):
    return lax.all_gather(
        value, "dp", axis_index_groups=column_groups(True), axis=0, tiled=True
    )


def sum_to_owners(partial):
    return lax.psum_scatter(
        partial, "dp", axis_index_groups=column_groups(True), scatter_dimension=0, tiled=True
    )


def gather_weights_plainly(local, w_gate, w_up, w_down, p):
    gathered = lax.all_gather(local, "dp", axis=0, tiled=True)
    cuts = column_cuts(w_gate, w_up, p, 2 * w_down.shape[0])
    came = [cuts[0]] + [swap(cuts[r], r << 1) for r in (1, 2, 3)]
    mine = by_source(came, p)
    wb = along_column(mine.reshape(-1, mine.shape[2]))
    return gathered, wb, along_column(w_down)


def merged(came, w_down, p):
    rows, columns = came[0].shape
    ff_rows, width = w_down.shape
    tall = 4 * rows
    side = width * ff_rows // tall
    rest = width - side
    low = tall - ff_rows

    def kernel(p_ref, *refs):
        wd, out = refs[4:]
        for r in range(4):
            start = pl.multiple_of((p_ref[0] ^ r) * rows, 16)
            out[pl.ds(start, rows), :columns] = refs[r][...]
        out[:ff_rows, columns:] = wd[:, :side]
        for k in range(ff_rows // low):
            at = columns + k * rest
            out[ff_rows:, at : at + rest] = wd[k * low : (k + 1) * low, side:]

    return pl.pallas_call(
        kernel,
        out_shape=jax.ShapeDtypeStruct((tall, columns + side), w_down.dtype),
        in_specs=[pl.BlockSpec(memory_space=pltpu.SMEM)]
        + [pl.BlockSpec(memory_space=pltpu.VMEM)] * 5,
        cost_estimate=NO_COST,
        name="merged",
    )(p[None], *came, w_down)


def w_down_from(whole, ff_rows, columns, width):
    side = whole.shape[1] - columns
    rest = width - side
    tall = width * ff_rows // side
    low = tall - ff_rows
    devices = whole.shape[0] // tall

    def kernel(ref, out, sem):
        copies = []
        for i in range(devices):
            top, to = i * tall, i * ff_rows
            pairs = [
                (
                    ref.at[pl.ds(top, ff_rows), pl.ds(columns, side)],
                    out.at[pl.ds(to, ff_rows), pl.ds(0, side)],
                )
            ]
            for k in range(ff_rows // low):
                pairs.append(
                    (
                        ref.at[pl.ds(top + ff_rows, low), pl.ds(columns + k * rest, rest)],
                        out.at[pl.ds(to + k * low, low), pl.ds(side, rest)],
                    )
                )
            for k, (source, target) in enumerate(pairs):
                copies.append(pltpu.make_async_copy(source, target, sem.at[i, k]))
        for copy in copies:
            copy.start()
        for copy in copies:
            copy.wait()

    return pl.pallas_call(
        kernel,
        out_shape=jax.ShapeDtypeStruct((devices * ff_rows, width), whole.dtype),
        in_specs=[pl.BlockSpec(memory_space=pl.ANY)],
        out_specs=pl.BlockSpec(memory_space=pltpu.VMEM),
        scratch_shapes=[pltpu.SemaphoreType.DMA((devices, 1 + ff_rows // low))],
        cost_estimate=NO_COST,
        name="w_down_from",
    )(whole)


def unset(shape, dtype):
    return pl.pallas_call(
        lambda out: None,
        out_shape=jax.ShapeDtypeStruct(shape, dtype),
        out_specs=pl.BlockSpec(memory_space=pl.ANY),
        name="unset",
    )()


def packed(pieces):
    widths = [piece.shape[1] for piece in pieces]
    rows = pieces[0].shape[0]

    def kernel(*refs):
        out = refs[-1]
        at = 0
        for ref, size in zip(refs[:-1], widths):
            out[:, at : at + size] = ref[...]
            at += size

    return pl.pallas_call(
        kernel,
        out_shape=jax.ShapeDtypeStruct((rows, sum(widths)), pieces[0].dtype),
        name="packed",
    )(*pieces)


def column_cuts_kernel(w_gate, w_up, p, part):
    rows, ff = w_gate.shape
    planes = ff // (4 * part)
    units = planes * part

    def kernel(p_ref, gate, up, *outs):
        for r, out in enumerate(outs):
            q = p_ref[0] ^ r
            for k in range(planes):
                start = pl.multiple_of((4 * k + q) * part, LANES)
                out[:, k * part : (k + 1) * part] = gate[:, pl.ds(start, part)]
                out[:, units + k * part : units + (k + 1) * part] = up[:, pl.ds(start, part)]

    shape = jax.ShapeDtypeStruct((rows, 2 * units), w_gate.dtype)
    return pl.pallas_call(
        kernel,
        out_shape=[shape] * 4,
        in_specs=[pl.BlockSpec(memory_space=pltpu.SMEM)]
        + [pl.BlockSpec(memory_space=pltpu.VMEM)] * 2,
        name="column_cuts",
    )(p[None], w_gate, w_up)


def gather_weights(local, w_gate, w_up, w_down, place_bits):
    z, y, x, c = place_bits
    p = 2 * y + x
    rows, columns = local.shape
    ff_rows, width = w_down.shape
    end = (z == 0) | (z == 3)
    up_pairs = [(0, 1), (1, 2), (2, 3)]
    down_pairs = [(1, 0), (2, 1), (3, 2)]
    far_pairs = [(0, 2), (3, 1)]
    out_pairs = [(1, 0), (2, 3)]
    z_b = jnp.where(z == 0, 1, z - 1)
    z_c = jnp.where(z < 2, 2, jnp.where(z == 2, 3, 1))
    z_d = jnp.where(z < 2, 3, 0)
    out = unset((4, 2, 2, 2, rows, columns), BF)

    def near_side(up, down):
        return jnp.where(z == 0, down, up)

    def to_pass_on(up, down):
        return jnp.where(z == 1, down, up)

    def put_x(out, piece, z_k, at_y, core):
        return place(out, piece[None, None, :, None], (z_k, at_y, 0, core, 0, 0))

    def put_y(out, piece, z_k, at_x, core):
        return place(out, piece[None, :, None, None], (z_k, 0, at_x, core, 0, 0))

    def in_order(bit, mine, theirs):
        return jnp.stack([jnp.where(bit == 0, mine, theirs), jnp.where(bit == 0, theirs, mine)])

    def put(out, pair, z_a, z_b, at_y, at_x, core):
        out = put_x(out, pair[0], z_a, at_y, core)
        return put_y(out, pair[1], z_b, at_x, core)

    with jax.named_scope("phase_0"):
        cuts = column_cuts_kernel(w_gate, w_up, p, 2 * ff_rows)
        crossing = (swap(cuts[1], 2), swap(cuts[2], 4), swap(cuts[3], 6))
        up, down = tied(along_z(local, up_pairs), along_z(local, down_pairs))
    with jax.named_scope("phase_1"):
        b = near_side(up, down)
        a, b, passing = tied(local, b, to_pass_on(up, down))
        a_x, b_y, far, first, *crossing = tied(
            swap(a, 2), swap(b, 4), along_z(a, far_pairs), along_z(passing, out_pairs), *crossing
        )
        ffn = merged((cuts[0], *crossing), w_down, p)
    with jax.named_scope("phase_2"):
        a2, b2, far = tied(in_order(x, a, a_x), in_order(y, b, b_y), far)
        near_1 = jnp.stack([a2, b2])
        a_far, b_far, second = tied(swap(a2, 4), swap(b2, 2), along_z(far, out_pairs))
        out = put(out, near_1, z, z_b, y, x, c)
    with jax.named_scope("ffn_weights"):
        ffn = along_column(tied(ffn, second)[0])
    with jax.named_scope("phase_3"):
        a, b = jnp.where(end, first, down), jnp.where(end, second, far)
        a, b, near_1 = tied(a, b, near_1)
        a_x, b_y, core_1 = tied(swap(a, 2), swap(b, 4), swap(near_1, 1))
        far_1 = jnp.stack([a_far, b_far])
        out = put(out, far_1, z, z_b, 1 - y, 1 - x, c)
    with jax.named_scope("phase_4"):
        a2, b2, far_1 = tied(in_order(x, a, a_x), in_order(y, b, b_y), far_1)
        a_far, b_far, core_2 = tied(swap(a2, 4), swap(b2, 2), swap(far_1, 1))
        out = put(out, core_1, z, z_b, y, x, 1 - c)
        near_2 = jnp.stack([a2, b2])
        out = put(out, near_2, z_c, z_d, y, x, c)
    with jax.named_scope("phase_5"):
        near_2, far_2 = tied(near_2, jnp.stack([a_far, b_far]))
        core_3, core_4 = tied(swap(near_2, 1), swap(far_2, 1))
        out = put(out, core_2, z, z_b, 1 - y, 1 - x, 1 - c)
        out = put(out, far_2, z_c, z_d, 1 - y, 1 - x, c)
        out = put(out, core_3, z_c, z_d, y, x, 1 - c)
        out = put(out, core_4, z_c, z_d, 1 - y, 1 - x, 1 - c)
        gathered = out.reshape(32 * rows, columns)
    return gathered, ffn


def block_sums(sets, tables, rows, dtype):
    columns = sets[0][0].shape[1]
    count = tables[0][0].shape[0]
    if rows % 16:
        results = []
        for arrays, table in zip(sets, tables):
            blocks = [a.reshape(-1, rows, columns)[t] for a, t in zip(arrays, table)]
            total = sum(block.astype(F32) for block in blocks)
            results.append(total.astype(dtype).reshape(count * rows, columns))
        return results
    sizes = [len(arrays) for arrays in sets]
    inputs = [array for arrays in sets for array in arrays]
    table = jnp.stack([t for group in tables for t in group]).astype(jnp.int32)

    def kernel(table, *refs):
        at = 0
        for size, out in zip(sizes, refs[len(inputs) :]):
            total = refs[at][...].astype(F32)
            for ref in refs[at + 1 : at + size]:
                total += ref[...].astype(F32)
            out[...] = total.astype(dtype)
            at += size

    def block(k):
        return pl.BlockSpec((rows, columns), lambda i, table: (table[k, i], 0))

    return pl.pallas_call(
        kernel,
        grid_spec=pltpu.PrefetchScalarGridSpec(
            num_scalar_prefetch=1,
            grid=(count,),
            in_specs=[block(k) for k in range(len(inputs))],
            out_specs=[pl.BlockSpec((rows, columns), lambda i, table: (i, 0))] * len(sets),
        ),
        out_shape=[jax.ShapeDtypeStruct((count * rows, columns), dtype)] * len(sets),
        compiler_params=pltpu.CompilerParams(vmem_limit_bytes=FFN_VMEM),
        cost_estimate=NO_COST,
        name="block_sums",
    )(table, *inputs)


class PlaneSum:
    def __init__(self, parts, rows, place_bits):
        self.parts, self.rows, self.place_bits = parts, rows, place_bits
        self.tall = parts[0].shape[0] // 8

    def block(self, x, y, half):
        return jnp.atleast_1d(4 * x + 2 * y + half)

    def sums(self, a, b, more_a, more_b, at_a, at_b, dtype):
        a_arrays, b_arrays = [*self.parts, *more_a], [*self.parts, *more_b]
        a_tables = [a, a] + [jnp.atleast_1d(i) for i in at_a]
        b_tables = [b, b] + [jnp.atleast_1d(i) for i in at_b]
        return block_sums([a_arrays, b_arrays], [a_tables, b_tables], self.tall, dtype)

    def step_1(self):
        z, y, x, c = self.place_bits
        i = jnp.arange(2)
        a, b = self.sums(self.block(i, 1 - y, 0), self.block(1 - x, i, 1), [], [], [], [], BF)
        return (swap(a, 4), swap(b, 2))

    def step_2(self, came):
        z, y, x, c = self.place_bits
        self.came = came
        a, b = self.block(1 - x, y, 0), self.block(x, 1 - y, 1)
        a, b = self.sums(a, b, [came[0]], [came[1]], [1 - x], [1 - y], BF)
        return (swap(a, 2), swap(b, 4))

    def step_3(self, came):
        z, y, x, c = self.place_bits
        a, b = self.block(x, y, 0), self.block(x, y, 1)
        more_a, more_b = [self.came[0], came[0]], [self.came[1], came[1]]
        a, b = self.sums(a, b, more_a, more_b, [x, 0], [y, 0], F32)
        shape = (self.tall // self.rows, self.rows, -1)
        return jnp.concatenate([a.reshape(shape), b.reshape(shape)])


def reordered(count, rows, order):
    place_of, row = jnp.arange(count) // rows, jnp.arange(count) % rows
    planes = count // rows // 8
    if order == "cxyz":
        core, chip = place_of // (4 * planes), place_of % (4 * planes)
        x, y, z = chip // (2 * planes), chip // planes % 2, chip % planes
    else:
        z, core, y, x = place_of // 8, place_of // 4 % 2, place_of // 2 % 2, place_of % 2
    source = (8 * z + 4 * y + 2 * x + core) * rows + row
    return (jnp.arange(count)[:, None] == source[None, :]).astype(BF)


def core_halves(values, c):
    width = values.shape[1] // 2
    return (
        lax.dynamic_slice_in_dim(values, c * width, width, 1),
        lax.dynamic_slice_in_dim(values, (1 - c) * width, width, 1),
    )


def split_gather(rows, beside=(), then=lambda pieces, *values: values):
    half = rows.shape[0] // 2
    a, b = rows[:half], rows[half:]
    a_x, b_y, *beside = tied(swap(a, 2), swap(b, 4), *beside)
    a2, b2 = tied(jnp.concatenate([a, a_x]), jnp.concatenate([b, b_y]))
    a_far, b_far, *beside = tied(swap(a2, 4), swap(b2, 2), *then((a2, b2), *beside))
    return (jnp.concatenate([a_far, b_far]), *beside)


def split_reduce(near, low, beside=(), later=lambda *values: values):
    two = low.shape[0] // 2
    one = two // 2
    came_a, came_b, *beside = tied(swap(low[:two], 4), swap(low[two:], 2), *beside)
    a = near[:two] + came_a.astype(F32)
    b = near[two:] + came_b.astype(F32)
    came_a, came_b, *beside = tied(
        swap(a[one:].astype(BF), 2), swap(b[one:].astype(BF), 4), *later(*beside)
    )
    own = jnp.concatenate([a[:one] + came_a.astype(F32), b[:one] + came_b.astype(F32)])
    return (own, *beside)


def spread_columns(came, p, part):
    units = came[0].shape[1] // 2
    natural = []
    for q in range(4):
        piece = came[3]
        for r in (0, 1, 2):
            piece = jnp.where(p == (q ^ r), came[r], piece)
        natural.append(piece.astype(F32))
    return tuple(
        jnp.concatenate(
            [
                natural[q][:, start + k * part : start + (k + 1) * part]
                for k in range(units // part)
                for q in range(4)
            ],
            axis=1,
        )
        for start in (0, units)
    )


def rotation_tables(length, width):
    half_width = width // 2
    position = jnp.arange(length, dtype=F32)[:, None]
    freq_rate = ROPE_BASE ** (-2.0 * jnp.arange(half_width, dtype=F32) / width)
    angle_table = position * freq_rate[None, :]
    return (jnp.cos(angle_table)[:, None, :], jnp.sin(angle_table)[:, None, :])


HEADS_AT_ONCE = 8


def rotation_lanes():
    cosine, sine = rotation_tables(SEQ, HEAD_SIZE)
    lanes = HEADS_AT_ONCE * 2
    return (jnp.tile(cosine[:, 0], (1, lanes)), jnp.tile(sine[:, 0], (1, lanes)))


def turned(value, cosine, sine, back):
    size = value.shape[1]
    half = HEAD_SIZE // 2
    lane = lax.broadcasted_iota(jnp.int32, value.shape, 1)
    right = pltpu.roll(value, size - half, 1)
    left = pltpu.roll(value, half, 1)
    first = lane % HEAD_SIZE < half
    other = jnp.where(first, right, -left) if back else jnp.where(first, -right, left)
    return value * cosine + other * sine


def lanes_of(shape):
    return lax.broadcasted_iota(jnp.int32, shape, 1)


def head_of(value, i):
    start = i * HEAD_SIZE
    window = start // LANES * LANES
    offset = start - window
    size = LANES if offset + HEAD_SIZE <= LANES else 2 * LANES
    head = value[:, window : window + size]
    if offset:
        head = pltpu.roll(head, size - offset, 1)
    head = head[:, :LANES]
    return jnp.where(lanes_of(head.shape) < HEAD_SIZE, head, 0.0)


def side_by_side(heads):
    lane = lanes_of(heads[0].shape)
    second = pltpu.roll(heads[1], 96, 1)
    third = pltpu.roll(heads[2], 64, 1)
    fourth = pltpu.roll(heads[3], 32, 1)
    return jnp.concatenate(
        [
            jnp.where(lane < 96, heads[0], second),
            jnp.where(lane < 64, second, third),
            jnp.where(lane < 32, third, fourth),
        ],
        axis=1,
    )


def row_softmax(query, key):
    scores = lax.dot_general(
        query, key, (((1,), (1,)), ((), ())), preferred_element_type=F32
    ) * (1.0 / math.sqrt(HEAD_SIZE))
    row = lax.broadcasted_iota(jnp.int32, scores.shape, 0)
    column = lax.broadcasted_iota(jnp.int32, scores.shape, 1)
    scores = jnp.where(row >= column, scores, MASK_FILL)
    weights = jnp.exp(scores - jnp.max(scores, axis=1, keepdims=True))
    return weights * (1.0 / jnp.sum(weights, axis=1, keepdims=True))


def attention_blocks(width, kv_width):
    q_size = HEADS_AT_ONCE * HEAD_SIZE
    kv_size = q_size * kv_width // width
    return q_size, kv_size


def attention_forward(raw, cosine, sine, width, kv_width):
    count = raw.shape[0]
    q_size, kv_size = attention_blocks(width, kv_width)
    steps = width // q_size
    per_kv = width // kv_width

    def kernel(q_raw, k_raw, v_raw, cosine, sine, q_out, k_out, v_out, mixed):
        q = turned(q_raw[...], cosine[...], sine[...], False).astype(BF)
        k = turned(k_raw[...], cosine[:, :kv_size], sine[:, :kv_size], False).astype(BF)
        v = v_raw[...].astype(BF)
        q_out[...] = q
        k_out[...] = k
        v_out[...] = v
        q, k, v = q.astype(F32), k.astype(F32), v.astype(F32)
        for group in range(HEADS_AT_ONCE // 4):
            outs = []
            for i in range(4 * group, 4 * group + 4):
                if i % per_kv == 0:
                    key = head_of(k, i // per_kv).astype(BF)
                    value = head_of(v, i // per_kv).astype(BF)
                probs = row_softmax(head_of(q, i).astype(BF), key)
                outs.append(jnp.dot(probs.astype(BF), value, preferred_element_type=F32))
            mixed[:, 384 * group : 384 * group + 384] = side_by_side(outs).astype(BF)

    def block(size, at):
        return pl.BlockSpec((SEQ, size), lambda s, j: (s, at // size + j))

    table = pl.BlockSpec((SEQ, q_size), lambda s, j: (0, 0))
    return pl.pallas_call(
        kernel,
        grid=(count // SEQ, steps),
        out_shape=[
            jax.ShapeDtypeStruct((count, width), BF),
            jax.ShapeDtypeStruct((count, kv_width), BF),
            jax.ShapeDtypeStruct((count, kv_width), BF),
            jax.ShapeDtypeStruct((count, width), BF),
        ],
        in_specs=[
            block(q_size, 0),
            block(kv_size, width),
            block(kv_size, width + kv_width),
            table,
            table,
        ],
        out_specs=[block(q_size, 0), block(kv_size, 0), block(kv_size, 0), block(q_size, 0)],
        cost_estimate=NO_COST,
        name="attention_forward",
    )(raw, raw, raw, cosine, sine)


def attention_backward(grad_mixed, q, k, v, cosine, sine):
    count, width = q.shape
    kv_width = k.shape[1]
    q_size, kv_size = attention_blocks(width, kv_width)
    steps = width // q_size
    per_kv = width // kv_width
    scale = 1.0 / math.sqrt(HEAD_SIZE)
    rows_rows = (((0,), (0,)), ((), ()))
    lanes_lanes = (((1,), (1,)), ((), ()))

    def kernel(d_ref, q_ref, k_ref, v_ref, cosine, sine, out):
        d, q = d_ref[...].astype(F32), q_ref[...].astype(F32)
        k, v = k_ref[...].astype(F32), v_ref[...].astype(F32)
        d_q, d_k, d_v = [], [], []
        for i in range(HEADS_AT_ONCE):
            if i % per_kv == 0:
                key = head_of(k, i // per_kv).astype(BF)
                value = head_of(v, i // per_kv).astype(BF)
            query, upstream = head_of(q, i).astype(BF), head_of(d, i).astype(BF)
            probs = row_softmax(query, key)
            d_probs = lax.dot_general(upstream, value, lanes_lanes, preferred_element_type=F32)
            d_scores = probs * (d_probs - jnp.sum(probs * d_probs, axis=1, keepdims=True))
            d_scores = d_scores.astype(BF)
            d_q.append(jnp.dot(d_scores, key, preferred_element_type=F32) * scale)
            part_k = lax.dot_general(d_scores, query, rows_rows, preferred_element_type=F32)
            part_v = lax.dot_general(
                probs.astype(BF), upstream, rows_rows, preferred_element_type=F32
            )
            if i % per_kv == 0:
                d_k.append(part_k)
                d_v.append(part_v)
            else:
                d_k[-1] += part_k
                d_v[-1] += part_v
        d_q = jnp.concatenate([side_by_side(d_q[g : g + 4]) for g in range(0, len(d_q), 4)], axis=1)
        d_q = turned(d_q, cosine[...], sine[...], True).astype(BF)
        d_k = side_by_side([part * scale for part in d_k])
        d_k = turned(d_k, cosine[:, :kv_size], sine[:, :kv_size], True).astype(BF)
        j = pl.program_id(1)
        out[:, pl.ds(pl.multiple_of(j * q_size, LANES), q_size)] = d_q
        at = pl.multiple_of(width + j * kv_size, LANES)
        out[:, pl.ds(at, kv_size)] = d_k
        at = pl.multiple_of(width + kv_width + j * kv_size, LANES)
        out[:, pl.ds(at, kv_size)] = side_by_side(d_v).astype(BF)

    def block(size):
        return pl.BlockSpec((SEQ, size), lambda s, j: (s, j))

    table = pl.BlockSpec((SEQ, q_size), lambda s, j: (0, 0))
    return pl.pallas_call(
        kernel,
        grid=(count // SEQ, steps),
        out_shape=jax.ShapeDtypeStruct((count, width + 2 * kv_width), BF),
        in_specs=[block(q_size), block(q_size), block(kv_size), block(kv_size), table, table],
        out_specs=pl.BlockSpec((SEQ, width + 2 * kv_width), lambda s, j: (s, 0)),
        cost_estimate=NO_COST,
        name="attention_backward",
    )(grad_mixed, q, k, v, cosine, sine)


def norm_rows(field_in, gain_vec):
    inv_scale = lax.rsqrt(jnp.mean(field_in * field_in, axis=-1, keepdims=True) + EPSILON)
    return (field_in * inv_scale * gain_vec, inv_scale)


def norm_back(upstream, field_in, inv_scale, gain_vec):
    gain_grad = jnp.sum(upstream * field_in * inv_scale, axis=0)
    scaled_up = upstream * gain_vec
    field_grad = inv_scale * scaled_up - field_in * inv_scale**3 * jnp.mean(
        scaled_up * field_in, axis=-1, keepdims=True
    )
    return (gain_grad, field_grad)


def ffn_forward(rows, w_both, w_down):
    units = w_down.shape[0]
    pre = mm(rows, w_both[:, : 2 * units])
    hidden = (jax.nn.silu(pre[:, :units]) * pre[:, units:]).astype(BF)
    return (mm(hidden, w_down), pre, hidden)


def ffn_backward(grad_low, pre, w_both, w_down):
    grad_hidden = mm_t(grad_low, w_down)
    units = w_down.shape[0]
    gate_pre, up_pre = pre[:, :units], pre[:, units:]
    gate_sigmoid = jax.nn.sigmoid(gate_pre)
    grad_gate = grad_hidden * up_pre * gate_sigmoid * (1.0 + gate_pre * (1.0 - gate_sigmoid))
    grad_up = grad_hidden * gate_pre * gate_sigmoid
    grads = jnp.concatenate([grad_gate.astype(BF), grad_up.astype(BF)], axis=1)
    return (mm_t(grads, w_both[:, : 2 * units]), grads)


FFN_TILE = 256
FFN_VMEM = 48 * 2**20


def tiles_of(w_both, w_down, units):
    width = w_down.shape[1]
    steps = units // FFN_TILE
    return [
        pl.BlockSpec((width, FFN_TILE), lambda j: (0, j)),
        pl.BlockSpec((width, FFN_TILE), lambda j: (0, j + steps)),
        pl.BlockSpec((FFN_TILE, width), lambda j: (j, 0)),
    ]


def whole(array):
    return pl.BlockSpec(array.shape, lambda j: (0,) * array.ndim)


def sigmoid(value):
    return 1.0 / (1.0 + jnp.exp(-value))


def ffn_forward_beside(pieces, w_both, w_down):
    units, width = w_down.shape
    steps = units // FFN_TILE
    sizes = [piece.shape[0] for piece in pieces]
    count = sum(sizes)
    kinds = ((width, BF), (units, BF), (units, F32), (units, F32))
    kept_specs = [
        pl.BlockSpec((count, width), lambda j: (0, 0)),
        pl.BlockSpec((count, FFN_TILE), lambda j: (0, j)),
        pl.BlockSpec((count, FFN_TILE), lambda j: (0, j)),
        pl.BlockSpec((count, FFN_TILE), lambda j: (0, j)),
    ]
    first = len(pieces) + 3

    def kernel(*refs):
        w_gate, w_up, w_low = refs[len(pieces) : first]
        y, rows, hidden, gate, up, total = refs[-6:]
        j = pl.program_id(0)

        @pl.when(j == 0)
        def _():
            at = 0
            for ref, size in zip(refs, sizes):
                rows[at : at + size] = ref[...]
                at += size

        gate_pre = jnp.dot(rows[...], w_gate[...], preferred_element_type=F32)
        up_pre = jnp.dot(rows[...], w_up[...], preferred_element_type=F32)
        gate[...] = gate_pre
        up[...] = up_pre
        hid = (gate_pre * sigmoid(gate_pre) * up_pre).astype(BF)
        hidden[...] = hid
        part = jnp.dot(hid, w_low[...], preferred_element_type=F32)

        @pl.when(j == 0)
        def _():
            total[...] = part

        @pl.when(j > 0)
        def _():
            total[...] += part

        @pl.when(j == steps - 1)
        def _():
            y[...] = total[...].astype(y.dtype)

    y_shape = jax.ShapeDtypeStruct((count, width), F32)
    outs = pl.pallas_call(
        kernel,
        grid=(steps,),
        out_shape=[y_shape] + [jax.ShapeDtypeStruct((count, w), t) for w, t in kinds],
        in_specs=[whole(piece) for piece in pieces]
        + tiles_of(w_both, w_down, units),
        out_specs=[whole(y_shape)] + kept_specs,
        scratch_shapes=[pltpu.VMEM((count, width), F32)],
        compiler_params=pltpu.CompilerParams(vmem_limit_bytes=FFN_VMEM),
        cost_estimate=NO_COST,
        name="ffn_forward_beside",
    )(*pieces, w_both, w_both, w_down)
    return tuple(outs)


def ffn_backward_beside(pieces, gate_pre, up_pre, w_both, w_down):
    units, width = w_down.shape
    steps = units // FFN_TILE
    sizes = [piece.shape[0] for piece in pieces]
    count = sum(sizes)
    kinds = ((width, BF), (2 * units, BF))
    kept_specs = [
        pl.BlockSpec((count, width), lambda j: (0, 0)),
        pl.BlockSpec((count, 2 * units), lambda j: (0, 0)),
    ]
    pre_spec = pl.BlockSpec((count, FFN_TILE), lambda j: (0, j))
    first = len(pieces) + 5
    dims = (((1,), (1,)), ((), ()))

    def kernel(*refs):
        gate, up, w_gate, w_up, w_low = refs[len(pieces) : first]
        m, rows, grads, total = refs[-4:]
        j = pl.program_id(0)

        @pl.when(j == 0)
        def _():
            at = 0
            for ref, size in zip(refs, sizes):
                rows[at : at + size] = ref[...]
                at += size

        grad_hidden = lax.dot_general(rows[...], w_low[...], dims, preferred_element_type=F32)
        g = gate[...]
        s = sigmoid(g)
        grad_gate = (grad_hidden * up[...] * s * (1.0 + g * (1.0 - s))).astype(BF)
        grad_up = (grad_hidden * g * s).astype(BF)
        start = pl.multiple_of(j * FFN_TILE, LANES)
        grads[:, pl.ds(start, FFN_TILE)] = grad_gate
        grads[:, pl.ds(start + units, FFN_TILE)] = grad_up
        part = lax.dot_general(grad_gate, w_gate[...], dims, preferred_element_type=F32)
        part += lax.dot_general(grad_up, w_up[...], dims, preferred_element_type=F32)

        @pl.when(j == 0)
        def _():
            total[...] = part

        @pl.when(j > 0)
        def _():
            total[...] += part

        @pl.when(j == steps - 1)
        def _():
            m[...] = total[...].astype(m.dtype)

    m_shape = jax.ShapeDtypeStruct((count, width), F32)
    outs = pl.pallas_call(
        kernel,
        grid=(steps,),
        out_shape=[m_shape] + [jax.ShapeDtypeStruct((count, w), t) for w, t in kinds],
        in_specs=[whole(piece) for piece in pieces]
        + [pre_spec] * 2
        + tiles_of(w_both, w_down, units),
        out_specs=[whole(m_shape)] + kept_specs,
        scratch_shapes=[pltpu.VMEM((count, width), F32)],
        compiler_params=pltpu.CompilerParams(vmem_limit_bytes=FFN_VMEM),
        cost_estimate=NO_COST,
        name="ffn_backward_beside",
    )(*pieces, gate_pre, up_pre, w_both, w_both, w_down)
    return tuple(outs)


def input_gradient(grad_raw, weights, tokens, inv_scale, gain, grad_res):
    count, wide = grad_raw.shape
    width = tokens.shape[1]
    tile = 2 * FFN_TILE
    steps = wide // tile

    def kernel(grads, w, tokens, inv_scale, gain, grad_res, out, gain_grad, total):
        j = pl.program_id(0)
        part = lax.dot_general(
            grads[...], w[...], (((1,), (1,)), ((), ())), preferred_element_type=F32
        )

        @pl.when(j == 0)
        def _():
            total[...] = part

        @pl.when(j > 0)
        def _():
            total[...] += part

        @pl.when(j == steps - 1)
        def _():
            up, field, inv = total[...], tokens[...].astype(F32), inv_scale[...]
            gain_grad[...] = jnp.sum(up * field * inv, axis=0, keepdims=True)
            scaled = up * gain[...]
            mean = jnp.mean(scaled * field, axis=1, keepdims=True)
            grad = inv * scaled - field * (inv * inv * inv) * mean
            out[...] = (grad_res[...] + grad).astype(BF)

    return pl.pallas_call(
        kernel,
        grid=(steps,),
        out_shape=[
            jax.ShapeDtypeStruct((count, width), BF),
            jax.ShapeDtypeStruct((1, width), F32),
        ],
        in_specs=[
            pl.BlockSpec((count, tile), lambda j: (0, j)),
            pl.BlockSpec((width, tile), lambda j: (0, j)),
            whole(tokens),
            whole(inv_scale),
            whole(gain),
            whole(grad_res),
        ],
        out_specs=[
            pl.BlockSpec((count, width), lambda j: (0, 0)),
            pl.BlockSpec((1, width), lambda j: (0, 0)),
        ],
        scratch_shapes=[pltpu.VMEM((count, width), F32)],
        compiler_params=pltpu.CompilerParams(vmem_limit_bytes=FFN_VMEM),
        cost_estimate=NO_COST,
        name="input_gradient",
    )(grad_raw, weights, tokens, inv_scale, gain, grad_res)


def products(pairs, dtype):
    tokens, rows = pairs[0][0].shape
    columns = pairs[0][1].shape[1]
    tile = columns // 4

    def kernel(*refs):
        total = None
        for i in range(len(pairs)):
            part = lax.dot_general(
                refs[2 * i][...],
                refs[2 * i + 1][...],
                (((0,), (0,)), ((), ())),
                preferred_element_type=F32,
            )
            total = part if total is None else total + part
        refs[-1][...] = total.astype(dtype)

    specs = [
        pl.BlockSpec((tokens, rows), lambda j: (0, 0)),
        pl.BlockSpec((tokens, tile), lambda j: (0, j)),
    ]
    return pl.pallas_call(
        kernel,
        grid=(columns // tile,),
        out_shape=jax.ShapeDtypeStruct((rows, columns), dtype),
        in_specs=specs * len(pairs),
        out_specs=pl.BlockSpec((rows, tile), lambda j: (0, j)),
        compiler_params=pltpu.CompilerParams(vmem_limit_bytes=FFN_VMEM),
        cost_estimate=NO_COST,
        name="products",
    )(*[array for pair in pairs for array in pair])


def body(
    tokens,
    teacher,
    valid_mask,
    w_query,
    key_weight_matrix,
    value_weight_matrix,
    w_output,
    w_gate,
    w_up,
    w_down,
    attn_gain,
    ffn_gain,
):
    n = lax.axis_size("dp")
    planes = n // 8
    position = lax.axis_index("dp")
    c, x, y, z = position % 2, position // 2 % 2, position // 4 % 2, position // 8
    bits = (z, y, x, c)
    p = position // 2 % 4
    rows = w_query.shape[0]
    width = w_query.shape[1]
    kv_width = key_weight_matrix.shape[1]
    ff_rows = w_down.shape[0]
    ff = w_gate.shape[1]
    count = tokens.shape[0]
    cosine, sine = rotation_lanes()

    part = 2 * ff_rows
    units = planes * part
    gains = jnp.stack([attn_gain, ffn_gain], axis=1)
    gains = jnp.pad(gains, ((0, 0), (0, LANES - 2)))
    local = packed([w_query, key_weight_matrix, value_weight_matrix, w_output, gains])
    if planes == 4:
        gathered, wb = gather_weights(local, w_gate, w_up, w_down, bits)
        wd = w_down_from(wb, ff_rows, 2 * units, width)
    else:
        gathered, wb, wd = gather_weights_plainly(local, w_gate, w_up, w_down, p)

    with jax.named_scope("attention_forward"):
        wide = width + 2 * kv_width
        wqkv = gathered[:, :wide]
        wo = gathered[:, wide : wide + width]
        gain_in = gathered[:, wide + width].astype(F32)
        gain_mid = gathered[:, wide + width + 1].astype(F32)
        inputs_f = tokens.astype(F32)
        normed, inv_attn = norm_rows(inputs_f, gain_in)
        normed_in = normed.astype(BF)
        raw = mm(normed_in, wqkv)
        query, key, value, mixed = attention_forward(raw, cosine, sine, width, kv_width)
        hidden_res = inputs_f + mm(mixed, wo)
        normed_two, inv_ffn = norm_rows(hidden_res, gain_mid)
        normed_mid = normed_two.astype(BF)

    with jax.named_scope("ffn_forward"):
        to_column = reordered(width, rows, "zcyx")
        far, y_near, *kept = split_gather(
            mm(normed_mid, to_column).astype(BF),
            (),
            lambda pieces: ffn_forward_beside(pieces, wb, wd),
        )
        near, hid_near, gate_near, up_near = kept
        y_far, pre_far, hid_far = ffn_forward(far, wb, wd)
        y_far, mixed, normed_in = tied(y_far, mixed, normed_in)
        by_side = reordered(width, rows, "cxyz")
        beside = (
            *core_halves(mm(mixed, by_side).astype(BF), c),
            *core_halves(mm(normed_in, by_side).astype(BF), c),
        )
        result, *halves = split_reduce(y_near, y_far.astype(BF), beside)
        mixed_mine, mixed_theirs, normed_mine, normed_theirs = halves
        result = hidden_res + result
        out_act = result.astype(BF)

    with jax.named_scope("loss"):
        mask_f = valid_mask.astype(F32)
        grad_out = (result - teacher.astype(F32)) * mask_f[:, None]
        sums = jnp.stack([jnp.sum(grad_out * grad_out), jnp.sum(mask_f)])
        sums = jnp.broadcast_to(sums[:, None], (2, LANES))

    high = n // 2
    rest = [1 << k for k in range(4, n.bit_length() - 2)]

    with jax.named_scope("ffn_backward"):
        def near_backward(pieces, sums):
            return (
                sums,
                swap(sums, 1),
                *ffn_backward_beside(pieces, gate_near, up_near, wb, wd),
            )

        d_far, sums, came, m_near, d_near, g_near = split_gather(
            grad_out.astype(BF), (sums,), near_backward
        )
        sums = sums + came
        for mask in rest:
            sums = sums + swap(sums, mask)
        m_far, g_far = ffn_backward(d_far, pre_far, wb, wd)
        m_near, m_far, sums = tied(m_near, m_far.astype(BF), sums)
        beside = (
            products([(near, g_near), (far, g_far)], BF),
            sums,
            swap(sums, 8),
        )

        owned_both = []

        def later(g_both, sums, came):
            owned_both.append(sum_to_owners(g_both))
            sums = sums + came
            g_down = products([(hid_near, d_near), (hid_far, d_far)], BF)
            return (g_down, sums, swap(sums, high))

        grad_mid, g_down, sums, came = split_reduce(m_near, m_far, beside, later)
        g_both = owned_both[0]
        sums = sums + came
        high_part = grad_mid.astype(BF)
        low_part = (grad_mid - high_part.astype(F32)).astype(BF)
        grad_mid = mm_t(high_part, to_column) + mm_t(low_part, to_column)

    with jax.named_scope("attention_backward"):
        grad_gain_mid, grad_res = norm_back(grad_mid, hidden_res, inv_ffn, gain_mid)
        grad_res = grad_out + grad_res
        res_low = grad_res.astype(BF)
        wo_came, came = tied(swap(t_mm(mixed_theirs, res_low).astype(BF), 1), swap(sums, 2))
        sums = sums + came
        g_wo = PlaneSum([t_mm(mixed_mine, res_low), wo_came], rows, bits)
        wo_moving = g_wo.step_1()
        grad_mixed = mm_t(res_low, wo).astype(BF)
        grad_raw = attention_backward(grad_mixed, query, key, value, cosine, sine)
        *wo_came, grad_raw = tied(*wo_moving, grad_raw)
        wo_moving = g_wo.step_2(wo_came)

    with jax.named_scope("q_k_v_weight_gradients"):
        qkv_came = swap(t_mm(normed_theirs, grad_raw).astype(BF), 1)
        g_qkv = t_mm(normed_mine, grad_raw)
        qkv_came, g_qkv, grad_raw, came, g_both, g_down, *wo_came = tied(
            qkv_came, g_qkv, grad_raw, swap(sums, 4), g_both, g_down, *wo_moving
        )
        g_down = sum_to_owners(g_down)
        sums = sums + came
        loss = sums[0, 0] / (sums[1, 0] * width)
        g_qkv = PlaneSum([g_qkv, qkv_came], rows, bits)
        qkv_moving = g_qkv.step_1()
        g_wo = g_wo.step_3(wo_came)
        if planes == 4:
            wo_moving = direct([g_wo], z)

    with jax.named_scope("input_gradient"):
        input_grad, grad_gain_in = input_gradient(
            grad_raw, gathered, tokens, inv_attn, gain_in[None], grad_res
        )
        gains = jnp.concatenate([grad_gain_in, grad_gain_mid[None]])

    with jax.named_scope("weight_gradients_to_owners"):
        if planes == 4:
            qkv_0, qkv_1, gains, wo_0, wo_1, wo_2 = tied(*qkv_moving, gains, *wo_moving)
            g_wo = owned([g_wo], (wo_0, wo_1, wo_2), z)
            qkv_came = (qkv_0, qkv_1)
        else:
            *qkv_came, gains = tied(*qkv_moving, gains)
            g_wo = z_reduce([g_wo])
        qkv_moving = g_qkv.step_2(qkv_came)
        for mask in (1, 8, high):
            gains = gains + swap(gains, mask)
        *qkv_came, gains, g_both, g_down = tied(*qkv_moving, gains, g_both, g_down)
        g_qkv = g_qkv.step_3(qkv_came)
        if planes == 4:
            moving = direct([g_qkv], z)
        g_both = g_both.reshape(4, rows, 2 * units)
        came = [pick(g_both, p ^ r, 0) for r in range(4)]
        gains_came, *moved = tied(swap(gains, 2), *[swap(came[r], r << 1) for r in (1, 2, 3)])
        gains = gains + gains_came
        for mask in rest:
            gains = gains + swap(gains, mask)
        grad_gate, grad_up = spread_columns([came[0]] + moved, p, part)
        gains = gains + swap(gains, 4)
        g_gains = lax.dynamic_slice_in_dim(gains, position * rows, rows, 1)
        if planes == 4:
            g_qkv = owned([g_qkv], moving, z)
        else:
            g_qkv = z_reduce([g_qkv])
        g_wq = g_qkv[:, :width]
        g_wk = g_qkv[:, width : width + kv_width]
        g_wv = g_qkv[:, width + kv_width :]

    return (
        out_act,
        loss,
        input_grad,
        g_wq,
        g_wk,
        g_wv,
        g_wo,
        grad_gate,
        grad_up,
        g_down.astype(F32),
        g_gains[0],
        g_gains[1],
    )


def solution(mesh):
    wide, flat = P("dp", None), P("dp")
    in_specs = (wide, wide, flat) + (wide,) * 7 + (flat, flat)
    out_specs = (wide, P(), wide) + (wide,) * 7 + (flat, flat)
    return jax.shard_map(body, mesh=mesh, in_specs=in_specs, out_specs=out_specs, check_vma=False)
```

```python
import math

import jax
import jax.numpy as jnp
from jax import lax
from jax.experimental import pallas as pl
from jax.experimental.pallas import tpu as pltpu
from jax.sharding import PartitionSpec as P

HEAD_SIZE = 96
SEQ = 128
EPSILON = 1e-05
ROPE_BASE = 100000.0
MASK_FILL = -1e30
LANES = 128

BF = jnp.bfloat16
F32 = jnp.float32
NO_COST = pl.CostEstimate(flops=1, bytes_accessed=1, transcendentals=0)


def dot(a, b, dims):
    return lax.dot_general(a, b, (dims, ((), ())), preferred_element_type=F32)


def mm(a, b):
    return dot(a, b, ((1,), (0,)))


def mm_t(a, b):
    return dot(a, b, ((1,), (1,)))


def t_mm(a, b):
    return dot(a, b, ((0,), (0,)))


def swap(value, mask):
    n = lax.axis_size("dp")
    return lax.ppermute(value, "dp", [(i, i ^ mask) for i in range(n)])


def column_groups(with_core):
    n = lax.axis_size("dp")
    planes = range(n // 8)
    if with_core:
        return [[8 * z + 2 * p + c for z in planes for c in range(2)] for p in range(4)]
    return [[8 * z + 2 * p + c for z in planes] for p in range(4) for c in range(2)]


def z_reduce(parts):
    total = sum(part.astype(F32) for part in parts)
    return lax.psum_scatter(
        total.astype(BF), "dp", axis_index_groups=column_groups(False), scatter_dimension=0
    ).astype(F32)


def summed(parts, index, axis):
    total = pick(parts[0], index, axis).astype(F32)
    for part in parts[1:]:
        total = total + pick(part, index, axis).astype(F32)
    return total


def owned(parts, came, z):
    own = summed(parts, z, 0)
    for piece in came:
        own = own + piece.astype(F32)
    return own


def direct(parts, z):
    return [swap(summed(parts, z ^ k, 0).astype(BF), 8 * k) for k in (3, 2, 1)]


def along_z(value, pairs):
    return lax.ppermute(
        value, "dp", [(8 * a + i, 8 * b + i) for a, b in pairs for i in range(8)]
    )


def tied(*values):
    return lax.optimization_barrier(values)


def place(out, piece, where):
    return lax.dynamic_update_slice(out, piece, where)


def pick(parts, index, axis):
    return lax.dynamic_index_in_dim(parts, index, axis, keepdims=False)


def column_cuts(w_gate, w_up, p, part):
    rows = w_gate.shape[0]
    gate_cut = w_gate.reshape(rows, -1, 4, part)
    up_cut = w_up.reshape(rows, -1, 4, part)
    cuts = []
    for r in range(4):
        gate = pick(gate_cut, p ^ r, 2).reshape(rows, -1)
        up = pick(up_cut, p ^ r, 2).reshape(rows, -1)
        cuts.append(jnp.concatenate([gate, up], axis=1))
    return cuts


def by_source(came, p):
    out = jnp.zeros((4,) + came[0].shape, BF)
    for r in range(4):
        out = place(out, came[r][None], (p ^ r, 0, 0))
    return out


def along_column(value):
    return lax.all_gather(
        value, "dp", axis_index_groups=column_groups(True), axis=0, tiled=True
    )


def sum_to_owners(partial):
    return lax.psum_scatter(
        partial, "dp", axis_index_groups=column_groups(True), scatter_dimension=0, tiled=True
    )


def gather_weights_plainly(local, w_gate, w_up, w_down, p):
    gathered = lax.all_gather(local, "dp", axis=0, tiled=True)
    cuts = column_cuts(w_gate, w_up, p, 2 * w_down.shape[0])
    came = [cuts[0]] + [swap(cuts[r], r << 1) for r in (1, 2, 3)]
    mine = by_source(came, p)
    wb = along_column(mine.reshape(-1, mine.shape[2]))
    return gathered, wb, along_column(w_down)


def merged(came, w_down, p):
    rows, columns = came[0].shape
    ff_rows, width = w_down.shape
    tall = 4 * rows
    side = width * ff_rows // tall
    rest = width - side
    low = tall - ff_rows

    def kernel(p_ref, *refs):
        wd, out = refs[4:]
        for r in range(4):
            start = pl.multiple_of((p_ref[0] ^ r) * rows, 16)
            out[pl.ds(start, rows), :columns] = refs[r][...]
        out[:ff_rows, columns:] = wd[:, :side]
        for k in range(ff_rows // low):
            at = columns + k * rest
            out[ff_rows:, at : at + rest] = wd[k * low : (k + 1) * low, side:]

    return pl.pallas_call(
        kernel,
        out_shape=jax.ShapeDtypeStruct((tall, columns + side), w_down.dtype),
        in_specs=[pl.BlockSpec(memory_space=pltpu.SMEM)]
        + [pl.BlockSpec(memory_space=pltpu.VMEM)] * 5,
        compiler_params=pltpu.CompilerParams(vmem_limit_bytes=8 * 2**20),
        cost_estimate=NO_COST,
        name="merged",
    )(p[None], *came, w_down)


def w_down_from(whole, ff_rows, columns, width):
    side = whole.shape[1] - columns
    rest = width - side
    tall = width * ff_rows // side
    low = tall - ff_rows
    devices = whole.shape[0] // tall

    def kernel(ref, out, sem):
        copies = []
        for i in range(devices):
            top, to = i * tall, i * ff_rows
            pairs = [
                (
                    ref.at[pl.ds(top, ff_rows), pl.ds(columns, side)],
                    out.at[pl.ds(to, ff_rows), pl.ds(0, side)],
                )
            ]
            for k in range(ff_rows // low):
                pairs.append(
                    (
                        ref.at[pl.ds(top + ff_rows, low), pl.ds(columns + k * rest, rest)],
                        out.at[pl.ds(to + k * low, low), pl.ds(side, rest)],
                    )
                )
            for k, (source, target) in enumerate(pairs):
                copies.append(pltpu.make_async_copy(source, target, sem.at[i, k]))
        for copy in copies:
            copy.start()
        for copy in copies:
            copy.wait()

    return pl.pallas_call(
        kernel,
        out_shape=jax.ShapeDtypeStruct((devices * ff_rows, width), whole.dtype),
        in_specs=[pl.BlockSpec(memory_space=pl.ANY)],
        out_specs=pl.BlockSpec(memory_space=pltpu.VMEM),
        scratch_shapes=[pltpu.SemaphoreType.DMA((devices, 1 + ff_rows // low))],
        compiler_params=pltpu.CompilerParams(vmem_limit_bytes=2 * FFN_VMEM),
        cost_estimate=NO_COST,
        name="w_down_from",
    )(whole)


def unset(shape, dtype):
    return pl.pallas_call(
        lambda out: None,
        out_shape=jax.ShapeDtypeStruct(shape, dtype),
        out_specs=pl.BlockSpec(memory_space=pl.ANY),
        name="unset",
    )()


def packed(pieces):
    widths = [piece.shape[1] for piece in pieces]
    rows = pieces[0].shape[0]

    def kernel(*refs):
        out = refs[-1]
        at = 0
        for ref, size in zip(refs[:-1], widths):
            out[:, at : at + size] = ref[...]
            at += size

    return pl.pallas_call(
        kernel,
        out_shape=jax.ShapeDtypeStruct((rows, sum(widths)), pieces[0].dtype),
        compiler_params=pltpu.CompilerParams(vmem_limit_bytes=8 * 2**20),
        name="packed",
    )(*pieces)


def column_cuts_kernel(w_gate, w_up, p, part):
    rows, ff = w_gate.shape
    planes = ff // (4 * part)
    units = planes * part

    def kernel(p_ref, gate, up, *outs):
        for r, out in enumerate(outs):
            q = p_ref[0] ^ r
            for k in range(planes):
                start = pl.multiple_of((4 * k + q) * part, LANES)
                out[:, k * part : (k + 1) * part] = gate[:, pl.ds(start, part)]
                out[:, units + k * part : units + (k + 1) * part] = up[:, pl.ds(start, part)]

    shape = jax.ShapeDtypeStruct((rows, 2 * units), w_gate.dtype)
    return pl.pallas_call(
        kernel,
        out_shape=[shape] * 4,
        in_specs=[pl.BlockSpec(memory_space=pltpu.SMEM)]
        + [pl.BlockSpec(memory_space=pltpu.VMEM)] * 2,
        compiler_params=pltpu.CompilerParams(vmem_limit_bytes=8 * 2**20),
        name="column_cuts",
    )(p[None], w_gate, w_up)


def gather_weights(local, w_gate, w_up, w_down, place_bits):
    z, y, x, c = place_bits
    p = 2 * y + x
    rows, columns = local.shape
    ff_rows, width = w_down.shape
    end = (z == 0) | (z == 3)
    up_pairs = [(0, 1), (1, 2), (2, 3)]
    down_pairs = [(1, 0), (2, 1), (3, 2)]
    far_pairs = [(0, 2), (3, 1)]
    out_pairs = [(1, 0), (2, 3)]
    z_b = jnp.where(z == 0, 1, z - 1)
    z_c = jnp.where(z < 2, 2, jnp.where(z == 2, 3, 1))
    z_d = jnp.where(z < 2, 3, 0)
    out = unset((4, 2, 2, 2, rows, columns), BF)

    def near_side(up, down):
        return jnp.where(z == 0, down, up)

    def to_pass_on(up, down):
        return jnp.where(z == 1, down, up)

    def put_x(out, piece, z_k, at_y, core):
        return place(out, piece[None, None, :, None], (z_k, at_y, 0, core, 0, 0))

    def put_y(out, piece, z_k, at_x, core):
        return place(out, piece[None, :, None, None], (z_k, 0, at_x, core, 0, 0))

    def in_order(bit, mine, theirs):
        return jnp.stack([jnp.where(bit == 0, mine, theirs), jnp.where(bit == 0, theirs, mine)])

    def put(out, pair, z_a, z_b, at_y, at_x, core):
        out = put_x(out, pair[0], z_a, at_y, core)
        return put_y(out, pair[1], z_b, at_x, core)

    with jax.named_scope("phase_0"):
        cuts = column_cuts_kernel(w_gate, w_up, p, 2 * ff_rows)
        crossing = (swap(cuts[1], 2), swap(cuts[2], 4), swap(cuts[3], 6))
        up, down = tied(along_z(local, up_pairs), along_z(local, down_pairs))
    with jax.named_scope("phase_1"):
        b = near_side(up, down)
        a, b, passing = tied(local, b, to_pass_on(up, down))
        a_x, b_y, far, first = tied(
            swap(a, 2), swap(b, 4), along_z(a, far_pairs), along_z(passing, out_pairs)
        )
    with jax.named_scope("phase_2"):
        a2, b2, far = tied(in_order(x, a, a_x), in_order(y, b, b_y), far)
        near_1 = jnp.stack([a2, b2])
        ffn = merged((cuts[0], *tied(*crossing)), w_down, p)
        a_far, b_far, second = tied(swap(a2, 4), swap(b2, 2), along_z(far, out_pairs))
        out = put(out, near_1, z, z_b, y, x, c)
    with jax.named_scope("ffn_weights"):
        ffn = along_column(tied(ffn, second)[0])
    with jax.named_scope("phase_3"):
        a, b = jnp.where(end, first, down), jnp.where(end, second, far)
        a, b, near_1 = tied(a, b, near_1)
        a_x, b_y, core_1 = tied(swap(a, 2), swap(b, 4), swap(near_1, 1))
        far_1 = jnp.stack([a_far, b_far])
        out = put(out, far_1, z, z_b, 1 - y, 1 - x, c)
    with jax.named_scope("phase_4"):
        a2, b2, far_1 = tied(in_order(x, a, a_x), in_order(y, b, b_y), far_1)
        a_far, b_far, core_2 = tied(swap(a2, 4), swap(b2, 2), swap(far_1, 1))
        out = put(out, core_1, z, z_b, y, x, 1 - c)
        near_2 = jnp.stack([a2, b2])
        out = put(out, near_2, z_c, z_d, y, x, c)
    with jax.named_scope("phase_5"):
        near_2, far_2 = tied(near_2, jnp.stack([a_far, b_far]))
        core_3, core_4 = tied(swap(near_2, 1), swap(far_2, 1))
        out = put(out, core_2, z, z_b, 1 - y, 1 - x, 1 - c)
        out = put(out, far_2, z_c, z_d, 1 - y, 1 - x, c)
        out = put(out, core_3, z_c, z_d, y, x, 1 - c)
        out = put(out, core_4, z_c, z_d, 1 - y, 1 - x, 1 - c)
        gathered = out.reshape(32 * rows, columns)
    return gathered, ffn


def block_sums(sets, tables, rows, dtype, limit):
    columns = sets[0][0].shape[1]
    count = tables[0][0].shape[0]
    if rows % 16:
        results = []
        for arrays, table in zip(sets, tables):
            blocks = [a.reshape(-1, rows, columns)[t] for a, t in zip(arrays, table)]
            total = sum(block.astype(F32) for block in blocks)
            results.append(total.astype(dtype).reshape(count * rows, columns))
        return results
    sizes = [len(arrays) for arrays in sets]
    inputs = [array for arrays in sets for array in arrays]
    table = jnp.stack([t for group in tables for t in group]).astype(jnp.int32)

    def kernel(table, *refs):
        at = 0
        for size, out in zip(sizes, refs[len(inputs) :]):
            total = refs[at][...].astype(F32)
            for ref in refs[at + 1 : at + size]:
                total += ref[...].astype(F32)
            out[...] = total.astype(dtype)
            at += size

    def block(k):
        return pl.BlockSpec((rows, columns), lambda i, table: (table[k, i], 0))

    return pl.pallas_call(
        kernel,
        grid_spec=pltpu.PrefetchScalarGridSpec(
            num_scalar_prefetch=1,
            grid=(count,),
            in_specs=[block(k) for k in range(len(inputs))],
            out_specs=[pl.BlockSpec((rows, columns), lambda i, table: (i, 0))] * len(sets),
        ),
        out_shape=[jax.ShapeDtypeStruct((count * rows, columns), dtype)] * len(sets),
        compiler_params=pltpu.CompilerParams(vmem_limit_bytes=limit),
        cost_estimate=NO_COST,
        name="block_sums",
    )(table, *inputs)


class PlaneSum:
    def __init__(self, parts, rows, place_bits):
        self.parts, self.rows, self.place_bits = parts, rows, place_bits
        self.tall = parts[0].shape[0] // 8

    def block(self, x, y, half):
        return jnp.atleast_1d(4 * x + 2 * y + half)

    def sums(self, a, b, more_a, more_b, at_a, at_b, dtype):
        a_arrays, b_arrays = [*self.parts, *more_a], [*self.parts, *more_b]
        a_tables = [a, a] + [jnp.atleast_1d(i) for i in at_a]
        b_tables = [b, b] + [jnp.atleast_1d(i) for i in at_b]
        small = not more_a and self.parts[0].shape[1] <= 12 * LANES
        limit = FFN_VMEM if small else 2 * FFN_VMEM
        return block_sums([a_arrays, b_arrays], [a_tables, b_tables], self.tall, dtype, limit)

    def step_1(self):
        z, y, x, c = self.place_bits
        i = jnp.arange(2)
        a, b = self.sums(self.block(i, 1 - y, 0), self.block(1 - x, i, 1), [], [], [], [], BF)
        return (swap(a, 4), swap(b, 2))

    def step_2(self, came):
        z, y, x, c = self.place_bits
        self.came = came
        a, b = self.block(1 - x, y, 0), self.block(x, 1 - y, 1)
        a, b = self.sums(a, b, [came[0]], [came[1]], [1 - x], [1 - y], BF)
        return (swap(a, 2), swap(b, 4))

    def step_3(self, came):
        z, y, x, c = self.place_bits
        a, b = self.block(x, y, 0), self.block(x, y, 1)
        more_a, more_b = [self.came[0], came[0]], [self.came[1], came[1]]
        a, b = self.sums(a, b, more_a, more_b, [x, 0], [y, 0], F32)
        shape = (self.tall // self.rows, self.rows, -1)
        return jnp.concatenate([a.reshape(shape), b.reshape(shape)])


def reordered(count, rows, order):
    place_of, row = jnp.arange(count) // rows, jnp.arange(count) % rows
    planes = count // rows // 8
    if order == "cxyz":
        core, chip = place_of // (4 * planes), place_of % (4 * planes)
        x, y, z = chip // (2 * planes), chip // planes % 2, chip % planes
    else:
        z, core, y, x = place_of // 8, place_of // 4 % 2, place_of // 2 % 2, place_of % 2
    source = (8 * z + 4 * y + 2 * x + core) * rows + row
    return (jnp.arange(count)[:, None] == source[None, :]).astype(BF)


def core_halves(values, c):
    width = values.shape[1] // 2
    return (
        lax.dynamic_slice_in_dim(values, c * width, width, 1),
        lax.dynamic_slice_in_dim(values, (1 - c) * width, width, 1),
    )


def split_gather(rows, beside=(), then=lambda pieces, *values: values):
    half = rows.shape[0] // 2
    a, b = rows[:half], rows[half:]
    a_x, b_y, *beside = tied(swap(a, 2), swap(b, 4), *beside)
    a2, b2 = tied(jnp.concatenate([a, a_x]), jnp.concatenate([b, b_y]))
    a_far, b_far, *beside = tied(swap(a2, 4), swap(b2, 2), *then((a2, b2), *beside))
    return ((a_far, b_far), *beside)


def split_reduce(near, far, beside=(), later=lambda *values: values):
    two = far[0].shape[0]
    one = two // 2
    came_a, came_b, *beside = tied(swap(far[0], 4), swap(far[1], 2), *beside)
    a = near[:two] + came_a.astype(F32)
    b = near[two:] + came_b.astype(F32)
    came_a, came_b, *beside = tied(
        swap(a[one:].astype(BF), 2), swap(b[one:].astype(BF), 4), *later(*beside)
    )
    own = jnp.concatenate([a[:one] + came_a.astype(F32), b[:one] + came_b.astype(F32)])
    return (own, *beside)


def spread_columns(came, p, part):
    units = came[0].shape[1] // 2
    natural = []
    for q in range(4):
        piece = came[3]
        for r in (0, 1, 2):
            piece = jnp.where(p == (q ^ r), came[r], piece)
        natural.append(piece.astype(F32))
    return tuple(
        jnp.concatenate(
            [
                natural[q][:, start + k * part : start + (k + 1) * part]
                for k in range(units // part)
                for q in range(4)
            ],
            axis=1,
        )
        for start in (0, units)
    )


def rotation_tables(length, width):
    half_width = width // 2
    position = jnp.arange(length, dtype=F32)[:, None]
    freq_rate = ROPE_BASE ** (-2.0 * jnp.arange(half_width, dtype=F32) / width)
    angle_table = position * freq_rate[None, :]
    return (jnp.cos(angle_table)[:, None, :], jnp.sin(angle_table)[:, None, :])


HEADS_AT_ONCE = 8


def rotation_lanes():
    cosine, sine = rotation_tables(SEQ, HEAD_SIZE)
    lanes = HEADS_AT_ONCE * 2
    return (jnp.tile(cosine[:, 0], (1, lanes)), jnp.tile(sine[:, 0], (1, lanes)))


def turned(value, cosine, sine, back):
    size = value.shape[1]
    half = HEAD_SIZE // 2
    lane = lax.broadcasted_iota(jnp.int32, value.shape, 1)
    right = pltpu.roll(value, size - half, 1)
    left = pltpu.roll(value, half, 1)
    first = lane % HEAD_SIZE < half
    other = jnp.where(first, right, -left) if back else jnp.where(first, -right, left)
    return value * cosine + other * sine


def lanes_of(shape):
    return lax.broadcasted_iota(jnp.int32, shape, 1)


def head_of(value, i):
    start = i * HEAD_SIZE
    window = start // LANES * LANES
    offset = start - window
    size = LANES if offset + HEAD_SIZE <= LANES else 2 * LANES
    head = value[:, window : window + size]
    if offset:
        head = pltpu.roll(head, size - offset, 1)
    head = head[:, :LANES]
    return jnp.where(lanes_of(head.shape) < HEAD_SIZE, head, 0.0)


def side_by_side(heads):
    lane = lanes_of(heads[0].shape)
    second = pltpu.roll(heads[1], 96, 1)
    third = pltpu.roll(heads[2], 64, 1)
    fourth = pltpu.roll(heads[3], 32, 1)
    return jnp.concatenate(
        [
            jnp.where(lane < 96, heads[0], second),
            jnp.where(lane < 64, second, third),
            jnp.where(lane < 32, third, fourth),
        ],
        axis=1,
    )


def row_softmax(query, key):
    scores = lax.dot_general(
        query, key, (((1,), (1,)), ((), ())), preferred_element_type=F32
    ) * (1.0 / math.sqrt(HEAD_SIZE))
    row = lax.broadcasted_iota(jnp.int32, scores.shape, 0)
    column = lax.broadcasted_iota(jnp.int32, scores.shape, 1)
    scores = jnp.where(row >= column, scores, MASK_FILL)
    weights = jnp.exp(scores - jnp.max(scores, axis=1, keepdims=True))
    return weights * (1.0 / jnp.sum(weights, axis=1, keepdims=True))


def attention_blocks(width, kv_width):
    q_size = HEADS_AT_ONCE * HEAD_SIZE
    kv_size = q_size * kv_width // width
    return q_size, kv_size


def attention_forward(raw, cosine, sine, width, kv_width):
    count = raw.shape[0]
    q_size, kv_size = attention_blocks(width, kv_width)
    steps = width // q_size
    per_kv = width // kv_width

    def kernel(q_raw, k_raw, v_raw, cosine, sine, q_out, k_out, v_out, mixed):
        q = turned(q_raw[...], cosine[...], sine[...], False).astype(BF)
        k = turned(k_raw[...], cosine[:, :kv_size], sine[:, :kv_size], False).astype(BF)
        v = v_raw[...].astype(BF)
        q_out[...] = q
        k_out[...] = k
        v_out[...] = v
        q, k, v = q.astype(F32), k.astype(F32), v.astype(F32)
        for group in range(HEADS_AT_ONCE // 4):
            outs = []
            for i in range(4 * group, 4 * group + 4):
                if i % per_kv == 0:
                    key = head_of(k, i // per_kv).astype(BF)
                    value = head_of(v, i // per_kv).astype(BF)
                probs = row_softmax(head_of(q, i).astype(BF), key)
                outs.append(jnp.dot(probs.astype(BF), value, preferred_element_type=F32))
            mixed[:, 384 * group : 384 * group + 384] = side_by_side(outs).astype(BF)

    def block(size, at):
        return pl.BlockSpec((SEQ, size), lambda s, j: (s, at // size + j))

    table = pl.BlockSpec((SEQ, q_size), lambda s, j: (0, 0))
    return pl.pallas_call(
        kernel,
        grid=(count // SEQ, steps),
        out_shape=[
            jax.ShapeDtypeStruct((count, width), BF),
            jax.ShapeDtypeStruct((count, kv_width), BF),
            jax.ShapeDtypeStruct((count, kv_width), BF),
            jax.ShapeDtypeStruct((count, width), BF),
        ],
        in_specs=[
            block(q_size, 0),
            block(kv_size, width),
            block(kv_size, width + kv_width),
            table,
            table,
        ],
        out_specs=[block(q_size, 0), block(kv_size, 0), block(kv_size, 0), block(q_size, 0)],
        compiler_params=pltpu.CompilerParams(vmem_limit_bytes=16 * 2**20),
        cost_estimate=NO_COST,
        name="attention_forward",
    )(raw, raw, raw, cosine, sine)


def attention_backward(grad_mixed, q, k, v, cosine, sine):
    count, width = q.shape
    kv_width = k.shape[1]
    q_size, kv_size = attention_blocks(width, kv_width)
    steps = width // q_size
    per_kv = width // kv_width
    scale = 1.0 / math.sqrt(HEAD_SIZE)
    rows_rows = (((0,), (0,)), ((), ()))
    lanes_lanes = (((1,), (1,)), ((), ()))

    def kernel(d_ref, q_ref, k_ref, v_ref, cosine, sine, out):
        d, q = d_ref[...].astype(F32), q_ref[...].astype(F32)
        k, v = k_ref[...].astype(F32), v_ref[...].astype(F32)
        d_q, d_k, d_v = [], [], []
        for i in range(HEADS_AT_ONCE):
            if i % per_kv == 0:
                key = head_of(k, i // per_kv).astype(BF)
                value = head_of(v, i // per_kv).astype(BF)
            query, upstream = head_of(q, i).astype(BF), head_of(d, i).astype(BF)
            probs = row_softmax(query, key)
            d_probs = lax.dot_general(upstream, value, lanes_lanes, preferred_element_type=F32)
            d_scores = probs * (d_probs - jnp.sum(probs * d_probs, axis=1, keepdims=True))
            d_scores = d_scores.astype(BF)
            d_q.append(jnp.dot(d_scores, key, preferred_element_type=F32) * scale)
            part_k = lax.dot_general(d_scores, query, rows_rows, preferred_element_type=F32)
            part_v = lax.dot_general(
                probs.astype(BF), upstream, rows_rows, preferred_element_type=F32
            )
            if i % per_kv == 0:
                d_k.append(part_k)
                d_v.append(part_v)
            else:
                d_k[-1] += part_k
                d_v[-1] += part_v
        d_q = jnp.concatenate([side_by_side(d_q[g : g + 4]) for g in range(0, len(d_q), 4)], axis=1)
        d_q = turned(d_q, cosine[...], sine[...], True).astype(BF)
        d_k = side_by_side([part * scale for part in d_k])
        d_k = turned(d_k, cosine[:, :kv_size], sine[:, :kv_size], True).astype(BF)
        j = pl.program_id(1)
        out[:, pl.ds(pl.multiple_of(j * q_size, LANES), q_size)] = d_q
        at = pl.multiple_of(width + j * kv_size, LANES)
        out[:, pl.ds(at, kv_size)] = d_k
        at = pl.multiple_of(width + kv_width + j * kv_size, LANES)
        out[:, pl.ds(at, kv_size)] = side_by_side(d_v).astype(BF)

    def block(size):
        return pl.BlockSpec((SEQ, size), lambda s, j: (s, j))

    table = pl.BlockSpec((SEQ, q_size), lambda s, j: (0, 0))
    return pl.pallas_call(
        kernel,
        grid=(count // SEQ, steps),
        out_shape=jax.ShapeDtypeStruct((count, width + 2 * kv_width), BF),
        in_specs=[block(q_size), block(q_size), block(kv_size), block(kv_size), table, table],
        out_specs=pl.BlockSpec((SEQ, width + 2 * kv_width), lambda s, j: (s, 0)),
        compiler_params=pltpu.CompilerParams(vmem_limit_bytes=16 * 2**20),
        cost_estimate=NO_COST,
        name="attention_backward",
    )(grad_mixed, q, k, v, cosine, sine)


def norm_rows(field_in, gain_vec):
    inv_scale = lax.rsqrt(jnp.mean(field_in * field_in, axis=-1, keepdims=True) + EPSILON)
    return (field_in * inv_scale * gain_vec, inv_scale)


def norm_back(upstream, field_in, inv_scale, gain_vec):
    gain_grad = jnp.sum(upstream * field_in * inv_scale, axis=0)
    scaled_up = upstream * gain_vec
    field_grad = inv_scale * scaled_up - field_in * inv_scale**3 * jnp.mean(
        scaled_up * field_in, axis=-1, keepdims=True
    )
    return (gain_grad, field_grad)


def ffn_forward(rows, w_both, w_down):
    units = w_down.shape[0]
    pre = mm(rows, w_both[:, : 2 * units])
    hidden = (jax.nn.silu(pre[:, :units]) * pre[:, units:]).astype(BF)
    return (mm(hidden, w_down), pre, hidden)


def ffn_backward(grad_low, pre, w_both, w_down):
    grad_hidden = mm_t(grad_low, w_down)
    units = w_down.shape[0]
    gate_pre, up_pre = pre[:, :units], pre[:, units:]
    gate_sigmoid = jax.nn.sigmoid(gate_pre)
    grad_gate = grad_hidden * up_pre * gate_sigmoid * (1.0 + gate_pre * (1.0 - gate_sigmoid))
    grad_up = grad_hidden * gate_pre * gate_sigmoid
    grads = jnp.concatenate([grad_gate.astype(BF), grad_up.astype(BF)], axis=1)
    return (mm_t(grads, w_both[:, : 2 * units]), grads)


FFN_TILE = 256
FFN_VMEM = 24 * 2**20


def tiles_of(w_both, w_down, units):
    width = w_down.shape[1]
    steps = units // FFN_TILE
    return [
        pl.BlockSpec((width, FFN_TILE), lambda j: (0, j)),
        pl.BlockSpec((width, FFN_TILE), lambda j: (0, j + steps)),
        pl.BlockSpec((FFN_TILE, width), lambda j: (j, 0)),
    ]


def whole(array):
    return pl.BlockSpec(array.shape, lambda j: (0,) * array.ndim)


def sigmoid(value):
    return 1.0 / (1.0 + jnp.exp(-value))


def ffn_forward_beside(pieces, w_both, w_down):
    units, width = w_down.shape
    steps = units // FFN_TILE
    sizes = [piece.shape[0] for piece in pieces]
    count = sum(sizes)
    kinds = ((width, BF), (units, BF), (units, F32), (units, F32))
    kept_specs = [
        pl.BlockSpec((count, width), lambda j: (0, 0)),
        pl.BlockSpec((count, FFN_TILE), lambda j: (0, j)),
        pl.BlockSpec((count, FFN_TILE), lambda j: (0, j)),
        pl.BlockSpec((count, FFN_TILE), lambda j: (0, j)),
    ]
    first = len(pieces) + 3

    def kernel(*refs):
        w_gate, w_up, w_low = refs[len(pieces) : first]
        y, rows, hidden, gate, up, total = refs[-6:]
        j = pl.program_id(0)

        @pl.when(j == 0)
        def _():
            at = 0
            for ref, size in zip(refs, sizes):
                rows[at : at + size] = ref[...]
                at += size

        gate_pre = jnp.dot(rows[...], w_gate[...], preferred_element_type=F32)
        up_pre = jnp.dot(rows[...], w_up[...], preferred_element_type=F32)
        gate[...] = gate_pre
        up[...] = up_pre
        hid = (gate_pre * sigmoid(gate_pre) * up_pre).astype(BF)
        hidden[...] = hid
        part = jnp.dot(hid, w_low[...], preferred_element_type=F32)

        @pl.when(j == 0)
        def _():
            total[...] = part

        @pl.when(j > 0)
        def _():
            total[...] += part

        @pl.when(j == steps - 1)
        def _():
            y[...] = total[...].astype(y.dtype)

    y_shape = jax.ShapeDtypeStruct((count, width), F32)
    outs = pl.pallas_call(
        kernel,
        grid=(steps,),
        out_shape=[y_shape] + [jax.ShapeDtypeStruct((count, w), t) for w, t in kinds],
        in_specs=[whole(piece) for piece in pieces]
        + tiles_of(w_both, w_down, units),
        out_specs=[whole(y_shape)] + kept_specs,
        scratch_shapes=[pltpu.VMEM((count, width), F32)],
        compiler_params=pltpu.CompilerParams(vmem_limit_bytes=FFN_VMEM),
        cost_estimate=NO_COST,
        name="ffn_forward_beside",
    )(*pieces, w_both, w_both, w_down)
    return tuple(outs)


def ffn_backward_beside(pieces, gate_pre, up_pre, w_both, w_down):
    units, width = w_down.shape
    steps = units // FFN_TILE
    sizes = [piece.shape[0] for piece in pieces]
    count = sum(sizes)
    kinds = ((width, BF), (2 * units, BF))
    kept_specs = [
        pl.BlockSpec((count, width), lambda j: (0, 0)),
        pl.BlockSpec((count, 2 * units), lambda j: (0, 0)),
    ]
    pre_spec = pl.BlockSpec((count, FFN_TILE), lambda j: (0, j))
    first = len(pieces) + 5
    dims = (((1,), (1,)), ((), ()))

    def kernel(*refs):
        gate, up, w_gate, w_up, w_low = refs[len(pieces) : first]
        m, rows, grads, total = refs[-4:]
        j = pl.program_id(0)

        @pl.when(j == 0)
        def _():
            at = 0
            for ref, size in zip(refs, sizes):
                rows[at : at + size] = ref[...]
                at += size

        grad_hidden = lax.dot_general(rows[...], w_low[...], dims, preferred_element_type=F32)
        g = gate[...]
        s = sigmoid(g)
        grad_gate = (grad_hidden * up[...] * s * (1.0 + g * (1.0 - s))).astype(BF)
        grad_up = (grad_hidden * g * s).astype(BF)
        start = pl.multiple_of(j * FFN_TILE, LANES)
        grads[:, pl.ds(start, FFN_TILE)] = grad_gate
        grads[:, pl.ds(start + units, FFN_TILE)] = grad_up
        part = lax.dot_general(grad_gate, w_gate[...], dims, preferred_element_type=F32)
        part += lax.dot_general(grad_up, w_up[...], dims, preferred_element_type=F32)

        @pl.when(j == 0)
        def _():
            total[...] = part

        @pl.when(j > 0)
        def _():
            total[...] += part

        @pl.when(j == steps - 1)
        def _():
            m[...] = total[...].astype(m.dtype)

    m_shape = jax.ShapeDtypeStruct((count, width), F32)
    outs = pl.pallas_call(
        kernel,
        grid=(steps,),
        out_shape=[m_shape] + [jax.ShapeDtypeStruct((count, w), t) for w, t in kinds],
        in_specs=[whole(piece) for piece in pieces]
        + [pre_spec] * 2
        + tiles_of(w_both, w_down, units),
        out_specs=[whole(m_shape)] + kept_specs,
        scratch_shapes=[pltpu.VMEM((count, width), F32)],
        compiler_params=pltpu.CompilerParams(vmem_limit_bytes=FFN_VMEM),
        cost_estimate=NO_COST,
        name="ffn_backward_beside",
    )(*pieces, gate_pre, up_pre, w_both, w_both, w_down)
    return tuple(outs)


def input_gradient(grad_raw, weights, tokens, inv_scale, gain, grad_res):
    count, wide = grad_raw.shape
    width = tokens.shape[1]
    tile = 2 * FFN_TILE
    steps = wide // tile

    def kernel(grads, w, tokens, inv_scale, gain, grad_res, out, gain_grad, total):
        j = pl.program_id(0)
        part = lax.dot_general(
            grads[...], w[...], (((1,), (1,)), ((), ())), preferred_element_type=F32
        )

        @pl.when(j == 0)
        def _():
            total[...] = part

        @pl.when(j > 0)
        def _():
            total[...] += part

        @pl.when(j == steps - 1)
        def _():
            up, field, inv = total[...], tokens[...].astype(F32), inv_scale[...]
            gain_grad[...] = jnp.sum(up * field * inv, axis=0, keepdims=True)
            scaled = up * gain[...]
            mean = jnp.mean(scaled * field, axis=1, keepdims=True)
            grad = inv * scaled - field * (inv * inv * inv) * mean
            out[...] = (grad_res[...] + grad).astype(BF)

    return pl.pallas_call(
        kernel,
        grid=(steps,),
        out_shape=[
            jax.ShapeDtypeStruct((count, width), BF),
            jax.ShapeDtypeStruct((1, width), F32),
        ],
        in_specs=[
            pl.BlockSpec((count, tile), lambda j: (0, j)),
            pl.BlockSpec((width, tile), lambda j: (0, j)),
            whole(tokens),
            whole(inv_scale),
            whole(gain),
            whole(grad_res),
        ],
        out_specs=[
            pl.BlockSpec((count, width), lambda j: (0, 0)),
            pl.BlockSpec((1, width), lambda j: (0, 0)),
        ],
        scratch_shapes=[pltpu.VMEM((count, width), F32)],
        compiler_params=pltpu.CompilerParams(vmem_limit_bytes=2 * FFN_VMEM),
        cost_estimate=NO_COST,
        name="input_gradient",
    )(grad_raw, weights, tokens, inv_scale, gain, grad_res)


def products(lefts, rights, dtype):
    rows, columns = lefts[0].shape[1], rights[0].shape[1]
    tile = columns // 4
    count = len(lefts)

    def kernel(*refs):
        total = None
        for a, b in zip(refs[:count], refs[count : 2 * count]):
            part = lax.dot_general(
                a[...], b[...], (((0,), (0,)), ((), ())), preferred_element_type=F32
            )
            total = part if total is None else total + part
        refs[-1][...] = total.astype(dtype)

    return pl.pallas_call(
        kernel,
        grid=(columns // tile,),
        out_shape=jax.ShapeDtypeStruct((rows, columns), dtype),
        in_specs=[whole(left) for left in lefts]
        + [pl.BlockSpec((right.shape[0], tile), lambda j: (0, j)) for right in rights],
        out_specs=pl.BlockSpec((rows, tile), lambda j: (0, j)),
        compiler_params=pltpu.CompilerParams(vmem_limit_bytes=FFN_VMEM),
        cost_estimate=NO_COST,
        name="products",
    )(*lefts, *rights)


def body(
    tokens,
    teacher,
    valid_mask,
    w_query,
    key_weight_matrix,
    value_weight_matrix,
    w_output,
    w_gate,
    w_up,
    w_down,
    attn_gain,
    ffn_gain,
):
    n = lax.axis_size("dp")
    planes = n // 8
    position = lax.axis_index("dp")
    c, x, y, z = position % 2, position // 2 % 2, position // 4 % 2, position // 8
    bits = (z, y, x, c)
    p = position // 2 % 4
    rows = w_query.shape[0]
    width = w_query.shape[1]
    kv_width = key_weight_matrix.shape[1]
    ff_rows = w_down.shape[0]
    ff = w_gate.shape[1]
    count = tokens.shape[0]
    cosine, sine = rotation_lanes()
    to_column, by_side = tied(reordered(width, rows, "zcyx"), reordered(width, rows, "cxyz"))

    part = 2 * ff_rows
    units = planes * part
    gains = jnp.stack([attn_gain, ffn_gain], axis=1)
    gains = jnp.pad(gains, ((0, 0), (0, LANES - 2)))
    local = packed([w_query, key_weight_matrix, value_weight_matrix, w_output, gains])
    if planes == 4:
        gathered, wb = gather_weights(local, w_gate, w_up, w_down, bits)
        wd = w_down_from(wb, ff_rows, 2 * units, width)
    else:
        gathered, wb, wd = gather_weights_plainly(local, w_gate, w_up, w_down, p)

    with jax.named_scope("attention_forward"):
        wide = width + 2 * kv_width
        wqkv = gathered[:, :wide]
        wo = gathered[:, wide : wide + width]
        gain_in = gathered[:, wide + width].astype(F32)
        gain_mid = gathered[:, wide + width + 1].astype(F32)
        inputs_f = tokens.astype(F32)
        normed, inv_attn = norm_rows(inputs_f, gain_in)
        normed_in = tied(normed.astype(BF))[0]
        raw = mm(normed_in, wqkv)
        query, key, value, mixed = attention_forward(raw, cosine, sine, width, kv_width)
        hidden_res = inputs_f + mm(mixed, wo)
        normed_two, inv_ffn = norm_rows(hidden_res, gain_mid)
        normed_mid = normed_two.astype(BF)

    with jax.named_scope("ffn_forward"):
        far, y_near, *kept = split_gather(
            mm(normed_mid, to_column).astype(BF),
            (),
            lambda pieces: ffn_forward_beside(pieces, wb, wd),
        )
        near, hid_near, gate_near, up_near = kept
        y_a, pre_a, hid_a = ffn_forward(far[0], wb, wd)
        y_b, pre_b, hid_b = ffn_forward(far[1], wb, wd)
        y_a, y_b = y_a.astype(BF), y_b.astype(BF)
        y_b, mixed, normed_in = tied(y_b, mixed, normed_in)
        beside = (
            *core_halves(mm(mixed, by_side).astype(BF), c),
            *core_halves(mm(normed_in, by_side).astype(BF), c),
        )
        result, *halves = split_reduce(y_near, (y_a, y_b), beside)
        mixed_mine, mixed_theirs, normed_mine, normed_theirs = halves
        result = hidden_res + result
        out_act = result.astype(BF)

    with jax.named_scope("loss"):
        mask_f = valid_mask.astype(F32)
        grad_out = (result - teacher.astype(F32)) * mask_f[:, None]

    high = n // 2
    rest = [1 << k for k in range(4, n.bit_length() - 2)]

    with jax.named_scope("ffn_backward"):
        def near_backward(pieces, grads):
            sums = jnp.stack([jnp.sum(grads * grads), jnp.sum(mask_f)])
            return (
                jnp.broadcast_to(sums[:, None], (2, LANES)),
                *ffn_backward_beside(pieces, gate_near, up_near, wb, wd),
            )

        d_far, sums, m_near, d_near, g_near = split_gather(
            grad_out.astype(BF), (grad_out,), near_backward
        )
        m_a, g_a = ffn_backward(d_far[0], pre_a, wb, wd)
        m_b, g_b = ffn_backward(d_far[1], pre_b, wb, wd)
        m_b, m_near, sums = tied(m_b.astype(BF), m_near, sums)
        came = swap(sums, 1)
        beside = (products([near, *far], [g_near, g_a, g_b], BF), sums, came)

        owned_both = []

        def later(g_both, sums, came):
            owned_both.append(sum_to_owners(g_both))
            sums = sums + came
            g_down = products([hid_near, hid_a, hid_b], [d_near, *d_far], BF)
            return (g_down, sums, swap(sums, 8))

        grad_mid, g_down, sums, came = split_reduce(
            m_near, (m_a.astype(BF), m_b), beside, later
        )
        g_both = owned_both[0]
        sums = sums + came
        for mask in rest:
            sums = sums + swap(sums, mask)
        high_part = grad_mid.astype(BF)
        low_part = (grad_mid - high_part.astype(F32)).astype(BF)
        grad_mid = mm_t(high_part, to_column) + mm_t(low_part, to_column)

    with jax.named_scope("attention_backward"):
        grad_gain_mid, grad_res = norm_back(grad_mid, hidden_res, inv_ffn, gain_mid)
        grad_res = grad_out + grad_res
        res_low = grad_res.astype(BF)
        wo_came, came = tied(swap(t_mm(mixed_theirs, res_low).astype(BF), 1), swap(sums, high))
        sums = sums + came
        g_wo = PlaneSum([t_mm(mixed_mine, res_low), wo_came], rows, bits)
        wo_moving = g_wo.step_1()
        grad_mixed = mm_t(res_low, wo).astype(BF)
        grad_raw = attention_backward(grad_mixed, query, key, value, cosine, sine)
        *wo_came, grad_raw, sums, came = tied(*wo_moving, grad_raw, sums, swap(sums, 2))
        sums = sums + came
        wo_moving = g_wo.step_2(wo_came)

    with jax.named_scope("q_k_v_weight_gradients"):
        qkv_came = swap(t_mm(normed_theirs, grad_raw).astype(BF), 1)
        g_qkv = t_mm(normed_mine, grad_raw)
        qkv_came, g_qkv, grad_raw, came, g_both, g_down, *wo_came = tied(
            qkv_came, g_qkv, grad_raw, swap(sums, 4), g_both, g_down, *wo_moving
        )
        g_down = sum_to_owners(g_down)
        sums = sums + came
        loss = sums[0, 0] / (sums[1, 0] * width)
        g_qkv = PlaneSum([g_qkv, qkv_came], rows, bits)
        qkv_moving = g_qkv.step_1()
        g_wo = g_wo.step_3(wo_came)
        wo_moving = direct([g_wo], z) if planes == 4 else []

    with jax.named_scope("input_gradient"):
        input_grad, grad_gain_in = input_gradient(
            grad_raw, gathered, tokens, inv_attn, gain_in[None], grad_res
        )
        gains = jnp.concatenate([grad_gain_in, grad_gain_mid[None]])

    with jax.named_scope("weight_gradients_to_owners"):
        *qkv_came, gains = tied(*qkv_moving, gains)
        qkv_moving = g_qkv.step_2(qkv_came)
        for mask in (1, 8, high):
            gains = gains + swap(gains, mask)
        qkv_0, qkv_1, gains, g_both, g_down, *wo_came = tied(
            *qkv_moving, gains, g_both, g_down, *wo_moving
        )
        qkv_came = (qkv_0, qkv_1)
        g_wo = owned([g_wo], wo_came, z) if planes == 4 else z_reduce([g_wo])
        g_qkv = g_qkv.step_3(qkv_came)
        if planes == 4:
            moving = direct([g_qkv], z)
        g_both = g_both.reshape(4, rows, 2 * units)
        came = [pick(g_both, p ^ r, 0) for r in range(4)]
        gains_came, *moved = tied(swap(gains, 2), *[swap(came[r], r << 1) for r in (1, 2, 3)])
        gains = gains + gains_came
        for mask in rest:
            gains = gains + swap(gains, mask)
        grad_gate, grad_up = spread_columns([came[0]] + moved, p, part)
        gains = gains + swap(gains, 4)
        g_gains = lax.dynamic_slice_in_dim(gains, position * rows, rows, 1)
        if planes == 4:
            g_qkv = owned([g_qkv], moving, z)
        else:
            g_qkv = z_reduce([g_qkv])
        g_wq = g_qkv[:, :width]
        g_wk = g_qkv[:, width : width + kv_width]
        g_wv = g_qkv[:, width + kv_width :]

    return (
        out_act,
        loss,
        input_grad,
        g_wq,
        g_wk,
        g_wv,
        g_wo,
        grad_gate,
        grad_up,
        g_down.astype(F32),
        g_gains[0],
        g_gains[1],
    )


def solution(mesh):
    wide, flat = P("dp", None), P("dp")
    in_specs = (wide, wide, flat) + (wide,) * 7 + (flat, flat)
    out_specs = (wide, P(), wide) + (wide,) * 7 + (flat, flat)
    return jax.shard_map(body, mesh=mesh, in_specs=in_specs, out_specs=out_specs, check_vma=False)
```

```python
import math

import jax
import jax.numpy as jnp
from jax import lax
from jax.experimental import pallas as pl
from jax.experimental.pallas import tpu as pltpu
from jax.sharding import PartitionSpec as P

HEAD_SIZE = 96
SEQ = 128
EPSILON = 1e-05
ROPE_BASE = 100000.0
MASK_FILL = -1e30
LANES = 128

BF = jnp.bfloat16
F32 = jnp.float32
NO_COST = pl.CostEstimate(flops=1, bytes_accessed=1, transcendentals=0)


def dot(a, b, dims):
    return lax.dot_general(a, b, (dims, ((), ())), preferred_element_type=F32)


def mm(a, b):
    return dot(a, b, ((1,), (0,)))


def mm_t(a, b):
    return dot(a, b, ((1,), (1,)))


def t_mm(a, b):
    return dot(a, b, ((0,), (0,)))


def swap(value, mask):
    n = lax.axis_size("dp")
    return lax.ppermute(value, "dp", [(i, i ^ mask) for i in range(n)])


def column_groups(with_core):
    n = lax.axis_size("dp")
    planes = range(n // 8)
    if with_core:
        return [[8 * z + 2 * p + c for z in planes for c in range(2)] for p in range(4)]
    return [[8 * z + 2 * p + c for z in planes] for p in range(4) for c in range(2)]


def z_reduce(parts):
    total = sum(part.astype(F32) for part in parts)
    return lax.psum_scatter(
        total.astype(BF), "dp", axis_index_groups=column_groups(False), scatter_dimension=0
    ).astype(F32)


def summed(parts, index, axis):
    total = pick(parts[0], index, axis).astype(F32)
    for part in parts[1:]:
        total = total + pick(part, index, axis).astype(F32)
    return total


def owned(parts, came, z):
    own = summed(parts, z, 0)
    for piece in came:
        own = own + piece.astype(F32)
    return own


def direct(parts, z):
    return [swap(summed(parts, z ^ k, 0).astype(BF), 8 * k) for k in (3, 2, 1)]


def along_z(value, pairs):
    return lax.ppermute(
        value, "dp", [(8 * a + i, 8 * b + i) for a, b in pairs for i in range(8)]
    )


def tied(*values):
    return lax.optimization_barrier(values)


def place(out, piece, where):
    return lax.dynamic_update_slice(out, piece, where)


def pick(parts, index, axis):
    return lax.dynamic_index_in_dim(parts, index, axis, keepdims=False)


def column_cuts(w_gate, w_up, p, part):
    rows = w_gate.shape[0]
    gate_cut = w_gate.reshape(rows, -1, 4, part)
    up_cut = w_up.reshape(rows, -1, 4, part)
    cuts = []
    for r in range(4):
        gate = pick(gate_cut, p ^ r, 2).reshape(rows, -1)
        up = pick(up_cut, p ^ r, 2).reshape(rows, -1)
        cuts.append(jnp.concatenate([gate, up], axis=1))
    return cuts


def by_source(came, p):
    out = jnp.zeros((4,) + came[0].shape, BF)
    for r in range(4):
        out = place(out, came[r][None], (p ^ r, 0, 0))
    return out


def along_column(value):
    return lax.all_gather(
        value, "dp", axis_index_groups=column_groups(True), axis=0, tiled=True
    )


def sum_to_owners(partial):
    return lax.psum_scatter(
        partial, "dp", axis_index_groups=column_groups(True), scatter_dimension=0, tiled=True
    )


def gather_weights_plainly(local, w_gate, w_up, w_down, p):
    gathered = lax.all_gather(local, "dp", axis=0, tiled=True)
    cuts = column_cuts(w_gate, w_up, p, 2 * w_down.shape[0])
    came = [cuts[0]] + [swap(cuts[r], r << 1) for r in (1, 2, 3)]
    mine = by_source(came, p)
    wb = along_column(mine.reshape(-1, mine.shape[2]))
    return gathered, wb, along_column(w_down)


def merged(came, w_down, p):
    rows, columns = came[0].shape
    ff_rows, width = w_down.shape
    tall = 4 * rows
    side = width * ff_rows // tall
    rest = width - side
    low = tall - ff_rows

    def kernel(p_ref, *refs):
        wd, out = refs[4:]
        for r in range(4):
            start = pl.multiple_of((p_ref[0] ^ r) * rows, 16)
            out[pl.ds(start, rows), :columns] = refs[r][...]
        out[:ff_rows, columns:] = wd[:, :side]
        for k in range(ff_rows // low):
            at = columns + k * rest
            out[ff_rows:, at : at + rest] = wd[k * low : (k + 1) * low, side:]

    return pl.pallas_call(
        kernel,
        out_shape=jax.ShapeDtypeStruct((tall, columns + side), w_down.dtype),
        in_specs=[pl.BlockSpec(memory_space=pltpu.SMEM)]
        + [pl.BlockSpec(memory_space=pltpu.VMEM)] * 5,
        compiler_params=pltpu.CompilerParams(vmem_limit_bytes=8 * 2**20),
        cost_estimate=NO_COST,
        name="merged",
    )(p[None], *came, w_down)


def w_down_from(whole, ff_rows, columns, width):
    side = whole.shape[1] - columns
    rest = width - side
    tall = width * ff_rows // side
    low = tall - ff_rows
    devices = whole.shape[0] // tall

    def kernel(ref, out, sem):
        copies = []
        for i in range(devices):
            top, to = i * tall, i * ff_rows
            pairs = [
                (
                    ref.at[pl.ds(top, ff_rows), pl.ds(columns, side)],
                    out.at[pl.ds(to, ff_rows), pl.ds(0, side)],
                )
            ]
            for k in range(ff_rows // low):
                pairs.append(
                    (
                        ref.at[pl.ds(top + ff_rows, low), pl.ds(columns + k * rest, rest)],
                        out.at[pl.ds(to + k * low, low), pl.ds(side, rest)],
                    )
                )
            for k, (source, target) in enumerate(pairs):
                copies.append(pltpu.make_async_copy(source, target, sem.at[i, k]))
        for copy in copies:
            copy.start()
        for copy in copies:
            copy.wait()

    return pl.pallas_call(
        kernel,
        out_shape=jax.ShapeDtypeStruct((devices * ff_rows, width), whole.dtype),
        in_specs=[pl.BlockSpec(memory_space=pl.ANY)],
        out_specs=pl.BlockSpec(memory_space=pltpu.VMEM),
        scratch_shapes=[pltpu.SemaphoreType.DMA((devices, 1 + ff_rows // low))],
        compiler_params=pltpu.CompilerParams(vmem_limit_bytes=2 * FFN_VMEM),
        cost_estimate=NO_COST,
        name="w_down_from",
    )(whole)


def unset(shape, dtype):
    return pl.pallas_call(
        lambda out: None,
        out_shape=jax.ShapeDtypeStruct(shape, dtype),
        out_specs=pl.BlockSpec(memory_space=pl.ANY),
        name="unset",
    )()


def packed(pieces):
    widths = [piece.shape[1] for piece in pieces]
    rows = pieces[0].shape[0]

    def kernel(*refs):
        out = refs[-1]
        at = 0
        for ref, size in zip(refs[:-1], widths):
            out[:, at : at + size] = ref[...]
            at += size

    return pl.pallas_call(
        kernel,
        out_shape=jax.ShapeDtypeStruct((rows, sum(widths)), pieces[0].dtype),
        compiler_params=pltpu.CompilerParams(vmem_limit_bytes=8 * 2**20),
        name="packed",
    )(*pieces)


def column_cuts_kernel(w_gate, w_up, p, part):
    rows, ff = w_gate.shape
    planes = ff // (4 * part)
    units = planes * part

    def kernel(p_ref, gate, up, *outs):
        for r, out in enumerate(outs):
            q = p_ref[0] ^ r
            for k in range(planes):
                start = pl.multiple_of((4 * k + q) * part, LANES)
                out[:, k * part : (k + 1) * part] = gate[:, pl.ds(start, part)]
                out[:, units + k * part : units + (k + 1) * part] = up[:, pl.ds(start, part)]

    shape = jax.ShapeDtypeStruct((rows, 2 * units), w_gate.dtype)
    return pl.pallas_call(
        kernel,
        out_shape=[shape] * 4,
        in_specs=[pl.BlockSpec(memory_space=pltpu.SMEM)]
        + [pl.BlockSpec(memory_space=pltpu.VMEM)] * 2,
        compiler_params=pltpu.CompilerParams(vmem_limit_bytes=8 * 2**20),
        name="column_cuts",
    )(p[None], w_gate, w_up)


def gather_weights(local, w_gate, w_up, w_down, place_bits):
    z, y, x, c = place_bits
    p = 2 * y + x
    rows, columns = local.shape
    ff_rows, width = w_down.shape
    end = (z == 0) | (z == 3)
    up_pairs = [(0, 1), (1, 2), (2, 3)]
    down_pairs = [(1, 0), (2, 1), (3, 2)]
    far_pairs = [(0, 2), (3, 1)]
    out_pairs = [(1, 0), (2, 3)]
    z_b = jnp.where(z == 0, 1, z - 1)
    z_c = jnp.where(z < 2, 2, jnp.where(z == 2, 3, 1))
    z_d = jnp.where(z < 2, 3, 0)
    out = unset((4, 2, 2, 2, rows, columns), BF)

    def near_side(up, down):
        return jnp.where(z == 0, down, up)

    def to_pass_on(up, down):
        return jnp.where(z == 1, down, up)

    def put_x(out, piece, z_k, at_y, core):
        return place(out, piece[None, None, :, None], (z_k, at_y, 0, core, 0, 0))

    def put_y(out, piece, z_k, at_x, core):
        return place(out, piece[None, :, None, None], (z_k, 0, at_x, core, 0, 0))

    def in_order(bit, mine, theirs):
        return jnp.stack([jnp.where(bit == 0, mine, theirs), jnp.where(bit == 0, theirs, mine)])

    def put(out, pair, z_a, z_b, at_y, at_x, core):
        out = put_x(out, pair[0], z_a, at_y, core)
        return put_y(out, pair[1], z_b, at_x, core)

    with jax.named_scope("phase_0"):
        cuts = column_cuts_kernel(w_gate, w_up, p, 2 * ff_rows)
        crossing = (swap(cuts[1], 2), swap(cuts[2], 4), swap(cuts[3], 6))
        up, down = tied(along_z(local, up_pairs), along_z(local, down_pairs))
    with jax.named_scope("phase_1"):
        b = near_side(up, down)
        a, b, passing = tied(local, b, to_pass_on(up, down))
        a_x, b_y, far, first = tied(
            swap(a, 2), swap(b, 4), along_z(a, far_pairs), along_z(passing, out_pairs)
        )
    with jax.named_scope("phase_2"):
        a2, b2, far = tied(in_order(x, a, a_x), in_order(y, b, b_y), far)
        near_1 = jnp.stack([a2, b2])
        ffn = merged((cuts[0], *tied(*crossing)), w_down, p)
        a_far, b_far, second = tied(swap(a2, 4), swap(b2, 2), along_z(far, out_pairs))
        out = put(out, near_1, z, z_b, y, x, c)
    with jax.named_scope("ffn_weights"):
        ffn = along_column(tied(ffn, second)[0])
    with jax.named_scope("phase_3"):
        a, b = jnp.where(end, first, down), jnp.where(end, second, far)
        a, b, near_1 = tied(a, b, near_1)
        a_x, b_y, core_1 = tied(swap(a, 2), swap(b, 4), swap(near_1, 1))
        far_1 = jnp.stack([a_far, b_far])
        out = put(out, far_1, z, z_b, 1 - y, 1 - x, c)
    with jax.named_scope("phase_4"):
        a2, b2, far_1 = tied(in_order(x, a, a_x), in_order(y, b, b_y), far_1)
        a_far, b_far, core_2 = tied(swap(a2, 4), swap(b2, 2), swap(far_1, 1))
        out = put(out, core_1, z, z_b, y, x, 1 - c)
        near_2 = jnp.stack([a2, b2])
        out = put(out, near_2, z_c, z_d, y, x, c)
    with jax.named_scope("phase_5"):
        near_2, far_2 = tied(near_2, jnp.stack([a_far, b_far]))
        core_3, core_4 = tied(swap(near_2, 1), swap(far_2, 1))
        out = put(out, core_2, z, z_b, 1 - y, 1 - x, 1 - c)
        out = put(out, far_2, z_c, z_d, 1 - y, 1 - x, c)
        out = put(out, core_3, z_c, z_d, y, x, 1 - c)
        out = put(out, core_4, z_c, z_d, 1 - y, 1 - x, 1 - c)
        gathered = out.reshape(32 * rows, columns)
    return gathered, ffn


class PlaneSum:
    def __init__(self, left, grads):
        self.left, self.grads = left, grads
        self.own = left.shape[1] // 2
        self.first = self.own // 2
        self.tall = self.first // 4

    def step_0(self):
        return swap(t_mm(self.left[:, self.own :], self.grads).astype(BF), 1)

    def step_1(self, came):
        first, both = self.first, 2 * self.tall
        sent = t_mm(self.left[:, :first], self.grads) + came[:first].astype(F32)
        sent = sent.astype(BF)
        self.rest = t_mm(self.left[:, first : self.own], self.grads) + came[first:].astype(F32)
        return (swap(sent[:both], 4), swap(sent[both:], 2))

    def step_2(self, came):
        self.came, tall = came, self.tall
        a = self.rest[:tall] + came[0][tall:].astype(F32)
        b = self.rest[tall : 2 * tall] + came[1][tall:].astype(F32)
        return (swap(a.astype(BF), 2), swap(b.astype(BF), 4))

    def step_3(self, came, rows):
        tall = self.tall
        sums = []
        for i in (0, 1):
            own = self.rest[(2 + i) * tall : (3 + i) * tall]
            own = own + self.came[i][:tall].astype(F32) + came[i].astype(F32)
            sums.append(own.reshape(tall // rows, rows, -1))
        return jnp.concatenate(sums)


def selection(source):
    return (jnp.arange(source.shape[0])[:, None] == source[None, :]).astype(BF)


def column_order(count, rows):
    place_of, row = jnp.arange(count) // rows, jnp.arange(count) % rows
    z, core, y, x = place_of // 8, place_of // 4 % 2, place_of // 2 % 2, place_of % 2
    return selection((8 * z + 4 * y + 2 * x + core) * rows + row)


def sending_order(count, rows, place_bits):
    z, y, x, c = place_bits
    at = jnp.arange(count)
    group, within = at // (count // 16) % 8, at % (count // 16)
    upper = jnp.isin(group, jnp.array([2, 3, 5, 7]))
    x_differs = jnp.isin(group, jnp.array([1, 2, 3, 4]))
    y_differs = jnp.isin(group, jnp.array([0, 1, 3, 5]))
    core = c ^ (at // (count // 2))
    planes = count // rows // 8
    z_of = upper * (planes // 2) + within // rows
    chip = 4 * z_of + 2 * (y ^ y_differs.astype(jnp.int32)) + (x ^ x_differs.astype(jnp.int32))
    return selection((2 * chip + core) * rows + within % rows)


def split_gather(rows, beside=(), then=lambda pieces, *values: values):
    half = rows.shape[0] // 2
    a, b = rows[:half], rows[half:]
    a_x, b_y, *beside = tied(swap(a, 2), swap(b, 4), *beside)
    a2, b2 = tied(jnp.concatenate([a, a_x]), jnp.concatenate([b, b_y]))
    a_far, b_far, *beside = tied(swap(a2, 4), swap(b2, 2), *then((a2, b2), *beside))
    return ((a_far, b_far), *beside)


def split_reduce(near, far, beside=(), later=lambda *values: values):
    two = far[0].shape[0]
    one = two // 2
    came_a, came_b, *beside = tied(swap(far[0], 4), swap(far[1], 2), *beside)
    a = near[:two] + came_a.astype(F32)
    b = near[two:] + came_b.astype(F32)
    came_a, came_b, *beside = tied(
        swap(a[one:].astype(BF), 2), swap(b[one:].astype(BF), 4), *later(*beside)
    )
    own = jnp.concatenate([a[:one] + came_a.astype(F32), b[:one] + came_b.astype(F32)])
    return (own, *beside)


def spread_columns(came, p, part):
    units = came[0].shape[1] // 2
    natural = []
    for q in range(4):
        piece = came[3]
        for r in (0, 1, 2):
            piece = jnp.where(p == (q ^ r), came[r], piece)
        natural.append(piece.astype(F32))
    return tuple(
        jnp.concatenate(
            [
                natural[q][:, start + k * part : start + (k + 1) * part]
                for k in range(units // part)
                for q in range(4)
            ],
            axis=1,
        )
        for start in (0, units)
    )


def rotation_tables(length, width):
    half_width = width // 2
    position = jnp.arange(length, dtype=F32)[:, None]
    freq_rate = ROPE_BASE ** (-2.0 * jnp.arange(half_width, dtype=F32) / width)
    angle_table = position * freq_rate[None, :]
    return (jnp.cos(angle_table)[:, None, :], jnp.sin(angle_table)[:, None, :])


HEADS_AT_ONCE = 8


def rotation_lanes():
    cosine, sine = rotation_tables(SEQ, HEAD_SIZE)
    lanes = HEADS_AT_ONCE * 2
    return (jnp.tile(cosine[:, 0], (1, lanes)), jnp.tile(sine[:, 0], (1, lanes)))


def turned(value, cosine, sine, back):
    size = value.shape[1]
    half = HEAD_SIZE // 2
    lane = lax.broadcasted_iota(jnp.int32, value.shape, 1)
    right = pltpu.roll(value, size - half, 1)
    left = pltpu.roll(value, half, 1)
    first = lane % HEAD_SIZE < half
    other = jnp.where(first, right, -left) if back else jnp.where(first, -right, left)
    return value * cosine + other * sine


def lanes_of(shape):
    return lax.broadcasted_iota(jnp.int32, shape, 1)


def head_of(value, i):
    start = i * HEAD_SIZE
    window = start // LANES * LANES
    offset = start - window
    size = LANES if offset + HEAD_SIZE <= LANES else 2 * LANES
    head = value[:, window : window + size]
    if offset:
        head = pltpu.roll(head, size - offset, 1)
    head = head[:, :LANES]
    return jnp.where(lanes_of(head.shape) < HEAD_SIZE, head, 0.0)


def side_by_side(heads):
    lane = lanes_of(heads[0].shape)
    second = pltpu.roll(heads[1], 96, 1)
    third = pltpu.roll(heads[2], 64, 1)
    fourth = pltpu.roll(heads[3], 32, 1)
    return jnp.concatenate(
        [
            jnp.where(lane < 96, heads[0], second),
            jnp.where(lane < 64, second, third),
            jnp.where(lane < 32, third, fourth),
        ],
        axis=1,
    )


def row_softmax(query, key):
    scores = lax.dot_general(
        query, key, (((1,), (1,)), ((), ())), preferred_element_type=F32
    ) * (1.0 / math.sqrt(HEAD_SIZE))
    row = lax.broadcasted_iota(jnp.int32, scores.shape, 0)
    column = lax.broadcasted_iota(jnp.int32, scores.shape, 1)
    scores = jnp.where(row >= column, scores, MASK_FILL)
    weights = jnp.exp(scores - jnp.max(scores, axis=1, keepdims=True))
    return weights * (1.0 / jnp.sum(weights, axis=1, keepdims=True))


def attention_blocks(width, kv_width):
    q_size = HEADS_AT_ONCE * HEAD_SIZE
    kv_size = q_size * kv_width // width
    return q_size, kv_size


def attention_forward(raw, cosine, sine, width, kv_width):
    count = raw.shape[0]
    q_size, kv_size = attention_blocks(width, kv_width)
    steps = width // q_size
    per_kv = width // kv_width

    def kernel(q_raw, k_raw, v_raw, cosine, sine, q_out, k_out, v_out, mixed):
        q = turned(q_raw[...], cosine[...], sine[...], False).astype(BF)
        k = turned(k_raw[...], cosine[:, :kv_size], sine[:, :kv_size], False).astype(BF)
        v = v_raw[...].astype(BF)
        q_out[...] = q
        k_out[...] = k
        v_out[...] = v
        q, k, v = q.astype(F32), k.astype(F32), v.astype(F32)
        for group in range(HEADS_AT_ONCE // 4):
            outs = []
            for i in range(4 * group, 4 * group + 4):
                if i % per_kv == 0:
                    key = head_of(k, i // per_kv).astype(BF)
                    value = head_of(v, i // per_kv).astype(BF)
                probs = row_softmax(head_of(q, i).astype(BF), key)
                outs.append(jnp.dot(probs.astype(BF), value, preferred_element_type=F32))
            mixed[:, 384 * group : 384 * group + 384] = side_by_side(outs).astype(BF)

    def block(size, at):
        return pl.BlockSpec((SEQ, size), lambda s, j: (s, at // size + j))

    table = pl.BlockSpec((SEQ, q_size), lambda s, j: (0, 0))
    return pl.pallas_call(
        kernel,
        grid=(count // SEQ, steps),
        out_shape=[
            jax.ShapeDtypeStruct((count, width), BF),
            jax.ShapeDtypeStruct((count, kv_width), BF),
            jax.ShapeDtypeStruct((count, kv_width), BF),
            jax.ShapeDtypeStruct((count, width), BF),
        ],
        in_specs=[
            block(q_size, 0),
            block(kv_size, width),
            block(kv_size, width + kv_width),
            table,
            table,
        ],
        out_specs=[block(q_size, 0), block(kv_size, 0), block(kv_size, 0), block(q_size, 0)],
        compiler_params=pltpu.CompilerParams(vmem_limit_bytes=16 * 2**20),
        cost_estimate=NO_COST,
        name="attention_forward",
    )(raw, raw, raw, cosine, sine)


def attention_backward(grad_mixed, q, k, v, cosine, sine):
    count, width = q.shape
    kv_width = k.shape[1]
    q_size, kv_size = attention_blocks(width, kv_width)
    steps = width // q_size
    per_kv = width // kv_width
    scale = 1.0 / math.sqrt(HEAD_SIZE)
    rows_rows = (((0,), (0,)), ((), ()))
    lanes_lanes = (((1,), (1,)), ((), ()))

    def kernel(d_ref, q_ref, k_ref, v_ref, cosine, sine, out):
        d, q = d_ref[...].astype(F32), q_ref[...].astype(F32)
        k, v = k_ref[...].astype(F32), v_ref[...].astype(F32)
        d_q, d_k, d_v = [], [], []
        for i in range(HEADS_AT_ONCE):
            if i % per_kv == 0:
                key = head_of(k, i // per_kv).astype(BF)
                value = head_of(v, i // per_kv).astype(BF)
            query, upstream = head_of(q, i).astype(BF), head_of(d, i).astype(BF)
            probs = row_softmax(query, key)
            d_probs = lax.dot_general(upstream, value, lanes_lanes, preferred_element_type=F32)
            d_scores = probs * (d_probs - jnp.sum(probs * d_probs, axis=1, keepdims=True))
            d_scores = d_scores.astype(BF)
            d_q.append(jnp.dot(d_scores, key, preferred_element_type=F32) * scale)
            part_k = lax.dot_general(d_scores, query, rows_rows, preferred_element_type=F32)
            part_v = lax.dot_general(
                probs.astype(BF), upstream, rows_rows, preferred_element_type=F32
            )
            if i % per_kv == 0:
                d_k.append(part_k)
                d_v.append(part_v)
            else:
                d_k[-1] += part_k
                d_v[-1] += part_v
        d_q = jnp.concatenate([side_by_side(d_q[g : g + 4]) for g in range(0, len(d_q), 4)], axis=1)
        d_q = turned(d_q, cosine[...], sine[...], True).astype(BF)
        d_k = side_by_side([part * scale for part in d_k])
        d_k = turned(d_k, cosine[:, :kv_size], sine[:, :kv_size], True).astype(BF)
        j = pl.program_id(1)
        out[:, pl.ds(pl.multiple_of(j * q_size, LANES), q_size)] = d_q
        at = pl.multiple_of(width + j * kv_size, LANES)
        out[:, pl.ds(at, kv_size)] = d_k
        at = pl.multiple_of(width + kv_width + j * kv_size, LANES)
        out[:, pl.ds(at, kv_size)] = side_by_side(d_v).astype(BF)

    def block(size):
        return pl.BlockSpec((SEQ, size), lambda s, j: (s, j))

    table = pl.BlockSpec((SEQ, q_size), lambda s, j: (0, 0))
    return pl.pallas_call(
        kernel,
        grid=(count // SEQ, steps),
        out_shape=jax.ShapeDtypeStruct((count, width + 2 * kv_width), BF),
        in_specs=[block(q_size), block(q_size), block(kv_size), block(kv_size), table, table],
        out_specs=pl.BlockSpec((SEQ, width + 2 * kv_width), lambda s, j: (s, 0)),
        compiler_params=pltpu.CompilerParams(vmem_limit_bytes=16 * 2**20),
        cost_estimate=NO_COST,
        name="attention_backward",
    )(grad_mixed, q, k, v, cosine, sine)


def norm_rows(field_in, gain_vec):
    inv_scale = lax.rsqrt(jnp.mean(field_in * field_in, axis=-1, keepdims=True) + EPSILON)
    return (field_in * inv_scale * gain_vec, inv_scale)


def norm_back(upstream, field_in, inv_scale, gain_vec):
    gain_grad = jnp.sum(upstream * field_in * inv_scale, axis=0)
    scaled_up = upstream * gain_vec
    field_grad = inv_scale * scaled_up - field_in * inv_scale**3 * jnp.mean(
        scaled_up * field_in, axis=-1, keepdims=True
    )
    return (gain_grad, field_grad)


def ffn_forward(rows, w_both, w_down):
    units = w_down.shape[0]
    pre = mm(rows, w_both[:, : 2 * units])
    hidden = (jax.nn.silu(pre[:, :units]) * pre[:, units:]).astype(BF)
    return (mm(hidden, w_down), pre, hidden)


def ffn_backward(grad_low, pre, w_both, w_down):
    grad_hidden = mm_t(grad_low, w_down)
    units = w_down.shape[0]
    gate_pre, up_pre = pre[:, :units], pre[:, units:]
    gate_sigmoid = jax.nn.sigmoid(gate_pre)
    grad_gate = grad_hidden * up_pre * gate_sigmoid * (1.0 + gate_pre * (1.0 - gate_sigmoid))
    grad_up = grad_hidden * gate_pre * gate_sigmoid
    grads = jnp.concatenate([grad_gate.astype(BF), grad_up.astype(BF)], axis=1)
    return (mm_t(grads, w_both[:, : 2 * units]), grads)


FFN_TILE = 256
FFN_VMEM = 24 * 2**20


def tiles_of(w_both, w_down, units):
    width = w_down.shape[1]
    steps = units // FFN_TILE
    return [
        pl.BlockSpec((width, FFN_TILE), lambda j: (0, j)),
        pl.BlockSpec((width, FFN_TILE), lambda j: (0, j + steps)),
        pl.BlockSpec((FFN_TILE, width), lambda j: (j, 0)),
    ]


def whole(array):
    return pl.BlockSpec(array.shape, lambda j: (0,) * array.ndim)


def sigmoid(value):
    return 1.0 / (1.0 + jnp.exp(-value))


def ffn_forward_beside(pieces, w_both, w_down):
    units, width = w_down.shape
    steps = units // FFN_TILE
    sizes = [piece.shape[0] for piece in pieces]
    count = sum(sizes)
    kinds = ((width, BF), (units, BF), (units, F32), (units, F32))
    kept_specs = [
        pl.BlockSpec((count, width), lambda j: (0, 0)),
        pl.BlockSpec((count, FFN_TILE), lambda j: (0, j)),
        pl.BlockSpec((count, FFN_TILE), lambda j: (0, j)),
        pl.BlockSpec((count, FFN_TILE), lambda j: (0, j)),
    ]
    first = len(pieces) + 3

    def kernel(*refs):
        w_gate, w_up, w_low = refs[len(pieces) : first]
        y, rows, hidden, gate, up, total = refs[-6:]
        j = pl.program_id(0)

        @pl.when(j == 0)
        def _():
            at = 0
            for ref, size in zip(refs, sizes):
                rows[at : at + size] = ref[...]
                at += size

        gate_pre = jnp.dot(rows[...], w_gate[...], preferred_element_type=F32)
        up_pre = jnp.dot(rows[...], w_up[...], preferred_element_type=F32)
        gate[...] = gate_pre
        up[...] = up_pre
        hid = (gate_pre * sigmoid(gate_pre) * up_pre).astype(BF)
        hidden[...] = hid
        part = jnp.dot(hid, w_low[...], preferred_element_type=F32)

        @pl.when(j == 0)
        def _():
            total[...] = part

        @pl.when(j > 0)
        def _():
            total[...] += part

        @pl.when(j == steps - 1)
        def _():
            y[...] = total[...].astype(y.dtype)

    y_shape = jax.ShapeDtypeStruct((count, width), F32)
    outs = pl.pallas_call(
        kernel,
        grid=(steps,),
        out_shape=[y_shape] + [jax.ShapeDtypeStruct((count, w), t) for w, t in kinds],
        in_specs=[whole(piece) for piece in pieces]
        + tiles_of(w_both, w_down, units),
        out_specs=[whole(y_shape)] + kept_specs,
        scratch_shapes=[pltpu.VMEM((count, width), F32)],
        compiler_params=pltpu.CompilerParams(vmem_limit_bytes=FFN_VMEM),
        cost_estimate=NO_COST,
        name="ffn_forward_beside",
    )(*pieces, w_both, w_both, w_down)
    return tuple(outs)


def ffn_backward_beside(pieces, gate_pre, up_pre, w_both, w_down):
    units, width = w_down.shape
    steps = units // FFN_TILE
    sizes = [piece.shape[0] for piece in pieces]
    count = sum(sizes)
    kinds = ((width, BF), (2 * units, BF))
    kept_specs = [
        pl.BlockSpec((count, width), lambda j: (0, 0)),
        pl.BlockSpec((count, 2 * units), lambda j: (0, 0)),
    ]
    pre_spec = pl.BlockSpec((count, FFN_TILE), lambda j: (0, j))
    first = len(pieces) + 5
    dims = (((1,), (1,)), ((), ()))

    def kernel(*refs):
        gate, up, w_gate, w_up, w_low = refs[len(pieces) : first]
        m, rows, grads, total = refs[-4:]
        j = pl.program_id(0)

        @pl.when(j == 0)
        def _():
            at = 0
            for ref, size in zip(refs, sizes):
                rows[at : at + size] = ref[...]
                at += size

        grad_hidden = lax.dot_general(rows[...], w_low[...], dims, preferred_element_type=F32)
        g = gate[...]
        s = sigmoid(g)
        grad_gate = (grad_hidden * up[...] * s * (1.0 + g * (1.0 - s))).astype(BF)
        grad_up = (grad_hidden * g * s).astype(BF)
        start = pl.multiple_of(j * FFN_TILE, LANES)
        grads[:, pl.ds(start, FFN_TILE)] = grad_gate
        grads[:, pl.ds(start + units, FFN_TILE)] = grad_up
        part = lax.dot_general(grad_gate, w_gate[...], dims, preferred_element_type=F32)
        part += lax.dot_general(grad_up, w_up[...], dims, preferred_element_type=F32)

        @pl.when(j == 0)
        def _():
            total[...] = part

        @pl.when(j > 0)
        def _():
            total[...] += part

        @pl.when(j == steps - 1)
        def _():
            m[...] = total[...].astype(m.dtype)

    m_shape = jax.ShapeDtypeStruct((count, width), F32)
    outs = pl.pallas_call(
        kernel,
        grid=(steps,),
        out_shape=[m_shape] + [jax.ShapeDtypeStruct((count, w), t) for w, t in kinds],
        in_specs=[whole(piece) for piece in pieces]
        + [pre_spec] * 2
        + tiles_of(w_both, w_down, units),
        out_specs=[whole(m_shape)] + kept_specs,
        scratch_shapes=[pltpu.VMEM((count, width), F32)],
        compiler_params=pltpu.CompilerParams(vmem_limit_bytes=FFN_VMEM),
        cost_estimate=NO_COST,
        name="ffn_backward_beside",
    )(*pieces, gate_pre, up_pre, w_both, w_both, w_down)
    return tuple(outs)


def input_gradient(grad_raw, weights, tokens, inv_scale, gain, grad_res):
    count, wide = grad_raw.shape
    width = tokens.shape[1]
    tile = 2 * FFN_TILE
    steps = wide // tile

    def kernel(grads, w, tokens, inv_scale, gain, grad_res, out, gain_grad, total):
        j = pl.program_id(0)
        part = lax.dot_general(
            grads[...], w[...], (((1,), (1,)), ((), ())), preferred_element_type=F32
        )

        @pl.when(j == 0)
        def _():
            total[...] = part

        @pl.when(j > 0)
        def _():
            total[...] += part

        @pl.when(j == steps - 1)
        def _():
            up, field, inv = total[...], tokens[...].astype(F32), inv_scale[...]
            gain_grad[...] = jnp.sum(up * field * inv, axis=0, keepdims=True)
            scaled = up * gain[...]
            mean = jnp.mean(scaled * field, axis=1, keepdims=True)
            grad = inv * scaled - field * (inv * inv * inv) * mean
            out[...] = (grad_res[...] + grad).astype(BF)

    return pl.pallas_call(
        kernel,
        grid=(steps,),
        out_shape=[
            jax.ShapeDtypeStruct((count, width), BF),
            jax.ShapeDtypeStruct((1, width), F32),
        ],
        in_specs=[
            pl.BlockSpec((count, tile), lambda j: (0, j)),
            pl.BlockSpec((width, tile), lambda j: (0, j)),
            whole(tokens),
            whole(inv_scale),
            whole(gain),
            whole(grad_res),
        ],
        out_specs=[
            pl.BlockSpec((count, width), lambda j: (0, 0)),
            pl.BlockSpec((1, width), lambda j: (0, 0)),
        ],
        scratch_shapes=[pltpu.VMEM((count, width), F32)],
        compiler_params=pltpu.CompilerParams(vmem_limit_bytes=2 * FFN_VMEM),
        cost_estimate=NO_COST,
        name="input_gradient",
    )(grad_raw, weights, tokens, inv_scale, gain, grad_res)


def products(lefts, rights, dtype):
    rows, columns = lefts[0].shape[1], rights[0].shape[1]
    tile = columns // 4
    count = len(lefts)

    def kernel(*refs):
        total = None
        for a, b in zip(refs[:count], refs[count : 2 * count]):
            part = lax.dot_general(
                a[...], b[...], (((0,), (0,)), ((), ())), preferred_element_type=F32
            )
            total = part if total is None else total + part
        refs[-1][...] = total.astype(dtype)

    return pl.pallas_call(
        kernel,
        grid=(columns // tile,),
        out_shape=jax.ShapeDtypeStruct((rows, columns), dtype),
        in_specs=[whole(left) for left in lefts]
        + [pl.BlockSpec((right.shape[0], tile), lambda j: (0, j)) for right in rights],
        out_specs=pl.BlockSpec((rows, tile), lambda j: (0, j)),
        compiler_params=pltpu.CompilerParams(vmem_limit_bytes=FFN_VMEM),
        cost_estimate=NO_COST,
        name="products",
    )(*lefts, *rights)


def body(
    tokens,
    teacher,
    valid_mask,
    w_query,
    key_weight_matrix,
    value_weight_matrix,
    w_output,
    w_gate,
    w_up,
    w_down,
    attn_gain,
    ffn_gain,
):
    n = lax.axis_size("dp")
    planes = n // 8
    position = lax.axis_index("dp")
    c, x, y, z = position % 2, position // 2 % 2, position // 4 % 2, position // 8
    bits = (z, y, x, c)
    p = position // 2 % 4
    rows = w_query.shape[0]
    width = w_query.shape[1]
    kv_width = key_weight_matrix.shape[1]
    ff_rows = w_down.shape[0]
    ff = w_gate.shape[1]
    count = tokens.shape[0]
    cosine, sine = rotation_lanes()
    to_column, to_senders = tied(column_order(width, rows), sending_order(width, rows, bits))

    part = 2 * ff_rows
    units = planes * part
    gains = jnp.stack([attn_gain, ffn_gain], axis=1)
    gains = jnp.pad(gains, ((0, 0), (0, LANES - 2)))
    local = packed([w_query, key_weight_matrix, value_weight_matrix, w_output, gains])
    if planes == 4:
        gathered, wb = gather_weights(local, w_gate, w_up, w_down, bits)
        wd = w_down_from(wb, ff_rows, 2 * units, width)
    else:
        gathered, wb, wd = gather_weights_plainly(local, w_gate, w_up, w_down, p)

    with jax.named_scope("attention_forward"):
        wide = width + 2 * kv_width
        wqkv = gathered[:, :wide]
        wo = gathered[:, wide : wide + width]
        gain_in = gathered[:, wide + width].astype(F32)
        gain_mid = gathered[:, wide + width + 1].astype(F32)
        inputs_f = tokens.astype(F32)
        normed, inv_attn = norm_rows(inputs_f, gain_in)
        normed_in = tied(normed.astype(BF))[0]
        raw = mm(normed_in, wqkv)
        query, key, value, mixed = attention_forward(raw, cosine, sine, width, kv_width)
        hidden_res = inputs_f + mm(mixed, wo)
        normed_two, inv_ffn = norm_rows(hidden_res, gain_mid)
        normed_mid = normed_two.astype(BF)

    with jax.named_scope("ffn_forward"):
        far, y_near, *kept = split_gather(
            mm(normed_mid, to_column).astype(BF),
            (),
            lambda pieces: ffn_forward_beside(pieces, wb, wd),
        )
        near, hid_near, gate_near, up_near = kept
        y_a, pre_a, hid_a = ffn_forward(far[0], wb, wd)
        y_b, pre_b, hid_b = ffn_forward(far[1], wb, wd)
        y_a, y_b = y_a.astype(BF), y_b.astype(BF)
        y_b, mixed, normed_in = tied(y_b, mixed, normed_in)
        beside = (mm(mixed, to_senders).astype(BF), mm(normed_in, to_senders).astype(BF))
        result, mixed_sent, normed_sent = split_reduce(y_near, (y_a, y_b), beside)
        result = hidden_res + result
        out_act = result.astype(BF)

    with jax.named_scope("loss"):
        mask_f = valid_mask.astype(F32)
        grad_out = (result - teacher.astype(F32)) * mask_f[:, None]

    high = n // 2
    rest = [1 << k for k in range(4, n.bit_length() - 2)]

    with jax.named_scope("ffn_backward"):
        def near_backward(pieces, grads):
            sums = jnp.stack([jnp.sum(grads * grads), jnp.sum(mask_f)])
            return (
                jnp.broadcast_to(sums[:, None], (2, LANES)),
                *ffn_backward_beside(pieces, gate_near, up_near, wb, wd),
            )

        d_far, sums, m_near, d_near, g_near = split_gather(
            grad_out.astype(BF), (grad_out,), near_backward
        )
        m_a, g_a = ffn_backward(d_far[0], pre_a, wb, wd)
        m_b, g_b = ffn_backward(d_far[1], pre_b, wb, wd)
        m_b, m_near, sums = tied(m_b.astype(BF), m_near, sums)
        came = swap(sums, 1)
        beside = (products([near, *far], [g_near, g_a, g_b], BF), sums, came)

        owned_both = []

        def later(g_both, sums, came):
            owned_both.append(sum_to_owners(g_both))
            sums = sums + came
            g_down = products([hid_near, hid_a, hid_b], [d_near, *d_far], BF)
            return (g_down, sums, swap(sums, 8))

        grad_mid, g_down, sums, came = split_reduce(
            m_near, (m_a.astype(BF), m_b), beside, later
        )
        g_both = owned_both[0]
        sums = sums + came
        for mask in rest:
            sums = sums + swap(sums, mask)
        high_part = grad_mid.astype(BF)
        low_part = (grad_mid - high_part.astype(F32)).astype(BF)
        grad_mid = mm_t(high_part, to_column) + mm_t(low_part, to_column)

    with jax.named_scope("attention_backward"):
        grad_gain_mid, grad_res = norm_back(grad_mid, hidden_res, inv_ffn, gain_mid)
        grad_res = grad_out + grad_res
        res_low = grad_res.astype(BF)
        g_wo = PlaneSum(mixed_sent, res_low)
        wo_came, came = tied(g_wo.step_0(), swap(sums, high))
        sums = sums + came
        wo_moving = g_wo.step_1(wo_came)
        grad_mixed = mm_t(res_low, wo).astype(BF)
        grad_raw = attention_backward(grad_mixed, query, key, value, cosine, sine)
        *wo_came, grad_raw, sums, came = tied(*wo_moving, grad_raw, sums, swap(sums, 2))
        sums = sums + came
        wo_moving = g_wo.step_2(wo_came)

    with jax.named_scope("q_k_v_weight_gradients"):
        g_qkv = PlaneSum(normed_sent, grad_raw)
        qkv_came, grad_raw, sums, came, g_both, g_down, *wo_came = tied(
            g_qkv.step_0(), grad_raw, sums, swap(sums, 4), g_both, g_down, *wo_moving
        )
        g_down = sum_to_owners(g_down)
        sums = sums + came
        loss = sums[0, 0] / (sums[1, 0] * width)
        qkv_moving = g_qkv.step_1(qkv_came)
        g_wo = g_wo.step_3(wo_came, rows)
        wo_moving = direct([g_wo], z) if planes == 4 else []

    with jax.named_scope("input_gradient"):
        input_grad, grad_gain_in = input_gradient(
            grad_raw, gathered, tokens, inv_attn, gain_in[None], grad_res
        )
        gains = jnp.concatenate([grad_gain_in, grad_gain_mid[None]])

    with jax.named_scope("weight_gradients_to_owners"):
        *qkv_came, gains = tied(*qkv_moving, gains)
        qkv_moving = g_qkv.step_2(qkv_came)
        for mask in (1, 8, high):
            gains = gains + swap(gains, mask)
        qkv_0, qkv_1, gains, g_both, g_down, *wo_came = tied(
            *qkv_moving, gains, g_both, g_down, *wo_moving
        )
        qkv_came = (qkv_0, qkv_1)
        g_wo = owned([g_wo], wo_came, z) if planes == 4 else z_reduce([g_wo])
        g_qkv = g_qkv.step_3(qkv_came, rows)
        if planes == 4:
            moving = direct([g_qkv], z)
        g_both = g_both.reshape(4, rows, 2 * units)
        came = [pick(g_both, p ^ r, 0) for r in range(4)]
        gains_came, *moved = tied(swap(gains, 2), *[swap(came[r], r << 1) for r in (1, 2, 3)])
        gains = gains + gains_came
        for mask in rest:
            gains = gains + swap(gains, mask)
        grad_gate, grad_up = spread_columns([came[0]] + moved, p, part)
        gains = gains + swap(gains, 4)
        g_gains = lax.dynamic_slice_in_dim(gains, position * rows, rows, 1)
        if planes == 4:
            g_qkv = owned([g_qkv], moving, z)
        else:
            g_qkv = z_reduce([g_qkv])
        g_wq = g_qkv[:, :width]
        g_wk = g_qkv[:, width : width + kv_width]
        g_wv = g_qkv[:, width + kv_width :]

    return (
        out_act,
        loss,
        input_grad,
        g_wq,
        g_wk,
        g_wv,
        g_wo,
        grad_gate,
        grad_up,
        g_down.astype(F32),
        g_gains[0],
        g_gains[1],
    )


def solution(mesh):
    wide, flat = P("dp", None), P("dp")
    in_specs = (wide, wide, flat) + (wide,) * 7 + (flat, flat)
    out_specs = (wide, P(), wide) + (wide,) * 7 + (flat, flat)
    return jax.shard_map(body, mesh=mesh, in_specs=in_specs, out_specs=out_specs, check_vma=False)
```

```python
import math

import jax
import jax.numpy as jnp
from jax import lax
from jax.experimental import pallas as pl
from jax.experimental.pallas import tpu as pltpu
from jax.sharding import PartitionSpec as P

HEAD_SIZE = 96
SEQ = 128
EPSILON = 1e-05
ROPE_BASE = 100000.0
MASK_FILL = -1e30
LANES = 128

BF = jnp.bfloat16
F32 = jnp.float32
NO_COST = pl.CostEstimate(flops=1, bytes_accessed=1, transcendentals=0)


def dot(a, b, dims):
    return lax.dot_general(a, b, (dims, ((), ())), preferred_element_type=F32)


def mm(a, b):
    return dot(a, b, ((1,), (0,)))


def mm_t(a, b):
    return dot(a, b, ((1,), (1,)))


def t_mm(a, b):
    return dot(a, b, ((0,), (0,)))


def swap(value, mask):
    n = lax.axis_size("dp")
    return lax.ppermute(value, "dp", [(i, i ^ mask) for i in range(n)])


def column_groups(with_core):
    n = lax.axis_size("dp")
    planes = range(n // 8)
    if with_core:
        return [[8 * z + 2 * p + c for z in planes for c in range(2)] for p in range(4)]
    return [[8 * z + 2 * p + c for z in planes] for p in range(4) for c in range(2)]


def z_reduce(parts):
    total = sum(part.astype(F32) for part in parts)
    return lax.psum_scatter(
        total.astype(BF), "dp", axis_index_groups=column_groups(False), scatter_dimension=0
    ).astype(F32)


def summed(parts, index, axis):
    total = pick(parts[0], index, axis).astype(F32)
    for part in parts[1:]:
        total = total + pick(part, index, axis).astype(F32)
    return total


def owned(parts, came, z):
    own = summed(parts, z, 0)
    for piece in came:
        own = own + piece.astype(F32)
    return own


def direct(parts, z):
    return [swap(summed(parts, z ^ k, 0).astype(BF), 8 * k) for k in (3, 2, 1)]


def along_z(value, pairs):
    return lax.ppermute(
        value, "dp", [(8 * a + i, 8 * b + i) for a, b in pairs for i in range(8)]
    )


def tied(*values):
    return lax.optimization_barrier(values)


def place(out, piece, where):
    return lax.dynamic_update_slice(out, piece, where)


def pick(parts, index, axis):
    return lax.dynamic_index_in_dim(parts, index, axis, keepdims=False)


def column_cuts(w_gate, w_up, p, part):
    rows = w_gate.shape[0]
    gate_cut = w_gate.reshape(rows, -1, 4, part)
    up_cut = w_up.reshape(rows, -1, 4, part)
    cuts = []
    for r in range(4):
        gate = pick(gate_cut, p ^ r, 2).reshape(rows, -1)
        up = pick(up_cut, p ^ r, 2).reshape(rows, -1)
        cuts.append(jnp.concatenate([gate, up], axis=1))
    return cuts


def by_source(came, p):
    out = jnp.zeros((4,) + came[0].shape, BF)
    for r in range(4):
        out = place(out, came[r][None], (p ^ r, 0, 0))
    return out


def along_column(value):
    return lax.all_gather(
        value, "dp", axis_index_groups=column_groups(True), axis=0, tiled=True
    )


def sum_to_owners(partial):
    return lax.psum_scatter(
        partial, "dp", axis_index_groups=column_groups(True), scatter_dimension=0, tiled=True
    )


def gather_weights_plainly(local, w_gate, w_up, w_down, p):
    gathered = lax.all_gather(local, "dp", axis=0, tiled=True)
    cuts = column_cuts(w_gate, w_up, p, 2 * w_down.shape[0])
    came = [cuts[0]] + [swap(cuts[r], r << 1) for r in (1, 2, 3)]
    mine = by_source(came, p)
    wb = along_column(mine.reshape(-1, mine.shape[2]))
    return gathered, wb, along_column(w_down)


def merged(came, w_down, p):
    rows, columns = came[0].shape
    ff_rows, width = w_down.shape
    tall = 4 * rows
    side = width * ff_rows // tall
    rest = width - side
    low = tall - ff_rows

    def kernel(p_ref, *refs):
        wd, out = refs[4:]
        for r in range(4):
            start = pl.multiple_of((p_ref[0] ^ r) * rows, 16)
            out[pl.ds(start, rows), :columns] = refs[r][...]
        out[:ff_rows, columns:] = wd[:, :side]
        for k in range(ff_rows // low):
            at = columns + k * rest
            out[ff_rows:, at : at + rest] = wd[k * low : (k + 1) * low, side:]

    return pl.pallas_call(
        kernel,
        out_shape=jax.ShapeDtypeStruct((tall, columns + side), w_down.dtype),
        in_specs=[pl.BlockSpec(memory_space=pltpu.SMEM)]
        + [pl.BlockSpec(memory_space=pltpu.VMEM)] * 5,
        compiler_params=pltpu.CompilerParams(vmem_limit_bytes=8 * 2**20),
        cost_estimate=NO_COST,
        name="merged",
    )(p[None], *came, w_down)


def w_down_from(whole, ff_rows, columns, width):
    side = whole.shape[1] - columns
    rest = width - side
    tall = width * ff_rows // side
    low = tall - ff_rows
    devices = whole.shape[0] // tall

    def kernel(ref, out, sem):
        copies = []
        for i in range(devices):
            top, to = i * tall, i * ff_rows
            pairs = [
                (
                    ref.at[pl.ds(top, ff_rows), pl.ds(columns, side)],
                    out.at[pl.ds(to, ff_rows), pl.ds(0, side)],
                )
            ]
            for k in range(ff_rows // low):
                pairs.append(
                    (
                        ref.at[pl.ds(top + ff_rows, low), pl.ds(columns + k * rest, rest)],
                        out.at[pl.ds(to + k * low, low), pl.ds(side, rest)],
                    )
                )
            for k, (source, target) in enumerate(pairs):
                copies.append(pltpu.make_async_copy(source, target, sem.at[i, k]))
        for copy in copies:
            copy.start()
        for copy in copies:
            copy.wait()

    return pl.pallas_call(
        kernel,
        out_shape=jax.ShapeDtypeStruct((devices * ff_rows, width), whole.dtype),
        in_specs=[pl.BlockSpec(memory_space=pl.ANY)],
        out_specs=pl.BlockSpec(memory_space=pltpu.VMEM),
        scratch_shapes=[pltpu.SemaphoreType.DMA((devices, 1 + ff_rows // low))],
        compiler_params=pltpu.CompilerParams(vmem_limit_bytes=2 * FFN_VMEM),
        cost_estimate=NO_COST,
        name="w_down_from",
    )(whole)


def unset(shape, dtype):
    return pl.pallas_call(
        lambda out: None,
        out_shape=jax.ShapeDtypeStruct(shape, dtype),
        out_specs=pl.BlockSpec(memory_space=pl.ANY),
        name="unset",
    )()


def packed(pieces):
    widths = [piece.shape[1] for piece in pieces]
    rows = pieces[0].shape[0]

    def kernel(*refs):
        out = refs[-1]
        at = 0
        for ref, size in zip(refs[:-1], widths):
            out[:, at : at + size] = ref[...]
            at += size

    return pl.pallas_call(
        kernel,
        out_shape=jax.ShapeDtypeStruct((rows, sum(widths)), pieces[0].dtype),
        compiler_params=pltpu.CompilerParams(vmem_limit_bytes=8 * 2**20),
        name="packed",
    )(*pieces)


def column_cuts_kernel(w_gate, w_up, p, part):
    rows, ff = w_gate.shape
    planes = ff // (4 * part)
    units = planes * part

    def kernel(p_ref, gate, up, *outs):
        for r, out in enumerate(outs):
            q = p_ref[0] ^ r
            for k in range(planes):
                start = pl.multiple_of((4 * k + q) * part, LANES)
                out[:, k * part : (k + 1) * part] = gate[:, pl.ds(start, part)]
                out[:, units + k * part : units + (k + 1) * part] = up[:, pl.ds(start, part)]

    shape = jax.ShapeDtypeStruct((rows, 2 * units), w_gate.dtype)
    return pl.pallas_call(
        kernel,
        out_shape=[shape] * 4,
        in_specs=[pl.BlockSpec(memory_space=pltpu.SMEM)]
        + [pl.BlockSpec(memory_space=pltpu.VMEM)] * 2,
        compiler_params=pltpu.CompilerParams(vmem_limit_bytes=8 * 2**20),
        name="column_cuts",
    )(p[None], w_gate, w_up)


def gather_weights(local, w_gate, w_up, w_down, place_bits):
    z, y, x, c = place_bits
    p = 2 * y + x
    rows, columns = local.shape
    ff_rows, width = w_down.shape
    end = (z == 0) | (z == 3)
    up_pairs = [(0, 1), (1, 2), (2, 3)]
    down_pairs = [(1, 0), (2, 1), (3, 2)]
    far_pairs = [(0, 2), (3, 1)]
    out_pairs = [(1, 0), (2, 3)]
    z_b = jnp.where(z == 0, 1, z - 1)
    z_c = jnp.where(z < 2, 2, jnp.where(z == 2, 3, 1))
    z_d = jnp.where(z < 2, 3, 0)
    out = unset((4, 2, 2, 2, rows, columns), BF)

    def near_side(up, down):
        return jnp.where(z == 0, down, up)

    def to_pass_on(up, down):
        return jnp.where(z == 1, down, up)

    def put_x(out, piece, z_k, at_y, core):
        return place(out, piece[None, None, :, None], (z_k, at_y, 0, core, 0, 0))

    def put_y(out, piece, z_k, at_x, core):
        return place(out, piece[None, :, None, None], (z_k, 0, at_x, core, 0, 0))

    def in_order(bit, mine, theirs):
        return jnp.stack([jnp.where(bit == 0, mine, theirs), jnp.where(bit == 0, theirs, mine)])

    def put(out, pair, z_a, z_b, at_y, at_x, core):
        out = put_x(out, pair[0], z_a, at_y, core)
        return put_y(out, pair[1], z_b, at_x, core)

    with jax.named_scope("phase_0"):
        cuts = column_cuts_kernel(w_gate, w_up, p, 2 * ff_rows)
        crossing = (swap(cuts[1], 2), swap(cuts[2], 4), swap(cuts[3], 6))
        up, down = tied(along_z(local, up_pairs), along_z(local, down_pairs))
    with jax.named_scope("phase_1"):
        b = near_side(up, down)
        a, b, passing = tied(local, b, to_pass_on(up, down))
        a_x, b_y, far, first = tied(
            swap(a, 2), swap(b, 4), along_z(a, far_pairs), along_z(passing, out_pairs)
        )
    with jax.named_scope("phase_2"):
        a2, b2, far = tied(in_order(x, a, a_x), in_order(y, b, b_y), far)
        near_1 = jnp.stack([a2, b2])
        ffn = merged((cuts[0], *tied(*crossing)), w_down, p)
        a_far, b_far, second, core_1 = tied(
            swap(a2, 4), swap(b2, 2), along_z(far, out_pairs), swap(near_1, 1)
        )
        out = put(out, near_1, z, z_b, y, x, c)
    with jax.named_scope("ffn_weights"):
        ffn = along_column(tied(ffn, second)[0])
    with jax.named_scope("phase_3"):
        a, b = jnp.where(end, first, down), jnp.where(end, second, far)
        a, b, far_1 = tied(a, b, jnp.stack([a_far, b_far]))
        a_x, b_y, core_2 = tied(swap(a, 2), swap(b, 4), swap(far_1, 1))
        out = put(out, core_1, z, z_b, y, x, 1 - c)
        out = put(out, far_1, z, z_b, 1 - y, 1 - x, c)
    with jax.named_scope("phase_4"):
        a2, b2 = tied(in_order(x, a, a_x), in_order(y, b, b_y))
        near_2 = jnp.stack([a2, b2])
        a_far, b_far, core_3 = tied(swap(a2, 4), swap(b2, 2), swap(near_2, 1))
        out = put(out, core_2, z, z_b, 1 - y, 1 - x, 1 - c)
        out = put(out, near_2, z_c, z_d, y, x, c)
    with jax.named_scope("phase_5"):
        far_2 = jnp.stack([a_far, b_far])
        core_4 = swap(far_2, 1)
        out = put(out, core_3, z_c, z_d, y, x, 1 - c)
        out = put(out, far_2, z_c, z_d, 1 - y, 1 - x, c)
        out = put(out, core_4, z_c, z_d, 1 - y, 1 - x, 1 - c)
        gathered = out.reshape(32 * rows, columns)
    return gathered, ffn


class PlaneSum:
    def __init__(self, left, grads):
        self.left, self.grads = left, grads
        self.own = left.shape[1] // 2
        self.first = self.own // 2
        self.tall = self.first // 4

    def step_0(self):
        return swap(t_mm(self.left[:, self.own :], self.grads).astype(BF), 1)

    def step_1(self, came):
        first, both = self.first, 2 * self.tall
        sent = t_mm(self.left[:, :first], self.grads) + came[:first].astype(F32)
        sent = sent.astype(BF)
        self.rest = t_mm(self.left[:, first : self.own], self.grads) + came[first:].astype(F32)
        return (swap(sent[:both], 4), swap(sent[both:], 2))

    def step_2(self, came):
        self.came, tall = came, self.tall
        a = self.rest[:tall] + came[0][tall:].astype(F32)
        b = self.rest[tall : 2 * tall] + came[1][tall:].astype(F32)
        return (swap(a.astype(BF), 2), swap(b.astype(BF), 4))

    def step_3(self, came, rows):
        tall = self.tall
        sums = []
        for i in (0, 1):
            own = self.rest[(2 + i) * tall : (3 + i) * tall]
            own = own + self.came[i][:tall].astype(F32) + came[i].astype(F32)
            sums.append(own.reshape(tall // rows, rows, -1))
        return jnp.concatenate(sums)


def selection(source):
    return (jnp.arange(source.shape[0])[:, None] == source[None, :]).astype(BF)


def column_order(count, rows):
    place_of, row = jnp.arange(count) // rows, jnp.arange(count) % rows
    z, core, y, x = place_of // 8, place_of // 4 % 2, place_of // 2 % 2, place_of % 2
    return selection((8 * z + 4 * y + 2 * x + core) * rows + row)


def sending_order(count, rows, place_bits):
    z, y, x, c = place_bits
    at = jnp.arange(count)
    group, within = at // (count // 16) % 8, at % (count // 16)
    upper = jnp.isin(group, jnp.array([2, 3, 5, 7]))
    x_differs = jnp.isin(group, jnp.array([1, 2, 3, 4]))
    y_differs = jnp.isin(group, jnp.array([0, 1, 3, 5]))
    core = c ^ (at // (count // 2))
    planes = count // rows // 8
    z_of = upper * (planes // 2) + within // rows
    chip = 4 * z_of + 2 * (y ^ y_differs.astype(jnp.int32)) + (x ^ x_differs.astype(jnp.int32))
    return selection((2 * chip + core) * rows + within % rows)


def split_gather(rows, beside=(), then=lambda pieces, *values: values):
    half = rows.shape[0] // 2
    a, b = rows[:half], rows[half:]
    a_x, b_y, *beside = tied(swap(a, 2), swap(b, 4), *beside)
    a2, b2 = tied(jnp.concatenate([a, a_x]), jnp.concatenate([b, b_y]))
    a_far, b_far, *beside = tied(swap(a2, 4), swap(b2, 2), *then((a2, b2), *beside))
    return ((a_far, b_far), *beside)


def split_reduce(near, far, beside=(), later=lambda *values: values):
    two = far[0].shape[0]
    one = two // 2
    came_a, came_b, *beside = tied(swap(far[0], 4), swap(far[1], 2), *beside)
    a = near[:two] + came_a.astype(F32)
    b = near[two:] + came_b.astype(F32)
    came_a, came_b, *beside = tied(
        swap(a[one:].astype(BF), 2), swap(b[one:].astype(BF), 4), *later(*beside)
    )
    own = jnp.concatenate([a[:one] + came_a.astype(F32), b[:one] + came_b.astype(F32)])
    return (own, *beside)


def spread_columns(came, p, part):
    units = came[0].shape[1] // 2
    natural = []
    for q in range(4):
        piece = came[3]
        for r in (0, 1, 2):
            piece = jnp.where(p == (q ^ r), came[r], piece)
        natural.append(piece.astype(F32))
    return tuple(
        jnp.concatenate(
            [
                natural[q][:, start + k * part : start + (k + 1) * part]
                for k in range(units // part)
                for q in range(4)
            ],
            axis=1,
        )
        for start in (0, units)
    )


def rotation_tables(length, width):
    half_width = width // 2
    position = jnp.arange(length, dtype=F32)[:, None]
    freq_rate = ROPE_BASE ** (-2.0 * jnp.arange(half_width, dtype=F32) / width)
    angle_table = position * freq_rate[None, :]
    return (jnp.cos(angle_table)[:, None, :], jnp.sin(angle_table)[:, None, :])


HEADS_AT_ONCE = 8


def rotation_lanes():
    cosine, sine = rotation_tables(SEQ, HEAD_SIZE)
    lanes = HEADS_AT_ONCE * 2
    return (jnp.tile(cosine[:, 0], (1, lanes)), jnp.tile(sine[:, 0], (1, lanes)))


def turned(value, cosine, sine, back):
    size = value.shape[1]
    half = HEAD_SIZE // 2
    lane = lax.broadcasted_iota(jnp.int32, value.shape, 1)
    right = pltpu.roll(value, size - half, 1)
    left = pltpu.roll(value, half, 1)
    first = lane % HEAD_SIZE < half
    other = jnp.where(first, right, -left) if back else jnp.where(first, -right, left)
    return value * cosine + other * sine


def lanes_of(shape):
    return lax.broadcasted_iota(jnp.int32, shape, 1)


def head_of(value, i):
    start = i * HEAD_SIZE
    window = start // LANES * LANES
    offset = start - window
    size = LANES if offset + HEAD_SIZE <= LANES else 2 * LANES
    head = value[:, window : window + size]
    if offset:
        head = pltpu.roll(head, size - offset, 1)
    head = head[:, :LANES]
    return jnp.where(lanes_of(head.shape) < HEAD_SIZE, head, 0.0)


def side_by_side(heads):
    lane = lanes_of(heads[0].shape)
    second = pltpu.roll(heads[1], 96, 1)
    third = pltpu.roll(heads[2], 64, 1)
    fourth = pltpu.roll(heads[3], 32, 1)
    return jnp.concatenate(
        [
            jnp.where(lane < 96, heads[0], second),
            jnp.where(lane < 64, second, third),
            jnp.where(lane < 32, third, fourth),
        ],
        axis=1,
    )


def row_softmax(query, key):
    scores = lax.dot_general(
        query, key, (((1,), (1,)), ((), ())), preferred_element_type=F32
    ) * (1.0 / math.sqrt(HEAD_SIZE))
    row = lax.broadcasted_iota(jnp.int32, scores.shape, 0)
    column = lax.broadcasted_iota(jnp.int32, scores.shape, 1)
    scores = jnp.where(row >= column, scores, MASK_FILL)
    weights = jnp.exp(scores - jnp.max(scores, axis=1, keepdims=True))
    return weights * (1.0 / jnp.sum(weights, axis=1, keepdims=True))


def attention_blocks(width, kv_width):
    q_size = HEADS_AT_ONCE * HEAD_SIZE
    kv_size = q_size * kv_width // width
    return q_size, kv_size


def attention_forward(raw, cosine, sine, width, kv_width):
    count = raw.shape[0]
    q_size, kv_size = attention_blocks(width, kv_width)
    steps = width // q_size
    per_kv = width // kv_width

    def kernel(q_raw, k_raw, v_raw, cosine, sine, q_out, k_out, v_out, mixed):
        q = turned(q_raw[...], cosine[...], sine[...], False).astype(BF)
        k = turned(k_raw[...], cosine[:, :kv_size], sine[:, :kv_size], False).astype(BF)
        v = v_raw[...].astype(BF)
        q_out[...] = q
        k_out[...] = k
        v_out[...] = v
        q, k, v = q.astype(F32), k.astype(F32), v.astype(F32)
        for group in range(HEADS_AT_ONCE // 4):
            outs = []
            for i in range(4 * group, 4 * group + 4):
                if i % per_kv == 0:
                    key = head_of(k, i // per_kv).astype(BF)
                    value = head_of(v, i // per_kv).astype(BF)
                probs = row_softmax(head_of(q, i).astype(BF), key)
                outs.append(jnp.dot(probs.astype(BF), value, preferred_element_type=F32))
            mixed[:, 384 * group : 384 * group + 384] = side_by_side(outs).astype(BF)

    def block(size, at):
        return pl.BlockSpec((SEQ, size), lambda s, j: (s, at // size + j))

    table = pl.BlockSpec((SEQ, q_size), lambda s, j: (0, 0))
    return pl.pallas_call(
        kernel,
        grid=(count // SEQ, steps),
        out_shape=[
            jax.ShapeDtypeStruct((count, width), BF),
            jax.ShapeDtypeStruct((count, kv_width), BF),
            jax.ShapeDtypeStruct((count, kv_width), BF),
            jax.ShapeDtypeStruct((count, width), BF),
        ],
        in_specs=[
            block(q_size, 0),
            block(kv_size, width),
            block(kv_size, width + kv_width),
            table,
            table,
        ],
        out_specs=[block(q_size, 0), block(kv_size, 0), block(kv_size, 0), block(q_size, 0)],
        compiler_params=pltpu.CompilerParams(vmem_limit_bytes=16 * 2**20),
        cost_estimate=NO_COST,
        name="attention_forward",
    )(raw, raw, raw, cosine, sine)


def attention_backward(grad_mixed, q, k, v, cosine, sine):
    count, width = q.shape
    kv_width = k.shape[1]
    q_size, kv_size = attention_blocks(width, kv_width)
    steps = width // q_size
    per_kv = width // kv_width
    scale = 1.0 / math.sqrt(HEAD_SIZE)
    rows_rows = (((0,), (0,)), ((), ()))
    lanes_lanes = (((1,), (1,)), ((), ()))

    def kernel(d_ref, q_ref, k_ref, v_ref, cosine, sine, out):
        d, q = d_ref[...].astype(F32), q_ref[...].astype(F32)
        k, v = k_ref[...].astype(F32), v_ref[...].astype(F32)
        d_q, d_k, d_v = [], [], []
        for i in range(HEADS_AT_ONCE):
            if i % per_kv == 0:
                key = head_of(k, i // per_kv).astype(BF)
                value = head_of(v, i // per_kv).astype(BF)
            query, upstream = head_of(q, i).astype(BF), head_of(d, i).astype(BF)
            probs = row_softmax(query, key)
            d_probs = lax.dot_general(upstream, value, lanes_lanes, preferred_element_type=F32)
            d_scores = probs * (d_probs - jnp.sum(probs * d_probs, axis=1, keepdims=True))
            d_scores = d_scores.astype(BF)
            d_q.append(jnp.dot(d_scores, key, preferred_element_type=F32) * scale)
            part_k = lax.dot_general(d_scores, query, rows_rows, preferred_element_type=F32)
            part_v = lax.dot_general(
                probs.astype(BF), upstream, rows_rows, preferred_element_type=F32
            )
            if i % per_kv == 0:
                d_k.append(part_k)
                d_v.append(part_v)
            else:
                d_k[-1] += part_k
                d_v[-1] += part_v
        d_q = jnp.concatenate([side_by_side(d_q[g : g + 4]) for g in range(0, len(d_q), 4)], axis=1)
        d_q = turned(d_q, cosine[...], sine[...], True).astype(BF)
        d_k = side_by_side([part * scale for part in d_k])
        d_k = turned(d_k, cosine[:, :kv_size], sine[:, :kv_size], True).astype(BF)
        j = pl.program_id(1)
        out[:, pl.ds(pl.multiple_of(j * q_size, LANES), q_size)] = d_q
        at = pl.multiple_of(width + j * kv_size, LANES)
        out[:, pl.ds(at, kv_size)] = d_k
        at = pl.multiple_of(width + kv_width + j * kv_size, LANES)
        out[:, pl.ds(at, kv_size)] = side_by_side(d_v).astype(BF)

    def block(size):
        return pl.BlockSpec((SEQ, size), lambda s, j: (s, j))

    table = pl.BlockSpec((SEQ, q_size), lambda s, j: (0, 0))
    return pl.pallas_call(
        kernel,
        grid=(count // SEQ, steps),
        out_shape=jax.ShapeDtypeStruct((count, width + 2 * kv_width), BF),
        in_specs=[block(q_size), block(q_size), block(kv_size), block(kv_size), table, table],
        out_specs=pl.BlockSpec((SEQ, width + 2 * kv_width), lambda s, j: (s, 0)),
        compiler_params=pltpu.CompilerParams(vmem_limit_bytes=16 * 2**20),
        cost_estimate=NO_COST,
        name="attention_backward",
    )(grad_mixed, q, k, v, cosine, sine)


def norm_rows(field_in, gain_vec):
    inv_scale = lax.rsqrt(jnp.mean(field_in * field_in, axis=-1, keepdims=True) + EPSILON)
    return (field_in * inv_scale * gain_vec, inv_scale)


def norm_back(upstream, field_in, inv_scale, gain_vec):
    gain_grad = jnp.sum(upstream * field_in * inv_scale, axis=0)
    scaled_up = upstream * gain_vec
    field_grad = inv_scale * scaled_up - field_in * inv_scale**3 * jnp.mean(
        scaled_up * field_in, axis=-1, keepdims=True
    )
    return (gain_grad, field_grad)


def ffn_forward(rows, w_both, w_down):
    units = w_down.shape[0]
    pre = mm(rows, w_both[:, : 2 * units])
    hidden = (jax.nn.silu(pre[:, :units]) * pre[:, units:]).astype(BF)
    return (mm(hidden, w_down), pre, hidden)


def ffn_backward(grad_low, pre, w_both, w_down):
    grad_hidden = mm_t(grad_low, w_down)
    units = w_down.shape[0]
    gate_pre, up_pre = pre[:, :units], pre[:, units:]
    gate_sigmoid = jax.nn.sigmoid(gate_pre)
    grad_gate = grad_hidden * up_pre * gate_sigmoid * (1.0 + gate_pre * (1.0 - gate_sigmoid))
    grad_up = grad_hidden * gate_pre * gate_sigmoid
    grads = jnp.concatenate([grad_gate.astype(BF), grad_up.astype(BF)], axis=1)
    return (mm_t(grads, w_both[:, : 2 * units]), grads)


FFN_TILE = 256
FFN_VMEM = 24 * 2**20


def tiles_of(w_both, w_down, units):
    width = w_down.shape[1]
    steps = units // FFN_TILE
    return [
        pl.BlockSpec((width, FFN_TILE), lambda j: (0, j)),
        pl.BlockSpec((width, FFN_TILE), lambda j: (0, j + steps)),
        pl.BlockSpec((FFN_TILE, width), lambda j: (j, 0)),
    ]


def whole(array):
    return pl.BlockSpec(array.shape, lambda j: (0,) * array.ndim)


def sigmoid(value):
    return 1.0 / (1.0 + jnp.exp(-value))


def ffn_forward_beside(pieces, w_both, w_down):
    units, width = w_down.shape
    steps = units // FFN_TILE
    sizes = [piece.shape[0] for piece in pieces]
    count = sum(sizes)
    kinds = ((width, BF), (units, BF), (units, F32), (units, F32))
    kept_specs = [
        pl.BlockSpec((count, width), lambda j: (0, 0)),
        pl.BlockSpec((count, FFN_TILE), lambda j: (0, j)),
        pl.BlockSpec((count, FFN_TILE), lambda j: (0, j)),
        pl.BlockSpec((count, FFN_TILE), lambda j: (0, j)),
    ]
    first = len(pieces) + 3

    def kernel(*refs):
        w_gate, w_up, w_low = refs[len(pieces) : first]
        y, rows, hidden, gate, up, total = refs[-6:]
        j = pl.program_id(0)

        @pl.when(j == 0)
        def _():
            at = 0
            for ref, size in zip(refs, sizes):
                rows[at : at + size] = ref[...]
                at += size

        gate_pre = jnp.dot(rows[...], w_gate[...], preferred_element_type=F32)
        up_pre = jnp.dot(rows[...], w_up[...], preferred_element_type=F32)
        gate[...] = gate_pre
        up[...] = up_pre
        hid = (gate_pre * sigmoid(gate_pre) * up_pre).astype(BF)
        hidden[...] = hid
        part = jnp.dot(hid, w_low[...], preferred_element_type=F32)

        @pl.when(j == 0)
        def _():
            total[...] = part

        @pl.when(j > 0)
        def _():
            total[...] += part

        @pl.when(j == steps - 1)
        def _():
            y[...] = total[...].astype(y.dtype)

    y_shape = jax.ShapeDtypeStruct((count, width), F32)
    outs = pl.pallas_call(
        kernel,
        grid=(steps,),
        out_shape=[y_shape] + [jax.ShapeDtypeStruct((count, w), t) for w, t in kinds],
        in_specs=[whole(piece) for piece in pieces]
        + tiles_of(w_both, w_down, units),
        out_specs=[whole(y_shape)] + kept_specs,
        scratch_shapes=[pltpu.VMEM((count, width), F32)],
        compiler_params=pltpu.CompilerParams(vmem_limit_bytes=FFN_VMEM),
        cost_estimate=NO_COST,
        name="ffn_forward_beside",
    )(*pieces, w_both, w_both, w_down)
    return tuple(outs)


def ffn_backward_beside(pieces, gate_pre, up_pre, w_both, w_down):
    units, width = w_down.shape
    steps = units // FFN_TILE
    sizes = [piece.shape[0] for piece in pieces]
    count = sum(sizes)
    kinds = ((width, BF), (2 * units, BF))
    kept_specs = [
        pl.BlockSpec((count, width), lambda j: (0, 0)),
        pl.BlockSpec((count, 2 * units), lambda j: (0, 0)),
    ]
    pre_spec = pl.BlockSpec((count, FFN_TILE), lambda j: (0, j))
    first = len(pieces) + 5
    dims = (((1,), (1,)), ((), ()))

    def kernel(*refs):
        gate, up, w_gate, w_up, w_low = refs[len(pieces) : first]
        m, rows, grads, total = refs[-4:]
        j = pl.program_id(0)

        @pl.when(j == 0)
        def _():
            at = 0
            for ref, size in zip(refs, sizes):
                rows[at : at + size] = ref[...]
                at += size

        grad_hidden = lax.dot_general(rows[...], w_low[...], dims, preferred_element_type=F32)
        g = gate[...]
        s = sigmoid(g)
        grad_gate = (grad_hidden * up[...] * s * (1.0 + g * (1.0 - s))).astype(BF)
        grad_up = (grad_hidden * g * s).astype(BF)
        start = pl.multiple_of(j * FFN_TILE, LANES)
        grads[:, pl.ds(start, FFN_TILE)] = grad_gate
        grads[:, pl.ds(start + units, FFN_TILE)] = grad_up
        part = lax.dot_general(grad_gate, w_gate[...], dims, preferred_element_type=F32)
        part += lax.dot_general(grad_up, w_up[...], dims, preferred_element_type=F32)

        @pl.when(j == 0)
        def _():
            total[...] = part

        @pl.when(j > 0)
        def _():
            total[...] += part

        @pl.when(j == steps - 1)
        def _():
            m[...] = total[...].astype(m.dtype)

    m_shape = jax.ShapeDtypeStruct((count, width), F32)
    outs = pl.pallas_call(
        kernel,
        grid=(steps,),
        out_shape=[m_shape] + [jax.ShapeDtypeStruct((count, w), t) for w, t in kinds],
        in_specs=[whole(piece) for piece in pieces]
        + [pre_spec] * 2
        + tiles_of(w_both, w_down, units),
        out_specs=[whole(m_shape)] + kept_specs,
        scratch_shapes=[pltpu.VMEM((count, width), F32)],
        compiler_params=pltpu.CompilerParams(vmem_limit_bytes=FFN_VMEM),
        cost_estimate=NO_COST,
        name="ffn_backward_beside",
    )(*pieces, gate_pre, up_pre, w_both, w_both, w_down)
    return tuple(outs)


def input_gradient(grad_raw, weights, tokens, inv_scale, gain, grad_res):
    count, wide = grad_raw.shape
    width = tokens.shape[1]
    tile = 2 * FFN_TILE
    steps = wide // tile

    def kernel(grads, w, tokens, inv_scale, gain, grad_res, out, gain_grad, total):
        j = pl.program_id(0)
        part = lax.dot_general(
            grads[...], w[...], (((1,), (1,)), ((), ())), preferred_element_type=F32
        )

        @pl.when(j == 0)
        def _():
            total[...] = part

        @pl.when(j > 0)
        def _():
            total[...] += part

        @pl.when(j == steps - 1)
        def _():
            up, field, inv = total[...], tokens[...].astype(F32), inv_scale[...]
            gain_grad[...] = jnp.sum(up * field * inv, axis=0, keepdims=True)
            scaled = up * gain[...]
            mean = jnp.mean(scaled * field, axis=1, keepdims=True)
            grad = inv * scaled - field * (inv * inv * inv) * mean
            out[...] = (grad_res[...] + grad).astype(BF)

    return pl.pallas_call(
        kernel,
        grid=(steps,),
        out_shape=[
            jax.ShapeDtypeStruct((count, width), BF),
            jax.ShapeDtypeStruct((1, width), F32),
        ],
        in_specs=[
            pl.BlockSpec((count, tile), lambda j: (0, j)),
            pl.BlockSpec((width, tile), lambda j: (0, j)),
            whole(tokens),
            whole(inv_scale),
            whole(gain),
            whole(grad_res),
        ],
        out_specs=[
            pl.BlockSpec((count, width), lambda j: (0, 0)),
            pl.BlockSpec((1, width), lambda j: (0, 0)),
        ],
        scratch_shapes=[pltpu.VMEM((count, width), F32)],
        compiler_params=pltpu.CompilerParams(vmem_limit_bytes=2 * FFN_VMEM),
        cost_estimate=NO_COST,
        name="input_gradient",
    )(grad_raw, weights, tokens, inv_scale, gain, grad_res)


def products(lefts, rights, dtype):
    rows, columns = lefts[0].shape[1], rights[0].shape[1]
    tile = columns // 4
    count = len(lefts)

    def kernel(*refs):
        total = None
        for a, b in zip(refs[:count], refs[count : 2 * count]):
            part = lax.dot_general(
                a[...], b[...], (((0,), (0,)), ((), ())), preferred_element_type=F32
            )
            total = part if total is None else total + part
        refs[-1][...] = total.astype(dtype)

    return pl.pallas_call(
        kernel,
        grid=(columns // tile,),
        out_shape=jax.ShapeDtypeStruct((rows, columns), dtype),
        in_specs=[whole(left) for left in lefts]
        + [pl.BlockSpec((right.shape[0], tile), lambda j: (0, j)) for right in rights],
        out_specs=pl.BlockSpec((rows, tile), lambda j: (0, j)),
        compiler_params=pltpu.CompilerParams(vmem_limit_bytes=FFN_VMEM),
        cost_estimate=NO_COST,
        name="products",
    )(*lefts, *rights)


def body(
    tokens,
    teacher,
    valid_mask,
    w_query,
    key_weight_matrix,
    value_weight_matrix,
    w_output,
    w_gate,
    w_up,
    w_down,
    attn_gain,
    ffn_gain,
):
    n = lax.axis_size("dp")
    planes = n // 8
    position = lax.axis_index("dp")
    c, x, y, z = position % 2, position // 2 % 2, position // 4 % 2, position // 8
    bits = (z, y, x, c)
    p = position // 2 % 4
    rows = w_query.shape[0]
    width = w_query.shape[1]
    kv_width = key_weight_matrix.shape[1]
    ff_rows = w_down.shape[0]
    ff = w_gate.shape[1]
    count = tokens.shape[0]
    cosine, sine = rotation_lanes()
    to_column, to_senders = tied(column_order(width, rows), sending_order(width, rows, bits))

    part = 2 * ff_rows
    units = planes * part
    gains = jnp.stack([attn_gain, ffn_gain], axis=1)
    gains = jnp.pad(gains, ((0, 0), (0, LANES - 2)))
    local = packed([w_query, key_weight_matrix, value_weight_matrix, w_output, gains])
    if planes == 4:
        gathered, wb = gather_weights(local, w_gate, w_up, w_down, bits)
        wd = w_down_from(wb, ff_rows, 2 * units, width)
    else:
        gathered, wb, wd = gather_weights_plainly(local, w_gate, w_up, w_down, p)

    with jax.named_scope("attention_forward"):
        wide = width + 2 * kv_width
        wqkv = gathered[:, :wide]
        wo = gathered[:, wide : wide + width]
        gain_in = gathered[:, wide + width].astype(F32)
        gain_mid = gathered[:, wide + width + 1].astype(F32)
        inputs_f = tokens.astype(F32)
        normed, inv_attn = norm_rows(inputs_f, gain_in)
        normed_in = tied(normed.astype(BF))[0]
        raw = mm(normed_in, wqkv)
        query, key, value, mixed = attention_forward(raw, cosine, sine, width, kv_width)
        hidden_res = inputs_f + mm(mixed, wo)
        normed_two, inv_ffn = norm_rows(hidden_res, gain_mid)
        normed_mid = normed_two.astype(BF)

    with jax.named_scope("ffn_forward"):
        far, y_near, *kept = split_gather(
            mm(normed_mid, to_column).astype(BF),
            (),
            lambda pieces: ffn_forward_beside(pieces, wb, wd),
        )
        near, hid_near, gate_near, up_near = kept
        y_a, pre_a, hid_a = ffn_forward(far[0], wb, wd)
        y_b, pre_b, hid_b = ffn_forward(far[1], wb, wd)
        y_a, y_b = y_a.astype(BF), y_b.astype(BF)
        y_b, mixed, normed_in = tied(y_b, mixed, normed_in)
        beside = (mm(mixed, to_senders).astype(BF), mm(normed_in, to_senders).astype(BF))
        result, mixed_sent, normed_sent = split_reduce(y_near, (y_a, y_b), beside)
        result = hidden_res + result
        out_act = result.astype(BF)

    with jax.named_scope("loss"):
        mask_f = valid_mask.astype(F32)
        grad_out = (result - teacher.astype(F32)) * mask_f[:, None]

    high = n // 2
    rest = [1 << k for k in range(4, n.bit_length() - 2)]

    with jax.named_scope("ffn_backward"):
        def near_backward(pieces, grads):
            sums = jnp.stack([jnp.sum(grads * grads), jnp.sum(mask_f)])
            return (
                jnp.broadcast_to(sums[:, None], (2, LANES)),
                *ffn_backward_beside(pieces, gate_near, up_near, wb, wd),
            )

        d_far, sums, m_near, d_near, g_near = split_gather(
            grad_out.astype(BF), (grad_out,), near_backward
        )
        m_a, g_a = ffn_backward(d_far[0], pre_a, wb, wd)
        m_b, g_b = ffn_backward(d_far[1], pre_b, wb, wd)
        m_b, m_near, sums = tied(m_b.astype(BF), m_near, sums)
        came = swap(sums, 1)
        beside = (products([near, *far], [g_near, g_a, g_b], BF), sums, came)

        owned_both = []

        def later(g_both, sums, came):
            owned_both.append(sum_to_owners(g_both))
            sums = sums + came
            g_down = products([hid_near, hid_a, hid_b], [d_near, *d_far], BF)
            return (g_down, sums, swap(sums, 8))

        grad_mid, g_down, sums, came = split_reduce(
            m_near, (m_a.astype(BF), m_b), beside, later
        )
        g_both = owned_both[0]
        sums = sums + came
        for mask in rest:
            sums = sums + swap(sums, mask)
        high_part = grad_mid.astype(BF)
        low_part = (grad_mid - high_part.astype(F32)).astype(BF)
        grad_mid = mm_t(high_part, to_column) + mm_t(low_part, to_column)

    with jax.named_scope("attention_backward"):
        grad_gain_mid, grad_res = norm_back(grad_mid, hidden_res, inv_ffn, gain_mid)
        grad_res = grad_out + grad_res
        res_low = grad_res.astype(BF)
        g_wo = PlaneSum(mixed_sent, res_low)
        wo_came, came, grad_mixed = tied(
            g_wo.step_0(), swap(sums, high), mm_t(res_low, wo).astype(BF)
        )
        sums = sums + came
        wo_moving = g_wo.step_1(wo_came)
        grad_raw = attention_backward(grad_mixed, query, key, value, cosine, sine)
        *wo_came, grad_raw, sums, came = tied(*wo_moving, grad_raw, sums, swap(sums, 2))
        sums = sums + came
        wo_moving = g_wo.step_2(wo_came)

    with jax.named_scope("input_gradient"):
        input_grad, grad_gain_in = input_gradient(
            grad_raw, gathered, tokens, inv_attn, gain_in[None], grad_res
        )
        gains = jnp.concatenate([grad_gain_in, grad_gain_mid[None]])

    with jax.named_scope("q_k_v_weight_gradients"):
        g_qkv = PlaneSum(normed_sent, grad_raw)
        qkv_came, gains, sums, came, g_both, g_down, *wo_came = tied(
            g_qkv.step_0(), gains, sums, swap(sums, 4), g_both, g_down, *wo_moving
        )
        g_down = sum_to_owners(g_down)
        sums = sums + came
        loss = sums[0, 0] / (sums[1, 0] * width)
        qkv_moving = g_qkv.step_1(qkv_came)
        g_wo = g_wo.step_3(wo_came, rows)
        wo_moving = direct([g_wo], z) if planes == 4 else []

    with jax.named_scope("weight_gradients_to_owners"):
        for mask in (1, 8, high):
            gains = gains + swap(gains, mask)
        *qkv_came, gains = tied(*qkv_moving, gains)
        qkv_moving = g_qkv.step_2(qkv_came)
        qkv_0, qkv_1, gains, g_both, g_down, *wo_came = tied(
            *qkv_moving, gains, g_both, g_down, *wo_moving
        )
        qkv_came = (qkv_0, qkv_1)
        g_wo = owned([g_wo], wo_came, z) if planes == 4 else z_reduce([g_wo])
        g_qkv, g_both = tied(g_qkv.step_3(qkv_came, rows), g_both)
        if planes == 4:
            moving = direct([g_qkv], z)
        gains = gains + swap(gains, 2)
        gains, g_both = tied(gains, g_both)
        g_both = g_both.reshape(4, rows, 2 * units)
        came = [pick(g_both, p ^ r, 0) for r in range(4)]
        gains_came, *moved = tied(swap(gains, 4), *[swap(came[r], r << 1) for r in (1, 2, 3)])
        gains = gains + gains_came
        for mask in rest:
            gains = gains + swap(gains, mask)
        grad_gate, grad_up = spread_columns([came[0]] + moved, p, part)
        g_gains = lax.dynamic_slice_in_dim(gains, position * rows, rows, 1)
        if planes == 4:
            g_qkv = owned([g_qkv], moving, z)
        else:
            g_qkv = z_reduce([g_qkv])
        g_wq = g_qkv[:, :width]
        g_wk = g_qkv[:, width : width + kv_width]
        g_wv = g_qkv[:, width + kv_width :]

    return (
        out_act,
        loss,
        input_grad,
        g_wq,
        g_wk,
        g_wv,
        g_wo,
        grad_gate,
        grad_up,
        g_down.astype(F32),
        g_gains[0],
        g_gains[1],
    )


def solution(mesh):
    wide, flat = P("dp", None), P("dp")
    in_specs = (wide, wide, flat) + (wide,) * 7 + (flat, flat)
    out_specs = (wide, P(), wide) + (wide,) * 7 + (flat, flat)
    return jax.shard_map(body, mesh=mesh, in_specs=in_specs, out_specs=out_specs, check_vma=False)
```

```python
import math

import jax
import jax.numpy as jnp
from jax import lax
from jax.experimental import pallas as pl
from jax.experimental.pallas import tpu as pltpu
from jax.sharding import PartitionSpec as P

HEAD_SIZE = 96
SEQ = 128
EPSILON = 1e-05
ROPE_BASE = 100000.0
MASK_FILL = -1e30
LANES = 128

BF = jnp.bfloat16
F32 = jnp.float32
NO_COST = pl.CostEstimate(flops=1, bytes_accessed=1, transcendentals=0)


def dot(a, b, dims):
    return lax.dot_general(a, b, (dims, ((), ())), preferred_element_type=F32)


def mm(a, b):
    return dot(a, b, ((1,), (0,)))


def mm_t(a, b):
    return dot(a, b, ((1,), (1,)))


def t_mm(a, b):
    return dot(a, b, ((0,), (0,)))


def swap(value, mask):
    n = lax.axis_size("dp")
    return lax.ppermute(value, "dp", [(i, i ^ mask) for i in range(n)])


def column_groups(with_core):
    n = lax.axis_size("dp")
    planes = range(n // 8)
    if with_core:
        return [[8 * z + 2 * p + c for z in planes for c in range(2)] for p in range(4)]
    return [[8 * z + 2 * p + c for z in planes] for p in range(4) for c in range(2)]


def z_reduce(parts):
    total = sum(part.astype(F32) for part in parts)
    return lax.psum_scatter(
        total.astype(BF), "dp", axis_index_groups=column_groups(False), scatter_dimension=0
    ).astype(F32)


def summed(parts, index, axis):
    total = pick(parts[0], index, axis).astype(F32)
    for part in parts[1:]:
        total = total + pick(part, index, axis).astype(F32)
    return total


def owned(parts, came, z):
    own = summed(parts, z, 0)
    for piece in came:
        own = own + piece.astype(F32)
    return own


def direct(parts, z):
    return [swap(summed(parts, z ^ k, 0).astype(BF), 8 * k) for k in (3, 2, 1)]


def along_z(value, pairs):
    return lax.ppermute(
        value, "dp", [(8 * a + i, 8 * b + i) for a, b in pairs for i in range(8)]
    )


def tied(*values):
    return lax.optimization_barrier(values)


def place(out, piece, where):
    return lax.dynamic_update_slice(out, piece, where)


def pick(parts, index, axis):
    return lax.dynamic_index_in_dim(parts, index, axis, keepdims=False)


def column_cuts(w_gate, w_up, p, part):
    rows = w_gate.shape[0]
    gate_cut = w_gate.reshape(rows, -1, 4, part)
    up_cut = w_up.reshape(rows, -1, 4, part)
    cuts = []
    for r in range(4):
        gate = pick(gate_cut, p ^ r, 2).reshape(rows, -1)
        up = pick(up_cut, p ^ r, 2).reshape(rows, -1)
        cuts.append(jnp.concatenate([gate, up], axis=1))
    return cuts


def by_source(came, p):
    out = jnp.zeros((4,) + came[0].shape, BF)
    for r in range(4):
        out = place(out, came[r][None], (p ^ r, 0, 0))
    return out


def along_column(value):
    return lax.all_gather(
        value, "dp", axis_index_groups=column_groups(True), axis=0, tiled=True
    )


def sum_to_owners(partial):
    return lax.psum_scatter(
        partial, "dp", axis_index_groups=column_groups(True), scatter_dimension=0, tiled=True
    )


def gather_weights_plainly(local, w_gate, w_up, w_down, p):
    gathered = lax.all_gather(local, "dp", axis=0, tiled=True)
    cuts = column_cuts(w_gate, w_up, p, 2 * w_down.shape[0])
    came = [cuts[0]] + [swap(cuts[r], r << 1) for r in (1, 2, 3)]
    mine = by_source(came, p)
    wb = along_column(mine.reshape(-1, mine.shape[2]))
    return gathered, wb, along_column(w_down)


def merged(came, w_down, p):
    rows, columns = came[0].shape
    ff_rows, width = w_down.shape
    tall = 4 * rows
    side = width * ff_rows // tall
    rest = width - side
    low = tall - ff_rows

    def kernel(p_ref, *refs):
        wd, out = refs[4:]
        for r in range(4):
            start = pl.multiple_of((p_ref[0] ^ r) * rows, 16)
            out[pl.ds(start, rows), :columns] = refs[r][...]
        out[:ff_rows, columns:] = wd[:, :side]
        for k in range(ff_rows // low):
            at = columns + k * rest
            out[ff_rows:, at : at + rest] = wd[k * low : (k + 1) * low, side:]

    return pl.pallas_call(
        kernel,
        out_shape=jax.ShapeDtypeStruct((tall, columns + side), w_down.dtype),
        in_specs=[pl.BlockSpec(memory_space=pltpu.SMEM)]
        + [pl.BlockSpec(memory_space=pltpu.VMEM)] * 5,
        compiler_params=pltpu.CompilerParams(vmem_limit_bytes=8 * 2**20),
        cost_estimate=NO_COST,
        name="merged",
    )(p[None], *came, w_down)


def w_down_from(whole, ff_rows, columns, width):
    side = whole.shape[1] - columns
    rest = width - side
    tall = width * ff_rows // side
    low = tall - ff_rows
    devices = whole.shape[0] // tall

    def kernel(ref, out, sem):
        copies = []
        for i in range(devices):
            top, to = i * tall, i * ff_rows
            pairs = [
                (
                    ref.at[pl.ds(top, ff_rows), pl.ds(columns, side)],
                    out.at[pl.ds(to, ff_rows), pl.ds(0, side)],
                )
            ]
            for k in range(ff_rows // low):
                pairs.append(
                    (
                        ref.at[pl.ds(top + ff_rows, low), pl.ds(columns + k * rest, rest)],
                        out.at[pl.ds(to + k * low, low), pl.ds(side, rest)],
                    )
                )
            for k, (source, target) in enumerate(pairs):
                copies.append(pltpu.make_async_copy(source, target, sem.at[i, k]))
        for copy in copies:
            copy.start()
        for copy in copies:
            copy.wait()

    return pl.pallas_call(
        kernel,
        out_shape=jax.ShapeDtypeStruct((devices * ff_rows, width), whole.dtype),
        in_specs=[pl.BlockSpec(memory_space=pl.ANY)],
        out_specs=pl.BlockSpec(memory_space=pltpu.VMEM),
        scratch_shapes=[pltpu.SemaphoreType.DMA((devices, 1 + ff_rows // low))],
        compiler_params=pltpu.CompilerParams(vmem_limit_bytes=2 * FFN_VMEM),
        cost_estimate=NO_COST,
        name="w_down_from",
    )(whole)


def unset(shape, dtype):
    return pl.pallas_call(
        lambda out: None,
        out_shape=jax.ShapeDtypeStruct(shape, dtype),
        out_specs=pl.BlockSpec(memory_space=pl.ANY),
        name="unset",
    )()


def packed(pieces):
    widths = [piece.shape[1] for piece in pieces]
    rows = pieces[0].shape[0]

    def kernel(*refs):
        out = refs[-1]
        at = 0
        for ref, size in zip(refs[:-1], widths):
            out[:, at : at + size] = ref[...]
            at += size

    return pl.pallas_call(
        kernel,
        out_shape=jax.ShapeDtypeStruct((rows, sum(widths)), pieces[0].dtype),
        compiler_params=pltpu.CompilerParams(vmem_limit_bytes=8 * 2**20),
        name="packed",
    )(*pieces)


def column_cuts_kernel(w_gate, w_up, p, part):
    rows, ff = w_gate.shape
    planes = ff // (4 * part)
    units = planes * part

    def kernel(p_ref, gate, up, *outs):
        for r, out in enumerate(outs):
            q = p_ref[0] ^ r
            for k in range(planes):
                start = pl.multiple_of((4 * k + q) * part, LANES)
                out[:, k * part : (k + 1) * part] = gate[:, pl.ds(start, part)]
                out[:, units + k * part : units + (k + 1) * part] = up[:, pl.ds(start, part)]

    shape = jax.ShapeDtypeStruct((rows, 2 * units), w_gate.dtype)
    return pl.pallas_call(
        kernel,
        out_shape=[shape] * 4,
        in_specs=[pl.BlockSpec(memory_space=pltpu.SMEM)]
        + [pl.BlockSpec(memory_space=pltpu.VMEM)] * 2,
        compiler_params=pltpu.CompilerParams(vmem_limit_bytes=8 * 2**20),
        name="column_cuts",
    )(p[None], w_gate, w_up)


def gather_weights(local, w_gate, w_up, w_down, place_bits):
    z, y, x, c = place_bits
    p = 2 * y + x
    rows, columns = local.shape
    ff_rows, width = w_down.shape
    end = (z == 0) | (z == 3)
    up_pairs = [(0, 1), (1, 2), (2, 3)]
    down_pairs = [(1, 0), (2, 1), (3, 2)]
    far_pairs = [(0, 2), (3, 1)]
    out_pairs = [(1, 0), (2, 3)]
    z_b = jnp.where(z == 0, 1, z - 1)
    z_c = jnp.where(z < 2, 2, jnp.where(z == 2, 3, 1))
    z_d = jnp.where(z < 2, 3, 0)
    out = unset((4, 2, 2, 2, rows, columns), BF)

    def near_side(up, down):
        return jnp.where(z == 0, down, up)

    def to_pass_on(up, down):
        return jnp.where(z == 1, down, up)

    def put_x(out, piece, z_k, at_y, core):
        return place(out, piece[None, None, :, None], (z_k, at_y, 0, core, 0, 0))

    def put_y(out, piece, z_k, at_x, core):
        return place(out, piece[None, :, None, None], (z_k, 0, at_x, core, 0, 0))

    def in_order(bit, mine, theirs):
        return jnp.stack([jnp.where(bit == 0, mine, theirs), jnp.where(bit == 0, theirs, mine)])

    def put(out, pair, z_a, z_b, at_y, at_x, core):
        out = put_x(out, pair[0], z_a, at_y, core)
        return put_y(out, pair[1], z_b, at_x, core)

    with jax.named_scope("phase_0"):
        cuts = column_cuts_kernel(w_gate, w_up, p, 2 * ff_rows)
        crossing = (swap(cuts[1], 2), swap(cuts[2], 4), swap(cuts[3], 6))
        up, down = tied(along_z(local, up_pairs), along_z(local, down_pairs))
    with jax.named_scope("phase_1"):
        b = near_side(up, down)
        a, b, passing = tied(local, b, to_pass_on(up, down))
        a_x, b_y, far, first = tied(
            swap(a, 2), swap(b, 4), along_z(a, far_pairs), along_z(passing, out_pairs)
        )
    with jax.named_scope("phase_2"):
        a2, b2, far = tied(in_order(x, a, a_x), in_order(y, b, b_y), far)
        near_1 = jnp.stack([a2, b2])
        ffn = merged((cuts[0], *tied(*crossing)), w_down, p)
        a_far, b_far, second, core_1 = tied(
            swap(a2, 4), swap(b2, 2), along_z(far, out_pairs), swap(near_1, 1)
        )
        out = put(out, near_1, z, z_b, y, x, c)
    with jax.named_scope("ffn_weights"):
        ffn = along_column(tied(ffn, second)[0])
    with jax.named_scope("phase_3"):
        a, b = jnp.where(end, first, down), jnp.where(end, second, far)
        a, b, far_1 = tied(a, b, jnp.stack([a_far, b_far]))
        a_x, b_y, core_2 = tied(swap(a, 2), swap(b, 4), swap(far_1, 1))
        out = put(out, core_1, z, z_b, y, x, 1 - c)
        out = put(out, far_1, z, z_b, 1 - y, 1 - x, c)
    with jax.named_scope("phase_4"):
        a2, b2 = tied(in_order(x, a, a_x), in_order(y, b, b_y))
        near_2 = jnp.stack([a2, b2])
        a_far, b_far, core_3 = tied(swap(a2, 4), swap(b2, 2), swap(near_2, 1))
        out = put(out, core_2, z, z_b, 1 - y, 1 - x, 1 - c)
        out = put(out, near_2, z_c, z_d, y, x, c)
    with jax.named_scope("phase_5"):
        far_2 = jnp.stack([a_far, b_far])
        core_4 = swap(far_2, 1)
        out = put(out, core_3, z_c, z_d, y, x, 1 - c)
        out = put(out, far_2, z_c, z_d, 1 - y, 1 - x, c)
        out = put(out, core_4, z_c, z_d, 1 - y, 1 - x, 1 - c)
        gathered = out.reshape(32 * rows, columns)
    return gathered, ffn


class PlaneSum:
    def __init__(self, left, grads):
        self.left, self.grads = left, grads
        self.own = left.shape[1] // 2
        self.first = self.own // 2
        self.tall = self.first // 4

    def step_0(self):
        return swap(t_mm(self.left[:, self.own :], self.grads).astype(BF), 1)

    def step_1(self, came):
        first, both = self.first, 2 * self.tall
        sent = t_mm(self.left[:, :first], self.grads) + came[:first].astype(F32)
        sent = sent.astype(BF)
        self.rest = t_mm(self.left[:, first : self.own], self.grads) + came[first:].astype(F32)
        return (swap(sent[:both], 4), swap(sent[both:], 2))

    def step_2(self, came):
        self.came, tall = came, self.tall
        a = self.rest[:tall] + came[0][tall:].astype(F32)
        b = self.rest[tall : 2 * tall] + came[1][tall:].astype(F32)
        return (swap(a.astype(BF), 2), swap(b.astype(BF), 4))

    def step_3(self, came, rows):
        tall = self.tall
        sums = []
        for i in (0, 1):
            own = self.rest[(2 + i) * tall : (3 + i) * tall]
            own = own + self.came[i][:tall].astype(F32) + came[i].astype(F32)
            sums.append(own.reshape(tall // rows, rows, -1))
        return jnp.concatenate(sums)


def selection(source):
    return (jnp.arange(source.shape[0])[:, None] == source[None, :]).astype(BF)


def column_order(count, rows):
    place_of, row = jnp.arange(count) // rows, jnp.arange(count) % rows
    z, core, y, x = place_of // 8, place_of // 4 % 2, place_of // 2 % 2, place_of % 2
    return selection((8 * z + 4 * y + 2 * x + core) * rows + row)


def sending_order(count, rows, place_bits):
    z, y, x, c = place_bits
    at = jnp.arange(count)
    group, within = at // (count // 16) % 8, at % (count // 16)
    upper = jnp.isin(group, jnp.array([2, 3, 5, 7]))
    x_differs = jnp.isin(group, jnp.array([1, 2, 3, 4]))
    y_differs = jnp.isin(group, jnp.array([0, 1, 3, 5]))
    core = c ^ (at // (count // 2))
    planes = count // rows // 8
    z_of = upper * (planes // 2) + within // rows
    chip = 4 * z_of + 2 * (y ^ y_differs.astype(jnp.int32)) + (x ^ x_differs.astype(jnp.int32))
    return selection((2 * chip + core) * rows + within % rows)


def split_gather(rows, beside=(), then=lambda pieces, *values: values):
    half = rows.shape[0] // 2
    a, b = rows[:half], rows[half:]
    a_x, b_y, *beside = tied(swap(a, 2), swap(b, 4), *beside)
    a2, b2 = tied(jnp.concatenate([a, a_x]), jnp.concatenate([b, b_y]))
    a_far, b_far, *beside = tied(swap(a2, 4), swap(b2, 2), *then((a2, b2), *beside))
    return ((a_far, b_far), *beside)


def split_reduce(near, far, beside=(), later=lambda *values: values):
    two = far[0].shape[0]
    one = two // 2
    came_a, came_b, *beside = tied(swap(far[0], 4), swap(far[1], 2), *beside)
    send_a = near[one:two] + came_a[one:].astype(F32)
    send_b = near[two + one :] + came_b[one:].astype(F32)
    own_a, own_b, *beside = tied(
        swap(send_a.astype(BF), 2), swap(send_b.astype(BF), 4), *later(*beside)
    )
    own_a = near[:one] + came_a[:one].astype(F32) + own_a.astype(F32)
    own_b = near[two : two + one] + came_b[:one].astype(F32) + own_b.astype(F32)
    own = jnp.concatenate([own_a, own_b])
    return (own, *beside)


def spread_columns(came, p, part):
    units = came[0].shape[1] // 2
    natural = []
    for q in range(4):
        piece = came[3]
        for r in (0, 1, 2):
            piece = jnp.where(p == (q ^ r), came[r], piece)
        natural.append(piece.astype(F32))
    return tuple(
        jnp.concatenate(
            [
                natural[q][:, start + k * part : start + (k + 1) * part]
                for k in range(units // part)
                for q in range(4)
            ],
            axis=1,
        )
        for start in (0, units)
    )


def rotation_tables(length, width):
    half_width = width // 2
    position = jnp.arange(length, dtype=F32)[:, None]
    freq_rate = ROPE_BASE ** (-2.0 * jnp.arange(half_width, dtype=F32) / width)
    angle_table = position * freq_rate[None, :]
    return (jnp.cos(angle_table)[:, None, :], jnp.sin(angle_table)[:, None, :])


HEADS_AT_ONCE = 8


def rotation_lanes():
    cosine, sine = rotation_tables(SEQ, HEAD_SIZE)
    lanes = HEADS_AT_ONCE * 2
    return (jnp.tile(cosine[:, 0], (1, lanes)), jnp.tile(sine[:, 0], (1, lanes)))


def turned(value, cosine, sine, back):
    size = value.shape[1]
    half = HEAD_SIZE // 2
    lane = lax.broadcasted_iota(jnp.int32, value.shape, 1)
    right = pltpu.roll(value, size - half, 1)
    left = pltpu.roll(value, half, 1)
    first = lane % HEAD_SIZE < half
    other = jnp.where(first, right, -left) if back else jnp.where(first, -right, left)
    return value * cosine + other * sine


def lanes_of(shape):
    return lax.broadcasted_iota(jnp.int32, shape, 1)


def head_of(value, i):
    start = i * HEAD_SIZE
    window = start // LANES * LANES
    offset = start - window
    size = LANES if offset + HEAD_SIZE <= LANES else 2 * LANES
    head = value[:, window : window + size]
    if offset:
        head = pltpu.roll(head, size - offset, 1)
    head = head[:, :LANES]
    return jnp.where(lanes_of(head.shape) < HEAD_SIZE, head, 0.0)


def side_by_side(heads):
    lane = lanes_of(heads[0].shape)
    second = pltpu.roll(heads[1], 96, 1)
    third = pltpu.roll(heads[2], 64, 1)
    fourth = pltpu.roll(heads[3], 32, 1)
    return jnp.concatenate(
        [
            jnp.where(lane < 96, heads[0], second),
            jnp.where(lane < 64, second, third),
            jnp.where(lane < 32, third, fourth),
        ],
        axis=1,
    )


def row_softmax(query, key):
    scores = lax.dot_general(
        query, key, (((1,), (1,)), ((), ())), preferred_element_type=F32
    ) * (1.0 / math.sqrt(HEAD_SIZE))
    row = lax.broadcasted_iota(jnp.int32, scores.shape, 0)
    column = lax.broadcasted_iota(jnp.int32, scores.shape, 1)
    scores = jnp.where(row >= column, scores, MASK_FILL)
    weights = jnp.exp(scores - jnp.max(scores, axis=1, keepdims=True))
    return weights * (1.0 / jnp.sum(weights, axis=1, keepdims=True))


def attention_blocks(width, kv_width):
    q_size = HEADS_AT_ONCE * HEAD_SIZE
    kv_size = q_size * kv_width // width
    return q_size, kv_size


def attention_forward(raw, cosine, sine, width, kv_width):
    count = raw.shape[0]
    q_size, kv_size = attention_blocks(width, kv_width)
    steps = width // q_size
    per_kv = width // kv_width

    def kernel(q_raw, k_raw, v_raw, cosine, sine, q_out, k_out, v_out, mixed):
        q = turned(q_raw[...], cosine[...], sine[...], False).astype(BF)
        k = turned(k_raw[...], cosine[:, :kv_size], sine[:, :kv_size], False).astype(BF)
        v = v_raw[...].astype(BF)
        q_out[...] = q
        k_out[...] = k
        v_out[...] = v
        q, k, v = q.astype(F32), k.astype(F32), v.astype(F32)
        for group in range(HEADS_AT_ONCE // 4):
            outs = []
            for i in range(4 * group, 4 * group + 4):
                if i % per_kv == 0:
                    key = head_of(k, i // per_kv).astype(BF)
                    value = head_of(v, i // per_kv).astype(BF)
                probs = row_softmax(head_of(q, i).astype(BF), key)
                outs.append(jnp.dot(probs.astype(BF), value, preferred_element_type=F32))
            mixed[:, 384 * group : 384 * group + 384] = side_by_side(outs).astype(BF)

    def block(size, at):
        return pl.BlockSpec((SEQ, size), lambda s, j: (s, at // size + j))

    table = pl.BlockSpec((SEQ, q_size), lambda s, j: (0, 0))
    return pl.pallas_call(
        kernel,
        grid=(count // SEQ, steps),
        out_shape=[
            jax.ShapeDtypeStruct((count, width), BF),
            jax.ShapeDtypeStruct((count, kv_width), BF),
            jax.ShapeDtypeStruct((count, kv_width), BF),
            jax.ShapeDtypeStruct((count, width), BF),
        ],
        in_specs=[
            block(q_size, 0),
            block(kv_size, width),
            block(kv_size, width + kv_width),
            table,
            table,
        ],
        out_specs=[block(q_size, 0), block(kv_size, 0), block(kv_size, 0), block(q_size, 0)],
        compiler_params=pltpu.CompilerParams(vmem_limit_bytes=16 * 2**20),
        cost_estimate=NO_COST,
        name="attention_forward",
    )(raw, raw, raw, cosine, sine)


def attention_backward(grad_mixed, q, k, v, cosine, sine):
    count, width = q.shape
    kv_width = k.shape[1]
    q_size, kv_size = attention_blocks(width, kv_width)
    steps = width // q_size
    per_kv = width // kv_width
    scale = 1.0 / math.sqrt(HEAD_SIZE)
    rows_rows = (((0,), (0,)), ((), ()))
    lanes_lanes = (((1,), (1,)), ((), ()))

    def kernel(d_ref, q_ref, k_ref, v_ref, cosine, sine, out):
        d, q = d_ref[...].astype(F32), q_ref[...].astype(F32)
        k, v = k_ref[...].astype(F32), v_ref[...].astype(F32)
        d_q, d_k, d_v = [], [], []
        for i in range(HEADS_AT_ONCE):
            if i % per_kv == 0:
                key = head_of(k, i // per_kv).astype(BF)
                value = head_of(v, i // per_kv).astype(BF)
            query, upstream = head_of(q, i).astype(BF), head_of(d, i).astype(BF)
            probs = row_softmax(query, key)
            d_probs = lax.dot_general(upstream, value, lanes_lanes, preferred_element_type=F32)
            d_scores = probs * (d_probs - jnp.sum(probs * d_probs, axis=1, keepdims=True))
            d_scores = d_scores.astype(BF)
            d_q.append(jnp.dot(d_scores, key, preferred_element_type=F32) * scale)
            part_k = lax.dot_general(d_scores, query, rows_rows, preferred_element_type=F32)
            part_v = lax.dot_general(
                probs.astype(BF), upstream, rows_rows, preferred_element_type=F32
            )
            if i % per_kv == 0:
                d_k.append(part_k)
                d_v.append(part_v)
            else:
                d_k[-1] += part_k
                d_v[-1] += part_v
        d_q = jnp.concatenate([side_by_side(d_q[g : g + 4]) for g in range(0, len(d_q), 4)], axis=1)
        d_q = turned(d_q, cosine[...], sine[...], True).astype(BF)
        d_k = side_by_side([part * scale for part in d_k])
        d_k = turned(d_k, cosine[:, :kv_size], sine[:, :kv_size], True).astype(BF)
        j = pl.program_id(1)
        out[:, pl.ds(pl.multiple_of(j * q_size, LANES), q_size)] = d_q
        at = pl.multiple_of(width + j * kv_size, LANES)
        out[:, pl.ds(at, kv_size)] = d_k
        at = pl.multiple_of(width + kv_width + j * kv_size, LANES)
        out[:, pl.ds(at, kv_size)] = side_by_side(d_v).astype(BF)

    def block(size):
        return pl.BlockSpec((SEQ, size), lambda s, j: (s, j))

    table = pl.BlockSpec((SEQ, q_size), lambda s, j: (0, 0))
    return pl.pallas_call(
        kernel,
        grid=(count // SEQ, steps),
        out_shape=jax.ShapeDtypeStruct((count, width + 2 * kv_width), BF),
        in_specs=[block(q_size), block(q_size), block(kv_size), block(kv_size), table, table],
        out_specs=pl.BlockSpec((SEQ, width + 2 * kv_width), lambda s, j: (s, 0)),
        compiler_params=pltpu.CompilerParams(vmem_limit_bytes=16 * 2**20),
        cost_estimate=NO_COST,
        name="attention_backward",
    )(grad_mixed, q, k, v, cosine, sine)


def norm_rows(field_in, gain_vec):
    inv_scale = lax.rsqrt(jnp.mean(field_in * field_in, axis=-1, keepdims=True) + EPSILON)
    return (field_in * inv_scale * gain_vec, inv_scale)


def norm_back(upstream, field_in, inv_scale, gain_vec):
    gain_grad = jnp.sum(upstream * field_in * inv_scale, axis=0)
    scaled_up = upstream * gain_vec
    field_grad = inv_scale * scaled_up - field_in * inv_scale**3 * jnp.mean(
        scaled_up * field_in, axis=-1, keepdims=True
    )
    return (gain_grad, field_grad)


def ffn_forward(rows, w_both, w_down):
    units = w_down.shape[0]
    pre = mm(rows, w_both[:, : 2 * units])
    hidden = (jax.nn.silu(pre[:, :units]) * pre[:, units:]).astype(BF)
    return (mm(hidden, w_down), pre, hidden)


def ffn_backward(grad_low, pre, w_both, w_down):
    grad_hidden = mm_t(grad_low, w_down)
    units = w_down.shape[0]
    gate_pre, up_pre = pre[:, :units], pre[:, units:]
    gate_sigmoid = jax.nn.sigmoid(gate_pre)
    grad_gate = grad_hidden * up_pre * gate_sigmoid * (1.0 + gate_pre * (1.0 - gate_sigmoid))
    grad_up = grad_hidden * gate_pre * gate_sigmoid
    grads = jnp.concatenate([grad_gate.astype(BF), grad_up.astype(BF)], axis=1)
    return (mm_t(grads, w_both[:, : 2 * units]), grads)


FFN_TILE = 256
FFN_VMEM = 24 * 2**20


def tiles_of(w_both, w_down, units):
    width = w_down.shape[1]
    steps = units // FFN_TILE
    return [
        pl.BlockSpec((width, FFN_TILE), lambda j: (0, j)),
        pl.BlockSpec((width, FFN_TILE), lambda j: (0, j + steps)),
        pl.BlockSpec((FFN_TILE, width), lambda j: (j, 0)),
    ]


def whole(array):
    return pl.BlockSpec(array.shape, lambda j: (0,) * array.ndim)


def sigmoid(value):
    return 1.0 / (1.0 + jnp.exp(-value))


def ffn_forward_beside(pieces, w_both, w_down):
    units, width = w_down.shape
    steps = units // FFN_TILE
    sizes = [piece.shape[0] for piece in pieces]
    count = sum(sizes)
    kinds = ((width, BF), (units, BF), (units, F32), (units, F32))
    kept_specs = [
        pl.BlockSpec((count, width), lambda j: (0, 0)),
        pl.BlockSpec((count, FFN_TILE), lambda j: (0, j)),
        pl.BlockSpec((count, FFN_TILE), lambda j: (0, j)),
        pl.BlockSpec((count, FFN_TILE), lambda j: (0, j)),
    ]
    first = len(pieces) + 3

    def kernel(*refs):
        w_gate, w_up, w_low = refs[len(pieces) : first]
        y, rows, hidden, gate, up, total = refs[-6:]
        j = pl.program_id(0)

        @pl.when(j == 0)
        def _():
            at = 0
            for ref, size in zip(refs, sizes):
                rows[at : at + size] = ref[...]
                at += size

        gate_pre = jnp.dot(rows[...], w_gate[...], preferred_element_type=F32)
        up_pre = jnp.dot(rows[...], w_up[...], preferred_element_type=F32)
        gate[...] = gate_pre
        up[...] = up_pre
        hid = (gate_pre * sigmoid(gate_pre) * up_pre).astype(BF)
        hidden[...] = hid
        part = jnp.dot(hid, w_low[...], preferred_element_type=F32)

        @pl.when(j == 0)
        def _():
            total[...] = part

        @pl.when(j > 0)
        def _():
            total[...] += part

        @pl.when(j == steps - 1)
        def _():
            y[...] = total[...].astype(y.dtype)

    y_shape = jax.ShapeDtypeStruct((count, width), F32)
    outs = pl.pallas_call(
        kernel,
        grid=(steps,),
        out_shape=[y_shape] + [jax.ShapeDtypeStruct((count, w), t) for w, t in kinds],
        in_specs=[whole(piece) for piece in pieces]
        + tiles_of(w_both, w_down, units),
        out_specs=[whole(y_shape)] + kept_specs,
        scratch_shapes=[pltpu.VMEM((count, width), F32)],
        compiler_params=pltpu.CompilerParams(vmem_limit_bytes=FFN_VMEM),
        cost_estimate=NO_COST,
        name="ffn_forward_beside",
    )(*pieces, w_both, w_both, w_down)
    return tuple(outs)


def ffn_backward_beside(pieces, gate_pre, up_pre, w_both, w_down):
    units, width = w_down.shape
    steps = units // FFN_TILE
    sizes = [piece.shape[0] for piece in pieces]
    count = sum(sizes)
    kinds = ((width, BF), (2 * units, BF))
    kept_specs = [
        pl.BlockSpec((count, width), lambda j: (0, 0)),
        pl.BlockSpec((count, 2 * units), lambda j: (0, 0)),
    ]
    pre_spec = pl.BlockSpec((count, FFN_TILE), lambda j: (0, j))
    first = len(pieces) + 5
    dims = (((1,), (1,)), ((), ()))

    def kernel(*refs):
        gate, up, w_gate, w_up, w_low = refs[len(pieces) : first]
        m, rows, grads, total = refs[-4:]
        j = pl.program_id(0)

        @pl.when(j == 0)
        def _():
            at = 0
            for ref, size in zip(refs, sizes):
                rows[at : at + size] = ref[...]
                at += size

        grad_hidden = lax.dot_general(rows[...], w_low[...], dims, preferred_element_type=F32)
        g = gate[...]
        s = sigmoid(g)
        grad_gate = (grad_hidden * up[...] * s * (1.0 + g * (1.0 - s))).astype(BF)
        grad_up = (grad_hidden * g * s).astype(BF)
        start = pl.multiple_of(j * FFN_TILE, LANES)
        grads[:, pl.ds(start, FFN_TILE)] = grad_gate
        grads[:, pl.ds(start + units, FFN_TILE)] = grad_up
        part = lax.dot_general(grad_gate, w_gate[...], dims, preferred_element_type=F32)
        part += lax.dot_general(grad_up, w_up[...], dims, preferred_element_type=F32)

        @pl.when(j == 0)
        def _():
            total[...] = part

        @pl.when(j > 0)
        def _():
            total[...] += part

        @pl.when(j == steps - 1)
        def _():
            m[...] = total[...].astype(m.dtype)

    m_shape = jax.ShapeDtypeStruct((count, width), F32)
    outs = pl.pallas_call(
        kernel,
        grid=(steps,),
        out_shape=[m_shape] + [jax.ShapeDtypeStruct((count, w), t) for w, t in kinds],
        in_specs=[whole(piece) for piece in pieces]
        + [pre_spec] * 2
        + tiles_of(w_both, w_down, units),
        out_specs=[whole(m_shape)] + kept_specs,
        scratch_shapes=[pltpu.VMEM((count, width), F32)],
        compiler_params=pltpu.CompilerParams(vmem_limit_bytes=FFN_VMEM),
        cost_estimate=NO_COST,
        name="ffn_backward_beside",
    )(*pieces, gate_pre, up_pre, w_both, w_both, w_down)
    return tuple(outs)


def input_gradient(grad_raw, weights, tokens, inv_scale, gain, grad_res):
    count, wide = grad_raw.shape
    width = tokens.shape[1]
    tile = 2 * FFN_TILE
    steps = wide // tile

    def kernel(grads, w, tokens, inv_scale, gain, grad_res, out, gain_grad, total):
        j = pl.program_id(0)
        part = lax.dot_general(
            grads[...], w[...], (((1,), (1,)), ((), ())), preferred_element_type=F32
        )

        @pl.when(j == 0)
        def _():
            total[...] = part

        @pl.when(j > 0)
        def _():
            total[...] += part

        @pl.when(j == steps - 1)
        def _():
            up, field, inv = total[...], tokens[...].astype(F32), inv_scale[...]
            gain_grad[...] = jnp.sum(up * field * inv, axis=0, keepdims=True)
            scaled = up * gain[...]
            mean = jnp.mean(scaled * field, axis=1, keepdims=True)
            grad = inv * scaled - field * (inv * inv * inv) * mean
            out[...] = (grad_res[...] + grad).astype(BF)

    return pl.pallas_call(
        kernel,
        grid=(steps,),
        out_shape=[
            jax.ShapeDtypeStruct((count, width), BF),
            jax.ShapeDtypeStruct((1, width), F32),
        ],
        in_specs=[
            pl.BlockSpec((count, tile), lambda j: (0, j)),
            pl.BlockSpec((width, tile), lambda j: (0, j)),
            whole(tokens),
            whole(inv_scale),
            whole(gain),
            whole(grad_res),
        ],
        out_specs=[
            pl.BlockSpec((count, width), lambda j: (0, 0)),
            pl.BlockSpec((1, width), lambda j: (0, 0)),
        ],
        scratch_shapes=[pltpu.VMEM((count, width), F32)],
        compiler_params=pltpu.CompilerParams(vmem_limit_bytes=2 * FFN_VMEM),
        cost_estimate=NO_COST,
        name="input_gradient",
    )(grad_raw, weights, tokens, inv_scale, gain, grad_res)


def products(lefts, rights, dtype):
    rows, columns = lefts[0].shape[1], rights[0].shape[1]
    tile = columns // 4
    count = len(lefts)

    def kernel(*refs):
        total = None
        for a, b in zip(refs[:count], refs[count : 2 * count]):
            part = lax.dot_general(
                a[...], b[...], (((0,), (0,)), ((), ())), preferred_element_type=F32
            )
            total = part if total is None else total + part
        refs[-1][...] = total.astype(dtype)

    return pl.pallas_call(
        kernel,
        grid=(columns // tile,),
        out_shape=jax.ShapeDtypeStruct((rows, columns), dtype),
        in_specs=[whole(left) for left in lefts]
        + [pl.BlockSpec((right.shape[0], tile), lambda j: (0, j)) for right in rights],
        out_specs=pl.BlockSpec((rows, tile), lambda j: (0, j)),
        compiler_params=pltpu.CompilerParams(vmem_limit_bytes=FFN_VMEM),
        cost_estimate=NO_COST,
        name="products",
    )(*lefts, *rights)


def body(
    tokens,
    teacher,
    valid_mask,
    w_query,
    key_weight_matrix,
    value_weight_matrix,
    w_output,
    w_gate,
    w_up,
    w_down,
    attn_gain,
    ffn_gain,
):
    n = lax.axis_size("dp")
    planes = n // 8
    position = lax.axis_index("dp")
    c, x, y, z = position % 2, position // 2 % 2, position // 4 % 2, position // 8
    bits = (z, y, x, c)
    p = position // 2 % 4
    rows = w_query.shape[0]
    width = w_query.shape[1]
    kv_width = key_weight_matrix.shape[1]
    ff_rows = w_down.shape[0]
    ff = w_gate.shape[1]
    count = tokens.shape[0]
    cosine, sine = rotation_lanes()
    to_column, to_senders = tied(column_order(width, rows), sending_order(width, rows, bits))

    part = 2 * ff_rows
    units = planes * part
    gains = jnp.stack([attn_gain, ffn_gain], axis=1)
    gains = jnp.pad(gains, ((0, 0), (0, LANES - 2)))
    local = packed([w_query, key_weight_matrix, value_weight_matrix, w_output, gains])
    if planes == 4:
        gathered, wb = gather_weights(local, w_gate, w_up, w_down, bits)
        wd = w_down_from(wb, ff_rows, 2 * units, width)
    else:
        gathered, wb, wd = gather_weights_plainly(local, w_gate, w_up, w_down, p)

    with jax.named_scope("attention_forward"):
        wide = width + 2 * kv_width
        wqkv = gathered[:, :wide]
        wo = gathered[:, wide : wide + width]
        gain_in = gathered[:, wide + width].astype(F32)
        gain_mid = gathered[:, wide + width + 1].astype(F32)
        inputs_f = tokens.astype(F32)
        normed, inv_attn = norm_rows(inputs_f, gain_in)
        normed_in = tied(normed.astype(BF))[0]
        raw = mm(normed_in, wqkv)
        query, key, value, mixed = attention_forward(raw, cosine, sine, width, kv_width)
        hidden_res = inputs_f + mm(mixed, wo)
        normed_two, inv_ffn = norm_rows(hidden_res, gain_mid)
        normed_mid = normed_two.astype(BF)

    with jax.named_scope("ffn_forward"):
        far, y_near, *kept = split_gather(
            mm(normed_mid, to_column).astype(BF),
            (),
            lambda pieces: ffn_forward_beside(pieces, wb, wd),
        )
        near, hid_near, gate_near, up_near = kept
        y_a, pre_a, hid_a = ffn_forward(far[0], wb, wd)
        y_b, pre_b, hid_b = ffn_forward(far[1], wb, wd)
        y_a, y_b = y_a.astype(BF), y_b.astype(BF)
        y_b, mixed, normed_in = tied(y_b, mixed, normed_in)
        beside = (mm(mixed, to_senders).astype(BF), mm(normed_in, to_senders).astype(BF))
        result, mixed_sent, normed_sent = split_reduce(y_near, (y_a, y_b), beside)
        result = hidden_res + result
        out_act = result.astype(BF)

    with jax.named_scope("loss"):
        mask_f = valid_mask.astype(F32)
        grad_out = (result - teacher.astype(F32)) * mask_f[:, None]

    high = n // 2
    rest = [1 << k for k in range(4, n.bit_length() - 2)]

    with jax.named_scope("ffn_backward"):
        def near_backward(pieces, grads):
            sums = jnp.stack([jnp.sum(grads * grads), jnp.sum(mask_f)])
            return (
                jnp.broadcast_to(sums[:, None], (2, LANES)),
                *ffn_backward_beside(pieces, gate_near, up_near, wb, wd),
            )

        d_far, sums, m_near, d_near, g_near = split_gather(
            grad_out.astype(BF), (grad_out,), near_backward
        )
        m_a, g_a = ffn_backward(d_far[0], pre_a, wb, wd)
        m_b, g_b = ffn_backward(d_far[1], pre_b, wb, wd)
        m_b, m_near, sums = tied(m_b.astype(BF), m_near, sums)
        came = swap(sums, 1)
        beside = (products([near, *far], [g_near, g_a, g_b], BF), sums, came)

        owned_both = []

        def later(g_both, sums, came):
            owned_both.append(sum_to_owners(g_both))
            sums = sums + came
            g_down = products([hid_near, hid_a, hid_b], [d_near, *d_far], BF)
            return (g_down, sums, swap(sums, 8))

        grad_mid, g_down, sums, came = split_reduce(
            m_near, (m_a.astype(BF), m_b), beside, later
        )
        g_both = owned_both[0]
        sums = sums + came
        for mask in rest:
            sums = sums + swap(sums, mask)
        high_part = grad_mid.astype(BF)
        low_part = (grad_mid - high_part.astype(F32)).astype(BF)
        grad_mid = mm_t(high_part, to_column) + mm_t(low_part, to_column)

    with jax.named_scope("attention_backward"):
        grad_gain_mid, grad_res = norm_back(grad_mid, hidden_res, inv_ffn, gain_mid)
        grad_res = grad_out + grad_res
        res_low = grad_res.astype(BF)
        g_wo = PlaneSum(mixed_sent, res_low)
        wo_came, came, grad_mixed = tied(
            g_wo.step_0(), swap(sums, high), mm_t(res_low, wo).astype(BF)
        )
        sums = sums + came
        wo_moving = g_wo.step_1(wo_came)
        grad_raw = attention_backward(grad_mixed, query, key, value, cosine, sine)
        *wo_came, grad_raw, sums, came = tied(*wo_moving, grad_raw, sums, swap(sums, 2))
        sums = sums + came
        wo_moving = g_wo.step_2(wo_came)

    with jax.named_scope("input_gradient"):
        input_grad, grad_gain_in = input_gradient(
            grad_raw, gathered, tokens, inv_attn, gain_in[None], grad_res
        )
        gains = jnp.concatenate([grad_gain_in, grad_gain_mid[None]])

    with jax.named_scope("q_k_v_weight_gradients"):
        g_qkv = PlaneSum(normed_sent, grad_raw)
        qkv_came, gains, sums, came, g_both, g_down, *wo_came = tied(
            g_qkv.step_0(), gains, sums, swap(sums, 4), g_both, g_down, *wo_moving
        )
        g_down = sum_to_owners(g_down)
        sums = sums + came
        loss = sums[0, 0] / (sums[1, 0] * width)
        qkv_moving = g_qkv.step_1(qkv_came)
        g_wo = g_wo.step_3(wo_came, rows)
        wo_moving = direct([g_wo], z) if planes == 4 else []

    with jax.named_scope("weight_gradients_to_owners"):
        for mask in (1, 8, high):
            gains = gains + swap(gains, mask)
        *qkv_came, gains = tied(*qkv_moving, gains)
        qkv_moving = g_qkv.step_2(qkv_came)
        qkv_0, qkv_1, gains, g_both, g_down, *wo_came = tied(
            *qkv_moving, gains, g_both, g_down, *wo_moving
        )
        qkv_came = (qkv_0, qkv_1)
        g_wo = owned([g_wo], wo_came, z) if planes == 4 else z_reduce([g_wo])
        g_qkv, g_both = tied(g_qkv.step_3(qkv_came, rows), g_both)
        if planes == 4:
            moving = direct([g_qkv], z)
        gains = gains + swap(gains, 2)
        gains, g_both = tied(gains, g_both)
        g_both = g_both.reshape(4, rows, 2 * units)
        came = [pick(g_both, p ^ r, 0) for r in range(4)]
        gains_came, *moved = tied(swap(gains, 4), *[swap(came[r], r << 1) for r in (1, 2, 3)])
        gains = gains + gains_came
        for mask in rest:
            gains = gains + swap(gains, mask)
        grad_gate, grad_up = spread_columns([came[0]] + moved, p, part)
        g_gains = lax.dynamic_slice_in_dim(gains, position * rows, rows, 1)
        if planes == 4:
            g_qkv = owned([g_qkv], moving, z)
        else:
            g_qkv = z_reduce([g_qkv])
        g_wq = g_qkv[:, :width]
        g_wk = g_qkv[:, width : width + kv_width]
        g_wv = g_qkv[:, width + kv_width :]

    return (
        out_act,
        loss,
        input_grad,
        g_wq,
        g_wk,
        g_wv,
        g_wo,
        grad_gate,
        grad_up,
        g_down.astype(F32),
        g_gains[0],
        g_gains[1],
    )


def solution(mesh):
    wide, flat = P("dp", None), P("dp")
    in_specs = (wide, wide, flat) + (wide,) * 7 + (flat, flat)
    out_specs = (wide, P(), wide) + (wide,) * 7 + (flat, flat)
    return jax.shard_map(body, mesh=mesh, in_specs=in_specs, out_specs=out_specs, check_vma=False)
```

```python
import math

import jax
import jax.numpy as jnp
from jax import lax
from jax.experimental import pallas as pl
from jax.experimental.pallas import tpu as pltpu
from jax.sharding import PartitionSpec as P

HEAD_SIZE = 96
SEQ = 128
EPSILON = 1e-05
ROPE_BASE = 100000.0
MASK_FILL = -1e30
LANES = 128

BF = jnp.bfloat16
F32 = jnp.float32
NO_COST = pl.CostEstimate(flops=1, bytes_accessed=1, transcendentals=0)


def dot(a, b, dims):
    return lax.dot_general(a, b, (dims, ((), ())), preferred_element_type=F32)


def mm(a, b):
    return dot(a, b, ((1,), (0,)))


def mm_t(a, b):
    return dot(a, b, ((1,), (1,)))


def t_mm(a, b):
    return dot(a, b, ((0,), (0,)))


def swap(value, mask):
    n = lax.axis_size("dp")
    return lax.ppermute(value, "dp", [(i, i ^ mask) for i in range(n)])


def column_groups(with_core):
    n = lax.axis_size("dp")
    planes = range(n // 8)
    if with_core:
        return [[8 * z + 2 * p + c for z in planes for c in range(2)] for p in range(4)]
    return [[8 * z + 2 * p + c for z in planes] for p in range(4) for c in range(2)]


def z_reduce(parts):
    total = sum(part.astype(F32) for part in parts)
    return lax.psum_scatter(
        total.astype(BF), "dp", axis_index_groups=column_groups(False), scatter_dimension=0
    ).astype(F32)


def summed(parts, index, axis):
    total = pick(parts[0], index, axis).astype(F32)
    for part in parts[1:]:
        total = total + pick(part, index, axis).astype(F32)
    return total


def owned(parts, came, z):
    own = summed(parts, z, 0)
    for piece in came:
        own = own + piece.astype(F32)
    return own


def direct(parts, z):
    return [swap(summed(parts, z ^ k, 0).astype(BF), 8 * k) for k in (3, 2, 1)]


def along_z(value, pairs):
    return lax.ppermute(
        value, "dp", [(8 * a + i, 8 * b + i) for a, b in pairs for i in range(8)]
    )


def tied(*values):
    return lax.optimization_barrier(values)


def place(out, piece, where):
    return lax.dynamic_update_slice(out, piece, where)


def pick(parts, index, axis):
    return lax.dynamic_index_in_dim(parts, index, axis, keepdims=False)


def column_cuts(w_gate, w_up, p, part):
    rows = w_gate.shape[0]
    gate_cut = w_gate.reshape(rows, -1, 4, part)
    up_cut = w_up.reshape(rows, -1, 4, part)
    cuts = []
    for r in range(4):
        gate = pick(gate_cut, p ^ r, 2).reshape(rows, -1)
        up = pick(up_cut, p ^ r, 2).reshape(rows, -1)
        cuts.append(jnp.concatenate([gate, up], axis=1))
    return cuts


def by_source(came, p):
    out = jnp.zeros((4,) + came[0].shape, BF)
    for r in range(4):
        out = place(out, came[r][None], (p ^ r, 0, 0))
    return out


def along_column(value):
    return lax.all_gather(
        value, "dp", axis_index_groups=column_groups(True), axis=0, tiled=True
    )


def sum_to_owners(partial):
    return lax.psum_scatter(
        partial, "dp", axis_index_groups=column_groups(True), scatter_dimension=0, tiled=True
    )


def gather_weights_plainly(local, w_gate, w_up, w_down, p):
    gathered = lax.all_gather(local, "dp", axis=0, tiled=True)
    cuts = column_cuts(w_gate, w_up, p, 2 * w_down.shape[0])
    came = [cuts[0]] + [swap(cuts[r], r << 1) for r in (1, 2, 3)]
    mine = by_source(came, p)
    wb = along_column(mine.reshape(-1, mine.shape[2]))
    return gathered, wb, along_column(w_down)


def merged(came, w_down, p):
    rows, columns = came[0].shape
    ff_rows, width = w_down.shape
    tall = 4 * rows
    side = width * ff_rows // tall
    rest = width - side
    low = tall - ff_rows

    def kernel(p_ref, *refs):
        wd, out = refs[4:]
        for r in range(4):
            start = pl.multiple_of((p_ref[0] ^ r) * rows, 16)
            out[pl.ds(start, rows), :columns] = refs[r][...]
        out[:ff_rows, columns:] = wd[:, :side]
        for k in range(ff_rows // low):
            at = columns + k * rest
            out[ff_rows:, at : at + rest] = wd[k * low : (k + 1) * low, side:]

    return pl.pallas_call(
        kernel,
        out_shape=jax.ShapeDtypeStruct((tall, columns + side), w_down.dtype),
        in_specs=[pl.BlockSpec(memory_space=pltpu.SMEM)]
        + [pl.BlockSpec(memory_space=pltpu.VMEM)] * 5,
        compiler_params=pltpu.CompilerParams(vmem_limit_bytes=8 * 2**20),
        cost_estimate=NO_COST,
        name="merged",
    )(p[None], *came, w_down)


def w_down_from(whole, ff_rows, columns, width):
    side = whole.shape[1] - columns
    rest = width - side
    tall = width * ff_rows // side
    low = tall - ff_rows
    devices = whole.shape[0] // tall

    def kernel(ref, out, sem):
        copies = []
        for i in range(devices):
            top, to = i * tall, i * ff_rows
            pairs = [
                (
                    ref.at[pl.ds(top, ff_rows), pl.ds(columns, side)],
                    out.at[pl.ds(to, ff_rows), pl.ds(0, side)],
                )
            ]
            for k in range(ff_rows // low):
                pairs.append(
                    (
                        ref.at[pl.ds(top + ff_rows, low), pl.ds(columns + k * rest, rest)],
                        out.at[pl.ds(to + k * low, low), pl.ds(side, rest)],
                    )
                )
            for k, (source, target) in enumerate(pairs):
                copies.append(pltpu.make_async_copy(source, target, sem.at[i, k]))
        for copy in copies:
            copy.start()
        for copy in copies:
            copy.wait()

    return pl.pallas_call(
        kernel,
        out_shape=jax.ShapeDtypeStruct((devices * ff_rows, width), whole.dtype),
        in_specs=[pl.BlockSpec(memory_space=pl.ANY)],
        out_specs=pl.BlockSpec(memory_space=pltpu.VMEM),
        scratch_shapes=[pltpu.SemaphoreType.DMA((devices, 1 + ff_rows // low))],
        compiler_params=pltpu.CompilerParams(vmem_limit_bytes=2 * FFN_VMEM),
        cost_estimate=NO_COST,
        name="w_down_from",
    )(whole)


def unset(shape, dtype):
    return pl.pallas_call(
        lambda out: None,
        out_shape=jax.ShapeDtypeStruct(shape, dtype),
        out_specs=pl.BlockSpec(memory_space=pl.ANY),
        name="unset",
    )()


def packed(pieces):
    widths = [piece.shape[1] for piece in pieces]
    rows = pieces[0].shape[0]

    def kernel(*refs):
        out = refs[-1]
        at = 0
        for ref, size in zip(refs[:-1], widths):
            out[:, at : at + size] = ref[...]
            at += size

    return pl.pallas_call(
        kernel,
        out_shape=jax.ShapeDtypeStruct((rows, sum(widths)), pieces[0].dtype),
        compiler_params=pltpu.CompilerParams(vmem_limit_bytes=8 * 2**20),
        name="packed",
    )(*pieces)


def column_cuts_kernel(w_gate, w_up, p, part):
    rows, ff = w_gate.shape
    planes = ff // (4 * part)
    units = planes * part

    def kernel(p_ref, gate, up, *outs):
        for r, out in enumerate(outs):
            q = p_ref[0] ^ r
            for k in range(planes):
                start = pl.multiple_of((4 * k + q) * part, LANES)
                out[:, k * part : (k + 1) * part] = gate[:, pl.ds(start, part)]
                out[:, units + k * part : units + (k + 1) * part] = up[:, pl.ds(start, part)]

    shape = jax.ShapeDtypeStruct((rows, 2 * units), w_gate.dtype)
    return pl.pallas_call(
        kernel,
        out_shape=[shape] * 4,
        in_specs=[pl.BlockSpec(memory_space=pltpu.SMEM)]
        + [pl.BlockSpec(memory_space=pltpu.VMEM)] * 2,
        compiler_params=pltpu.CompilerParams(vmem_limit_bytes=8 * 2**20),
        name="column_cuts",
    )(p[None], w_gate, w_up)


def gather_weights(local, w_gate, w_up, w_down, place_bits):
    z, y, x, c = place_bits
    p = 2 * y + x
    rows, columns = local.shape
    ff_rows, width = w_down.shape
    end = (z == 0) | (z == 3)
    up_pairs = [(0, 1), (1, 2), (2, 3)]
    down_pairs = [(1, 0), (2, 1), (3, 2)]
    far_pairs = [(0, 2), (3, 1)]
    out_pairs = [(1, 0), (2, 3)]
    z_b = jnp.where(z == 0, 1, z - 1)
    z_c = jnp.where(z < 2, 2, jnp.where(z == 2, 3, 1))
    z_d = jnp.where(z < 2, 3, 0)
    out = unset((4, 2, 2, 2, rows, columns), BF)

    def near_side(up, down):
        return jnp.where(z == 0, down, up)

    def to_pass_on(up, down):
        return jnp.where(z == 1, down, up)

    def put_x(out, piece, z_k, at_y, core):
        return place(out, piece[None, None, :, None], (z_k, at_y, 0, core, 0, 0))

    def put_y(out, piece, z_k, at_x, core):
        return place(out, piece[None, :, None, None], (z_k, 0, at_x, core, 0, 0))

    def in_order(bit, mine, theirs):
        return jnp.stack([jnp.where(bit == 0, mine, theirs), jnp.where(bit == 0, theirs, mine)])

    def put(out, pair, z_a, z_b, at_y, at_x, core):
        out = put_x(out, pair[0], z_a, at_y, core)
        return put_y(out, pair[1], z_b, at_x, core)

    with jax.named_scope("phase_0"):
        cuts = column_cuts_kernel(w_gate, w_up, p, 2 * ff_rows)
        crossing = (swap(cuts[1], 2), swap(cuts[2], 4), swap(cuts[3], 6))
        up, down = tied(along_z(local, up_pairs), along_z(local, down_pairs))
    with jax.named_scope("phase_1"):
        b = near_side(up, down)
        a, b, passing = tied(local, b, to_pass_on(up, down))
        a_x, b_y, far, first = tied(
            swap(a, 2), swap(b, 4), along_z(a, far_pairs), along_z(passing, out_pairs)
        )
    with jax.named_scope("phase_2"):
        a2, b2, far = tied(in_order(x, a, a_x), in_order(y, b, b_y), far)
        near_1 = jnp.stack([a2, b2])
        ffn = merged((cuts[0], *tied(*crossing)), w_down, p)
        a_far, b_far, second, core_1 = tied(
            swap(a2, 4), swap(b2, 2), along_z(far, out_pairs), swap(near_1, 1)
        )
        out = put(out, near_1, z, z_b, y, x, c)
    with jax.named_scope("ffn_weights"):
        ffn = along_column(tied(ffn, second)[0])
    with jax.named_scope("phase_3"):
        a, b = jnp.where(end, first, down), jnp.where(end, second, far)
        a, b, far_1 = tied(a, b, jnp.stack([a_far, b_far]))
        a_x, b_y, core_2 = tied(swap(a, 2), swap(b, 4), swap(far_1, 1))
        out = put(out, core_1, z, z_b, y, x, 1 - c)
        out = put(out, far_1, z, z_b, 1 - y, 1 - x, c)
    with jax.named_scope("phase_4"):
        a2, b2 = tied(in_order(x, a, a_x), in_order(y, b, b_y))
        near_2 = jnp.stack([a2, b2])
        a_far, b_far, core_3 = tied(swap(a2, 4), swap(b2, 2), swap(near_2, 1))
        out = put(out, core_2, z, z_b, 1 - y, 1 - x, 1 - c)
        out = put(out, near_2, z_c, z_d, y, x, c)
    with jax.named_scope("phase_5"):
        far_2 = jnp.stack([a_far, b_far])
        core_4 = swap(far_2, 1)
        out = put(out, core_3, z_c, z_d, y, x, 1 - c)
        out = put(out, far_2, z_c, z_d, 1 - y, 1 - x, c)
        out = put(out, core_4, z_c, z_d, 1 - y, 1 - x, 1 - c)
        gathered = out.reshape(32 * rows, columns)
    return gathered, ffn


class PlaneSum:
    def __init__(self, left, grads):
        self.left, self.grads = left, grads
        self.own = left.shape[1] // 2
        self.first = self.own // 2
        self.tall = self.first // 4

    def step_0(self):
        return swap(t_mm(self.left[:, self.own :], self.grads).astype(BF), 1)

    def step_1(self, came):
        first, both = self.first, 2 * self.tall
        sent = t_mm(self.left[:, :first], self.grads) + came[:first].astype(F32)
        sent = sent.astype(BF)
        self.rest = t_mm(self.left[:, first : self.own], self.grads) + came[first:].astype(F32)
        return (swap(sent[:both], 4), swap(sent[both:], 2))

    def step_2(self, came):
        self.came, tall = came, self.tall
        a = self.rest[:tall] + came[0][tall:].astype(F32)
        b = self.rest[tall : 2 * tall] + came[1][tall:].astype(F32)
        return (swap(a.astype(BF), 2), swap(b.astype(BF), 4))

    def step_3(self, came, rows):
        tall = self.tall
        sums = []
        for i in (0, 1):
            own = self.rest[(2 + i) * tall : (3 + i) * tall]
            own = own + self.came[i][:tall].astype(F32) + came[i].astype(F32)
            sums.append(own.reshape(tall // rows, rows, -1))
        return jnp.concatenate(sums)


def selection(source):
    return (jnp.arange(source.shape[0])[:, None] == source[None, :]).astype(BF)


def column_order(count, rows):
    place_of, row = jnp.arange(count) // rows, jnp.arange(count) % rows
    z, core, y, x = place_of // 8, place_of // 4 % 2, place_of // 2 % 2, place_of % 2
    return selection((8 * z + 4 * y + 2 * x + core) * rows + row)


def sending_order(count, rows, place_bits):
    z, y, x, c = place_bits
    at = jnp.arange(count)
    group, within = at // (count // 16) % 8, at % (count // 16)
    upper = jnp.isin(group, jnp.array([2, 3, 5, 7]))
    x_differs = jnp.isin(group, jnp.array([1, 2, 3, 4]))
    y_differs = jnp.isin(group, jnp.array([0, 1, 3, 5]))
    core = c ^ (at // (count // 2))
    planes = count // rows // 8
    z_of = upper * (planes // 2) + within // rows
    chip = 4 * z_of + 2 * (y ^ y_differs.astype(jnp.int32)) + (x ^ x_differs.astype(jnp.int32))
    return selection((2 * chip + core) * rows + within % rows)


def split_gather(rows, beside=(), then=lambda pieces, *values: values):
    half = rows.shape[0] // 2
    a, b = rows[:half], rows[half:]
    a_x, b_y, *beside = tied(swap(a, 2), swap(b, 4), *beside)
    a2, b2 = tied(jnp.concatenate([a, a_x]), jnp.concatenate([b, b_y]))
    a_far, b_far, *beside = tied(swap(a2, 4), swap(b2, 2), *then((a2, b2), *beside))
    return ((a_far, b_far), *beside)


def split_reduce(near, far, beside=(), later=lambda *values: values):
    two = far[0].shape[0]
    one = two // 2
    came_a, came_b, *beside = tied(swap(far[0], 4), swap(far[1], 2), *beside)
    send_a = near[one:two] + came_a[one:].astype(F32)
    send_b = near[two + one :] + came_b[one:].astype(F32)
    own_a, own_b, *beside = tied(
        swap(send_a.astype(BF), 2), swap(send_b.astype(BF), 4), *later(*beside)
    )
    own_a = near[:one] + came_a[:one].astype(F32) + own_a.astype(F32)
    own_b = near[two : two + one] + came_b[:one].astype(F32) + own_b.astype(F32)
    own = jnp.concatenate([own_a, own_b])
    return (own, *beside)


def spread_columns(came, p, part):
    units = came[0].shape[1] // 2
    natural = []
    for q in range(4):
        piece = came[3]
        for r in (0, 1, 2):
            piece = jnp.where(p == (q ^ r), came[r], piece)
        natural.append(piece.astype(F32))
    return tuple(
        jnp.concatenate(
            [
                natural[q][:, start + k * part : start + (k + 1) * part]
                for k in range(units // part)
                for q in range(4)
            ],
            axis=1,
        )
        for start in (0, units)
    )


def rotation_tables(length, width):
    half_width = width // 2
    position = jnp.arange(length, dtype=F32)[:, None]
    freq_rate = ROPE_BASE ** (-2.0 * jnp.arange(half_width, dtype=F32) / width)
    angle_table = position * freq_rate[None, :]
    return (jnp.cos(angle_table)[:, None, :], jnp.sin(angle_table)[:, None, :])


HEADS_AT_ONCE = 8


def rotation_lanes():
    cosine, sine = rotation_tables(SEQ, HEAD_SIZE)
    lanes = HEADS_AT_ONCE * 2
    return (jnp.tile(cosine[:, 0], (1, lanes)), jnp.tile(sine[:, 0], (1, lanes)))


def turned(value, cosine, sine, back):
    size = value.shape[1]
    half = HEAD_SIZE // 2
    lane = lax.broadcasted_iota(jnp.int32, value.shape, 1)
    right = pltpu.roll(value, size - half, 1)
    left = pltpu.roll(value, half, 1)
    first = lane % HEAD_SIZE < half
    other = jnp.where(first, right, -left) if back else jnp.where(first, -right, left)
    return value * cosine + other * sine


def lanes_of(shape):
    return lax.broadcasted_iota(jnp.int32, shape, 1)


def head_of(value, i):
    start = i * HEAD_SIZE
    window = start // LANES * LANES
    offset = start - window
    size = LANES if offset + HEAD_SIZE <= LANES else 2 * LANES
    head = value[:, window : window + size]
    if offset:
        head = pltpu.roll(head, size - offset, 1)
    head = head[:, :LANES]
    return jnp.where(lanes_of(head.shape) < HEAD_SIZE, head, 0.0)


def side_by_side(heads):
    lane = lanes_of(heads[0].shape)
    second = pltpu.roll(heads[1], 96, 1)
    third = pltpu.roll(heads[2], 64, 1)
    fourth = pltpu.roll(heads[3], 32, 1)
    return jnp.concatenate(
        [
            jnp.where(lane < 96, heads[0], second),
            jnp.where(lane < 64, second, third),
            jnp.where(lane < 32, third, fourth),
        ],
        axis=1,
    )


def row_softmax(query, key):
    scores = lax.dot_general(
        query, key, (((1,), (1,)), ((), ())), preferred_element_type=F32
    ) * (1.0 / math.sqrt(HEAD_SIZE))
    row = lax.broadcasted_iota(jnp.int32, scores.shape, 0)
    column = lax.broadcasted_iota(jnp.int32, scores.shape, 1)
    scores = jnp.where(row >= column, scores, MASK_FILL)
    weights = jnp.exp(scores - jnp.max(scores, axis=1, keepdims=True))
    return weights * (1.0 / jnp.sum(weights, axis=1, keepdims=True))


def attention_blocks(width, kv_width):
    q_size = HEADS_AT_ONCE * HEAD_SIZE
    kv_size = q_size * kv_width // width
    return q_size, kv_size


def attention_forward(raw, cosine, sine, width, kv_width):
    count = raw.shape[0]
    q_size, kv_size = attention_blocks(width, kv_width)
    steps = width // q_size
    per_kv = width // kv_width

    def kernel(q_raw, k_raw, v_raw, cosine, sine, q_out, k_out, v_out, mixed):
        q = turned(q_raw[...], cosine[...], sine[...], False).astype(BF)
        k = turned(k_raw[...], cosine[:, :kv_size], sine[:, :kv_size], False).astype(BF)
        v = v_raw[...].astype(BF)
        q_out[...] = q
        k_out[...] = k
        v_out[...] = v
        q, k, v = q.astype(F32), k.astype(F32), v.astype(F32)
        for group in range(HEADS_AT_ONCE // 4):
            outs = []
            for i in range(4 * group, 4 * group + 4):
                if i % per_kv == 0:
                    key = head_of(k, i // per_kv).astype(BF)
                    value = head_of(v, i // per_kv).astype(BF)
                probs = row_softmax(head_of(q, i).astype(BF), key)
                outs.append(jnp.dot(probs.astype(BF), value, preferred_element_type=F32))
            mixed[:, 384 * group : 384 * group + 384] = side_by_side(outs).astype(BF)

    def block(size, at):
        return pl.BlockSpec((SEQ, size), lambda s, j: (s, at // size + j))

    table = pl.BlockSpec((SEQ, q_size), lambda s, j: (0, 0))
    return pl.pallas_call(
        kernel,
        grid=(count // SEQ, steps),
        out_shape=[
            jax.ShapeDtypeStruct((count, width), BF),
            jax.ShapeDtypeStruct((count, kv_width), BF),
            jax.ShapeDtypeStruct((count, kv_width), BF),
            jax.ShapeDtypeStruct((count, width), BF),
        ],
        in_specs=[
            block(q_size, 0),
            block(kv_size, width),
            block(kv_size, width + kv_width),
            table,
            table,
        ],
        out_specs=[block(q_size, 0), block(kv_size, 0), block(kv_size, 0), block(q_size, 0)],
        compiler_params=pltpu.CompilerParams(vmem_limit_bytes=16 * 2**20),
        cost_estimate=NO_COST,
        name="attention_forward",
    )(raw, raw, raw, cosine, sine)


def attention_backward(grad_mixed, q, k, v, cosine, sine):
    count, width = q.shape
    kv_width = k.shape[1]
    q_size, kv_size = attention_blocks(width, kv_width)
    steps = width // q_size
    per_kv = width // kv_width
    scale = 1.0 / math.sqrt(HEAD_SIZE)
    rows_rows = (((0,), (0,)), ((), ()))
    lanes_lanes = (((1,), (1,)), ((), ()))

    def kernel(d_ref, q_ref, k_ref, v_ref, cosine, sine, out):
        d, q = d_ref[...].astype(F32), q_ref[...].astype(F32)
        k, v = k_ref[...].astype(F32), v_ref[...].astype(F32)
        d_q, d_k, d_v = [], [], []
        for i in range(HEADS_AT_ONCE):
            if i % per_kv == 0:
                key = head_of(k, i // per_kv).astype(BF)
                value = head_of(v, i // per_kv).astype(BF)
            query, upstream = head_of(q, i).astype(BF), head_of(d, i).astype(BF)
            probs = row_softmax(query, key)
            d_probs = lax.dot_general(upstream, value, lanes_lanes, preferred_element_type=F32)
            d_scores = probs * (d_probs - jnp.sum(probs * d_probs, axis=1, keepdims=True))
            d_scores = d_scores.astype(BF)
            d_q.append(jnp.dot(d_scores, key, preferred_element_type=F32) * scale)
            part_k = lax.dot_general(d_scores, query, rows_rows, preferred_element_type=F32)
            part_v = lax.dot_general(
                probs.astype(BF), upstream, rows_rows, preferred_element_type=F32
            )
            if i % per_kv == 0:
                d_k.append(part_k)
                d_v.append(part_v)
            else:
                d_k[-1] += part_k
                d_v[-1] += part_v
        d_q = jnp.concatenate([side_by_side(d_q[g : g + 4]) for g in range(0, len(d_q), 4)], axis=1)
        d_q = turned(d_q, cosine[...], sine[...], True).astype(BF)
        d_k = side_by_side([part * scale for part in d_k])
        d_k = turned(d_k, cosine[:, :kv_size], sine[:, :kv_size], True).astype(BF)
        j = pl.program_id(1)
        out[:, pl.ds(pl.multiple_of(j * q_size, LANES), q_size)] = d_q
        at = pl.multiple_of(width + j * kv_size, LANES)
        out[:, pl.ds(at, kv_size)] = d_k
        at = pl.multiple_of(width + kv_width + j * kv_size, LANES)
        out[:, pl.ds(at, kv_size)] = side_by_side(d_v).astype(BF)

    def block(size):
        return pl.BlockSpec((SEQ, size), lambda s, j: (s, j))

    table = pl.BlockSpec((SEQ, q_size), lambda s, j: (0, 0))
    return pl.pallas_call(
        kernel,
        grid=(count // SEQ, steps),
        out_shape=jax.ShapeDtypeStruct((count, width + 2 * kv_width), BF),
        in_specs=[block(q_size), block(q_size), block(kv_size), block(kv_size), table, table],
        out_specs=pl.BlockSpec((SEQ, width + 2 * kv_width), lambda s, j: (s, 0)),
        compiler_params=pltpu.CompilerParams(vmem_limit_bytes=16 * 2**20),
        cost_estimate=NO_COST,
        name="attention_backward",
    )(grad_mixed, q, k, v, cosine, sine)


def norm_rows(field_in, gain_vec):
    inv_scale = lax.rsqrt(jnp.mean(field_in * field_in, axis=-1, keepdims=True) + EPSILON)
    return (field_in * inv_scale * gain_vec, inv_scale)


def norm_back(upstream, field_in, inv_scale, gain_vec):
    gain_grad = jnp.sum(upstream * field_in * inv_scale, axis=0)
    scaled_up = upstream * gain_vec
    field_grad = inv_scale * scaled_up - field_in * inv_scale**3 * jnp.mean(
        scaled_up * field_in, axis=-1, keepdims=True
    )
    return (gain_grad, field_grad)


def ffn_forward(rows, w_both, w_down):
    units = w_down.shape[0]
    pre = mm(rows, w_both[:, : 2 * units])
    hidden = (jax.nn.silu(pre[:, :units]) * pre[:, units:]).astype(BF)
    return (mm(hidden, w_down), pre, hidden)


def ffn_backward(grad_low, pre, w_both, w_down):
    grad_hidden = mm_t(grad_low, w_down)
    units = w_down.shape[0]
    gate_pre, up_pre = pre[:, :units], pre[:, units:]
    gate_sigmoid = jax.nn.sigmoid(gate_pre)
    grad_gate = grad_hidden * up_pre * gate_sigmoid * (1.0 + gate_pre * (1.0 - gate_sigmoid))
    grad_up = grad_hidden * gate_pre * gate_sigmoid
    grads = jnp.concatenate([grad_gate.astype(BF), grad_up.astype(BF)], axis=1)
    return (mm_t(grads, w_both[:, : 2 * units]), grads)


FFN_TILE = 256
FFN_VMEM = 24 * 2**20


def tiles_of(w_both, w_down, units):
    width = w_down.shape[1]
    steps = units // FFN_TILE
    return [
        pl.BlockSpec((width, FFN_TILE), lambda j: (0, j)),
        pl.BlockSpec((width, FFN_TILE), lambda j: (0, j + steps)),
        pl.BlockSpec((FFN_TILE, width), lambda j: (j, 0)),
    ]


def whole(array):
    return pl.BlockSpec(array.shape, lambda j: (0,) * array.ndim)


def sigmoid(value):
    return 1.0 / (1.0 + jnp.exp(-value))


def ffn_forward_beside(pieces, w_both, w_down):
    units, width = w_down.shape
    steps = units // FFN_TILE
    sizes = [piece.shape[0] for piece in pieces]
    count = sum(sizes)
    kinds = ((width, BF), (units, BF), (units, F32), (units, F32))
    kept_specs = [
        pl.BlockSpec((count, width), lambda j: (0, 0)),
        pl.BlockSpec((count, FFN_TILE), lambda j: (0, j)),
        pl.BlockSpec((count, FFN_TILE), lambda j: (0, j)),
        pl.BlockSpec((count, FFN_TILE), lambda j: (0, j)),
    ]
    first = len(pieces) + 3

    def kernel(*refs):
        w_gate, w_up, w_low = refs[len(pieces) : first]
        y, rows, hidden, gate, up, total = refs[-6:]
        j = pl.program_id(0)

        @pl.when(j == 0)
        def _():
            at = 0
            for ref, size in zip(refs, sizes):
                rows[at : at + size] = ref[...]
                at += size

        gate_pre = jnp.dot(rows[...], w_gate[...], preferred_element_type=F32)
        up_pre = jnp.dot(rows[...], w_up[...], preferred_element_type=F32)
        gate[...] = gate_pre
        up[...] = up_pre
        hid = (gate_pre * sigmoid(gate_pre) * up_pre).astype(BF)
        hidden[...] = hid
        part = jnp.dot(hid, w_low[...], preferred_element_type=F32)

        @pl.when(j == 0)
        def _():
            total[...] = part

        @pl.when(j > 0)
        def _():
            total[...] += part

        @pl.when(j == steps - 1)
        def _():
            y[...] = total[...].astype(y.dtype)

    y_shape = jax.ShapeDtypeStruct((count, width), F32)
    outs = pl.pallas_call(
        kernel,
        grid=(steps,),
        out_shape=[y_shape] + [jax.ShapeDtypeStruct((count, w), t) for w, t in kinds],
        in_specs=[whole(piece) for piece in pieces]
        + tiles_of(w_both, w_down, units),
        out_specs=[whole(y_shape)] + kept_specs,
        scratch_shapes=[pltpu.VMEM((count, width), F32)],
        compiler_params=pltpu.CompilerParams(vmem_limit_bytes=FFN_VMEM),
        cost_estimate=NO_COST,
        name="ffn_forward_beside",
    )(*pieces, w_both, w_both, w_down)
    return tuple(outs)


def ffn_backward_beside(pieces, gate_pre, up_pre, w_both, w_down):
    units, width = w_down.shape
    steps = units // FFN_TILE
    sizes = [piece.shape[0] for piece in pieces]
    count = sum(sizes)
    kinds = ((width, BF), (2 * units, BF))
    kept_specs = [
        pl.BlockSpec((count, width), lambda j: (0, 0)),
        pl.BlockSpec((count, 2 * units), lambda j: (0, 0)),
    ]
    pre_spec = pl.BlockSpec((count, FFN_TILE), lambda j: (0, j))
    first = len(pieces) + 5
    dims = (((1,), (1,)), ((), ()))

    def kernel(*refs):
        gate, up, w_gate, w_up, w_low = refs[len(pieces) : first]
        m, rows, grads, total = refs[-4:]
        j = pl.program_id(0)

        @pl.when(j == 0)
        def _():
            at = 0
            for ref, size in zip(refs, sizes):
                rows[at : at + size] = ref[...]
                at += size

        grad_hidden = lax.dot_general(rows[...], w_low[...], dims, preferred_element_type=F32)
        g = gate[...]
        s = sigmoid(g)
        grad_gate = (grad_hidden * up[...] * s * (1.0 + g * (1.0 - s))).astype(BF)
        grad_up = (grad_hidden * g * s).astype(BF)
        start = pl.multiple_of(j * FFN_TILE, LANES)
        grads[:, pl.ds(start, FFN_TILE)] = grad_gate
        grads[:, pl.ds(start + units, FFN_TILE)] = grad_up
        part = lax.dot_general(grad_gate, w_gate[...], dims, preferred_element_type=F32)
        part += lax.dot_general(grad_up, w_up[...], dims, preferred_element_type=F32)

        @pl.when(j == 0)
        def _():
            total[...] = part

        @pl.when(j > 0)
        def _():
            total[...] += part

        @pl.when(j == steps - 1)
        def _():
            m[...] = total[...].astype(m.dtype)

    m_shape = jax.ShapeDtypeStruct((count, width), F32)
    outs = pl.pallas_call(
        kernel,
        grid=(steps,),
        out_shape=[m_shape] + [jax.ShapeDtypeStruct((count, w), t) for w, t in kinds],
        in_specs=[whole(piece) for piece in pieces]
        + [pre_spec] * 2
        + tiles_of(w_both, w_down, units),
        out_specs=[whole(m_shape)] + kept_specs,
        scratch_shapes=[pltpu.VMEM((count, width), F32)],
        compiler_params=pltpu.CompilerParams(vmem_limit_bytes=FFN_VMEM),
        cost_estimate=NO_COST,
        name="ffn_backward_beside",
    )(*pieces, gate_pre, up_pre, w_both, w_both, w_down)
    return tuple(outs)


def input_gradient(grad_raw, weights, tokens, inv_scale, gain, grad_res):
    count, wide = grad_raw.shape
    width = tokens.shape[1]
    tile = 2 * FFN_TILE
    steps = wide // tile

    def kernel(grads, w, tokens, inv_scale, gain, grad_res, out, gain_grad, total):
        j = pl.program_id(0)
        part = lax.dot_general(
            grads[...], w[...], (((1,), (1,)), ((), ())), preferred_element_type=F32
        )

        @pl.when(j == 0)
        def _():
            total[...] = part

        @pl.when(j > 0)
        def _():
            total[...] += part

        @pl.when(j == steps - 1)
        def _():
            up, field, inv = total[...], tokens[...].astype(F32), inv_scale[...]
            gain_grad[...] = jnp.sum(up * field * inv, axis=0, keepdims=True)
            scaled = up * gain[...]
            mean = jnp.mean(scaled * field, axis=1, keepdims=True)
            grad = inv * scaled - field * (inv * inv * inv) * mean
            out[...] = (grad_res[...] + grad).astype(BF)

    return pl.pallas_call(
        kernel,
        grid=(steps,),
        out_shape=[
            jax.ShapeDtypeStruct((count, width), BF),
            jax.ShapeDtypeStruct((1, width), F32),
        ],
        in_specs=[
            pl.BlockSpec((count, tile), lambda j: (0, j)),
            pl.BlockSpec((width, tile), lambda j: (0, j)),
            whole(tokens),
            whole(inv_scale),
            whole(gain),
            whole(grad_res),
        ],
        out_specs=[
            pl.BlockSpec((count, width), lambda j: (0, 0)),
            pl.BlockSpec((1, width), lambda j: (0, 0)),
        ],
        scratch_shapes=[pltpu.VMEM((count, width), F32)],
        compiler_params=pltpu.CompilerParams(vmem_limit_bytes=2 * FFN_VMEM),
        cost_estimate=NO_COST,
        name="input_gradient",
    )(grad_raw, weights, tokens, inv_scale, gain, grad_res)


def products(lefts, rights, dtype):
    rows, columns = lefts[0].shape[1], rights[0].shape[1]
    tile = columns // 4
    count = len(lefts)

    def kernel(*refs):
        total = None
        for a, b in zip(refs[:count], refs[count : 2 * count]):
            part = lax.dot_general(
                a[...], b[...], (((0,), (0,)), ((), ())), preferred_element_type=F32
            )
            total = part if total is None else total + part
        refs[-1][...] = total.astype(dtype)

    return pl.pallas_call(
        kernel,
        grid=(columns // tile,),
        out_shape=jax.ShapeDtypeStruct((rows, columns), dtype),
        in_specs=[whole(left) for left in lefts]
        + [pl.BlockSpec((right.shape[0], tile), lambda j: (0, j)) for right in rights],
        out_specs=pl.BlockSpec((rows, tile), lambda j: (0, j)),
        compiler_params=pltpu.CompilerParams(vmem_limit_bytes=FFN_VMEM),
        cost_estimate=NO_COST,
        name="products",
    )(*lefts, *rights)


def body(
    tokens,
    teacher,
    valid_mask,
    w_query,
    key_weight_matrix,
    value_weight_matrix,
    w_output,
    w_gate,
    w_up,
    w_down,
    attn_gain,
    ffn_gain,
):
    n = lax.axis_size("dp")
    planes = n // 8
    position = lax.axis_index("dp")
    c, x, y, z = position % 2, position // 2 % 2, position // 4 % 2, position // 8
    bits = (z, y, x, c)
    p = position // 2 % 4
    rows = w_query.shape[0]
    width = w_query.shape[1]
    kv_width = key_weight_matrix.shape[1]
    ff_rows = w_down.shape[0]
    ff = w_gate.shape[1]
    count = tokens.shape[0]
    cosine, sine = rotation_lanes()
    to_column, to_senders = tied(column_order(width, rows), sending_order(width, rows, bits))

    part = 2 * ff_rows
    units = planes * part
    gains = jnp.stack([attn_gain, ffn_gain], axis=1)
    gains = jnp.pad(gains, ((0, 0), (0, LANES - 2)))
    local = packed([w_query, key_weight_matrix, value_weight_matrix, w_output, gains])
    if planes == 4:
        gathered, wb = gather_weights(local, w_gate, w_up, w_down, bits)
        wd = w_down_from(wb, ff_rows, 2 * units, width)
    else:
        gathered, wb, wd = gather_weights_plainly(local, w_gate, w_up, w_down, p)

    with jax.named_scope("attention_forward"):
        wide = width + 2 * kv_width
        wqkv = gathered[:, :wide]
        wo = gathered[:, wide : wide + width]
        gain_in = gathered[:, wide + width].astype(F32)
        gain_mid = gathered[:, wide + width + 1].astype(F32)
        inputs_f = tokens.astype(F32)
        normed, inv_attn = norm_rows(inputs_f, gain_in)
        normed_in = tied(normed.astype(BF))[0]
        raw = mm(normed_in, wqkv)
        query, key, value, mixed = attention_forward(raw, cosine, sine, width, kv_width)
        hidden_res = inputs_f + mm(mixed, wo)
        normed_two, inv_ffn = norm_rows(hidden_res, gain_mid)
        normed_mid = normed_two.astype(BF)

    with jax.named_scope("ffn_forward"):
        far, y_near, *kept = split_gather(
            mm(normed_mid, to_column).astype(BF),
            (),
            lambda pieces: ffn_forward_beside(pieces, wb, wd),
        )
        near, hid_near, gate_near, up_near = kept
        y_a, pre_a, hid_a = ffn_forward(far[0], wb, wd)
        y_b, pre_b, hid_b = ffn_forward(far[1], wb, wd)
        y_a, y_b = y_a.astype(BF), y_b.astype(BF)
        y_b, mixed, normed_in = tied(y_b, mixed, normed_in)
        beside = (mm(mixed, to_senders).astype(BF), mm(normed_in, to_senders).astype(BF))
        result, mixed_sent, normed_sent = split_reduce(y_near, (y_a, y_b), beside)
        result = hidden_res + result
        out_act = result.astype(BF)

    with jax.named_scope("loss"):
        mask_f = valid_mask.astype(F32)
        grad_out = (result - teacher.astype(F32)) * mask_f[:, None]

    high = n // 2
    rest = [1 << k for k in range(4, n.bit_length() - 2)]

    with jax.named_scope("ffn_backward"):
        d_far, m_near, d_near, g_near = split_gather(
            grad_out.astype(BF),
            (),
            lambda pieces: ffn_backward_beside(pieces, gate_near, up_near, wb, wd),
        )
        m_a, g_a = ffn_backward(d_far[0], pre_a, wb, wd)
        m_b, g_b = ffn_backward(d_far[1], pre_b, wb, wd)
        m_b, m_near, grads = tied(m_b.astype(BF), m_near, grad_out)
        sums = jnp.stack([jnp.sum(grads * grads), jnp.sum(mask_f)])
        sums = jnp.broadcast_to(sums[:, None], (2, LANES))
        came = swap(sums, 1)
        beside = (products([near, *far], [g_near, g_a, g_b], BF), sums, came)

        owned_both = []

        def later(g_both, sums, came):
            owned_both.append(sum_to_owners(g_both))
            sums = sums + came
            g_down = products([hid_near, hid_a, hid_b], [d_near, *d_far], BF)
            return (g_down, sums, swap(sums, 8))

        grad_mid, g_down, sums, came = split_reduce(
            m_near, (m_a.astype(BF), m_b), beside, later
        )
        g_both = owned_both[0]
        sums = sums + came
        for mask in rest:
            sums = sums + swap(sums, mask)
        high_part = grad_mid.astype(BF)
        low_part = (grad_mid - high_part.astype(F32)).astype(BF)
        grad_mid = mm_t(high_part, to_column) + mm_t(low_part, to_column)

    with jax.named_scope("attention_backward"):
        grad_gain_mid, grad_res = norm_back(grad_mid, hidden_res, inv_ffn, gain_mid)
        grad_res = grad_out + grad_res
        res_low = grad_res.astype(BF)
        g_wo = PlaneSum(mixed_sent, res_low)
        wo_came, came, grad_mixed = tied(
            g_wo.step_0(), swap(sums, high), mm_t(res_low, wo).astype(BF)
        )
        sums = sums + came
        wo_moving = g_wo.step_1(wo_came)
        grad_raw = attention_backward(grad_mixed, query, key, value, cosine, sine)
        *wo_came, grad_raw, sums, came = tied(*wo_moving, grad_raw, sums, swap(sums, 2))
        sums = sums + came
        wo_moving = g_wo.step_2(wo_came)

    with jax.named_scope("input_gradient"):
        input_grad, grad_gain_in = input_gradient(
            grad_raw, gathered, tokens, inv_attn, gain_in[None], grad_res
        )
        gains = jnp.concatenate([grad_gain_in, grad_gain_mid[None]])

    with jax.named_scope("q_k_v_weight_gradients"):
        g_qkv = PlaneSum(normed_sent, grad_raw)
        qkv_came, gains, sums, came, g_both, g_down, *wo_came = tied(
            g_qkv.step_0(), gains, sums, swap(sums, 4), g_both, g_down, *wo_moving
        )
        g_down = sum_to_owners(g_down)
        sums = sums + came
        loss = sums[0, 0] / (sums[1, 0] * width)
        qkv_moving = g_qkv.step_1(qkv_came)
        g_wo = g_wo.step_3(wo_came, rows)
        wo_moving = direct([g_wo], z) if planes == 4 else []

    with jax.named_scope("weight_gradients_to_owners"):
        for mask in (1, 8, high):
            gains = gains + swap(gains, mask)
        *qkv_came, gains = tied(*qkv_moving, gains)
        qkv_moving = g_qkv.step_2(qkv_came)
        *qkv_came, gains, g_both, g_down = tied(*qkv_moving, gains, g_both, g_down)
        g_qkv, g_both, *wo_came = tied(g_qkv.step_3(qkv_came, rows), g_both, *wo_moving)
        g_wo = owned([g_wo], wo_came, z) if planes == 4 else z_reduce([g_wo])
        if planes == 4:
            moving = direct([g_qkv], z)
        gains = gains + swap(gains, 2)
        gains, g_both = tied(gains, g_both)
        g_both = g_both.reshape(4, rows, 2 * units)
        came = [pick(g_both, p ^ r, 0) for r in range(4)]
        gains_came, *moved = tied(swap(gains, 4), *[swap(came[r], r << 1) for r in (1, 2, 3)])
        gains = gains + gains_came
        for mask in rest:
            gains = gains + swap(gains, mask)
        grad_gate, grad_up = spread_columns([came[0]] + moved, p, part)
        g_gains = lax.dynamic_slice_in_dim(gains, position * rows, rows, 1)
        if planes == 4:
            g_qkv = owned([g_qkv], moving, z)
        else:
            g_qkv = z_reduce([g_qkv])
        g_wq = g_qkv[:, :width]
        g_wk = g_qkv[:, width : width + kv_width]
        g_wv = g_qkv[:, width + kv_width :]

    return (
        out_act,
        loss,
        input_grad,
        g_wq,
        g_wk,
        g_wv,
        g_wo,
        grad_gate,
        grad_up,
        g_down.astype(F32),
        g_gains[0],
        g_gains[1],
    )


def solution(mesh):
    wide, flat = P("dp", None), P("dp")
    in_specs = (wide, wide, flat) + (wide,) * 7 + (flat, flat)
    out_specs = (wide, P(), wide) + (wide,) * 7 + (flat, flat)
    return jax.shard_map(body, mesh=mesh, in_specs=in_specs, out_specs=out_specs, check_vma=False)
```
